32 devices in a mesh: seq: 4 (over z), tm: 8 (over y, x, core).
Axes of the slice: x: 2, y: 2, z: 4, core: 2. Of those that a mesh axis runs over, the one named last changes fastest.
Arguments:
- inputs: bfloat16 [8, 1024, 2304], P('seq', 'tm'), may hold values from -6 to 6
- weight_one: bfloat16 [2, 3, 2304, 2304], P(None, None, 'tm'), may hold values from -0.09375 to 0.09375
- fbias_one: float32 [2304], P('tm'), may hold values from 2 to 9, as said below
- weight_two: bfloat16 [2, 3, 2304, 2304], P(None, None, 'tm'), may hold values from -0.09375 to 0.09375
- fbias_two: float32 [2304], P('tm'), may hold values from 2 to 9, as said below
- cotangent: bfloat16 [8, 1024, 2304], P('seq', 'tm'), may hold values from -6 to 6
- cluster_starts: int32 [8, 4], P('seq'), may hold values from 512 to 992
Outputs:
- hidden_two: bfloat16 [8, 1024, 2304], P('seq', 'tm')
- input_grad: bfloat16 [8, 1024, 2304], P('seq', 'tm')
- grad_weight_one: float32 [2, 3, 2304, 2304], P(None, None, 'tm')
- grad_fbias_one: float32 [2304], P('tm')
- grad_weight_two: float32 [2, 3, 2304, 2304], P(None, None, 'tm')
- grad_fbias_two: float32 [2304], P('tm')
The draws below stay inside these ranges and needn't reach their ends.
Inputs may be any that keep to these rules, and one draw needn't show every extreme that they name: `fbias_one`: forget gate biases, spread between fast and slow forgetting over the hidden units. `fbias_two`: forget gate biases, spread between fast and slow forgetting over the hidden units. `cluster_starts`: each start lies in the second half of its sequence, with room for a whole cluster; clusters may intersect.
All inputs are finite; a program needn't handle non-finite values.
Results may differ from the reference program's by a relative error of at most 0.011.
Values may be sent and summed in bfloat16 or wider, within the bound.
A program may use at most 320 MiB of HBM per device.

```python
import math
import jax
import jax.numpy as jnp
from jax import lax

D = 2304
SEQS = 2
KSPOT = 4
CLUSTER = 32
L = 1024
NSEQ = 8
N_SEQ = 4


def draw_bias_law(key):
    fraction = jax.random.uniform(key, (D,), jnp.float32)
    low_end = math.log(8.0)
    high_end = math.log(L) + 0.5
    return low_end + fraction * (high_end - low_end)


def draw_fbias_one(key, part):
    return draw_bias_law(jax.random.fold_in(key, 11))


def draw_fbias_two(key, part):
    return draw_bias_law(jax.random.fold_in(key, 23))


def set_ends(array, stream_key, least, high):
    place = [jax.random.randint(jax.random.fold_in(stream_key, axis), (), 0, length) for axis, length in enumerate(array.shape)]
    main_axis = array.shape.index(max(array.shape))
    neighbour = place[:main_axis] + [(place[main_axis] + 1) % array.shape[main_axis]] + place[main_axis + 1:]
    return array.at[tuple(place)].set(least).at[tuple(neighbour)].set(high)


def steps_of(rng, dims, cuts, low, top_value):
    gain, own = 1.0, jax.random.fold_in(rng, 6)
    for position, blocks in cuts:
        draws = jnp.exp(jax.random.uniform(jax.random.fold_in(own, position), (blocks,), jnp.float32, low / len(cuts), top_value / len(cuts)))
        gain = gain * jnp.repeat(draws, dims[position] // blocks).reshape([-1 if axis == position else 1 for axis in range(len(dims))])
    return gain


def noise(stream_key, dims, spread, reach, shards=(), kind=jnp.bfloat16):
    loudness = steps_of(stream_key, dims, shards, -0.22, 0.18) if shards else 1.0
    drawn = jax.random.normal(stream_key, dims, jnp.float32) * spread * loudness
    return jnp.minimum(jnp.maximum(drawn, -reach), reach).astype(kind)


def setup_inputs(seed: int = 0) -> dict:
    splits = jax.random.split(jax.random.key(seed), 8)
    return {
        "inputs": noise(splits[0], (NSEQ, L, D), 1.0, 6.0, ((0, 4), (1, 8))),
        "weight_one": noise(splits[1], (2, 3, D, D), (2 * D) ** -0.5, 0.09375, ((2, 8),)),
        "fbias_one": draw_fbias_one(jax.random.fold_in(splits[7], 71), 0),
        "weight_two": noise(splits[3], (2, 3, D, D), (2 * D) ** -0.5, 0.09375, ((2, 8),)),
        "fbias_two": draw_fbias_two(jax.random.fold_in(splits[7], 71), 0),
        "cotangent": noise(splits[5], (NSEQ, L, D), 1.0, 6.0, ((0, 4), (1, 8))),
        "cluster_starts": set_ends(jax.random.randint(splits[6], (NSEQ, KSPOT), L // 2, L - CLUSTER + 1), jax.random.fold_in(splits[6], 1), L // 2, L - CLUSTER).astype(jnp.int32),
    }


@jax.custom_vjp
def low(v):
    return lax.optimization_barrier(v.astype(jnp.bfloat16)).astype(jnp.float32)

@jax.custom_vjp
def low_back(v):
    return v

def low_keep(v):
    return (low(v), None)

def low_pass(kept, grad):
    return (grad,)

def back_keep(v):
    return (v, None)

def back_low(kept, grad):
    return (low(grad),)
low.defvjp(low_keep, low_pass)
low_back.defvjp(back_keep, back_low)

def affine_chain(earlier, later):
    return (earlier[0] * later[0], later[0] * earlier[1] + later[1])

def qrnn_layer(layer_in, weight, fbias):
    shifted = jnp.pad(layer_in[:, :-1], ((0, 0), (1, 0), (0, 0)))
    preact = jnp.einsum('gtd,khd->gtkh', layer_in, weight[0], precision=lax.Precision.HIGHEST)
    preact = preact + jnp.einsum('gtd,khd->gtkh', shifted, weight[1], precision=lax.Precision.HIGHEST)
    zero_row = jnp.zeros_like(fbias)
    preact = preact + jnp.stack([zero_row, fbias, zero_row])
    preact = low_back(low(preact))
    candidate = jnp.tanh(preact[:, :, 0])
    forget = jax.nn.sigmoid(preact[:, :, 1])
    outgate = jax.nn.sigmoid(preact[:, :, 2])
    cell_state = lax.associative_scan(affine_chain, (forget, (1.0 - forget) * candidate), axis=1)[1]
    return low_back(low(outgate * cell_state))

def two_layers(layer_in, wfirst, bfirst, wsecond, bsecond):
    return qrnn_layer(qrnn_layer(layer_in, wfirst, bfirst), wsecond, bsecond)

def reference(inputs, weight_one, fbias_one, weight_two, fbias_two, cotangent, cluster_starts):
    wfirst = weight_one.astype(jnp.float32)
    wsecond = weight_two.astype(jnp.float32)
    grouped_in = inputs.reshape(N_SEQ, SEQS, L, D)
    grouped_cot = cotangent.reshape(N_SEQ, SEQS, L, D)
    grouped_starts = cluster_starts.reshape(N_SEQ, SEQS, KSPOT)
    steps_all = jnp.arange(L, dtype=jnp.int32)

    def one_group(totals, item):
        group_in, group_cot, group_starts = item
        inside = (steps_all[None, None, :] >= group_starts[:, :, None]) & (steps_all[None, None, :] < group_starts[:, :, None] + CLUSTER)
        keep_mask = jnp.any(inside, axis=1)
        grad_seed = jnp.where(keep_mask[:, :, None], group_cot.astype(jnp.float32), jnp.float32(0.0))
        result, pullback = jax.vjp(two_layers, group_in.astype(jnp.float32), wfirst, fbias_one, wsecond, fbias_two)
        grad_in, grad_wa, grad_ba, grad_wb, grad_bb = pullback(grad_seed)
        totals = (totals[0] + grad_wa, totals[1] + grad_ba, totals[2] + grad_wb, totals[3] + grad_bb)
        return (totals, (result.astype(jnp.bfloat16), grad_in.astype(jnp.bfloat16)))
    start_totals = (jnp.zeros((2, 3, D, D), jnp.float32), jnp.zeros((D,), jnp.float32), jnp.zeros((2, 3, D, D), jnp.float32), jnp.zeros((D,), jnp.float32))
    totals, outputs = lax.scan(one_group, start_totals, (grouped_in, grouped_cot, grouped_starts))
    hidden_two = outputs[0].reshape(NSEQ, L, D)
    input_grad = outputs[1].reshape(NSEQ, L, D)
    return (hidden_two, input_grad, totals[0], totals[1], totals[2], totals[3])
```

```python
import functools

import jax
import jax.numpy as jnp
from jax import lax
from jax.experimental import pallas as pl
from jax.experimental.pallas import tpu as pltpu
from jax.sharding import PartitionSpec as P

CLUSTER = 32
LANES = 128
ROWS = 16
F32 = jnp.float32
BF16 = jnp.bfloat16


def sigmoid(v):
    return 0.5 * jnp.tanh(0.5 * v) + 0.5


def shift_lanes(v, amount, lane, fill):
    moved = pltpu.roll(v, amount % LANES, axis=1)
    gone = lane < amount if amount > 0 else lane >= LANES + amount
    return jnp.where(gone, fill, moved)


def lane_chain(factor, value, lane, sign):
    step = 1
    while step < LANES:
        value = value + factor * shift_lanes(value, sign * step, lane, 0.0)
        factor = factor * shift_lanes(factor, sign * step, lane, 1.0)
        step *= 2
    return value


def pool_forward(seq, p_ref, b_ref, pre_ref, cell_ref, h_ref, hidden, groups):
    lane = lax.broadcasted_iota(jnp.int32, (ROWS, LANES), 1)

    def tile(r, carry):
        rows = pl.ds(pl.multiple_of(r * ROWS, ROWS), ROWS)
        bias = b_ref[rows, :]

        def gate(g, j):
            cols = pl.ds(j * LANES, LANES)
            now = p_ref[g, rows, cols]
            if j:
                past = p_ref[3 + g, rows, pl.ds((j - 1) * LANES, LANES)]
            else:
                past = shift_lanes(p_ref[3 + g, rows, pl.ds((groups - 1) * LANES, LANES)], 1, lane, 0.0)
            total = now + past
            if g == 1:
                total = total + bias
            total = total.astype(BF16)
            pre_ref[seq, g, rows, cols] = total
            return total.astype(F32)

        factors, values = [], []
        for j in range(groups):
            candidate = jnp.tanh(gate(0, j))
            forget = sigmoid(gate(1, j))
            fresh = (1.0 - forget) * candidate
            if j:
                values.append(forget * values[-1] + fresh)
                factors.append(forget * factors[-1])
            else:
                values.append(fresh)
                factors.append(forget)
        entering = shift_lanes(lane_chain(factors[-1], values[-1], lane, 1), 1, lane, 0.0)
        for j in range(groups):
            cols = pl.ds(j * LANES, LANES)
            cell = values[j] + factors[j] * entering
            cell_ref[seq, rows, cols] = cell
            h_ref[seq, rows, cols] = (sigmoid(gate(2, j)) * cell).astype(BF16)
        return carry

    lax.fori_loop(0, hidden // ROWS, tile, 0)


def pool_backward(seq, g_ref, pre_ref, cell_ref, d_ref, db_ref, hidden, groups):
    lane = lax.broadcasted_iota(jnp.int32, (ROWS, LANES), 1)

    def tile(r, carry):
        rows = pl.ds(pl.multiple_of(r * ROWS, ROWS), ROWS)

        def at(j):
            return pl.ds(j * LANES, LANES)

        def put(g, j, v):
            v = v.astype(BF16)
            d_ref[seq, g, rows, at(j)] = v
            if j:
                d_ref[seq, 3 + g, rows, at(j - 1)] = v
            else:
                d_ref[seq, 3 + g, rows, at(groups - 1)] = shift_lanes(v.astype(F32), -1, lane, 0.0).astype(BF16)
            return v

        factors, values = [None] * groups, [None] * groups
        later = None
        for j in reversed(range(groups)):
            grad = g_ref[seq, rows, at(j)].astype(F32)
            own = grad * sigmoid(pre_ref[seq, 2, rows, at(j)].astype(F32))
            if later is None:
                values[j] = own
                factors[j] = jnp.ones_like(own)
            else:
                values[j] = own + later * values[j + 1]
                factors[j] = later * factors[j + 1]
            later = sigmoid(pre_ref[seq, 1, rows, at(j)].astype(F32))
        chain = lane_chain(later * factors[0], later * values[0], lane, -1)
        entering = shift_lanes(chain, -1, lane, 0.0)
        total = jnp.zeros((ROWS, LANES), F32)
        for j in range(groups):
            grad = g_ref[seq, rows, at(j)].astype(F32)
            carried = values[j] + factors[j] * entering
            candidate = jnp.tanh(pre_ref[seq, 0, rows, at(j)].astype(F32))
            forget = sigmoid(pre_ref[seq, 1, rows, at(j)].astype(F32))
            outgate = sigmoid(pre_ref[seq, 2, rows, at(j)].astype(F32))
            cell = cell_ref[seq, rows, at(j)]
            if j:
                before = cell_ref[seq, rows, at(j - 1)]
            else:
                before = shift_lanes(cell_ref[seq, rows, at(groups - 1)], 1, lane, 0.0)
            put(0, j, carried * (1.0 - forget) * (1.0 - candidate * candidate))
            total = total + put(1, j, carried * (before - candidate) * forget * (1.0 - forget)).astype(F32)
            put(2, j, grad * cell * outgate * (1.0 - outgate))
        db_ref[seq, rows, :] = jnp.sum(total, axis=1, keepdims=True)
        return carry

    lax.fori_loop(0, hidden // ROWS, tile, 0)


def products(w_ref, x_ref, p_ref, hidden, length, token_major):
    wide = 256

    def strip(c, carry):
        cols = pl.ds(pl.multiple_of(c * wide, wide), wide)
        if token_major:
            rhs, dims = x_ref[0, cols, :], (((1,), (1,)), ((), ()))
        else:
            rhs, dims = x_ref[0, :, cols], (((1,), (0,)), ((), ()))
        for k in range(6):
            p_ref[k, :, cols] = lax.dot_general(w_ref[k], rhs, dims, preferred_element_type=F32)
        return carry

    lax.fori_loop(0, length // wide, strip, 0)


def first_kernel(hidden, length, w_ref, b_ref, x_ref, pre_ref, cell_ref, h_ref, p_ref):
    products(w_ref, x_ref, p_ref, hidden, length, True)
    pool_forward(0, p_ref, b_ref, pre_ref, cell_ref, h_ref, hidden, length // LANES)


def second_kernel(hidden, length, w_ref, b_ref, x_ref, g_ref, h_ref, d_ref, db_ref, p_ref, pre_ref, cell_ref):
    products(w_ref, x_ref, p_ref, hidden, length, False)
    groups = length // LANES
    pool_forward(0, p_ref, b_ref, pre_ref, cell_ref, h_ref, hidden, groups)
    pool_backward(0, g_ref, pre_ref, cell_ref, d_ref, db_ref, hidden, groups)


def back_kernel(hidden, length, g_ref, pre_ref, cell_ref, d_ref, db_ref):
    pool_backward(0, g_ref, pre_ref, cell_ref, d_ref, db_ref, hidden, length // LANES)


def per_seq(*dims):
    return pl.BlockSpec((1,) + dims, lambda s: (s,) + (0,) * len(dims))


def whole(*dims):
    return pl.BlockSpec(dims, lambda s: (0,) * len(dims), pipeline_mode=pl.Buffered(1))


PARAMS = pltpu.CompilerParams(vmem_limit_bytes=62 * 1024 * 1024, dimension_semantics=("arbitrary",))


def run_first(weight, bias, gathered):
    seqs, length, width = gathered.shape
    hidden = weight.shape[1]
    shape = jax.ShapeDtypeStruct
    return pl.pallas_call(
        functools.partial(first_kernel, hidden, length),
        name="layer_one_forward",
        grid=(seqs,),
        in_specs=[whole(6, hidden, width), whole(hidden, 1), per_seq(length, width)],
        out_specs=[per_seq(3, hidden, length), per_seq(hidden, length), per_seq(hidden, length)],
        out_shape=[
            shape((seqs, 3, hidden, length), BF16),
            shape((seqs, hidden, length), F32),
            shape((seqs, hidden, length), BF16),
        ],
        scratch_shapes=[pltpu.VMEM((6, hidden, length), F32)],
        compiler_params=PARAMS,
    )(weight, bias, gathered)


def run_second(weight, bias, gathered, grad):
    seqs, width, length = gathered.shape
    hidden = weight.shape[1]
    shape = jax.ShapeDtypeStruct
    return pl.pallas_call(
        functools.partial(second_kernel, hidden, length),
        name="layer_two_forward_and_pool_backward",
        grid=(seqs,),
        in_specs=[whole(6, hidden, width), whole(hidden, 1), per_seq(width, length), per_seq(hidden, length)],
        out_specs=[per_seq(hidden, length), per_seq(6, hidden, length), per_seq(hidden, 1)],
        out_shape=[
            shape((seqs, hidden, length), BF16),
            shape((seqs, 6, hidden, length), BF16),
            shape((seqs, hidden, 1), F32),
        ],
        scratch_shapes=[
            pltpu.VMEM((6, hidden, length), F32),
            pltpu.VMEM((1, 3, hidden, length), BF16),
            pltpu.VMEM((1, hidden, length), F32),
        ],
        compiler_params=PARAMS,
    )(weight, bias, gathered, grad)


def run_back(grad, pre, cell):
    seqs, hidden, length = grad.shape
    shape = jax.ShapeDtypeStruct
    return pl.pallas_call(
        functools.partial(back_kernel, hidden, length),
        name="layer_one_pool_backward",
        grid=(seqs,),
        in_specs=[per_seq(hidden, length), per_seq(3, hidden, length), per_seq(hidden, length)],
        out_specs=[per_seq(6, hidden, length), per_seq(hidden, 1)],
        out_shape=[shape((seqs, 6, hidden, length), BF16), shape((seqs, hidden, 1), F32)],
        compiler_params=PARAMS,
    )(grad, pre, cell)


def per_device(inputs, weight_one, fbias_one, weight_two, fbias_two, cotangent, cluster_starts):
    seqs, span, width = inputs.shape
    count = lax.axis_size("tm")
    length = span * count
    groups = length // LANES
    part = LANES // count
    hidden = weight_one.shape[2]
    w1 = weight_one.reshape(6, hidden, width)
    w2 = weight_two.reshape(6, hidden, width)

    def to_columns(v):
        return v.reshape(seqs, part, groups, width).transpose(0, 2, 1, 3)

    steps = lax.axis_index("tm") * span + jnp.arange(span, dtype=jnp.int32)
    starts = cluster_starts[:, :, None]
    keep = jnp.any((steps >= starts) & (steps < starts + CLUSTER), axis=1)
    seed = jnp.where(keep[:, :, None], cotangent, jnp.zeros_like(cotangent))
    seed = seed.reshape(seqs, part, groups, count, hidden)
    seed = lax.all_to_all(seed, "tm", split_axis=3, concat_axis=1, tiled=True)
    seed = seed.reshape(seqs, LANES, groups, hidden).transpose(0, 3, 2, 1).reshape(seqs, hidden, length)

    x = lax.all_gather(to_columns(inputs), "tm", axis=2, tiled=True).reshape(seqs, length, width)
    pre1, cell1, h1 = run_first(w1, fbias_one[:, None], x)
    h1 = lax.all_gather(h1, "tm", axis=1, tiled=True)
    h2, d2, db2 = run_second(w2, fbias_two[:, None], h1, seed)

    out = h2.reshape(seqs, hidden, groups, count, part)
    out = lax.all_to_all(out, "tm", split_axis=3, concat_axis=1, tiled=True)
    out = out.reshape(seqs, width, groups, part).transpose(0, 3, 2, 1).reshape(seqs, span, width)

    d2 = d2.reshape(seqs, 6 * hidden, length)
    flat2 = w2.reshape(6 * hidden, width)
    gw2 = jnp.einsum("skt,sdt->kd", d2, h1, preferred_element_type=F32).astype(BF16)
    gw2 = lax.psum(gw2, "seq")
    gx2 = jnp.einsum("kd,skt->sdt", flat2, d2, preferred_element_type=F32).astype(BF16)
    gx2 = lax.psum_scatter(gx2, "tm", scatter_dimension=1, tiled=True)

    d1, db1 = run_back(gx2, pre1, cell1)
    d1 = d1.reshape(seqs, 6 * hidden, length)
    flat1 = w1.reshape(6 * hidden, width)
    gw1 = jnp.einsum("skt,std->kd", d1, x, preferred_element_type=F32).astype(BF16)
    gw1 = lax.psum(gw1, "seq")
    gx1 = jnp.einsum("kd,skt->std", flat1, d1, preferred_element_type=F32).astype(BF16)
    gx1 = gx1.reshape(seqs, groups, LANES, width)
    gx1 = lax.psum_scatter(gx1, "tm", scatter_dimension=2, tiled=True)
    gx1 = gx1.transpose(0, 2, 1, 3).reshape(seqs, span, width)

    db = lax.psum(jnp.stack([db1, db2]).sum(axis=(1, 3)), "seq")
    shape = weight_one.shape
    return (out, gx1, gw1.astype(F32).reshape(shape), db[0], gw2.astype(F32).reshape(shape), db[1])


def solution(mesh):
    placed = (
        P("seq", "tm", None),
        P(None, None, "tm", None),
        P("tm"),
        P(None, None, "tm", None),
        P("tm"),
        P("seq", "tm", None),
        P("seq", None),
    )
    return jax.shard_map(
        per_device,
        mesh=mesh,
        in_specs=placed,
        out_specs=(
            P("seq", "tm", None),
            P("seq", "tm", None),
            P(None, None, "tm", None),
            P("tm"),
            P(None, None, "tm", None),
            P("tm"),
        ),
        check_vma=False,
    )
```

```python
import functools

import jax
import jax.numpy as jnp
from jax import lax
from jax.experimental import pallas as pl
from jax.experimental.pallas import tpu as pltpu
from jax.sharding import PartitionSpec as P

CLUSTER = 32
LANES = 128
ROWS = 48
F32 = jnp.float32
BF16 = jnp.bfloat16
ANY = pl.BlockSpec(memory_space=pl.ANY)
MESH = pl.DeviceIdType.MESH
NN = (((1,), (0,)), ((), ()))
NT = (((1,), (1,)), ((), ()))
TN = (((0,), (0,)), ((), ()))


def dot(a, b, dims):
    return lax.dot_general(a, b, dims, preferred_element_type=F32)


def sigmoid(v):
    return 1.0 / (1.0 + jnp.exp(-v))


def tiles(count, rows, body):
    def step(r, carry):
        body(pl.multiple_of(r * rows, rows))
        return carry

    lax.fori_loop(0, count // rows, step, 0)


def shift_lanes(v, amount, lane, fill):
    moved = pltpu.roll(v, amount % LANES, axis=1)
    gone = lane < amount if amount > 0 else lane >= LANES + amount
    return jnp.where(gone, fill, moved)


def lane_chain(factor, value, lane, sign):
    step = 1
    while step < LANES:
        value = value + factor * shift_lanes(value, sign * step, lane, 0.0)
        factor = factor * shift_lanes(factor, sign * step, lane, 1.0)
        step *= 2
    return value


def pool_forward(first, p_ref, b_ref, pre_ref, cell_ref, h_ref, factor_ref, edge_ref, hidden, groups):
    lane = lax.broadcasted_iota(jnp.int32, (ROWS, LANES), 1)

    def at(j, start=0):
        return pl.ds(start + j * LANES, LANES)

    def gates(r):
        rows = pl.ds(r, ROWS)
        value = factor = None
        for j in range(groups):
            got = []
            for g in range(3):
                now = p_ref[pl.ds(g * hidden + r, ROWS), at(j)]
                tap = pl.ds((3 + g) * hidden + r, ROWS)
                if j:
                    past = p_ref[tap, at(j - 1)]
                else:
                    past = shift_lanes(p_ref[tap, at(groups - 1)], 1, lane, 0.0)
                total = now + past
                if g == 1:
                    total = total + b_ref[rows, :]
                total = total.astype(BF16)
                pre_ref[pl.ds(g * hidden + r, ROWS), at(j, first)] = total
                got.append(total.astype(F32))
            forget = sigmoid(got[1])
            fresh = (1.0 - forget) * jnp.tanh(got[0])
            if j:
                value = forget * value + fresh
                factor = forget * factor
            else:
                value, factor = fresh, forget
            cell_ref[rows, at(j, first)] = value
            factor_ref[rows, at(j)] = factor

    tiles(hidden, ROWS, gates)

    def chain(r):
        rows = pl.ds(r, ROWS)
        value = lane_chain(factor_ref[rows, at(groups - 1)], cell_ref[rows, at(groups - 1, first)], lane, 1)
        edge_ref[rows, :] = shift_lanes(value, 1, lane, 0.0)

    tiles(hidden, ROWS, chain)

    def finish(r):
        rows = pl.ds(r, ROWS)
        edge = edge_ref[rows, :]
        for j in range(groups):
            cell = cell_ref[rows, at(j, first)] + factor_ref[rows, at(j)] * edge
            cell_ref[rows, at(j, first)] = cell
            outgate = sigmoid(pre_ref[pl.ds(2 * hidden + r, ROWS), at(j, first)].astype(F32))
            h_ref[rows, at(j, first)] = (outgate * cell).astype(BF16)

    tiles(hidden, ROWS, finish)


def pool_backward(first, g_ref, pre_ref, cell_ref, target, d_ref, db_ref, work_ref, edge_ref, hidden, groups):
    lane = lax.broadcasted_iota(jnp.int32, (ROWS, LANES), 1)

    def at(j, start=0):
        return pl.ds(start + j * LANES, LANES)

    def gate(g, r, j):
        return pre_ref[pl.ds(g * hidden + r, ROWS), at(j, first)].astype(F32)

    def start(r):
        rows = pl.ds(r, ROWS)
        later = value = factor = None
        for j in reversed(range(groups)):
            own = g_ref[rows, at(j, first)].astype(F32) * sigmoid(gate(2, r, j))
            if later is None:
                value, factor = own, jnp.ones_like(own)
            else:
                value = own + later * value
                factor = later * factor
            work_ref[0, rows, at(j)] = value
            work_ref[1, rows, at(j)] = factor
            later = sigmoid(gate(1, r, j))
        edge_ref[0, rows, :] = later * value
        edge_ref[1, rows, :] = later * factor

    tiles(hidden, ROWS, start)

    def chain(r):
        rows = pl.ds(r, ROWS)
        value = lane_chain(edge_ref[1, rows, :], edge_ref[0, rows, :], lane, -1)
        edge_ref[0, rows, :] = shift_lanes(value, -1, lane, 0.0)

    tiles(hidden, ROWS, chain)

    def finish(r):
        rows = pl.ds(r, ROWS)
        edge = edge_ref[0, rows, :]
        total = jnp.zeros((ROWS, LANES), F32)
        before = shift_lanes(cell_ref[rows, at(groups - 1, first)], 1, lane, 0.0)
        for j in range(groups):
            carried = work_ref[0, rows, at(j)] + work_ref[1, rows, at(j)] * edge
            candidate = jnp.tanh(gate(0, r, j))
            forget = sigmoid(gate(1, r, j))
            outgate = sigmoid(gate(2, r, j))
            cell = cell_ref[rows, at(j, first)]
            keep = carried * (1.0 - forget)
            got = (
                keep * (1.0 - candidate * candidate),
                keep * forget * (before - candidate),
                g_ref[rows, at(j, first)].astype(F32) * cell * outgate * (1.0 - outgate),
            )
            before = cell
            for g, v in enumerate(got):
                v = v.astype(BF16)
                if g == 1:
                    total = total + v.astype(F32)
                d_ref[pl.ds(g * hidden + r, ROWS), at(j, target)] = v
                tap = pl.ds((3 + g) * hidden + r, ROWS)
                if j:
                    d_ref[tap, at(j - 1, target)] = v
                else:
                    d_ref[tap, at(groups - 1, target)] = shift_lanes(v.astype(F32), -1, lane, 0.0).astype(BF16)
        db_ref[rows, :] = jnp.sum(total, axis=1, keepdims=True)

    tiles(hidden, ROWS, finish)


def first_kernel(hidden, length, w_ref, b_ref, x_ref, pre_ref, cell_ref, h_ref, p_ref, work_ref, edge_ref):
    def strip(c):
        cols = pl.ds(c, 512)
        p_ref[:, cols] = dot(w_ref[...], x_ref[cols, :], NT)

    tiles(length, 512, strip)
    pool_forward(0, p_ref, b_ref, pre_ref, cell_ref, h_ref, work_ref, edge_ref, hidden, length // LANES)


def second_kernel(
    hidden, length, w_ref, b_ref, x_ref, g_ref, h_ref, d_ref, db_ref, p_ref, pre_ref, cell_ref, work_ref, edge_ref
):
    def strip(c):
        cols = pl.ds(c, 512)
        p_ref[:, cols] = dot(w_ref[...], x_ref[:, cols], NN)

    tiles(length, 512, strip)
    groups = length // LANES
    pool_forward(0, p_ref, b_ref, pre_ref, cell_ref, h_ref, work_ref.at[0], edge_ref.at[0], hidden, groups)
    pool_backward(0, g_ref, pre_ref, cell_ref, 0, d_ref, db_ref.at[0], work_ref, edge_ref, hidden, groups)


def back_kernel(hidden, length, g_ref, pre_ref, cell_ref, d_ref, db_ref, work_ref, edge_ref):
    pool_backward(0, g_ref, pre_ref, cell_ref, 0, d_ref, db_ref.at[0], work_ref, edge_ref, hidden, length // LANES)


def columns(rows, length):
    return pl.BlockSpec((rows, length), lambda s: (0, s))


def fixed(*dims):
    return pl.BlockSpec(dims, lambda s: (0,) * len(dims), pipeline_mode=pl.Buffered(1))


def params(**more):
    return pltpu.CompilerParams(vmem_limit_bytes=63 * 1024 * 1024, **more)


shape = jax.ShapeDtypeStruct


def run_first(seqs, weight, bias, gathered):
    (wide, width), total = weight.shape, gathered.shape[0]
    hidden, length = wide // 6, total // seqs
    return pl.pallas_call(
        functools.partial(first_kernel, hidden, length),
        name="layer_one_forward",
        grid=(seqs,),
        in_specs=[fixed(wide, width), fixed(hidden, 1), pl.BlockSpec((length, width), lambda s: (s, 0))],
        out_specs=[columns(3 * hidden, length), columns(hidden, length), columns(hidden, length)],
        out_shape=[shape((3 * hidden, total), BF16), shape((hidden, total), F32), shape((hidden, total), BF16)],
        scratch_shapes=[
            pltpu.VMEM((wide, length), F32),
            pltpu.VMEM((hidden, length), F32),
            pltpu.VMEM((hidden, LANES), F32),
        ],
        compiler_params=params(),
    )(weight, bias, gathered)


def run_second(seqs, weight, bias, gathered, grad):
    (wide, width), total = weight.shape, gathered.shape[1]
    hidden, length = wide // 6, total // seqs
    return pl.pallas_call(
        functools.partial(second_kernel, hidden, length),
        name="layer_two_forward_and_pool_backward",
        grid=(seqs,),
        in_specs=[fixed(wide, width), fixed(hidden, 1), columns(width, length), columns(hidden, length)],
        out_specs=[columns(hidden, length), columns(wide, length), pl.BlockSpec((1, hidden, 1), lambda s: (s, 0, 0))],
        out_shape=[shape((hidden, total), BF16), shape((wide, total), BF16), shape((seqs, hidden, 1), F32)],
        scratch_shapes=[
            pltpu.VMEM((wide, length), F32),
            pltpu.VMEM((3 * hidden, length), BF16),
            pltpu.VMEM((hidden, length), F32),
            pltpu.VMEM((2, hidden, length), F32),
            pltpu.VMEM((2, hidden, LANES), F32),
        ],
        compiler_params=params(),
    )(weight, bias, gathered, grad)


def run_back(seqs, grad, pre, cell):
    hidden, total = grad.shape
    length = total // seqs
    return pl.pallas_call(
        functools.partial(back_kernel, hidden, length),
        name="layer_one_pool_backward",
        grid=(seqs,),
        in_specs=[columns(hidden, length), columns(3 * hidden, length), columns(hidden, length)],
        out_specs=[columns(6 * hidden, length), pl.BlockSpec((1, hidden, 1), lambda s: (s, 0, 0))],
        out_shape=[shape((6 * hidden, total), BF16), shape((seqs, hidden, 1), F32)],
        scratch_shapes=[pltpu.VMEM((2, hidden, length), F32), pltpu.VMEM((2, hidden, LANES), F32)],
        compiler_params=params(),
    )(grad, pre, cell)


UNITS = 18
THIRDS = 3
SLOTS = 6
AHEAD = 4


class Here:
    def __init__(self):
        self.z = lax.axis_index("seq")
        self.b = lax.axis_index("tm")
        self.c = lax.rem(self.b, 2)
        self.x = lax.rem(self.b // 2, 2)
        self.y = self.b // 4
        self.core = dict(seq=self.z, tm=self.b + 1 - 2 * self.c)
        self.across_x = dict(seq=self.z, tm=self.b + 2 - 4 * self.x)
        self.across_y = dict(seq=self.z, tm=self.b + 4 - 8 * self.y)
        self.pair = dict(seq=self.z + 1 - 2 * lax.rem(self.z, 2), tm=self.b)
        self.middle = dict(seq=3 - self.z, tm=self.b)
        self.peers = [dict(seq=self.z, tm=lax.rem(self.b + d, 8)) for d in range(1, 8)]
        self.is_end = jnp.logical_or(self.z == 0, self.z == 3)
        self.is_centre = jnp.logical_and(self.z > 0, self.z < 3)


def remote(src, dst, send, recv, target):
    return pltpu.make_async_remote_copy(
        src_ref=src, dst_ref=dst, send_sem=send, recv_sem=recv, device_id=target, device_id_type=MESH
    )


def both(a, b):
    if isinstance(a, bool) and isinstance(b, bool):
        return a and b
    return jnp.logical_and(a, b)


def signal(sem, target):
    pl.semaphore_signal(sem, inc=1, device_id=target, device_id_type=MESH)


def meet(here, everyone):
    barrier = pltpu.get_barrier_semaphore()
    near = here.peers if everyone else [here.core, here.across_x, here.across_y]
    targets = near + [here.pair, here.middle]
    for target in targets:
        signal(barrier, target)
    pl.semaphore_wait(barrier, len(targets))


class SeqSum:
    def __init__(self, here, hidden, third, own, ring_in, ring_mid, total, out, sems, credits):
        self.here, self.hidden, self.third = here, hidden, third
        self.own, self.ring_in, self.ring_mid, self.total, self.out = own, ring_in, ring_mid, total, out
        self.sems = sems
        self.credit_in, self.credit_mid, self.credit_out = credits

    def inward(self, u):
        i = lax.rem(u, SLOTS)
        return remote(self.own.at[u], self.ring_in.at[i], self.sems.at[0, i], self.sems.at[1, i], self.here.pair)

    def across(self, u):
        i = lax.rem(u, SLOTS)
        return remote(self.own.at[u], self.ring_mid.at[i], self.sems.at[2, i], self.sems.at[3, i], self.here.middle)

    def outward(self, u):
        i = lax.rem(u, SLOTS)
        return remote(self.total.at[i], self.ring_in.at[i], self.sems.at[4, i], self.sems.at[5, i], self.here.pair)

    def store(self, u, ring):
        i = lax.rem(u, SLOTS)
        cols = pl.ds(pl.multiple_of((u // 6) * self.third, LANES), self.third)
        return pltpu.make_async_copy(ring.at[i], self.out.at[lax.rem(u, 6), :, cols], self.sems.at[6, i])

    def add(self, dst, i, a, ia, b, ib):
        def rows(r):
            at = pl.ds(r, ROWS)
            dst[i, at, :] = a[ia, at, :] + b[ib, at, :]

        tiles(self.hidden, ROWS, rows)

    def offer(self, u):
        @pl.when(self.here.is_end)
        def _():
            @pl.when(u >= SLOTS)
            def _():
                pl.semaphore_wait(self.credit_in, 1)
                self.inward(u - SLOTS).wait_send()

            self.inward(u).start()

    def gather(self, u):
        i = lax.rem(u, SLOTS)
        self.inward(u).wait_recv()
        self.add(self.own, u, self.own, u, self.ring_in, i)

        @pl.when(u + SLOTS < UNITS)
        def _():
            signal(self.credit_in, self.here.pair)

        @pl.when(u >= SLOTS)
        def _():
            pl.semaphore_wait(self.credit_mid, 1)
            self.across(u - SLOTS).wait_send()

        self.across(u).start()

    def finish(self, u):
        i = lax.rem(u, SLOTS)
        self.across(u).wait_recv()

        @pl.when(u >= SLOTS)
        def _():
            pl.semaphore_wait(self.credit_out, 1)
            self.outward(u - SLOTS).wait_send()
            self.store(u - SLOTS, self.total).wait()

        self.add(self.total, i, self.own, u, self.ring_mid, i)

        @pl.when(u + SLOTS < UNITS)
        def _():
            signal(self.credit_mid, self.here.middle)

        self.outward(u).start()
        self.store(u, self.total).start()

    def accept(self, u):
        self.outward(u).wait_recv()
        self.store(u, self.ring_in).start()

        @pl.when(u > 0)
        def _():
            self.store(u - 1, self.ring_in).wait()

            @pl.when(u - 1 + SLOTS < UNITS)
            def _():
                signal(self.credit_out, self.here.pair)

    def tick(self, n):
        @pl.when(self.here.is_centre)
        def _():
            @pl.when(n < UNITS)
            def _():
                self.gather(n)

            @pl.when(both(n >= 1, n <= UNITS))
            def _():
                self.finish(n - 1)

        @pl.when(n + AHEAD < UNITS)
        def _():
            self.offer(n + AHEAD)

        @pl.when(n >= 2)
        def _():
            @pl.when(self.here.is_end)
            def _():
                self.accept(n - 2)

    def drain(self):
        @pl.when(self.here.is_centre)
        def _():
            for u in range(UNITS - SLOTS, UNITS):
                self.across(u).wait_send()
                self.outward(u).wait_send()
                self.store(u, self.total).wait()

        @pl.when(self.here.is_end)
        def _():
            for u in range(UNITS - SLOTS, UNITS):
                self.inward(u).wait_send()
            self.store(UNITS - 1, self.ring_in).wait()


class RankSum:
    def __init__(self, here, part, pairs, wide_x, wide_y, last_x, last_y, sems):
        self.here, self.part, self.pairs = here, part, pairs
        self.wide_x, self.wide_y, self.last_x, self.last_y, self.sems = wide_x, wide_y, last_x, last_y, sems
        self.rows = part.shape[3]
        self.upper = pl.ds(0, self.rows // 2)
        self.lower = pl.ds(self.rows // 2, self.rows // 2)
        self.step = 16

    def copy(self, k, s, src, dst, target):
        return remote(src, dst, self.sems.at[s, k, 0], self.sems.at[s, k, 1], target)

    def swap(self, s):
        return self.copy(0, s, self.part.at[:, :, 1 - self.here.c], self.pairs.at[s], self.here.core)

    def wide(self, s):
        h = self.here
        return (
            self.copy(1, s, self.pairs.at[s, :, 1 - h.x, self.upper], self.wide_x.at[s], h.across_x),
            self.copy(2, s, self.pairs.at[s, 1 - h.y, :, self.lower], self.wide_y.at[s], h.across_y),
        )

    def last(self, s):
        h = self.here
        return (
            self.copy(3, s, self.pairs.at[s, 1 - h.y, h.x, self.upper], self.last_y.at[s], h.across_y),
            self.copy(4, s, self.pairs.at[s, h.y, 1 - h.x, self.lower], self.last_x.at[s], h.across_x),
        )

    def start(self, s):
        self.swap(s).start()

    def cross(self, s):
        h = self.here
        self.swap(s).wait()

        def rows(r):
            at = pl.ds(r, self.step)
            for y in range(2):
                for x in range(2):
                    self.pairs[s, y, x, at, :] = self.pairs[s, y, x, at, :] + self.part[y, x, h.c, at, :]

        tiles(self.rows, self.step, rows)
        for copy in self.wide(s):
            copy.start()

    def turn(self, s):
        h = self.here
        half = self.rows // 2
        for copy in self.wide(s):
            copy.wait()

        def rows(r):
            at, low = pl.ds(r, self.step), pl.ds(half + r, self.step)
            for k in range(2):
                self.pairs[s, k, h.x, at, :] = self.pairs[s, k, h.x, at, :] + self.wide_x[s, k, at, :]
                self.pairs[s, h.y, k, low, :] = self.pairs[s, h.y, k, low, :] + self.wide_y[s, k, at, :]

        tiles(half, self.step, rows)
        for copy in self.last(s):
            copy.start()

    def done(self, s, out):
        h = self.here
        half = self.rows // 2
        for copy in self.last(s):
            copy.wait()

        def rows(r):
            at, low = pl.ds(r, self.step), pl.ds(half + r, self.step)
            out[at, :] = self.pairs[s, h.y, h.x, at, :] + self.last_y[s, at, :]
            out[low, :] = self.pairs[s, h.y, h.x, low, :] + self.last_x[s, at, :]

        tiles(half, self.step, rows)


def sum_scratch(seqs, hidden, third, rows, cols):
    return [
        pltpu.VMEM((UNITS, hidden, third), BF16),
        pltpu.VMEM((SLOTS, hidden, third), BF16),
        pltpu.VMEM((SLOTS, hidden, third), BF16),
        pltpu.VMEM((SLOTS, hidden, third), BF16),
        pltpu.SemaphoreType.DMA((7, SLOTS)),
        pltpu.SemaphoreType.REGULAR,
        pltpu.SemaphoreType.REGULAR,
        pltpu.SemaphoreType.REGULAR,
        pltpu.VMEM((2, 2, 2, rows, cols), BF16),
        pltpu.VMEM((seqs, 2, 2, rows, cols), BF16),
        pltpu.VMEM((seqs, 2, rows // 2, cols), BF16),
        pltpu.VMEM((seqs, 2, rows // 2, cols), BF16),
        pltpu.VMEM((seqs, rows // 2, cols), BF16),
        pltpu.VMEM((seqs, rows // 2, cols), BF16),
        pltpu.SemaphoreType.DMA((seqs, 5, 2)),
        pltpu.SemaphoreType.DMA((8,)),
    ]


def backward_kernel(second, seqs, hidden, length, width, *refs):
    third = width // THIRDS
    if second:
        d_in, r_in, w_in, pre_in, cell_in, h_in, gw_out, d_out, db_out, h_out = refs[:10]
        dv, wv, rv, pre, cell, work, edge, grad, hsem = refs[10:19]
        rest = refs[19:]
    else:
        d_in, r_in, w_in, gw_out, gx_out = refs[:5]
        dv, wv, rv, gxv = refs[5:9]
        rest = refs[9:]
    own, ring_in, ring_mid, total, zsem, *credits = rest[:8]
    rank_refs, lsem = rest[8:15], rest[15]
    here = Here()
    ar = SeqSum(here, hidden, third, own, ring_in, ring_mid, total, gw_out, zsem, credits)
    rs = RankSum(here, *rank_refs)
    groups = length // LANES

    def columns_of(s):
        return pl.ds(s * length, length)

    def rhs(t):
        if second:
            src = r_in.at[pl.ds(t * third, third), :]
        else:
            src = r_in.at[:, pl.ds(t * third, third)]
        return pltpu.make_async_copy(src, rv.at[t % 2], lsem.at[t % 2])

    loads = [pltpu.make_async_copy(d_in, dv, lsem.at[2]), pltpu.make_async_copy(w_in, wv, lsem.at[3])]
    if second:
        loads.append(pltpu.make_async_copy(pre_in, pre, lsem.at[4]))
        loads.append(pltpu.make_async_copy(cell_in, cell, lsem.at[5]))
    loads[0].start()
    rhs(0).start()
    for copy in loads[1:]:
        copy.start()
    rhs(1).start()
    meet(here, second)
    spread = []
    if second:
        spread.append(pltpu.make_async_copy(h_in.at[here.b], h_out.at[here.b], hsem.at[0, 0]))
        for d, peer in enumerate(here.peers, 1):
            spread.append(remote(h_in.at[peer["tm"]], h_out.at[here.b], hsem.at[d, 0], hsem.at[d, 1], peer))
        for copy in spread:
            copy.start()

    def units(t, ks):
        for k in ks:
            rows = pl.ds(k * hidden, hidden)
            own[t * 6 + k] = dot(dv[rows, :], rv[t % 2], NT if second else NN).astype(BF16)
            if t * 6 + k < AHEAD:
                ar.offer(t * 6 + k)

    def part(s, piece):
        if second:
            i, start = piece // 2, piece % 2 * (length // 2)
            lhs = pl.ds(i * (width // 2), width // 2)

            def strip(c):
                cols = pl.ds(pl.multiple_of(start + c, 256), 256)
                src = pl.ds(pl.multiple_of(s * length + start + c, 256), 256)
                got = dot(wv[:, lhs], dv[:, src], TN).astype(BF16)
                rs.part[i, :, :, :, cols] = got.reshape(2, 2, hidden, 256)

            tiles(length // 2, 256, strip)
        else:
            rows = LANES // 8
            low, high = (width // 256 * q // 4 * 256 for q in (piece, piece + 1))

            def strip(c):
                cols = pl.ds(pl.multiple_of(low + c, 256), 256)
                got = dot(dv[:, columns_of(s)], wv[:, cols], TN).astype(BF16)
                for j in range(groups):
                    block = got[j * LANES : (j + 1) * LANES].reshape(2, 2, 2, rows, 256)
                    rs.part[:, :, :, pl.ds(j * rows, rows), cols] = block

            tiles(high - low, 256, strip)

    ticks = iter(range(UNITS + 2))

    def tick():
        ar.tick(next(ticks))

    def settle(s):
        rs.done(s, grad.at[:, columns_of(s)] if second else gxv.at[s])

    loads[0].wait()
    rhs(0).wait()
    units(0, range(6))
    rhs(2).start()
    loads[1].wait()
    part(0, 0)
    part(0, 1)
    tick()
    part(0, 2)
    part(0, 3)
    rs.start(0)
    tick()
    rhs(1).wait()
    units(1, range(3))
    rs.cross(0)
    tick()
    part(1, 0)
    part(1, 1)
    part(1, 2)
    tick()
    part(1, 3)
    rs.start(1)
    units(1, range(3, 6))
    tick()
    rs.turn(0)
    rhs(2).wait()
    units(2, range(2))
    rs.cross(1)
    units(2, range(2, 4))
    tick()
    units(2, range(4, 6))
    settle(0)
    if second:
        for copy in loads[2:]:
            copy.wait()
        stores = [
            pltpu.make_async_copy(dv.at[:, columns_of(s)], d_out.at[:, columns_of(s)], lsem.at[6 + s])
            for s in range(seqs)
        ]

        def pool(s):
            first = s * length
            pool_backward(first, grad, pre, cell, first, dv, db_out.at[s], work, edge, hidden, groups)
            stores[s].start()

        tick()
        pool(0)
    else:
        tick()
    rs.turn(1)
    tick()
    tick()
    settle(1)
    if second:
        pool(1)
    else:
        stores = [pltpu.make_async_copy(gxv, gx_out, lsem.at[6])]
        stores[0].start()

    def more(n, carry):
        ar.tick(n)
        return carry

    lax.fori_loop(next(ticks), UNITS + 2, more, 0)
    ar.drain()
    for copy in stores + spread:
        copy.wait()


def run_backward(seqs, d, rhs, weight, layer_one=None):
    second = layer_one is not None
    (wide, width), total = weight.shape, d.shape[1]
    hidden, length = wide // 6, total // seqs
    third, span = width // THIRDS, length // 8
    outs = [shape((6, hidden, width), BF16)]
    scratch = [pltpu.VMEM((wide, total), BF16), pltpu.VMEM((wide, width), BF16)]
    if second:
        outs += [shape((wide, total), BF16), shape((seqs, hidden, 1), F32), shape(layer_one[2].shape, BF16)]
        specs = [ANY, ANY, pl.BlockSpec(memory_space=pltpu.VMEM), ANY]
        rows, cols = hidden, length
        scratch += [
            pltpu.VMEM((2, third, total), BF16),
            pltpu.VMEM((3 * hidden, total), BF16),
            pltpu.VMEM((hidden, total), F32),
            pltpu.VMEM((2, hidden, length), F32),
            pltpu.VMEM((2, hidden, LANES), F32),
            pltpu.VMEM((hidden, total), BF16),
            pltpu.SemaphoreType.DMA((8, 2)),
        ]
    else:
        outs += [shape((seqs, span, width), BF16)]
        specs = [ANY, ANY]
        rows, cols = span, width
        scratch += [pltpu.VMEM((2, total, third), BF16), pltpu.VMEM((seqs, span, width), BF16)]
    operands = (d, rhs, weight) + (layer_one or ())
    return pl.pallas_call(
        functools.partial(backward_kernel, second, seqs, hidden, length, width),
        name="layer_two_backward" if second else "layer_one_backward",
        in_specs=[ANY] * len(operands),
        out_specs=specs,
        out_shape=outs,
        scratch_shapes=scratch + sum_scratch(seqs, hidden, third, rows, cols),
        compiler_params=params(collective_id=1 if second else 2, has_side_effects=True),
    )(*operands)


def per_device(line, inputs, weight_one, fbias_one, weight_two, fbias_two, cotangent, cluster_starts):
    seqs, span, width = inputs.shape
    count = lax.axis_size("tm")
    length = span * count
    groups = length // LANES
    piece = LANES // count
    hidden = weight_one.shape[2]
    total = seqs * length
    w1 = weight_one.reshape(6 * hidden, width)
    w2 = weight_two.reshape(6 * hidden, width)

    steps = lax.axis_index("tm") * span + jnp.arange(span, dtype=jnp.int32)
    starts = cluster_starts[:, :, None]
    keep = jnp.any((steps >= starts) & (steps < starts + CLUSTER), axis=1)
    seed = jnp.where(keep[:, :, None], cotangent, jnp.zeros_like(cotangent))
    seed = seed.reshape(seqs, piece, groups, count, hidden)
    seed = lax.all_to_all(seed, "tm", split_axis=3, concat_axis=1, tiled=True)
    seed = seed.reshape(seqs, LANES, groups, hidden).transpose(3, 0, 2, 1).reshape(hidden, total)

    x = inputs.reshape(seqs, piece, groups, width).transpose(0, 2, 1, 3)
    x = lax.all_gather(x, "tm", axis=2, tiled=True).reshape(total, width)
    pre1, cell1, h1 = run_first(seqs, w1, fbias_one[:, None], x)
    h1 = lax.all_gather(h1, "tm", axis=0, tiled=True)
    h2, d2, db2 = run_second(seqs, w2, fbias_two[:, None], h1, seed)

    h2 = h2.reshape(hidden, seqs, groups, count, piece)
    if line:
        h2 = h2.transpose(3, 1, 2, 4, 0).reshape(count, seqs * groups * piece, hidden)
        gw2, d1, db1, h2 = run_backward(seqs, d2, h1, w2, (pre1, cell1, h2))
        h2 = h2.reshape(count, seqs, groups, piece, hidden).transpose(1, 3, 2, 0, 4)
        gw1, gx1 = run_backward(seqs, d1, x, w1)
        gx1 = gx1.reshape(seqs, groups, piece, width)
    else:
        h2 = lax.all_to_all(h2, "tm", split_axis=3, concat_axis=0, tiled=True)
        h2 = h2.reshape(width, seqs, groups, piece).transpose(1, 3, 2, 0)
        gw2 = lax.psum(dot(d2, h1, NT).astype(BF16), "seq")
        gx2 = lax.psum_scatter(dot(w2, d2, TN).astype(BF16), "tm", scatter_dimension=0, tiled=True)
        d1, db1 = run_back(seqs, gx2, pre1, cell1)
        gw1 = lax.psum(dot(d1, x, NN).astype(BF16), "seq")
        gx1 = dot(d1, w1, TN).astype(BF16).reshape(seqs, groups, LANES, width)
        gx1 = lax.psum_scatter(gx1, "tm", scatter_dimension=2, tiled=True)
    out = h2.reshape(seqs, span, width)
    gx1 = gx1.transpose(0, 2, 1, 3).reshape(seqs, span, width)
    db = lax.psum(jnp.stack([db1, db2]).sum(axis=(1, 3)), "seq")
    dims = weight_one.shape
    return (out, gx1, gw1.astype(F32).reshape(dims), db[0], gw2.astype(F32).reshape(dims), db[1])


def solution(mesh):
    placed = (
        P("seq", "tm", None),
        P(None, None, "tm", None),
        P("tm"),
        P(None, None, "tm", None),
        P("tm"),
        P("seq", "tm", None),
        P("seq", None),
    )
    return jax.shard_map(
        functools.partial(per_device, dict(mesh.shape) == {"seq": 4, "tm": 8}),
        mesh=mesh,
        in_specs=placed,
        out_specs=(
            P("seq", "tm", None),
            P("seq", "tm", None),
            P(None, None, "tm", None),
            P("tm"),
            P(None, None, "tm", None),
            P("tm"),
        ),
        check_vma=False,
    )
```

```python
import functools

import jax
import jax.numpy as jnp
from jax import lax
from jax.experimental import pallas as pl
from jax.experimental.pallas import tpu as pltpu
from jax.sharding import PartitionSpec as P

CLUSTER = 32
LANES = 128
ROWS = 48
F32 = jnp.float32
BF16 = jnp.bfloat16
ANY = pl.BlockSpec(memory_space=pl.ANY)
MESH = pl.DeviceIdType.MESH
NN = (((1,), (0,)), ((), ()))
NT = (((1,), (1,)), ((), ()))
TN = (((0,), (0,)), ((), ()))


def dot(a, b, dims):
    return lax.dot_general(a, b, dims, preferred_element_type=F32)


def sigmoid(v):
    return 1.0 / (1.0 + jnp.exp(-v))


def tiles(count, rows, body):
    def step(r, carry):
        body(pl.multiple_of(r * rows, rows))
        return carry

    lax.fori_loop(0, count // rows, step, 0)


def shift_lanes(v, amount, lane, fill):
    moved = pltpu.roll(v, amount % LANES, axis=1)
    gone = lane < amount if amount > 0 else lane >= LANES + amount
    return jnp.where(gone, fill, moved)


def lane_chain(factor, value, lane, sign):
    step = 1
    while step < LANES:
        value = value + factor * shift_lanes(value, sign * step, lane, 0.0)
        factor = factor * shift_lanes(factor, sign * step, lane, 1.0)
        step *= 2
    return value


def pool_forward(first, p_ref, b_ref, pre_ref, cell_ref, target, h_ref, factor_ref, edge_ref, hidden, groups):
    lane = lax.broadcasted_iota(jnp.int32, (ROWS, LANES), 1)

    def at(j, start=0):
        return pl.ds(start + j * LANES, LANES)

    def gates(r):
        rows = pl.ds(r, ROWS)
        value = factor = None
        for j in range(groups):
            got = []
            for g in range(3):
                now = p_ref[pl.ds(g * hidden + r, ROWS), at(j)]
                tap = pl.ds((3 + g) * hidden + r, ROWS)
                if j:
                    past = p_ref[tap, at(j - 1)]
                else:
                    past = shift_lanes(p_ref[tap, at(groups - 1)], 1, lane, 0.0)
                total = now + past
                if g == 1:
                    total = total + b_ref[rows, :]
                total = total.astype(BF16)
                pre_ref[pl.ds(g * hidden + r, ROWS), at(j, first)] = total
                got.append(total.astype(F32))
            forget = sigmoid(got[1])
            fresh = (1.0 - forget) * jnp.tanh(got[0])
            if j:
                value = forget * value + fresh
                factor = forget * factor
            else:
                value, factor = fresh, forget
            cell_ref[rows, at(j, first)] = value
            factor_ref[rows, at(j)] = factor

    tiles(hidden, ROWS, gates)

    def chain(r):
        rows = pl.ds(r, ROWS)
        value = lane_chain(factor_ref[rows, at(groups - 1)], cell_ref[rows, at(groups - 1, first)], lane, 1)
        edge_ref[rows, :] = shift_lanes(value, 1, lane, 0.0)

    tiles(hidden, ROWS, chain)

    def finish(r):
        rows = pl.ds(r, ROWS)
        edge = edge_ref[rows, :]
        for j in range(groups):
            cell = cell_ref[rows, at(j, first)] + factor_ref[rows, at(j)] * edge
            cell_ref[rows, at(j, first)] = cell
            outgate = sigmoid(pre_ref[pl.ds(2 * hidden + r, ROWS), at(j, first)].astype(F32))
            h_ref[rows, at(j, target)] = (outgate * cell).astype(BF16)

    tiles(hidden, ROWS, finish)


def pool_backward(first, g_ref, pre_ref, cell_ref, target, d_ref, db_ref, work_ref, edge_ref, hidden, groups):
    lane = lax.broadcasted_iota(jnp.int32, (ROWS, LANES), 1)

    def at(j, start=0):
        return pl.ds(start + j * LANES, LANES)

    def gate(g, r, j):
        return pre_ref[pl.ds(g * hidden + r, ROWS), at(j, first)].astype(F32)

    def start(r):
        rows = pl.ds(r, ROWS)
        later = value = factor = None
        for j in reversed(range(groups)):
            own = g_ref[rows, at(j, first)].astype(F32) * sigmoid(gate(2, r, j))
            if later is None:
                value, factor = own, jnp.ones_like(own)
            else:
                value = own + later * value
                factor = later * factor
            work_ref[0, rows, at(j)] = value
            work_ref[1, rows, at(j)] = factor
            later = sigmoid(gate(1, r, j))
        edge_ref[0, rows, :] = later * value
        edge_ref[1, rows, :] = later * factor

    tiles(hidden, ROWS, start)

    def chain(r):
        rows = pl.ds(r, ROWS)
        value = lane_chain(edge_ref[1, rows, :], edge_ref[0, rows, :], lane, -1)
        edge_ref[0, rows, :] = shift_lanes(value, -1, lane, 0.0)

    tiles(hidden, ROWS, chain)

    def finish(r):
        rows = pl.ds(r, ROWS)
        edge = edge_ref[0, rows, :]
        total = jnp.zeros((ROWS, LANES), F32)
        before = shift_lanes(cell_ref[rows, at(groups - 1, first)], 1, lane, 0.0)
        for j in range(groups):
            carried = work_ref[0, rows, at(j)] + work_ref[1, rows, at(j)] * edge
            candidate = jnp.tanh(gate(0, r, j))
            forget = sigmoid(gate(1, r, j))
            outgate = sigmoid(gate(2, r, j))
            cell = cell_ref[rows, at(j, first)]
            keep = carried * (1.0 - forget)
            got = (
                keep * (1.0 - candidate * candidate),
                keep * forget * (before - candidate),
                g_ref[rows, at(j, first)].astype(F32) * cell * outgate * (1.0 - outgate),
            )
            before = cell
            for g, v in enumerate(got):
                v = v.astype(BF16)
                if g == 1:
                    total = total + v.astype(F32)
                d_ref[pl.ds(g * hidden + r, ROWS), at(j, target)] = v
                tap = pl.ds((3 + g) * hidden + r, ROWS)
                if j:
                    d_ref[tap, at(j - 1, target)] = v
                else:
                    d_ref[tap, at(groups - 1, target)] = shift_lanes(v.astype(F32), -1, lane, 0.0).astype(BF16)
        db_ref[rows, :] = jnp.sum(total, axis=1, keepdims=True)

    tiles(hidden, ROWS, finish)


def first_kernel(hidden, length, w_ref, b_ref, x_ref, pre_ref, cell_ref, h_ref, p_ref, work_ref, edge_ref):
    def strip(c):
        cols = pl.ds(c, 512)
        p_ref[:, cols] = dot(w_ref[...], x_ref[cols, :], NT)

    tiles(length, 512, strip)
    pool_forward(0, p_ref, b_ref, pre_ref, cell_ref, 0, h_ref, work_ref, edge_ref, hidden, length // LANES)


def second_kernel(
    hidden, length, w_ref, b_ref, x_ref, g_ref, h_ref, d_ref, db_ref, p_ref, pre_ref, cell_ref, work_ref, edge_ref
):
    def strip(c):
        cols = pl.ds(c, 512)
        p_ref[:, cols] = dot(w_ref[...], x_ref[:, cols], NN)

    tiles(length, 512, strip)
    groups = length // LANES
    pool_forward(0, p_ref, b_ref, pre_ref, cell_ref, 0, h_ref, work_ref.at[0], edge_ref.at[0], hidden, groups)
    pool_backward(0, g_ref, pre_ref, cell_ref, 0, d_ref, db_ref.at[0], work_ref, edge_ref, hidden, groups)


def back_kernel(hidden, length, g_ref, pre_ref, cell_ref, d_ref, db_ref, work_ref, edge_ref):
    pool_backward(0, g_ref, pre_ref, cell_ref, 0, d_ref, db_ref.at[0], work_ref, edge_ref, hidden, length // LANES)


def columns(rows, length):
    return pl.BlockSpec((rows, length), lambda s: (0, s))


def fixed(*dims):
    return pl.BlockSpec(dims, lambda s: (0,) * len(dims), pipeline_mode=pl.Buffered(1))


def params(**more):
    return pltpu.CompilerParams(vmem_limit_bytes=63 * 1024 * 1024, **more)


shape = jax.ShapeDtypeStruct


def run_first(seqs, weight, bias, gathered):
    (wide, width), total = weight.shape, gathered.shape[0]
    hidden, length = wide // 6, total // seqs
    return pl.pallas_call(
        functools.partial(first_kernel, hidden, length),
        name="layer_one_forward",
        grid=(seqs,),
        in_specs=[fixed(wide, width), fixed(hidden, 1), pl.BlockSpec((length, width), lambda s: (s, 0))],
        out_specs=[columns(3 * hidden, length), columns(hidden, length), columns(hidden, length)],
        out_shape=[shape((3 * hidden, total), BF16), shape((hidden, total), F32), shape((hidden, total), BF16)],
        scratch_shapes=[
            pltpu.VMEM((wide, length), F32),
            pltpu.VMEM((hidden, length), F32),
            pltpu.VMEM((hidden, LANES), F32),
        ],
        compiler_params=params(),
    )(weight, bias, gathered)


def run_second(seqs, weight, bias, gathered, grad):
    (wide, width), total = weight.shape, gathered.shape[1]
    hidden, length = wide // 6, total // seqs
    return pl.pallas_call(
        functools.partial(second_kernel, hidden, length),
        name="layer_two_forward_and_pool_backward",
        grid=(seqs,),
        in_specs=[fixed(wide, width), fixed(hidden, 1), columns(width, length), columns(hidden, length)],
        out_specs=[columns(hidden, length), columns(wide, length), pl.BlockSpec((1, hidden, 1), lambda s: (s, 0, 0))],
        out_shape=[shape((hidden, total), BF16), shape((wide, total), BF16), shape((seqs, hidden, 1), F32)],
        scratch_shapes=[
            pltpu.VMEM((wide, length), F32),
            pltpu.VMEM((3 * hidden, length), BF16),
            pltpu.VMEM((hidden, length), F32),
            pltpu.VMEM((2, hidden, length), F32),
            pltpu.VMEM((2, hidden, LANES), F32),
        ],
        compiler_params=params(),
    )(weight, bias, gathered, grad)


def run_back(seqs, grad, pre, cell):
    hidden, total = grad.shape
    length = total // seqs
    return pl.pallas_call(
        functools.partial(back_kernel, hidden, length),
        name="layer_one_pool_backward",
        grid=(seqs,),
        in_specs=[columns(hidden, length), columns(3 * hidden, length), columns(hidden, length)],
        out_specs=[columns(6 * hidden, length), pl.BlockSpec((1, hidden, 1), lambda s: (s, 0, 0))],
        out_shape=[shape((6 * hidden, total), BF16), shape((seqs, hidden, 1), F32)],
        scratch_shapes=[pltpu.VMEM((2, hidden, length), F32), pltpu.VMEM((2, hidden, LANES), F32)],
        compiler_params=params(),
    )(grad, pre, cell)


UNITS = 18
THIRDS = 3
SLOTS = 6
AHEAD = 4


class Here:
    def __init__(self):
        self.z = lax.axis_index("seq")
        self.b = lax.axis_index("tm")
        self.c = lax.rem(self.b, 2)
        self.x = lax.rem(self.b // 2, 2)
        self.y = self.b // 4
        self.core = dict(seq=self.z, tm=self.b + 1 - 2 * self.c)
        self.across_x = dict(seq=self.z, tm=self.b + 2 - 4 * self.x)
        self.across_y = dict(seq=self.z, tm=self.b + 4 - 8 * self.y)
        self.pair = dict(seq=self.z + 1 - 2 * lax.rem(self.z, 2), tm=self.b)
        self.middle = dict(seq=3 - self.z, tm=self.b)
        self.peers = [dict(seq=self.z, tm=lax.rem(self.b + d, 8)) for d in range(1, 8)]
        self.is_end = jnp.logical_or(self.z == 0, self.z == 3)
        self.is_centre = jnp.logical_and(self.z > 0, self.z < 3)


def remote(src, dst, send, recv, target):
    return pltpu.make_async_remote_copy(
        src_ref=src, dst_ref=dst, send_sem=send, recv_sem=recv, device_id=target, device_id_type=MESH
    )


def both(a, b):
    if isinstance(a, bool) and isinstance(b, bool):
        return a and b
    return jnp.logical_and(a, b)


def signal(sem, target):
    pl.semaphore_signal(sem, inc=1, device_id=target, device_id_type=MESH)


def meet(targets):
    barrier = pltpu.get_barrier_semaphore()
    for target in targets:
        signal(barrier, target)
    pl.semaphore_wait(barrier, len(targets))


class SeqSum:
    def __init__(self, here, hidden, third, own, ring_in, ring_mid, total, out, sems, credits):
        self.here, self.hidden, self.third = here, hidden, third
        self.own, self.ring_in, self.ring_mid, self.total, self.out = own, ring_in, ring_mid, total, out
        self.sems = sems
        self.credit_in, self.credit_mid, self.credit_out = credits

    def inward(self, u):
        i = lax.rem(u, SLOTS)
        return remote(self.own.at[u], self.ring_in.at[i], self.sems.at[0, i], self.sems.at[1, i], self.here.pair)

    def across(self, u):
        i = lax.rem(u, SLOTS)
        return remote(self.own.at[u], self.ring_mid.at[i], self.sems.at[2, i], self.sems.at[3, i], self.here.middle)

    def outward(self, u):
        i = lax.rem(u, SLOTS)
        return remote(self.total.at[i], self.ring_in.at[i], self.sems.at[4, i], self.sems.at[5, i], self.here.pair)

    def store(self, u, ring):
        i = lax.rem(u, SLOTS)
        cols = pl.ds(pl.multiple_of((u // 6) * self.third, LANES), self.third)
        return pltpu.make_async_copy(ring.at[i], self.out.at[lax.rem(u, 6), :, cols], self.sems.at[6, i])

    def add(self, dst, i, a, ia, b, ib):
        def rows(r):
            at = pl.ds(r, ROWS)
            dst[i, at, :] = a[ia, at, :] + b[ib, at, :]

        tiles(self.hidden, ROWS, rows)

    def offer(self, u):
        @pl.when(self.here.is_end)
        def _():
            @pl.when(u >= SLOTS)
            def _():
                pl.semaphore_wait(self.credit_in, 1)
                self.inward(u - SLOTS).wait_send()

            self.inward(u).start()

    def gather(self, u):
        i = lax.rem(u, SLOTS)
        self.inward(u).wait_recv()
        self.add(self.own, u, self.own, u, self.ring_in, i)

        @pl.when(u + SLOTS < UNITS)
        def _():
            signal(self.credit_in, self.here.pair)

        @pl.when(u >= SLOTS)
        def _():
            pl.semaphore_wait(self.credit_mid, 1)
            self.across(u - SLOTS).wait_send()

        self.across(u).start()

    def finish(self, u):
        i = lax.rem(u, SLOTS)
        self.across(u).wait_recv()

        @pl.when(u >= SLOTS)
        def _():
            pl.semaphore_wait(self.credit_out, 1)
            self.outward(u - SLOTS).wait_send()
            self.store(u - SLOTS, self.total).wait()

        self.add(self.total, i, self.own, u, self.ring_mid, i)

        @pl.when(u + SLOTS < UNITS)
        def _():
            signal(self.credit_mid, self.here.middle)

        self.outward(u).start()
        self.store(u, self.total).start()

    def accept(self, u):
        self.outward(u).wait_recv()
        self.store(u, self.ring_in).start()

        @pl.when(u > 0)
        def _():
            self.store(u - 1, self.ring_in).wait()

            @pl.when(u - 1 + SLOTS < UNITS)
            def _():
                signal(self.credit_out, self.here.pair)

    def tick(self, n):
        @pl.when(self.here.is_centre)
        def _():
            @pl.when(n < UNITS)
            def _():
                self.gather(n)

            @pl.when(both(n >= 1, n <= UNITS))
            def _():
                self.finish(n - 1)

        @pl.when(n + AHEAD < UNITS)
        def _():
            self.offer(n + AHEAD)

        @pl.when(n >= 2)
        def _():
            @pl.when(self.here.is_end)
            def _():
                self.accept(n - 2)

    def drain(self):
        @pl.when(self.here.is_centre)
        def _():
            for u in range(UNITS - SLOTS, UNITS):
                self.across(u).wait_send()
                self.outward(u).wait_send()
                self.store(u, self.total).wait()

        @pl.when(self.here.is_end)
        def _():
            for u in range(UNITS - SLOTS, UNITS):
                self.inward(u).wait_send()
            self.store(UNITS - 1, self.ring_in).wait()


class RankSum:
    def __init__(self, here, part, pairs, wide_x, wide_y, last_x, last_y, sems):
        self.here, self.part, self.pairs = here, part, pairs
        self.wide_x, self.wide_y, self.last_x, self.last_y, self.sems = wide_x, wide_y, last_x, last_y, sems
        self.rows = part.shape[3]
        self.upper = pl.ds(0, self.rows // 2)
        self.lower = pl.ds(self.rows // 2, self.rows // 2)
        self.step = 16

    def copy(self, k, s, src, dst, target):
        return remote(src, dst, self.sems.at[s, k, 0], self.sems.at[s, k, 1], target)

    def swap(self, s):
        return self.copy(0, s, self.part.at[:, :, 1 - self.here.c], self.pairs.at[s], self.here.core)

    def wide(self, s):
        h = self.here
        return (
            self.copy(1, s, self.pairs.at[s, :, 1 - h.x, self.upper], self.wide_x.at[s], h.across_x),
            self.copy(2, s, self.pairs.at[s, 1 - h.y, :, self.lower], self.wide_y.at[s], h.across_y),
        )

    def last(self, s):
        h = self.here
        return (
            self.copy(3, s, self.pairs.at[s, 1 - h.y, h.x, self.upper], self.last_y.at[s], h.across_y),
            self.copy(4, s, self.pairs.at[s, h.y, 1 - h.x, self.lower], self.last_x.at[s], h.across_x),
        )

    def start(self, s):
        self.swap(s).start()

    def cross(self, s):
        h = self.here
        self.swap(s).wait()

        def rows(r):
            at = pl.ds(r, self.step)
            for y in range(2):
                for x in range(2):
                    self.pairs[s, y, x, at, :] = self.pairs[s, y, x, at, :] + self.part[y, x, h.c, at, :]

        tiles(self.rows, self.step, rows)
        for copy in self.wide(s):
            copy.start()

    def turn(self, s):
        h = self.here
        half = self.rows // 2
        for copy in self.wide(s):
            copy.wait()

        def rows(r):
            at, low = pl.ds(r, self.step), pl.ds(half + r, self.step)
            for k in range(2):
                self.pairs[s, k, h.x, at, :] = self.pairs[s, k, h.x, at, :] + self.wide_x[s, k, at, :]
                self.pairs[s, h.y, k, low, :] = self.pairs[s, h.y, k, low, :] + self.wide_y[s, k, at, :]

        tiles(half, self.step, rows)
        for copy in self.last(s):
            copy.start()

    def done(self, s, out):
        h = self.here
        half = self.rows // 2
        for copy in self.last(s):
            copy.wait()

        def rows(r):
            at, low = pl.ds(r, self.step), pl.ds(half + r, self.step)
            out[at, :] = self.pairs[s, h.y, h.x, at, :] + self.last_y[s, at, :]
            out[low, :] = self.pairs[s, h.y, h.x, low, :] + self.last_x[s, at, :]

        tiles(half, self.step, rows)


def sum_scratch(seqs, hidden, third, rows, cols):
    return [
        pltpu.VMEM((UNITS, hidden, third), BF16),
        pltpu.VMEM((SLOTS, hidden, third), BF16),
        pltpu.VMEM((SLOTS, hidden, third), BF16),
        pltpu.VMEM((SLOTS, hidden, third), BF16),
        pltpu.SemaphoreType.DMA((7, SLOTS)),
        pltpu.SemaphoreType.REGULAR,
        pltpu.SemaphoreType.REGULAR,
        pltpu.SemaphoreType.REGULAR,
        pltpu.VMEM((2, 2, 2, rows, cols), BF16),
        pltpu.VMEM((seqs, 2, 2, rows, cols), BF16),
        pltpu.VMEM((seqs, 2, rows // 2, cols), BF16),
        pltpu.VMEM((seqs, 2, rows // 2, cols), BF16),
        pltpu.VMEM((seqs, rows // 2, cols), BF16),
        pltpu.VMEM((seqs, rows // 2, cols), BF16),
        pltpu.SemaphoreType.DMA((seqs, 5, 2)),
        pltpu.SemaphoreType.DMA((8,)),
    ]


def backward_kernel(second, seqs, hidden, length, width, *refs):
    third = width // THIRDS
    if second:
        d_in, r_in, w_in, pre_in, cell_in, h_in, gw_out, d_out, db_out, h_out = refs[:10]
        dv, wv, rv, pre, cell, work, edge, grad, hsem = refs[10:19]
        rest = refs[19:]
    else:
        d_in, r_in, w_in, gw_out, gx_out = refs[:5]
        dv, wv, rv, gxv = refs[5:9]
        rest = refs[9:]
    own, ring_in, ring_mid, total, zsem, *credits = rest[:8]
    rank_refs, lsem = rest[8:15], rest[15]
    here = Here()
    ar = SeqSum(here, hidden, third, own, ring_in, ring_mid, total, gw_out, zsem, credits)
    rs = RankSum(here, *rank_refs)
    groups = length // LANES

    def columns_of(s):
        return pl.ds(s * length, length)

    def rhs(t):
        if second:
            src = r_in.at[pl.ds(t * third, third), :]
        else:
            src = r_in.at[:, pl.ds(t * third, third)]
        return pltpu.make_async_copy(src, rv.at[t % 2], lsem.at[t % 2])

    loads = [pltpu.make_async_copy(d_in, dv, lsem.at[2]), pltpu.make_async_copy(w_in, wv, lsem.at[3])]
    if second:
        loads.append(pltpu.make_async_copy(pre_in, pre, lsem.at[4]))
        loads.append(pltpu.make_async_copy(cell_in, cell, lsem.at[5]))
    loads[0].start()
    rhs(0).start()
    for copy in loads[1:]:
        copy.start()
    rhs(1).start()
    near = here.peers if second else [here.core, here.across_x, here.across_y]
    meet(near + [here.pair, here.middle])
    spread = []
    if second:
        spread.append(pltpu.make_async_copy(h_in.at[here.b], h_out.at[here.b], hsem.at[0, 0]))
        for d, peer in enumerate(here.peers, 1):
            spread.append(remote(h_in.at[peer["tm"]], h_out.at[here.b], hsem.at[d, 0], hsem.at[d, 1], peer))
        for copy in spread:
            copy.start()

    def units(t, ks):
        for k in ks:
            rows = pl.ds(k * hidden, hidden)
            own[t * 6 + k] = dot(dv[rows, :], rv[t % 2], NT if second else NN).astype(BF16)
            if t * 6 + k < AHEAD:
                ar.offer(t * 6 + k)

    def part(s, piece):
        if second:
            i, start = piece // 2, piece % 2 * (length // 2)
            lhs = pl.ds(i * (width // 2), width // 2)

            def strip(c):
                cols = pl.ds(pl.multiple_of(start + c, 256), 256)
                src = pl.ds(pl.multiple_of(s * length + start + c, 256), 256)
                got = dot(wv[:, lhs], dv[:, src], TN).astype(BF16)
                rs.part[i, :, :, :, cols] = got.reshape(2, 2, hidden, 256)

            tiles(length // 2, 256, strip)
        else:
            rows = LANES // 8
            low, high = (width // 256 * q // 4 * 256 for q in (piece, piece + 1))

            def strip(c):
                cols = pl.ds(pl.multiple_of(low + c, 256), 256)
                got = dot(dv[:, columns_of(s)], wv[:, cols], TN).astype(BF16)
                for j in range(groups):
                    block = got[j * LANES : (j + 1) * LANES].reshape(2, 2, 2, rows, 256)
                    rs.part[:, :, :, pl.ds(j * rows, rows), cols] = block

            tiles(high - low, 256, strip)

    ticks = iter(range(UNITS + 2))

    def tick():
        ar.tick(next(ticks))

    def settle(s):
        rs.done(s, grad.at[:, columns_of(s)] if second else gxv.at[s])

    loads[0].wait()
    rhs(0).wait()
    units(0, range(6))
    rhs(2).start()
    loads[1].wait()
    part(0, 0)
    part(0, 1)
    tick()
    part(0, 2)
    part(0, 3)
    rs.start(0)
    tick()
    rhs(1).wait()
    units(1, range(3))
    rs.cross(0)
    tick()
    part(1, 0)
    part(1, 1)
    part(1, 2)
    tick()
    part(1, 3)
    rs.start(1)
    units(1, range(3, 6))
    tick()
    rs.turn(0)
    rhs(2).wait()
    units(2, range(2))
    rs.cross(1)
    units(2, range(2, 4))
    tick()
    units(2, range(4, 6))
    settle(0)
    if second:
        for copy in loads[2:]:
            copy.wait()
        stores = [
            pltpu.make_async_copy(dv.at[:, columns_of(s)], d_out.at[:, columns_of(s)], lsem.at[6 + s])
            for s in range(seqs)
        ]

        def pool(s):
            first = s * length
            pool_backward(first, grad, pre, cell, first, dv, db_out.at[s], work, edge, hidden, groups)
            stores[s].start()

        tick()
        pool(0)
    else:
        tick()
    rs.turn(1)
    tick()
    tick()
    settle(1)
    if second:
        pool(1)
    else:
        stores = [pltpu.make_async_copy(gxv, gx_out, lsem.at[6])]
        stores[0].start()

    def more(n, carry):
        ar.tick(n)
        return carry

    lax.fori_loop(next(ticks), UNITS + 2, more, 0)
    ar.drain()
    for copy in stores + spread:
        copy.wait()


def run_backward(seqs, d, rhs, weight, layer_one=None):
    second = layer_one is not None
    (wide, width), total = weight.shape, d.shape[1]
    hidden, length = wide // 6, total // seqs
    third, span = width // THIRDS, length // 8
    outs = [shape((6, hidden, width), BF16)]
    scratch = [pltpu.VMEM((wide, total), BF16), pltpu.VMEM((wide, width), BF16)]
    if second:
        outs += [shape((wide, total), BF16), shape((seqs, hidden, 1), F32), shape(layer_one[2].shape, BF16)]
        specs = [ANY, ANY, pl.BlockSpec(memory_space=pltpu.VMEM), ANY]
        rows, cols = hidden, length
        scratch += [
            pltpu.VMEM((2, third, total), BF16),
            pltpu.VMEM((3 * hidden, total), BF16),
            pltpu.VMEM((hidden, total), F32),
            pltpu.VMEM((2, hidden, length), F32),
            pltpu.VMEM((2, hidden, LANES), F32),
            pltpu.VMEM((hidden, total), BF16),
            pltpu.SemaphoreType.DMA((8, 2)),
        ]
    else:
        outs += [shape((seqs, span, width), BF16)]
        specs = [ANY, ANY]
        rows, cols = span, width
        scratch += [pltpu.VMEM((2, total, third), BF16), pltpu.VMEM((seqs, span, width), BF16)]
    operands = (d, rhs, weight) + (layer_one or ())
    return pl.pallas_call(
        functools.partial(backward_kernel, second, seqs, hidden, length, width),
        name="layer_two_backward" if second else "layer_one_backward",
        in_specs=[ANY] * len(operands),
        out_specs=specs,
        out_shape=outs,
        scratch_shapes=scratch + sum_scratch(seqs, hidden, third, rows, cols),
        compiler_params=params(collective_id=1 if second else 2, has_side_effects=True),
    )(*operands)


class Gather:
    def __init__(self, here, own, region, sems):
        h, b = here, here.b
        bx, by = h.across_x["tm"], h.across_y["tm"]
        bd = bx + 4 - 8 * h.y
        plan = (
            (own, region(b, None), h.across_x),
            (own, region(b, None), h.across_y),
            (own, region(b, None), h.core),
            (region(bx, 1), region(bx, 1), h.across_y),
            (region(by, 0), region(by, 0), h.across_x),
            (region(bx, None), region(bx, None), h.core),
            (region(by, None), region(by, None), h.core),
            (region(bd, 0), region(bd, 0), h.core),
            (region(bd, 1), region(bd, 1), h.core),
        )
        self.copies = [remote(src, dst, sems.at[k, 0], sems.at[k, 1], to) for k, (src, dst, to) in enumerate(plan)]

    def start(self):
        for k in (0, 1, 2):
            self.copies[k].start()

    def relay(self):
        self.copies[0].wait_recv()
        self.copies[3].start()
        self.copies[1].wait_recv()
        self.copies[4].start()
        self.copies[5].start()
        self.copies[6].start()

    def share(self):
        self.copies[4].wait_recv()
        self.copies[7].start()
        self.copies[3].wait_recv()
        self.copies[8].start()
        for k in (2, 5, 6, 7, 8):
            self.copies[k].wait_recv()

    def drain(self):
        for copy in self.copies:
            copy.wait_send()


def forward_kernel(seqs, hidden, length, width, *refs):
    x_in, w1_in, w2_in, seed_in, b1, b2, starts = refs[:7]
    x_out, h1_out, pre_out, cell_out, h2_out, d_out, db_out = refs[7:14]
    xg, hg, w, p, pre, cell, work, edge, dv, seed, grad, hv, h2t, xsem, hsem, ssem, lsem = refs[14:]
    here = Here()
    groups = length // LANES
    piece = LANES // 8

    def columns_of(s):
        return pl.ds(s * length, length)

    def x_region(s):
        def region(b, half):
            js = pl.ds(0, groups) if half is None else pl.ds(half * (groups // 2), groups // 2)
            return xg.at[s, js, b]

        return region

    def h_region(s):
        def region(b, half):
            rows = pl.ds(0, hidden) if half is None else pl.ds(half * (hidden // 2), hidden // 2)
            return hg.at[b, rows, columns_of(s)]

        return region

    def load(src, dst, k):
        return pltpu.make_async_copy(src, dst, lsem.at[k])

    load_w1 = load(w1_in, w, 0)
    load_w2 = load(w2_in, w, 0)
    mine = [load(x_in.at[s], xg.at[s, :, here.b], 1 + s) for s in range(seqs)]
    store_x = [load(xg.at[s], x_out.at[s], 3 + s) for s in range(seqs)]
    store_h = [load(hg.at[:, :, columns_of(s)], h1_out.at[:, :, columns_of(s)], 5 + s) for s in range(seqs)]
    store_p = [load(pre.at[:, columns_of(s)], pre_out.at[:, columns_of(s)], 7 + s) for s in range(seqs)]
    store_c = [load(cell.at[:, columns_of(s)], cell_out.at[:, columns_of(s)], 9 + s) for s in range(seqs)]
    store_d = [load(dv.at[s], d_out.at[:, columns_of(s)], 11 + s) for s in range(seqs)]
    store_o = load(h2t, h2_out, 13)

    load_w1.start()
    for copy in mine:
        copy.start()
    meet(here.peers)
    xs = [Gather(here, x_in.at[s], x_region(s), xsem.at[s]) for s in range(seqs)]
    hs = [Gather(here, h_region(s)(here.b, None), h_region(s), hsem.at[s]) for s in range(seqs)]

    late = [
        (remote(seed_in.at[peer["tm"]], seed.at[:, :, here.b], ssem.at[d, 0], ssem.at[d, 1], peer), peer)
        for d, peer in enumerate(here.peers, 1)
    ]

    def first_products(s):
        for i in range(2):
            js = pl.ds(i * (groups // 2), groups // 2)
            rhs = xg[s, js].reshape(length // 2, width)
            p[:, pl.ds(i * (length // 2), length // 2)] = dot(w[...], rhs, NT)

    def second_products(s):
        for i in range(2):
            cols = pl.ds(s * length + i * (length // 2), length // 2)
            rhs = hg[:, :, cols].reshape(width, length // 2)
            p[:, pl.ds(i * (length // 2), length // 2)] = dot(w[...], rhs, NN)

    def first_pool(s):
        first = s * length
        pool_forward(first, p, b1, pre, cell, first, hg.at[here.b], work.at[0], edge.at[0], hidden, groups)

    def second_pool(s):
        pool_forward(s * length, p, b2, pre, cell, 0, hv, work.at[0], edge.at[0], hidden, groups)
        rows = lax.broadcasted_iota(jnp.int32, (LANES, LANES), 0)
        cols = lax.broadcasted_iota(jnp.int32, (LANES, LANES), 1)
        eye = (rows == cols).astype(BF16)
        for j in range(groups):
            turned = dot(eye, hv[:, pl.ds(j * LANES, LANES)], NT).astype(BF16)
            at = pl.ds((s * groups + j) * piece, piece)
            h2t[:, at, :] = turned.reshape(8, piece, hidden)

    def incoming(s):
        rows = lax.broadcasted_iota(jnp.int32, (hidden, hidden), 0)
        cols = lax.broadcasted_iota(jnp.int32, (hidden, hidden), 1)
        eye = (rows == cols).astype(BF16)
        lane = lax.broadcasted_iota(jnp.int32, (1, LANES), 1)
        for j in range(groups):
            block = seed[s, j].reshape(LANES, hidden)
            turned = dot(eye, block, NT)
            step = lane * groups + j
            keep = jnp.zeros((1, LANES), jnp.bool_)
            for k in range(starts.shape[1]):
                begin = starts[s, k]
                keep = jnp.logical_or(keep, jnp.logical_and(step >= begin, step < begin + CLUSTER))
            keep = jnp.broadcast_to(keep, (hidden, LANES))
            grad[:, pl.ds(s * length + j * LANES, LANES)] = jnp.where(keep, turned, 0.0).astype(BF16)

    def pool_back(s):
        pool_backward(s * length, grad, pre, cell, 0, dv.at[s], db_out.at[s], work, edge, hidden, groups)
        store_d[s].start()

    xs[0].start()
    seed[:, :, pl.ds(0, 4)] = jnp.zeros((seqs, groups, 4, piece, hidden), BF16)
    xs[0].relay()
    xs[1].start()
    xs[0].share()
    mine[0].wait()
    store_x[0].start()
    load_w1.wait()
    first_products(0)
    xs[1].relay()
    first_pool(0)
    hs[0].start()
    store_p[0].start()
    store_c[0].start()
    xs[1].share()
    mine[1].wait()
    store_x[1].start()
    first_products(1)
    load_w2.start()
    hs[0].relay()
    first_pool(1)
    hs[1].start()
    store_p[1].start()
    store_c[1].start()

    @pl.when(here.y == 1)
    def _():
        pltpu.make_async_copy(seed_in.at[here.b], seed.at[:, :, here.b], ssem.at[0, 0]).start()
        for copy, _ in late:
            copy.start()

    hs[0].share()
    store_h[0].start()
    load_w2.wait()
    second_products(0)
    hs[1].relay()
    store_p[0].wait()
    store_c[0].wait()
    second_pool(0)
    hs[1].share()
    store_h[1].start()
    second_products(1)
    store_p[1].wait()
    store_c[1].wait()
    second_pool(1)
    store_o.start()

    @pl.when(here.y == 1)
    def _():
        pltpu.make_async_copy(seed_in.at[here.b], seed.at[:, :, here.b], ssem.at[0, 0]).wait()
        for copy, _ in late:
            copy.wait_send()

    for d, (copy, _) in enumerate(late, 1):
        source = lax.rem(here.b + 8 - d, 8)

        @pl.when(source >= 4)
        def _(copy=copy):
            copy.wait_recv()

    for s in range(seqs):
        incoming(s)
        pool_back(s)
    for gather in xs + hs:
        gather.drain()
    for copy in store_x + store_h + store_d + [store_o]:
        copy.wait()


def run_forward(x, w1, b1, w2, b2, seed, starts):
    seqs, groups, piece, width = x.shape
    hidden, length = w1.shape[0] // 6, groups * LANES
    total = seqs * length
    vmem = pl.BlockSpec(memory_space=pltpu.VMEM)
    return pl.pallas_call(
        functools.partial(forward_kernel, seqs, hidden, length, width),
        name="forward",
        in_specs=[ANY, ANY, ANY, ANY, vmem, vmem, pl.BlockSpec(memory_space=pltpu.SMEM)],
        out_specs=[ANY, ANY, ANY, ANY, ANY, ANY, vmem],
        out_shape=[
            shape((seqs, groups, 8, piece, width), BF16),
            shape((8, hidden, total), BF16),
            shape((3 * hidden, total), BF16),
            shape((hidden, total), F32),
            shape((8, seqs * groups * piece, hidden), BF16),
            shape((6 * hidden, total), BF16),
            shape((seqs, hidden, 1), F32),
        ],
        scratch_shapes=[
            pltpu.VMEM((seqs, groups, 8, piece, width), BF16),
            pltpu.VMEM((8, hidden, total), BF16),
            pltpu.VMEM((6 * hidden, width), BF16),
            pltpu.VMEM((6 * hidden, length), F32),
            pltpu.VMEM((3 * hidden, total), BF16),
            pltpu.VMEM((hidden, total), F32),
            pltpu.VMEM((2, hidden, length), F32),
            pltpu.VMEM((2, hidden, LANES), F32),
            pltpu.VMEM((seqs, 6 * hidden, length), BF16),
            pltpu.VMEM((seqs, groups, 8, piece, hidden), BF16),
            pltpu.VMEM((hidden, total), BF16),
            pltpu.VMEM((hidden, length), BF16),
            pltpu.VMEM((8, seqs * groups * piece, hidden), BF16),
            pltpu.SemaphoreType.DMA((seqs, 9, 2)),
            pltpu.SemaphoreType.DMA((seqs, 9, 2)),
            pltpu.SemaphoreType.DMA((8, 2)),
            pltpu.SemaphoreType.DMA((14,)),
        ],
        compiler_params=params(collective_id=0, has_side_effects=True),
    )(x, w1, w2, seed, b1, b2, starts)


def per_device(line, inputs, weight_one, fbias_one, weight_two, fbias_two, cotangent, cluster_starts):
    seqs, span, width = inputs.shape
    count = lax.axis_size("tm")
    length = span * count
    groups = length // LANES
    piece = LANES // count
    hidden = weight_one.shape[2]
    total = seqs * length
    w1 = weight_one.reshape(6 * hidden, width)
    w2 = weight_two.reshape(6 * hidden, width)

    x = inputs.reshape(seqs, piece, groups, width).transpose(0, 2, 1, 3)
    bias1, bias2 = fbias_one[:, None], fbias_two[:, None]
    seed = cotangent.reshape(seqs, piece, groups, count, hidden)
    if line:
        seed = seed.transpose(3, 0, 2, 1, 4)
        x, h1, pre1, cell1, h2, d2, db2 = run_forward(x, w1, bias1, w2, bias2, seed, cluster_starts)
        x, h1 = x.reshape(total, width), h1.reshape(width, total)
        gw2, d1, db1, h2 = run_backward(seqs, d2, h1, w2, (pre1, cell1, h2))
        h2 = h2.reshape(count, seqs, groups, piece, hidden).transpose(1, 3, 2, 0, 4)
        gw1, gx1 = run_backward(seqs, d1, x, w1)
        gx1 = gx1.reshape(seqs, groups, piece, width)
    else:
        steps = lax.axis_index("tm") * span + jnp.arange(span, dtype=jnp.int32)
        starts = cluster_starts[:, :, None]
        keep = jnp.any((steps >= starts) & (steps < starts + CLUSTER), axis=1)
        seed = jnp.where(keep.reshape(seqs, piece, groups, 1, 1), seed, jnp.zeros_like(seed))
        seed = lax.all_to_all(seed, "tm", split_axis=3, concat_axis=1, tiled=True)
        seed = seed.reshape(seqs, LANES, groups, hidden).transpose(3, 0, 2, 1).reshape(hidden, total)
        x = lax.all_gather(x, "tm", axis=2, tiled=True).reshape(total, width)
        pre1, cell1, h1 = run_first(seqs, w1, bias1, x)
        h1 = lax.all_gather(h1, "tm", axis=0, tiled=True)
        h2, d2, db2 = run_second(seqs, w2, bias2, h1, seed)
        h2 = h2.reshape(hidden, seqs, groups, count, piece)
        h2 = lax.all_to_all(h2, "tm", split_axis=3, concat_axis=0, tiled=True)
        h2 = h2.reshape(width, seqs, groups, piece).transpose(1, 3, 2, 0)
        gw2 = lax.psum(dot(d2, h1, NT).astype(BF16), "seq")
        gx2 = lax.psum_scatter(dot(w2, d2, TN).astype(BF16), "tm", scatter_dimension=0, tiled=True)
        d1, db1 = run_back(seqs, gx2, pre1, cell1)
        gw1 = lax.psum(dot(d1, x, NN).astype(BF16), "seq")
        gx1 = dot(d1, w1, TN).astype(BF16).reshape(seqs, groups, LANES, width)
        gx1 = lax.psum_scatter(gx1, "tm", scatter_dimension=2, tiled=True)
    out = h2.reshape(seqs, span, width)
    gx1 = gx1.transpose(0, 2, 1, 3).reshape(seqs, span, width)
    db = lax.psum(jnp.stack([db1, db2]).sum(axis=(1, 3)), "seq")
    dims = weight_one.shape
    return (out, gx1, gw1.astype(F32).reshape(dims), db[0], gw2.astype(F32).reshape(dims), db[1])


def solution(mesh):
    placed = (
        P("seq", "tm", None),
        P(None, None, "tm", None),
        P("tm"),
        P(None, None, "tm", None),
        P("tm"),
        P("seq", "tm", None),
        P("seq", None),
    )
    return jax.shard_map(
        functools.partial(per_device, dict(mesh.shape) == {"seq": 4, "tm": 8}),
        mesh=mesh,
        in_specs=placed,
        out_specs=(
            P("seq", "tm", None),
            P("seq", "tm", None),
            P(None, None, "tm", None),
            P("tm"),
            P(None, None, "tm", None),
            P("tm"),
        ),
        check_vma=False,
    )
```

```python
import functools

import jax
import jax.numpy as jnp
from jax import lax
from jax.experimental import pallas as pl
from jax.experimental.pallas import tpu as pltpu
from jax.sharding import PartitionSpec as P

CLUSTER = 32
LANES = 128
ROWS = 48
F32 = jnp.float32
BF16 = jnp.bfloat16
ANY = pl.BlockSpec(memory_space=pl.ANY)
MESH = pl.DeviceIdType.MESH
NN = (((1,), (0,)), ((), ()))
NT = (((1,), (1,)), ((), ()))
TN = (((0,), (0,)), ((), ()))


def dot(a, b, dims):
    return lax.dot_general(a, b, dims, preferred_element_type=F32)


def sigmoid(v):
    return 1.0 / (1.0 + jnp.exp(-v))


def tiles(count, rows, body):
    def step(r, carry):
        body(pl.multiple_of(r * rows, rows))
        return carry

    lax.fori_loop(0, count // rows, step, 0)


def shift_lanes(v, amount, lane, fill):
    moved = pltpu.roll(v, amount % LANES, axis=1)
    gone = lane < amount if amount > 0 else lane >= LANES + amount
    return jnp.where(gone, fill, moved)


def lane_chain(factor, value, lane, sign):
    step = 1
    while step < LANES:
        value = value + factor * shift_lanes(value, sign * step, lane, 0.0)
        factor = factor * shift_lanes(factor, sign * step, lane, 1.0)
        step *= 2
    return value


def pool_forward(first, p_ref, b_ref, pre_ref, cell_ref, target, h_ref, factor_ref, edge_ref, hidden, groups):
    lane = lax.broadcasted_iota(jnp.int32, (ROWS, LANES), 1)

    def at(j, start=0):
        return pl.ds(start + j * LANES, LANES)

    def gates(r):
        rows = pl.ds(r, ROWS)
        value = factor = None
        for j in range(groups):
            got = []
            for g in range(3):
                now = p_ref[pl.ds(g * hidden + r, ROWS), at(j)]
                tap = pl.ds((3 + g) * hidden + r, ROWS)
                if j:
                    past = p_ref[tap, at(j - 1)]
                else:
                    past = shift_lanes(p_ref[tap, at(groups - 1)], 1, lane, 0.0)
                total = now + past
                if g == 1:
                    total = total + b_ref[rows, :]
                total = total.astype(BF16)
                pre_ref[pl.ds(g * hidden + r, ROWS), at(j, first)] = total
                got.append(total.astype(F32))
            forget = sigmoid(got[1])
            fresh = (1.0 - forget) * jnp.tanh(got[0])
            if j:
                value = forget * value + fresh
                factor = forget * factor
            else:
                value, factor = fresh, forget
            cell_ref[rows, at(j, first)] = value
            factor_ref[rows, at(j)] = factor

    tiles(hidden, ROWS, gates)

    def chain(r):
        rows = pl.ds(r, ROWS)
        value = lane_chain(factor_ref[rows, at(groups - 1)], cell_ref[rows, at(groups - 1, first)], lane, 1)
        edge_ref[rows, :] = shift_lanes(value, 1, lane, 0.0)

    tiles(hidden, ROWS, chain)

    def finish(r):
        rows = pl.ds(r, ROWS)
        edge = edge_ref[rows, :]
        for j in range(groups):
            cell = cell_ref[rows, at(j, first)] + factor_ref[rows, at(j)] * edge
            cell_ref[rows, at(j, first)] = cell
            outgate = sigmoid(pre_ref[pl.ds(2 * hidden + r, ROWS), at(j, first)].astype(F32))
            h_ref[rows, at(j, target)] = (outgate * cell).astype(BF16)

    tiles(hidden, ROWS, finish)


def put_gate(d_ref, g, r, j, v, target, lane, hidden, groups):
    d_ref[pl.ds(g * hidden + r, ROWS), pl.ds(target + j * LANES, LANES)] = v
    tap = pl.ds((3 + g) * hidden + r, ROWS)
    if j:
        d_ref[tap, pl.ds(target + (j - 1) * LANES, LANES)] = v
    else:
        moved = shift_lanes(v.astype(F32), -1, lane, 0.0).astype(BF16)
        d_ref[tap, pl.ds(target + (groups - 1) * LANES, LANES)] = moved


def outgate_backward(first, g_ref, pre_ref, cell_ref, d_ref, hidden, groups):
    lane = lax.broadcasted_iota(jnp.int32, (ROWS, LANES), 1)

    def body(r):
        rows = pl.ds(r, ROWS)
        for j in range(groups):
            at = pl.ds(first + j * LANES, LANES)
            outgate = sigmoid(pre_ref[pl.ds(2 * hidden + r, ROWS), at].astype(F32))
            v = g_ref[rows, at].astype(F32) * cell_ref[rows, at] * outgate * (1.0 - outgate)
            put_gate(d_ref, 2, r, j, v.astype(BF16), 0, lane, hidden, groups)

    tiles(hidden, ROWS, body)


def pool_backward(
    first, g_ref, pre_ref, cell_ref, target, d_ref, db_ref, work_ref, edge_ref, hidden, groups, carried_only=False
):
    lane = lax.broadcasted_iota(jnp.int32, (ROWS, LANES), 1)

    def at(j, start=0):
        return pl.ds(start + j * LANES, LANES)

    def gate(g, r, j):
        return pre_ref[pl.ds(g * hidden + r, ROWS), at(j, first)].astype(F32)

    def start(r):
        rows = pl.ds(r, ROWS)
        later = value = factor = None
        for j in reversed(range(groups)):
            own = g_ref[rows, at(j, first)].astype(F32) * sigmoid(gate(2, r, j))
            if later is None:
                value, factor = own, jnp.ones_like(own)
            else:
                value = own + later * value
                factor = later * factor
            work_ref[0, rows, at(j)] = value
            work_ref[1, rows, at(j)] = factor
            later = sigmoid(gate(1, r, j))
        edge_ref[0, rows, :] = later * value
        edge_ref[1, rows, :] = later * factor

    tiles(hidden, ROWS, start)

    def chain(r):
        rows = pl.ds(r, ROWS)
        value = lane_chain(edge_ref[1, rows, :], edge_ref[0, rows, :], lane, -1)
        edge_ref[0, rows, :] = shift_lanes(value, -1, lane, 0.0)

    tiles(hidden, ROWS, chain)

    def finish(r):
        rows = pl.ds(r, ROWS)
        edge = edge_ref[0, rows, :]
        total = jnp.zeros((ROWS, LANES), F32)
        before = shift_lanes(cell_ref[rows, at(groups - 1, first)], 1, lane, 0.0)
        for j in range(groups):
            carried = work_ref[0, rows, at(j)] + work_ref[1, rows, at(j)] * edge
            candidate = jnp.tanh(gate(0, r, j))
            forget = sigmoid(gate(1, r, j))
            cell = cell_ref[rows, at(j, first)]
            keep = carried * (1.0 - forget)
            got = [keep * (1.0 - candidate * candidate), keep * forget * (before - candidate)]
            if not carried_only:
                outgate = sigmoid(gate(2, r, j))
                got.append(g_ref[rows, at(j, first)].astype(F32) * cell * outgate * (1.0 - outgate))
            before = cell
            for g, v in enumerate(got):
                v = v.astype(BF16)
                if g == 1:
                    total = total + v.astype(F32)
                put_gate(d_ref, g, r, j, v, target, lane, hidden, groups)
        db_ref[rows, :] = jnp.sum(total, axis=1, keepdims=True)

    tiles(hidden, ROWS, finish)


def first_kernel(hidden, length, w_ref, b_ref, x_ref, pre_ref, cell_ref, h_ref, p_ref, work_ref, edge_ref):
    def strip(c):
        cols = pl.ds(c, 512)
        p_ref[:, cols] = dot(w_ref[...], x_ref[cols, :], NT)

    tiles(length, 512, strip)
    pool_forward(0, p_ref, b_ref, pre_ref, cell_ref, 0, h_ref, work_ref, edge_ref, hidden, length // LANES)


def second_kernel(
    hidden, length, w_ref, b_ref, x_ref, g_ref, h_ref, d_ref, db_ref, p_ref, pre_ref, cell_ref, work_ref, edge_ref
):
    def strip(c):
        cols = pl.ds(c, 512)
        p_ref[:, cols] = dot(w_ref[...], x_ref[:, cols], NN)

    tiles(length, 512, strip)
    groups = length // LANES
    pool_forward(0, p_ref, b_ref, pre_ref, cell_ref, 0, h_ref, work_ref.at[0], edge_ref.at[0], hidden, groups)
    pool_backward(0, g_ref, pre_ref, cell_ref, 0, d_ref, db_ref.at[0], work_ref, edge_ref, hidden, groups)


def back_kernel(hidden, length, g_ref, pre_ref, cell_ref, d_ref, db_ref, work_ref, edge_ref):
    pool_backward(0, g_ref, pre_ref, cell_ref, 0, d_ref, db_ref.at[0], work_ref, edge_ref, hidden, length // LANES)


def columns(rows, length):
    return pl.BlockSpec((rows, length), lambda s: (0, s))


def fixed(*dims):
    return pl.BlockSpec(dims, lambda s: (0,) * len(dims), pipeline_mode=pl.Buffered(1))


def params(**more):
    return pltpu.CompilerParams(vmem_limit_bytes=63 * 1024 * 1024, **more)


shape = jax.ShapeDtypeStruct


def run_first(seqs, weight, bias, gathered):
    (wide, width), total = weight.shape, gathered.shape[0]
    hidden, length = wide // 6, total // seqs
    return pl.pallas_call(
        functools.partial(first_kernel, hidden, length),
        name="layer_one_forward",
        grid=(seqs,),
        in_specs=[fixed(wide, width), fixed(hidden, 1), pl.BlockSpec((length, width), lambda s: (s, 0))],
        out_specs=[columns(3 * hidden, length), columns(hidden, length), columns(hidden, length)],
        out_shape=[shape((3 * hidden, total), BF16), shape((hidden, total), F32), shape((hidden, total), BF16)],
        scratch_shapes=[
            pltpu.VMEM((wide, length), F32),
            pltpu.VMEM((hidden, length), F32),
            pltpu.VMEM((hidden, LANES), F32),
        ],
        compiler_params=params(),
    )(weight, bias, gathered)


def run_second(seqs, weight, bias, gathered, grad):
    (wide, width), total = weight.shape, gathered.shape[1]
    hidden, length = wide // 6, total // seqs
    return pl.pallas_call(
        functools.partial(second_kernel, hidden, length),
        name="layer_two_forward_and_pool_backward",
        grid=(seqs,),
        in_specs=[fixed(wide, width), fixed(hidden, 1), columns(width, length), columns(hidden, length)],
        out_specs=[columns(hidden, length), columns(wide, length), pl.BlockSpec((1, hidden, 1), lambda s: (s, 0, 0))],
        out_shape=[shape((hidden, total), BF16), shape((wide, total), BF16), shape((seqs, hidden, 1), F32)],
        scratch_shapes=[
            pltpu.VMEM((wide, length), F32),
            pltpu.VMEM((3 * hidden, length), BF16),
            pltpu.VMEM((hidden, length), F32),
            pltpu.VMEM((2, hidden, length), F32),
            pltpu.VMEM((2, hidden, LANES), F32),
        ],
        compiler_params=params(),
    )(weight, bias, gathered, grad)


def run_back(seqs, grad, pre, cell):
    hidden, total = grad.shape
    length = total // seqs
    return pl.pallas_call(
        functools.partial(back_kernel, hidden, length),
        name="layer_one_pool_backward",
        grid=(seqs,),
        in_specs=[columns(hidden, length), columns(3 * hidden, length), columns(hidden, length)],
        out_specs=[columns(6 * hidden, length), pl.BlockSpec((1, hidden, 1), lambda s: (s, 0, 0))],
        out_shape=[shape((6 * hidden, total), BF16), shape((seqs, hidden, 1), F32)],
        scratch_shapes=[pltpu.VMEM((2, hidden, length), F32), pltpu.VMEM((2, hidden, LANES), F32)],
        compiler_params=params(),
    )(grad, pre, cell)


THIRDS = 3
PIECES = 3
SLOTS = 12
AHEAD = 6


class Here:
    def __init__(self):
        self.z = lax.axis_index("seq")
        self.b = lax.axis_index("tm")
        self.c = lax.rem(self.b, 2)
        self.x = lax.rem(self.b // 2, 2)
        self.y = self.b // 4
        self.core = dict(seq=self.z, tm=self.b + 1 - 2 * self.c)
        self.across_x = dict(seq=self.z, tm=self.b + 2 - 4 * self.x)
        self.across_y = dict(seq=self.z, tm=self.b + 4 - 8 * self.y)
        self.pair = dict(seq=self.z + 1 - 2 * lax.rem(self.z, 2), tm=self.b)
        self.middle = dict(seq=3 - self.z, tm=self.b)
        self.line = [dict(seq=lax.rem(self.z + d, 4), tm=self.b) for d in range(1, 4)]
        self.peers = [dict(seq=self.z, tm=lax.rem(self.b + d, 8)) for d in range(1, 8)]
        self.is_end = jnp.logical_or(self.z == 0, self.z == 3)
        self.is_centre = jnp.logical_and(self.z > 0, self.z < 3)


def remote(src, dst, send, recv, target):
    return pltpu.make_async_remote_copy(
        src_ref=src, dst_ref=dst, send_sem=send, recv_sem=recv, device_id=target, device_id_type=MESH
    )


def both(a, b):
    if isinstance(a, bool) and isinstance(b, bool):
        return a and b
    return jnp.logical_and(a, b)


def signal(sem, target):
    pl.semaphore_signal(sem, inc=1, device_id=target, device_id_type=MESH)


def meet(targets):
    barrier = pltpu.get_barrier_semaphore()
    for target in targets:
        signal(barrier, target)
    pl.semaphore_wait(barrier, len(targets))


class SeqSum:
    def __init__(self, here, gates, hidden, third, own, ring_in, ring_mid, total, out, sems, credits):
        self.here, self.third, self.rows = here, third, hidden // PIECES
        self.gates, self.blocks = gates, 2 * gates * THIRDS
        self.units = self.blocks * PIECES
        self.own, self.ring_in, self.ring_mid, self.total, self.out = own, ring_in, ring_mid, total, out
        self.sems = sems
        self.credit_in, self.credit_mid, self.credit_out = credits

    def rows_of(self, u):
        return pl.ds(pl.multiple_of(lax.rem(u, PIECES) * self.rows, 16), self.rows)

    def mine(self, u):
        return self.own.at[u // PIECES, self.rows_of(u)]

    def inward(self, u):
        i = lax.rem(u, SLOTS)
        return remote(self.mine(u), self.ring_in.at[i], self.sems.at[0, i], self.sems.at[1, i], self.here.pair)

    def across(self, u):
        i = lax.rem(u, SLOTS)
        return remote(self.mine(u), self.ring_mid.at[i], self.sems.at[2, i], self.sems.at[3, i], self.here.middle)

    def outward(self, u):
        i = lax.rem(u, SLOTS)
        return remote(self.total.at[i], self.ring_in.at[i], self.sems.at[4, i], self.sems.at[5, i], self.here.pair)

    def store(self, u, ring):
        i, block = lax.rem(u, SLOTS), u // PIECES
        cols = pl.ds(pl.multiple_of((block // (2 * self.gates)) * self.third, LANES), self.third)
        to = self.out.at[self.product(block), self.rows_of(u), cols]
        return pltpu.make_async_copy(ring.at[i], to, self.sems.at[6, i])

    def product(self, block):
        k = lax.rem(block, 2 * self.gates)
        return k if self.gates == 3 else (k // 2) * 3 + lax.rem(k, 2)

    def add(self, dst, a, b):
        def rows(r):
            at = pl.ds(r, ROWS)
            dst[at, :] = a[at, :] + b[at, :]

        tiles(self.rows, ROWS, rows)

    def offer(self, u):
        @pl.when(self.here.is_end)
        def _():
            @pl.when(u >= SLOTS)
            def _():
                pl.semaphore_wait(self.credit_in, 1)
                self.inward(u - SLOTS).wait_send()

            self.inward(u).start()

    def gather(self, u):
        i = lax.rem(u, SLOTS)
        self.inward(u).wait_recv()
        self.add(self.mine(u), self.mine(u), self.ring_in.at[i])

        @pl.when(u + SLOTS < self.units)
        def _():
            signal(self.credit_in, self.here.pair)

        @pl.when(u >= SLOTS)
        def _():
            pl.semaphore_wait(self.credit_mid, 1)
            self.across(u - SLOTS).wait_send()

        self.across(u).start()

    def finish(self, u):
        i = lax.rem(u, SLOTS)
        self.across(u).wait_recv()

        @pl.when(u >= SLOTS)
        def _():
            pl.semaphore_wait(self.credit_out, 1)
            self.outward(u - SLOTS).wait_send()
            self.store(u - SLOTS, self.total).wait()

        self.add(self.total.at[i], self.mine(u), self.ring_mid.at[i])

        @pl.when(u + SLOTS < self.units)
        def _():
            signal(self.credit_mid, self.here.middle)

        self.outward(u).start()
        self.store(u, self.total).start()

    def accept(self, u):
        self.outward(u).wait_recv()
        self.store(u, self.ring_in).start()

        @pl.when(u > 0)
        def _():
            self.store(u - 1, self.ring_in).wait()

            @pl.when(u - 1 + SLOTS < self.units)
            def _():
                signal(self.credit_out, self.here.pair)

    def tick(self, n):
        @pl.when(self.here.is_centre)
        def _():
            @pl.when(n < self.units)
            def _():
                self.gather(n)

            @pl.when(both(n >= 1, n <= self.units))
            def _():
                self.finish(n - 1)

        @pl.when(n + AHEAD < self.units)
        def _():
            self.offer(n + AHEAD)

        @pl.when(n >= 2)
        def _():
            @pl.when(self.here.is_end)
            def _():
                self.accept(n - 2)

    def drain(self):
        @pl.when(self.here.is_centre)
        def _():
            for u in range(self.units - SLOTS, self.units):
                self.across(u).wait_send()
                self.outward(u).wait_send()
                self.store(u, self.total).wait()

        @pl.when(self.here.is_end)
        def _():
            for u in range(self.units - SLOTS, self.units):
                self.inward(u).wait_send()
            self.store(self.units - 1, self.ring_in).wait()


class RankSum:
    def __init__(self, here, part, pairs, wide_x, wide_y, last_x, last_y, sems):
        self.here, self.part, self.pairs = here, part, pairs
        self.wide_x, self.wide_y, self.last_x, self.last_y, self.sems = wide_x, wide_y, last_x, last_y, sems
        self.rows = part.shape[3]
        self.upper = pl.ds(0, self.rows // 2)
        self.lower = pl.ds(self.rows // 2, self.rows // 2)
        self.step = 16

    def copy(self, k, s, src, dst, target):
        return remote(src, dst, self.sems.at[s, k, 0], self.sems.at[s, k, 1], target)

    def swap(self, s):
        return self.copy(0, s, self.part.at[:, :, 1 - self.here.c], self.pairs.at[s], self.here.core)

    def wide(self, s):
        h = self.here
        return (
            self.copy(1, s, self.pairs.at[s, :, 1 - h.x, self.upper], self.wide_x.at[s], h.across_x),
            self.copy(2, s, self.pairs.at[s, 1 - h.y, :, self.lower], self.wide_y.at[s], h.across_y),
        )

    def last(self, s):
        h = self.here
        return (
            self.copy(3, s, self.pairs.at[s, 1 - h.y, h.x, self.upper], self.last_y.at[s], h.across_y),
            self.copy(4, s, self.pairs.at[s, h.y, 1 - h.x, self.lower], self.last_x.at[s], h.across_x),
        )

    def start(self, s):
        self.swap(s).start()

    def cross(self, s):
        h = self.here
        self.swap(s).wait()

        def rows(r):
            at = pl.ds(r, self.step)
            for y in range(2):
                for x in range(2):
                    self.pairs[s, y, x, at, :] = self.pairs[s, y, x, at, :] + self.part[y, x, h.c, at, :]

        tiles(self.rows, self.step, rows)
        for copy in self.wide(s):
            copy.start()

    def turn(self, s):
        h = self.here
        half = self.rows // 2
        for copy in self.wide(s):
            copy.wait()

        def rows(r):
            at, low = pl.ds(r, self.step), pl.ds(half + r, self.step)
            for k in range(2):
                self.pairs[s, k, h.x, at, :] = self.pairs[s, k, h.x, at, :] + self.wide_x[s, k, at, :]
                self.pairs[s, h.y, k, low, :] = self.pairs[s, h.y, k, low, :] + self.wide_y[s, k, at, :]

        tiles(half, self.step, rows)
        for copy in self.last(s):
            copy.start()

    def done(self, s, out):
        h = self.here
        half = self.rows // 2
        for copy in self.last(s):
            copy.wait()

        def rows(r):
            at, low = pl.ds(r, self.step), pl.ds(half + r, self.step)
            out[at, :] = self.pairs[s, h.y, h.x, at, :] + self.last_y[s, at, :]
            out[low, :] = self.pairs[s, h.y, h.x, low, :] + self.last_x[s, at, :]

        tiles(half, self.step, rows)


def sum_scratch(seqs, hidden, third, rows, cols):
    return [
        pltpu.VMEM((18, hidden, third), BF16),
        pltpu.VMEM((SLOTS, hidden // PIECES, third), BF16),
        pltpu.VMEM((SLOTS, hidden // PIECES, third), BF16),
        pltpu.VMEM((SLOTS, hidden // PIECES, third), BF16),
        pltpu.SemaphoreType.DMA((7, SLOTS)),
        pltpu.SemaphoreType.REGULAR,
        pltpu.SemaphoreType.REGULAR,
        pltpu.SemaphoreType.REGULAR,
        pltpu.VMEM((2, 2, 2, rows, cols), BF16),
        pltpu.VMEM((seqs, 2, 2, rows, cols), BF16),
        pltpu.VMEM((seqs, 2, rows // 2, cols), BF16),
        pltpu.VMEM((seqs, 2, rows // 2, cols), BF16),
        pltpu.VMEM((seqs, rows // 2, cols), BF16),
        pltpu.VMEM((seqs, rows // 2, cols), BF16),
        pltpu.SemaphoreType.DMA((seqs, 5, 2)),
        pltpu.SemaphoreType.DMA((17,)),
    ]


def backward_kernel(second, seqs, hidden, length, width, *refs):
    third = width // THIRDS
    if second:
        d_in, r_in, w_in, pre_in, cell_in, h_in, sel_in, dsel_in = refs[:8]
        gw_out, d_out, db_out, h_out, sel_out = refs[8:13]
        dv, wv, rv, pre, cell, work, edge, grad, picked, dsel, hsem, psem = refs[13:25]
        rest = refs[25:]
    else:
        d_in, r_in, w_in, db1_in, db2_in, gw_out, gx_out, db_out = refs[:8]
        dv, wv, rv, gxv, dbv, dsem = refs[8:14]
        rest = refs[14:]
    own, ring_in, ring_mid, total, zsem, *credits = rest[:8]
    rank_refs, lsem = rest[8:15], rest[15]
    here = Here()
    gates = 2 if second else 3
    ar = SeqSum(here, gates, hidden, third, own, ring_in, ring_mid, total, gw_out, zsem, credits)
    rs = RankSum(here, *rank_refs)
    groups, piece = length // LANES, LANES // 8

    def columns_of(s):
        return pl.ds(s * length, length)

    def rhs(t):
        if second:
            src = r_in.at[pl.ds(t * third, third), :]
        else:
            src = r_in.at[:, pl.ds(t * third, third)]
        return pltpu.make_async_copy(src, rv.at[t % 2], lsem.at[t % 2])

    loads = [pltpu.make_async_copy(d_in, dv, lsem.at[2]), pltpu.make_async_copy(w_in, wv, lsem.at[3])]
    if second:
        loads.append(pltpu.make_async_copy(pre_in, pre, lsem.at[4]))
        loads.append(pltpu.make_async_copy(cell_in, cell, lsem.at[5]))
    loads[0].start()
    rhs(0).start()
    for copy in loads[1:]:
        copy.start()
    rhs(1).start()
    if second:
        meet(here.peers + [here.pair, here.middle])
        loads.append(pltpu.make_async_copy(dsel_in, dsel, lsem.at[8]))
        loads[-1].start()

        def halves(start, half):
            size = hidden if half is None else hidden // 2
            return pl.ds(start + (half or 0) * size, size)

        gather = Gather(
            here,
            lambda b, half: sel_out.at[:, halves(b * hidden, half)],
            psem,
            lambda half: sel_in.at[:, halves(0, half)],
        )
        keep = pltpu.make_async_copy(sel_in, sel_out.at[:, pl.ds(here.b * hidden, hidden)], lsem.at[9])
        keep.start()
        others = [pltpu.make_async_copy(h_in.at[here.b], h_out.at[here.b], hsem.at[0, 0])]
        for d, peer in enumerate(here.peers, 1):
            others.append(remote(h_in.at[peer["tm"]], h_out.at[here.b], hsem.at[d, 0], hsem.at[d, 1], peer))
    else:
        meet([here.core, here.across_x, here.across_y] + here.line)
        dbv[here.z] = jnp.zeros((8, hidden), F32)
        for layer, db in enumerate((db1_in, db2_in)):
            dbv[here.z, layer : layer + 1, :] = to_row(sum(db[s] for s in range(1, seqs)) + db[0])
        others = []
        for d, peer in enumerate(here.line, 1):
            others.append(remote(dbv.at[here.z], dbv.at[here.z], dsem.at[d, 0], dsem.at[d, 1], peer))
    if not second:
        for copy in others:
            copy.start()

    done = [0]

    def units(t, low, high):
        def unit(k, carry):
            block = t * (2 * gates) + k
            rows = pl.ds(pl.multiple_of(ar.product(block) * hidden, 16), hidden)
            own[block] = dot(dv[rows, :], rv[t % 2], NT if second else NN).astype(BF16)
            for i in range(PIECES):
                u = block * PIECES + i

                @pl.when(u < AHEAD)
                def _(u=u):
                    ar.offer(u)

            return carry

        lax.fori_loop(low, high, unit, 0)
        done[0] = (t * 2 * gates + high) * PIECES

    def strips(s, q):
        if second:
            i, start = q // 2, lax.rem(q, 2) * (length // 2)
            lhs = pl.ds(pl.multiple_of(i * (width // 2), LANES), width // 2)

            def strip(c):
                cols = pl.ds(pl.multiple_of(start + c, 256), 256)
                src = pl.ds(pl.multiple_of(s * length + start + c, 256), 256)
                got = dot(wv[:, lhs], dv[:, src], TN).astype(BF16)
                rs.part[i, :, :, :, cols] = got.reshape(2, 2, hidden, 256)

            tiles(length // 2, 256, strip)
        else:

            def strip(c, carry):
                cols = pl.ds(pl.multiple_of(c * 256, 256), 256)
                got = dot(dv[:, columns_of(s)], wv[:, cols], TN).astype(BF16)
                for j in range(groups):
                    block = got[j * LANES : (j + 1) * LANES].reshape(2, 2, 2, piece, 256)
                    rs.part[:, :, :, pl.ds(j * piece, piece), cols] = block
                return carry

            count = width // 256
            lax.fori_loop(count * q // 4, count * (q + 1) // 4, strip, 0)

    spent = [0]

    def tick(count=1):
        for _ in range(count):
            assert spent[0] + AHEAD < min(done[0], ar.units) or done[0] == ar.units
            ar.tick(spent[0])
            spent[0] += 1

    def input_grad(s):
        first = spent[0]
        assert first + 3 + AHEAD < done[0]

        def quarter(q, carry):
            strips(s, q)
            ar.tick(first + q)
            return carry

        lax.fori_loop(0, 4, quarter, 0)
        spent[0] += 4

    def settle(s):
        if second:
            rs.done(s, grad.at[:, columns_of(s)])
        else:
            rs.done(s, gxv.at[s])
            gxv[s] = dot(reorder(piece, groups, True), gxv[s], NN).astype(BF16)

    def outgate_load(t):
        return pltpu.make_async_copy(sel_out.at[:, pl.ds(t * third, third)], picked, lsem.at[10])

    def outgate_store(t, tap):
        to = gw_out.at[2 + 3 * tap, :, pl.ds(t * third, third)]
        return pltpu.make_async_copy(own.at[ar.blocks + 2 * t + tap], to, lsem.at[11 + 2 * t + tap])

    count = 2 * gates
    loads[0].wait()
    rhs(0).wait()
    units(0, 0, count)
    rhs(2).start()
    loads[1].wait()
    input_grad(0)
    rs.start(0)
    tick()
    rhs(1).wait()
    units(1, 0, 2)
    rs.cross(0)
    tick(2)
    units(1, 2, 4)
    input_grad(1)
    rs.start(1)
    units(1, 4, count)
    rs.turn(0)
    rhs(2).wait()
    tick(2)
    units(2, 0, 2)
    tick()
    rs.cross(1)
    units(2, 2, 4)
    tick()
    units(2, 4, count)
    settle(0)
    tick(2)
    if second:
        for copy in loads[2:4]:
            copy.wait()
        stores = [
            pltpu.make_async_copy(dv.at[:, columns_of(s)], d_out.at[:, columns_of(s)], lsem.at[6 + s])
            for s in range(seqs)
        ]

        def pool(s):
            first = s * length
            pool_backward(first, grad, pre, cell, first, dv, db_out.at[s], work, edge, hidden, groups)
            stores[s].start()

        pool(0)
    tick()
    rs.turn(1)
    if second:
        gather.start()
    tick(3)
    settle(1)
    if second:
        pool(1)
        tick(2)
        gather.relay()
        for copy in others:
            copy.start()
        tick(4)
        gather.share()
        keep.wait()
        outgate_load(0).start()
        loads[4].wait()
        tick()
        for t in range(THIRDS):
            outgate_load(t).wait()
            for tap in range(2):
                own[ar.blocks + 2 * t + tap] = dot(dsel[...], picked[tap], NT).astype(BF16)
                outgate_store(t, tap).start()
            if t + 1 < THIRDS:
                outgate_load(t + 1).start()
            tick()
        gather.drain()
        stores += [outgate_store(t, tap) for t in range(THIRDS) for tap in range(2)]
    else:
        stores = [pltpu.make_async_copy(gxv, gx_out, lsem.at[6])]
        stores[0].start()

    def more(n, carry):
        ar.tick(n)
        return carry

    lax.fori_loop(spent[0], ar.units + 2, more, 0)
    ar.drain()
    for copy in stores + others:
        copy.wait()
    if not second:
        db_out[...] = dbv[0] + dbv[1] + dbv[2] + dbv[3]


def run_backward(seqs, d, rhs, weight, second, more):
    (wide, width), total = weight.shape, d.shape[1]
    hidden, length = wide // 6, total // seqs
    third, span = width // THIRDS, length // 8
    outs = [shape((6, hidden, width), BF16)]
    scratch = [pltpu.VMEM((wide, total), BF16), pltpu.VMEM((wide, width), BF16)]
    if second:
        outs += [shape((wide, total), BF16), shape((seqs, hidden, 1), F32), shape(more[2].shape, BF16)]
        picked = more[3].shape[2]
        outs += [shape((2, width, picked), BF16)]
        specs = [ANY, ANY, pl.BlockSpec(memory_space=pltpu.VMEM), ANY, ANY]
        rows, cols = hidden, length
        scratch += [
            pltpu.VMEM((2, third, total), BF16),
            pltpu.VMEM((3 * hidden, total), BF16),
            pltpu.VMEM((hidden, total), F32),
            pltpu.VMEM((2, hidden, length), F32),
            pltpu.VMEM((2, hidden, LANES), F32),
            pltpu.VMEM((hidden, total), BF16),
            pltpu.VMEM((2, third, picked), BF16),
            pltpu.VMEM((hidden, picked), BF16),
            pltpu.SemaphoreType.DMA((8, 2)),
            pltpu.SemaphoreType.DMA((11, 2)),
        ]
    else:
        outs += [shape((seqs, span, width), BF16), shape((8, hidden), F32)]
        specs = [ANY, ANY, pl.BlockSpec(memory_space=pltpu.VMEM)]
        rows, cols = span, width
        scratch += [
            pltpu.VMEM((2, total, third), BF16),
            pltpu.VMEM((seqs, span, width), BF16),
            pltpu.VMEM((4, 8, hidden), F32),
            pltpu.SemaphoreType.DMA((4, 2)),
        ]
    operands = (d, rhs, weight) + more
    return pl.pallas_call(
        functools.partial(backward_kernel, second, seqs, hidden, length, width),
        name="layer_two_backward" if second else "layer_one_backward",
        in_specs=[ANY] * (3 + 5 * second) + [pl.BlockSpec(memory_space=pltpu.VMEM)] * (2 - 2 * second),
        out_specs=specs,
        out_shape=outs,
        scratch_shapes=scratch + sum_scratch(seqs, hidden, third, rows, cols),
        compiler_params=params(collective_id=1 if second else 2, has_side_effects=True),
    )(*operands)


def reorder(piece, groups, back):
    span = piece * groups
    a = lax.broadcasted_iota(jnp.int32, (span, span), 1 if back else 0)
    b = lax.broadcasted_iota(jnp.int32, (span, span), 0 if back else 1)
    return (b == lax.rem(a, piece) * groups + a // piece).astype(BF16)


def to_row(column):
    n = column.shape[0]
    same = lax.broadcasted_iota(jnp.int32, (n, n), 0) == lax.broadcasted_iota(jnp.int32, (n, n), 1)
    return jnp.sum(jnp.where(same, column, 0.0), axis=0, keepdims=True)


def to_column(row):
    n = row.shape[1]
    same = lax.broadcasted_iota(jnp.int32, (n, n), 0) == lax.broadcasted_iota(jnp.int32, (n, n), 1)
    return jnp.sum(jnp.where(same, row, 0.0), axis=1, keepdims=True)


class Gather:
    def __init__(self, here, region, sems, own=None):
        h, b = here, here.b
        own = own or (lambda half: region(b, half))
        bx, by = h.across_x["tm"], h.across_y["tm"]
        bd = bx + 4 - 8 * h.y
        plan = (
            (b, 1, h.across_x),
            (b, 0, h.across_y),
            (b, 0, h.across_x),
            (b, 1, h.across_y),
            (b, None, h.core),
            (bx, 1, h.across_y),
            (by, 0, h.across_x),
            (bx, None, h.core),
            (by, None, h.core),
            (bd, 0, h.core),
            (bd, 1, h.core),
        )
        self.copies = []
        for k, (block, half, to) in enumerate(plan):
            src = own(half) if k < 5 else region(block, half)
            self.copies.append(remote(src, region(block, half), sems.at[k, 0], sems.at[k, 1], to))

    def start(self):
        for k in range(5):
            self.copies[k].start()

    def relay(self):
        self.copies[0].wait_recv()
        self.copies[5].start()
        self.copies[1].wait_recv()
        self.copies[6].start()

    def share(self):
        self.copies[2].wait_recv()
        self.copies[7].start()
        self.copies[3].wait_recv()
        self.copies[8].start()
        self.copies[6].wait_recv()
        self.copies[9].start()
        self.copies[5].wait_recv()
        self.copies[10].start()
        for k in (4, 7, 8, 9, 10):
            self.copies[k].wait_recv()

    def drain(self):
        for copy in self.copies:
            copy.wait_send()


def forward_kernel(seqs, hidden, length, width, *refs):
    x_in, w1_in, w2_in, cot_in, b1_in, b2_in, starts = refs[:7]
    x_out, h1_out, pre_out, cell_out, h2_out, d_out, db_out, sel_out, dsel_out = refs[7:16]
    xg, hg, w, p, pre, cell, work, edge, dv, seed, grad, hv, h2t, raw, cot, sent, b1, b2, pick, sel, dsel = refs[16:37]
    xsem, hsem, ssem, zsem, lsem = refs[37:]
    here = Here()
    groups = length // LANES
    piece = LANES // 8

    def columns_of(s):
        return pl.ds(s * length, length)

    def x_region(s):
        def region(b, half):
            js = pl.ds(0, groups) if half is None else pl.ds(half * (groups // 2), groups // 2)
            return xg.at[s, js, b]

        return region

    def h_region(s):
        def region(b, half):
            rows = pl.ds(0, hidden) if half is None else pl.ds(half * (hidden // 2), hidden // 2)
            return hg.at[b, rows, columns_of(s)]

        return region

    def load(src, dst, k):
        return pltpu.make_async_copy(src, dst, lsem.at[k])

    load_w1 = load(w1_in, w, 0)
    load_w2 = load(w2_in, w, 0)
    load_x = [load(x_in.at[s], raw.at[s], 1 + s) for s in range(seqs)]
    load_c = load(cot_in, cot, 14)
    store_x = [load(xg.at[s], x_out.at[s], 3 + s) for s in range(seqs)]
    store_h = [load(hg.at[:, :, columns_of(s)], h1_out.at[:, :, columns_of(s)], 5 + s) for s in range(seqs)]
    store_p = [load(pre.at[:, columns_of(s)], pre_out.at[:, columns_of(s)], 7 + s) for s in range(seqs)]
    store_c = [load(cell.at[:, columns_of(s)], cell_out.at[:, columns_of(s)], 9 + s) for s in range(seqs)]
    store_d = [load(dv.at[s], d_out.at[:, columns_of(s)], 11 + s) for s in range(seqs)]
    store_o = load(h2t, h2_out, 13)

    for copy in load_x:
        copy.start()
    load_w1.start()
    load_c.start()
    meet(here.peers + here.line)
    xs = [Gather(here, x_region(s), xsem.at[s]) for s in range(seqs)]
    hs = [Gather(here, h_region(s), hsem.at[s]) for s in range(seqs)]
    order = reorder(piece, groups, False)

    def place(s):
        load_x[s].wait()
        xg[s, :, here.b] = dot(order, raw[s], NN).astype(BF16).reshape(groups, piece, width)
        xs[s].start()

    def prepare():
        load_c.wait()
        for s in range(seqs):
            turned = dot(order, cot[s], NN).astype(BF16)
            for b in range(8):
                block = turned[:, b * hidden : (b + 1) * hidden]
                sent[b, s] = block.reshape(groups, piece, hidden)
        seed[:, :, pl.ds(0, 4)] = jnp.zeros((seqs, groups, 4, piece, hidden), BF16)
        for s in range(seqs):
            prepare_pick(s)
        b1[...] = to_column(b1_in[...])
        b2[...] = to_column(b2_in[...])

    late = [
        (remote(sent.at[peer["tm"]], seed.at[:, :, here.b], ssem.at[d, 0], ssem.at[d, 1], peer), peer)
        for d, peer in enumerate(here.peers, 1)
    ]

    def products(rhs, dims):
        def block(r):
            rows = pl.ds(r, hidden)
            p[rows, :] = dot(w[rows, :], rhs(), dims)

        tiles(6 * hidden, hidden, block)

    def first_products(s):
        products(lambda: xg[s].reshape(length, width), NT)

    def second_products(s):
        products(lambda: hg[:, :, columns_of(s)].reshape(width, length), NN)

    def first_pool(s):
        first = s * length
        pool_forward(first, p, b1, pre, cell, first, hg.at[here.b], work.at[0], edge.at[0], hidden, groups)

    def second_pool(s):
        pool_forward(s * length, p, b2, pre, cell, 0, hv, work.at[0], edge.at[0], hidden, groups)
        rows = lax.broadcasted_iota(jnp.int32, (LANES, LANES), 0)
        cols = lax.broadcasted_iota(jnp.int32, (LANES, LANES), 1)
        eye = (rows == cols).astype(BF16)
        for j in range(groups):
            turned = dot(eye, hv[:, pl.ds(j * LANES, LANES)], NT).astype(BF16)
            at = pl.ds((s * groups + j) * piece, piece)
            h2t[:, at, :] = turned.reshape(8, piece, hidden)

    def incoming(s):
        rows = lax.broadcasted_iota(jnp.int32, (hidden, hidden), 0)
        cols = lax.broadcasted_iota(jnp.int32, (hidden, hidden), 1)
        eye = (rows == cols).astype(BF16)
        lane = lax.broadcasted_iota(jnp.int32, (1, LANES), 1)
        for j in range(groups):
            block = seed[s, j].reshape(LANES, hidden)
            turned = dot(eye, block, NT)
            step = lane * groups + j
            keep = jnp.zeros((1, LANES), jnp.bool_)
            for k in range(starts.shape[1]):
                begin = starts[s, k]
                keep = jnp.logical_or(keep, jnp.logical_and(step >= begin, step < begin + CLUSTER))
            keep = jnp.broadcast_to(keep, (hidden, LANES))
            grad[:, pl.ds(s * length + j * LANES, LANES)] = jnp.where(keep, turned, 0.0).astype(BF16)

    def pool_back(s):
        pool_backward(s * length, grad, pre, cell, 0, dv.at[s], db_out.at[s], work, edge, hidden, groups, True)
        store_d[s].start()

    def cluster_steps(s):
        lane = lax.broadcasted_iota(jnp.int32, (1, LANES), 1)
        step = lax.rem(lane, CLUSTER)
        for k in range(starts.shape[1]):
            step = step + jnp.where(lane // CLUSTER == k, starts[s, k], 0)
        return lane, step

    def prepare_pick(s):
        _, step = cluster_steps(s)
        for j in range(groups):
            code = lax.broadcasted_iota(jnp.int32, (LANES, LANES), 0) * groups + j
            at = pl.ds(j * LANES, LANES)
            pick[s, at, pl.ds(0, LANES)] = (code == step).astype(BF16)
            pick[s, at, pl.ds(LANES, LANES)] = (code == step - 1).astype(BF16)

    def held(s, count):
        start = here.z * (seqs * LANES) + s * LANES
        return pl.ds(pl.multiple_of(start, LANES), count * LANES)

    def pick_hidden(s):
        got = dot(hg[here.b, :, columns_of(s)], pick[s], NN).astype(BF16)
        for tap in range(2):
            sel[tap, :, held(s, 1)] = got[:, tap * LANES : (tap + 1) * LANES]

    def pick_grad(s):
        lane, step = cluster_steps(s)
        again = jnp.zeros((1, LANES), jnp.bool_)
        for k in range(starts.shape[1] - 1):
            begin = starts[s, k]
            inside = jnp.logical_and(step >= begin, step < begin + CLUSTER)
            again = jnp.logical_or(again, jnp.logical_and(inside, lane // CLUSTER > k))
        got = dot(dv[s, pl.ds(2 * hidden, hidden), :], pick[s, :, pl.ds(0, LANES)], NN)
        dsel[:, held(s, 1)] = jnp.where(jnp.broadcast_to(again, (hidden, LANES)), 0.0, got).astype(BF16)

    spread_h = []
    spread_d = []
    for d, peer in enumerate(here.line, 1):
        at = sel.at[:, :, held(0, seqs)]
        spread_h.append(remote(at, at, zsem.at[d, 0], zsem.at[d, 1], peer))
        at = dsel.at[:, held(0, seqs)]
        spread_d.append(remote(at, at, zsem.at[d, 2], zsem.at[d, 3], peer))
    store_s = load(sel, sel_out, 15)
    store_e = load(dsel, dsel_out, 16)

    place(0)
    prepare()
    xs[0].relay()
    place(1)
    xs[0].share()
    store_x[0].start()
    load_w1.wait()
    first_products(0)
    xs[1].relay()
    first_pool(0)
    hs[0].start()
    store_p[0].start()
    store_c[0].start()
    xs[1].share()
    store_x[1].start()
    first_products(1)
    load_w2.start()
    hs[0].relay()
    first_pool(1)
    hs[1].start()
    store_p[1].start()
    store_c[1].start()

    for s in range(seqs):
        pick_hidden(s)
    for copy in spread_h:
        copy.start()
    hs[0].share()
    store_h[0].start()
    load_w2.wait()
    second_products(0)
    hs[1].relay()

    @pl.when(here.y == 1)
    def _():
        pltpu.make_async_copy(sent.at[here.b], seed.at[:, :, here.b], ssem.at[0, 0]).start()
        for copy, _ in late:
            copy.start()

    store_p[0].wait()
    store_c[0].wait()
    second_pool(0)
    hs[1].share()
    store_h[1].start()
    second_products(1)
    store_p[1].wait()
    store_c[1].wait()
    second_pool(1)
    store_o.start()

    @pl.when(here.y == 1)
    def _():
        pltpu.make_async_copy(sent.at[here.b], seed.at[:, :, here.b], ssem.at[0, 0]).wait()
        for copy, _ in late:
            copy.wait_send()

    for d, (copy, _) in enumerate(late, 1):
        source = lax.rem(here.b + 8 - d, 8)

        @pl.when(source >= 4)
        def _(copy=copy):
            copy.wait_recv()

    for s in range(seqs):
        incoming(s)
        outgate_backward(s * length, grad, pre, cell, dv.at[s], hidden, groups)
        pick_grad(s)
    for copy in spread_d:
        copy.start()
    for copy in spread_h:
        copy.wait()
    store_s.start()
    for s in range(seqs):
        pool_back(s)
    for gather in xs + hs:
        gather.drain()
    for copy in spread_d:
        copy.wait()
    store_e.start()
    for copy in store_x + store_h + store_d + [store_o, store_s, store_e]:
        copy.wait()


def run_forward(x, w1, b1, w2, b2, cotangent, starts):
    seqs, span, width = x.shape
    hidden, length, piece = w1.shape[0] // 6, span * 8, LANES // 8
    groups = length // LANES
    total, picked = seqs * length, 4 * seqs * LANES
    assert starts.shape[1] * CLUSTER == LANES
    vmem = pl.BlockSpec(memory_space=pltpu.VMEM)
    return pl.pallas_call(
        functools.partial(forward_kernel, seqs, hidden, length, width),
        name="forward",
        in_specs=[ANY, ANY, ANY, ANY, vmem, vmem, pl.BlockSpec(memory_space=pltpu.SMEM)],
        out_specs=[ANY, ANY, ANY, ANY, ANY, ANY, vmem, ANY, ANY],
        out_shape=[
            shape((seqs, groups, 8, piece, width), BF16),
            shape((8, hidden, total), BF16),
            shape((3 * hidden, total), BF16),
            shape((hidden, total), F32),
            shape((8, seqs * groups * piece, hidden), BF16),
            shape((6 * hidden, total), BF16),
            shape((seqs, hidden, 1), F32),
            shape((2, hidden, picked), BF16),
            shape((hidden, picked), BF16),
        ],
        scratch_shapes=[
            pltpu.VMEM((seqs, groups, 8, piece, width), BF16),
            pltpu.VMEM((8, hidden, total), BF16),
            pltpu.VMEM((6 * hidden, width), BF16),
            pltpu.VMEM((6 * hidden, length), F32),
            pltpu.VMEM((3 * hidden, total), BF16),
            pltpu.VMEM((hidden, total), F32),
            pltpu.VMEM((2, hidden, length), F32),
            pltpu.VMEM((2, hidden, LANES), F32),
            pltpu.VMEM((seqs, 6 * hidden, length), BF16),
            pltpu.VMEM((seqs, groups, 8, piece, hidden), BF16),
            pltpu.VMEM((hidden, total), BF16),
            pltpu.VMEM((hidden, length), BF16),
            pltpu.VMEM((8, seqs * groups * piece, hidden), BF16),
            pltpu.VMEM((seqs, span, width), BF16),
            pltpu.VMEM((seqs, span, width), BF16),
            pltpu.VMEM((8, seqs, groups, piece, hidden), BF16),
            pltpu.VMEM((hidden, 1), F32),
            pltpu.VMEM((hidden, 1), F32),
            pltpu.VMEM((seqs, length, 2 * LANES), BF16),
            pltpu.VMEM((2, hidden, picked), BF16),
            pltpu.VMEM((hidden, picked), BF16),
            pltpu.SemaphoreType.DMA((seqs, 11, 2)),
            pltpu.SemaphoreType.DMA((seqs, 11, 2)),
            pltpu.SemaphoreType.DMA((8, 2)),
            pltpu.SemaphoreType.DMA((4, 4)),
            pltpu.SemaphoreType.DMA((17,)),
        ],
        compiler_params=params(collective_id=0, has_side_effects=True),
    )(x, w1, w2, cotangent, b1, b2, starts)


def per_device(line, inputs, weight_one, fbias_one, weight_two, fbias_two, cotangent, cluster_starts):
    seqs, span, width = inputs.shape
    count = lax.axis_size("tm")
    length = span * count
    groups = length // LANES
    piece = LANES // count
    hidden = weight_one.shape[2]
    total = seqs * length
    w1 = weight_one.reshape(6 * hidden, width)
    w2 = weight_two.reshape(6 * hidden, width)

    if line:
        x, h1, pre1, cell1, h2, d2, db2, *picked = run_forward(
            inputs, w1, fbias_one[None], w2, fbias_two[None], cotangent, cluster_starts
        )
        x, h1 = x.reshape(total, width), h1.reshape(width, total)
        gw2, d1, db1, h2, _ = run_backward(seqs, d2, h1, w2, True, (pre1, cell1, h2, *picked))
        h2 = h2.reshape(count, seqs, groups, piece, hidden).transpose(1, 3, 2, 0, 4)
        gw1, gx1, db = run_backward(seqs, d1, x, w1, False, (db1, db2))
    else:
        x = inputs.reshape(seqs, piece, groups, width).transpose(0, 2, 1, 3)
        bias1, bias2 = fbias_one[:, None], fbias_two[:, None]
        seed = cotangent.reshape(seqs, piece, groups, count, hidden)
        steps = lax.axis_index("tm") * span + jnp.arange(span, dtype=jnp.int32)
        starts = cluster_starts[:, :, None]
        keep = jnp.any((steps >= starts) & (steps < starts + CLUSTER), axis=1)
        seed = jnp.where(keep.reshape(seqs, piece, groups, 1, 1), seed, jnp.zeros_like(seed))
        seed = lax.all_to_all(seed, "tm", split_axis=3, concat_axis=1, tiled=True)
        seed = seed.reshape(seqs, LANES, groups, hidden).transpose(3, 0, 2, 1).reshape(hidden, total)
        x = lax.all_gather(x, "tm", axis=2, tiled=True).reshape(total, width)
        pre1, cell1, h1 = run_first(seqs, w1, bias1, x)
        h1 = lax.all_gather(h1, "tm", axis=0, tiled=True)
        h2, d2, db2 = run_second(seqs, w2, bias2, h1, seed)
        h2 = h2.reshape(hidden, seqs, groups, count, piece)
        h2 = lax.all_to_all(h2, "tm", split_axis=3, concat_axis=0, tiled=True)
        h2 = h2.reshape(width, seqs, groups, piece).transpose(1, 3, 2, 0)
        gw2 = lax.psum(dot(d2, h1, NT).astype(BF16), "seq")
        gx2 = lax.psum_scatter(dot(w2, d2, TN).astype(BF16), "tm", scatter_dimension=0, tiled=True)
        d1, db1 = run_back(seqs, gx2, pre1, cell1)
        gw1 = lax.psum(dot(d1, x, NN).astype(BF16), "seq")
        gx1 = dot(d1, w1, TN).astype(BF16).reshape(seqs, groups, LANES, width)
        gx1 = lax.psum_scatter(gx1, "tm", scatter_dimension=2, tiled=True)
        gx1 = gx1.transpose(0, 2, 1, 3).reshape(seqs, span, width)
        db = lax.psum(jnp.stack([db1, db2]).sum(axis=(1, 3)), "seq")
    out = h2.reshape(seqs, span, width)
    dims = weight_one.shape
    return (out, gx1, gw1.astype(F32).reshape(dims), db[0], gw2.astype(F32).reshape(dims), db[1])


def solution(mesh):
    placed = (
        P("seq", "tm", None),
        P(None, None, "tm", None),
        P("tm"),
        P(None, None, "tm", None),
        P("tm"),
        P("seq", "tm", None),
        P("seq", None),
    )
    return jax.shard_map(
        functools.partial(per_device, dict(mesh.shape) == {"seq": 4, "tm": 8}),
        mesh=mesh,
        in_specs=placed,
        out_specs=(
            P("seq", "tm", None),
            P("seq", "tm", None),
            P(None, None, "tm", None),
            P("tm"),
            P(None, None, "tm", None),
            P("tm"),
        ),
        check_vma=False,
    )
```

```python
import functools

import jax
import jax.numpy as jnp
from jax import lax
from jax.experimental import pallas as pl
from jax.experimental.pallas import tpu as pltpu
from jax.sharding import PartitionSpec as P

CLUSTER = 32
LANES = 128
ROWS = 48
F32 = jnp.float32
BF16 = jnp.bfloat16
ANY = pl.BlockSpec(memory_space=pl.ANY)
MESH = pl.DeviceIdType.MESH
NN = (((1,), (0,)), ((), ()))
NT = (((1,), (1,)), ((), ()))
TN = (((0,), (0,)), ((), ()))


def dot(a, b, dims):
    return lax.dot_general(a, b, dims, preferred_element_type=F32)


def sigmoid(v):
    return 1.0 / (1.0 + jnp.exp(-v))


def tiles(count, rows, body):
    def step(r, carry):
        body(pl.multiple_of(r * rows, rows))
        return carry

    lax.fori_loop(0, count // rows, step, 0)


def shift_lanes(v, amount, lane, fill):
    moved = pltpu.roll(v, amount % LANES, axis=1)
    gone = lane < amount if amount > 0 else lane >= LANES + amount
    return jnp.where(gone, fill, moved)


def lane_chain(factor, value, lane, sign):
    step = 1
    while step < LANES:
        value = value + factor * shift_lanes(value, sign * step, lane, 0.0)
        factor = factor * shift_lanes(factor, sign * step, lane, 1.0)
        step *= 2
    return value


def pool_forward(first, p_ref, b_ref, pre_ref, cell_ref, target, h_ref, factor_ref, edge_ref, hidden, groups):
    lane = lax.broadcasted_iota(jnp.int32, (ROWS, LANES), 1)

    def at(j, start=0):
        return pl.ds(start + j * LANES, LANES)

    def gates(r):
        rows = pl.ds(r, ROWS)
        value = factor = None
        for j in range(groups):
            got = []
            for g in range(3):
                now = p_ref[pl.ds(g * hidden + r, ROWS), at(j)]
                tap = pl.ds((3 + g) * hidden + r, ROWS)
                if j:
                    past = p_ref[tap, at(j - 1)]
                else:
                    past = shift_lanes(p_ref[tap, at(groups - 1)], 1, lane, 0.0)
                total = now + past
                if g == 1:
                    total = total + b_ref[rows, :]
                total = total.astype(BF16)
                pre_ref[pl.ds(g * hidden + r, ROWS), at(j, first)] = total
                got.append(total.astype(F32))
            forget = sigmoid(got[1])
            fresh = (1.0 - forget) * jnp.tanh(got[0])
            if j:
                value = forget * value + fresh
                factor = forget * factor
            else:
                value, factor = fresh, forget
            cell_ref[rows, at(j, first)] = value
            factor_ref[rows, at(j)] = factor

    tiles(hidden, ROWS, gates)

    def chain(r):
        rows = pl.ds(r, ROWS)
        value = lane_chain(factor_ref[rows, at(groups - 1)], cell_ref[rows, at(groups - 1, first)], lane, 1)
        edge_ref[rows, :] = shift_lanes(value, 1, lane, 0.0)

    tiles(hidden, ROWS, chain)

    def finish(r):
        rows = pl.ds(r, ROWS)
        edge = edge_ref[rows, :]
        for j in range(groups):
            cell = cell_ref[rows, at(j, first)] + factor_ref[rows, at(j)] * edge
            cell_ref[rows, at(j, first)] = cell
            outgate = sigmoid(pre_ref[pl.ds(2 * hidden + r, ROWS), at(j, first)].astype(F32))
            h_ref[rows, at(j, target)] = (outgate * cell).astype(BF16)

    tiles(hidden, ROWS, finish)


def put_gate(d_ref, g, r, j, v, target, lane, hidden, groups):
    d_ref[pl.ds(g * hidden + r, ROWS), pl.ds(target + j * LANES, LANES)] = v
    tap = pl.ds((3 + g) * hidden + r, ROWS)
    if j:
        d_ref[tap, pl.ds(target + (j - 1) * LANES, LANES)] = v
    else:
        moved = shift_lanes(v.astype(F32), -1, lane, 0.0).astype(BF16)
        d_ref[tap, pl.ds(target + (groups - 1) * LANES, LANES)] = moved


def outgate_backward(first, g_ref, pre_ref, cell_ref, d_ref, hidden, groups):
    lane = lax.broadcasted_iota(jnp.int32, (ROWS, LANES), 1)

    def body(r):
        rows = pl.ds(r, ROWS)
        for j in range(groups):
            at = pl.ds(first + j * LANES, LANES)
            outgate = sigmoid(pre_ref[pl.ds(2 * hidden + r, ROWS), at].astype(F32))
            v = g_ref[rows, at].astype(F32) * cell_ref[rows, at] * outgate * (1.0 - outgate)
            put_gate(d_ref, 2, r, j, v.astype(BF16), 0, lane, hidden, groups)

    tiles(hidden, ROWS, body)


def pool_backward(
    first, g_ref, pre_ref, cell_ref, target, d_ref, db_ref, work_ref, edge_ref, hidden, groups, carried_only=False
):
    lane = lax.broadcasted_iota(jnp.int32, (ROWS, LANES), 1)

    def at(j, start=0):
        return pl.ds(start + j * LANES, LANES)

    def gate(g, r, j):
        return pre_ref[pl.ds(g * hidden + r, ROWS), at(j, first)].astype(F32)

    def start(r):
        rows = pl.ds(r, ROWS)
        later = value = factor = None
        for j in reversed(range(groups)):
            own = g_ref[rows, at(j, first)].astype(F32) * sigmoid(gate(2, r, j))
            if later is None:
                value, factor = own, jnp.ones_like(own)
            else:
                value = own + later * value
                factor = later * factor
            work_ref[0, rows, at(j)] = value
            work_ref[1, rows, at(j)] = factor
            later = sigmoid(gate(1, r, j))
        edge_ref[0, rows, :] = later * value
        edge_ref[1, rows, :] = later * factor

    tiles(hidden, ROWS, start)

    def chain(r):
        rows = pl.ds(r, ROWS)
        value = lane_chain(edge_ref[1, rows, :], edge_ref[0, rows, :], lane, -1)
        edge_ref[0, rows, :] = shift_lanes(value, -1, lane, 0.0)

    tiles(hidden, ROWS, chain)

    def finish(r):
        rows = pl.ds(r, ROWS)
        edge = edge_ref[0, rows, :]
        total = jnp.zeros((ROWS, LANES), F32)
        before = shift_lanes(cell_ref[rows, at(groups - 1, first)], 1, lane, 0.0)
        for j in range(groups):
            carried = work_ref[0, rows, at(j)] + work_ref[1, rows, at(j)] * edge
            candidate = jnp.tanh(gate(0, r, j))
            forget = sigmoid(gate(1, r, j))
            cell = cell_ref[rows, at(j, first)]
            keep = carried * (1.0 - forget)
            got = [keep * (1.0 - candidate * candidate), keep * forget * (before - candidate)]
            if not carried_only:
                outgate = sigmoid(gate(2, r, j))
                got.append(g_ref[rows, at(j, first)].astype(F32) * cell * outgate * (1.0 - outgate))
            before = cell
            for g, v in enumerate(got):
                v = v.astype(BF16)
                if g == 1:
                    total = total + v.astype(F32)
                put_gate(d_ref, g, r, j, v, target, lane, hidden, groups)
        db_ref[rows, :] = jnp.sum(total, axis=1, keepdims=True)

    tiles(hidden, ROWS, finish)


def first_kernel(hidden, length, w_ref, b_ref, x_ref, pre_ref, cell_ref, h_ref, p_ref, work_ref, edge_ref):
    def strip(c):
        cols = pl.ds(c, 512)
        p_ref[:, cols] = dot(w_ref[...], x_ref[cols, :], NT)

    tiles(length, 512, strip)
    pool_forward(0, p_ref, b_ref, pre_ref, cell_ref, 0, h_ref, work_ref, edge_ref, hidden, length // LANES)


def second_kernel(
    hidden, length, w_ref, b_ref, x_ref, g_ref, h_ref, d_ref, db_ref, p_ref, pre_ref, cell_ref, work_ref, edge_ref
):
    def strip(c):
        cols = pl.ds(c, 512)
        p_ref[:, cols] = dot(w_ref[...], x_ref[:, cols], NN)

    tiles(length, 512, strip)
    groups = length // LANES
    pool_forward(0, p_ref, b_ref, pre_ref, cell_ref, 0, h_ref, work_ref.at[0], edge_ref.at[0], hidden, groups)
    pool_backward(0, g_ref, pre_ref, cell_ref, 0, d_ref, db_ref.at[0], work_ref, edge_ref, hidden, groups)


def back_kernel(hidden, length, g_ref, pre_ref, cell_ref, d_ref, db_ref, work_ref, edge_ref):
    pool_backward(0, g_ref, pre_ref, cell_ref, 0, d_ref, db_ref.at[0], work_ref, edge_ref, hidden, length // LANES)


def columns(rows, length):
    return pl.BlockSpec((rows, length), lambda s: (0, s))


def fixed(*dims):
    return pl.BlockSpec(dims, lambda s: (0,) * len(dims), pipeline_mode=pl.Buffered(1))


def params(**more):
    return pltpu.CompilerParams(vmem_limit_bytes=63 * 1024 * 1024, **more)


shape = jax.ShapeDtypeStruct


def run_first(seqs, weight, bias, gathered):
    (wide, width), total = weight.shape, gathered.shape[0]
    hidden, length = wide // 6, total // seqs
    return pl.pallas_call(
        functools.partial(first_kernel, hidden, length),
        name="layer_one_forward",
        grid=(seqs,),
        in_specs=[fixed(wide, width), fixed(hidden, 1), pl.BlockSpec((length, width), lambda s: (s, 0))],
        out_specs=[columns(3 * hidden, length), columns(hidden, length), columns(hidden, length)],
        out_shape=[shape((3 * hidden, total), BF16), shape((hidden, total), F32), shape((hidden, total), BF16)],
        scratch_shapes=[
            pltpu.VMEM((wide, length), F32),
            pltpu.VMEM((hidden, length), F32),
            pltpu.VMEM((hidden, LANES), F32),
        ],
        compiler_params=params(),
    )(weight, bias, gathered)


def run_second(seqs, weight, bias, gathered, grad):
    (wide, width), total = weight.shape, gathered.shape[1]
    hidden, length = wide // 6, total // seqs
    return pl.pallas_call(
        functools.partial(second_kernel, hidden, length),
        name="layer_two_forward_and_pool_backward",
        grid=(seqs,),
        in_specs=[fixed(wide, width), fixed(hidden, 1), columns(width, length), columns(hidden, length)],
        out_specs=[columns(hidden, length), columns(wide, length), pl.BlockSpec((1, hidden, 1), lambda s: (s, 0, 0))],
        out_shape=[shape((hidden, total), BF16), shape((wide, total), BF16), shape((seqs, hidden, 1), F32)],
        scratch_shapes=[
            pltpu.VMEM((wide, length), F32),
            pltpu.VMEM((3 * hidden, length), BF16),
            pltpu.VMEM((hidden, length), F32),
            pltpu.VMEM((2, hidden, length), F32),
            pltpu.VMEM((2, hidden, LANES), F32),
        ],
        compiler_params=params(),
    )(weight, bias, gathered, grad)


def run_back(seqs, grad, pre, cell):
    hidden, total = grad.shape
    length = total // seqs
    return pl.pallas_call(
        functools.partial(back_kernel, hidden, length),
        name="layer_one_pool_backward",
        grid=(seqs,),
        in_specs=[columns(hidden, length), columns(3 * hidden, length), columns(hidden, length)],
        out_specs=[columns(6 * hidden, length), pl.BlockSpec((1, hidden, 1), lambda s: (s, 0, 0))],
        out_shape=[shape((6 * hidden, total), BF16), shape((seqs, hidden, 1), F32)],
        scratch_shapes=[pltpu.VMEM((2, hidden, length), F32), pltpu.VMEM((2, hidden, LANES), F32)],
        compiler_params=params(),
    )(grad, pre, cell)


THIRDS = 3
PIECES = 3
SLOTS = 12
AHEAD = 6
BEHIND = 2


class Here:
    def __init__(self):
        self.z = lax.axis_index("seq")
        self.b = lax.axis_index("tm")
        self.c = lax.rem(self.b, 2)
        self.x = lax.rem(self.b // 2, 2)
        self.y = self.b // 4
        self.core = dict(seq=self.z, tm=self.b + 1 - 2 * self.c)
        self.across_x = dict(seq=self.z, tm=self.b + 2 - 4 * self.x)
        self.across_y = dict(seq=self.z, tm=self.b + 4 - 8 * self.y)
        self.pair = dict(seq=self.z + 1 - 2 * lax.rem(self.z, 2), tm=self.b)
        self.middle = dict(seq=3 - self.z, tm=self.b)
        self.line = [dict(seq=lax.rem(self.z + d, 4), tm=self.b) for d in range(1, 4)]
        self.peers = [dict(seq=self.z, tm=lax.rem(self.b + d, 8)) for d in range(1, 8)]
        self.is_end = jnp.logical_or(self.z == 0, self.z == 3)
        self.is_centre = jnp.logical_and(self.z > 0, self.z < 3)


def remote(src, dst, send, recv, target):
    return pltpu.make_async_remote_copy(
        src_ref=src, dst_ref=dst, send_sem=send, recv_sem=recv, device_id=target, device_id_type=MESH
    )


def both(a, b):
    if isinstance(a, bool) and isinstance(b, bool):
        return a and b
    return jnp.logical_and(a, b)


def signal(sem, target):
    pl.semaphore_signal(sem, inc=1, device_id=target, device_id_type=MESH)


def meet(targets):
    barrier = pltpu.get_barrier_semaphore()
    for target in targets:
        signal(barrier, target)
    pl.semaphore_wait(barrier, len(targets))


class SeqSum:
    def __init__(self, here, gates, hidden, third, own, ring_in, ring_mid, total, out, sems, credits):
        self.here, self.third, self.rows = here, third, hidden // PIECES
        self.gates, self.blocks = gates, 2 * gates * THIRDS
        self.units = self.blocks * PIECES
        self.own, self.ring_in, self.ring_mid, self.total, self.out = own, ring_in, ring_mid, total, out
        self.sems = sems
        self.credit_in, self.credit_mid, self.credit_out = credits

    def rows_of(self, u):
        return pl.ds(pl.multiple_of(lax.rem(u, PIECES) * self.rows, 16), self.rows)

    def mine(self, u):
        return self.own.at[u // PIECES, self.rows_of(u)]

    def inward(self, u):
        i = lax.rem(u, SLOTS)
        return remote(self.mine(u), self.ring_in.at[i], self.sems.at[0, i], self.sems.at[1, i], self.here.pair)

    def across(self, u):
        i = lax.rem(u, SLOTS)
        return remote(self.mine(u), self.ring_mid.at[i], self.sems.at[2, i], self.sems.at[3, i], self.here.middle)

    def outward(self, u):
        i = lax.rem(u, SLOTS)
        return remote(self.total.at[i], self.ring_in.at[i], self.sems.at[4, i], self.sems.at[5, i], self.here.pair)

    def store(self, u, ring):
        i, block = lax.rem(u, SLOTS), u // PIECES
        cols = pl.ds(pl.multiple_of((block // (2 * self.gates)) * self.third, LANES), self.third)
        to = self.out.at[self.product(block), self.rows_of(u), cols]
        return pltpu.make_async_copy(ring.at[i], to, self.sems.at[6, i])

    def product(self, block):
        k = lax.rem(block, 2 * self.gates)
        return k if self.gates == 3 else (k // 2) * 3 + lax.rem(k, 2)

    def add(self, dst, a, b):
        def rows(r):
            at = pl.ds(r, ROWS)
            dst[at, :] = a[at, :] + b[at, :]

        tiles(self.rows, ROWS, rows)

    def offer(self, u):
        @pl.when(self.here.is_end)
        def _():
            @pl.when(u >= SLOTS)
            def _():
                pl.semaphore_wait(self.credit_in, 1)
                self.inward(u - SLOTS).wait_send()

            self.inward(u).start()

    def gather(self, u):
        i = lax.rem(u, SLOTS)
        self.inward(u).wait_recv()
        self.add(self.mine(u), self.mine(u), self.ring_in.at[i])

        @pl.when(u + SLOTS < self.units)
        def _():
            signal(self.credit_in, self.here.pair)

        @pl.when(u >= SLOTS)
        def _():
            pl.semaphore_wait(self.credit_mid, 1)
            self.across(u - SLOTS).wait_send()

        self.across(u).start()

    def finish(self, u):
        i = lax.rem(u, SLOTS)
        self.across(u).wait_recv()

        @pl.when(u >= SLOTS)
        def _():
            pl.semaphore_wait(self.credit_out, 1)
            self.outward(u - SLOTS).wait_send()
            self.store(u - SLOTS, self.total).wait()

        self.add(self.total.at[i], self.mine(u), self.ring_mid.at[i])

        @pl.when(u + SLOTS < self.units)
        def _():
            signal(self.credit_mid, self.here.middle)

        self.outward(u).start()
        self.store(u, self.total).start()

    def accept(self, u):
        self.outward(u).wait_recv()
        self.store(u, self.ring_in).start()

        @pl.when(u > 0)
        def _():
            self.store(u - 1, self.ring_in).wait()

            @pl.when(u - 1 + SLOTS < self.units)
            def _():
                signal(self.credit_out, self.here.pair)

    def tick(self, n):
        @pl.when(self.here.is_centre)
        def _():
            @pl.when(n < self.units)
            def _():
                self.gather(n)

            @pl.when(both(n >= BEHIND, n < self.units + BEHIND))
            def _():
                self.finish(n - BEHIND)

        @pl.when(n + AHEAD < self.units)
        def _():
            self.offer(n + AHEAD)

        @pl.when(n >= BEHIND + 2)
        def _():
            @pl.when(self.here.is_end)
            def _():
                self.accept(n - BEHIND - 2)

    def drain(self):
        @pl.when(self.here.is_centre)
        def _():
            for u in range(self.units - SLOTS, self.units):
                self.across(u).wait_send()
                self.outward(u).wait_send()
                self.store(u, self.total).wait()

        @pl.when(self.here.is_end)
        def _():
            for u in range(self.units - SLOTS, self.units):
                self.inward(u).wait_send()
            self.store(self.units - 1, self.ring_in).wait()


class RankSum:
    def __init__(self, here, part, pairs, wide_x, wide_y, last_x, last_y, sems):
        self.here, self.part, self.pairs = here, part, pairs
        self.wide_x, self.wide_y, self.last_x, self.last_y, self.sems = wide_x, wide_y, last_x, last_y, sems
        self.rows = part.shape[3]
        self.upper = pl.ds(0, self.rows // 2)
        self.lower = pl.ds(self.rows // 2, self.rows // 2)
        self.step = 16

    def copy(self, k, s, src, dst, target):
        return remote(src, dst, self.sems.at[s, k, 0], self.sems.at[s, k, 1], target)

    def swap(self, s):
        return self.copy(0, s, self.part.at[:, :, 1 - self.here.c], self.pairs.at[s], self.here.core)

    def wide(self, s):
        h = self.here
        return (
            self.copy(1, s, self.pairs.at[s, :, 1 - h.x, self.upper], self.wide_x.at[s], h.across_x),
            self.copy(2, s, self.pairs.at[s, 1 - h.y, :, self.lower], self.wide_y.at[s], h.across_y),
        )

    def last(self, s):
        h = self.here
        return (
            self.copy(3, s, self.pairs.at[s, 1 - h.y, h.x, self.upper], self.last_y.at[s], h.across_y),
            self.copy(4, s, self.pairs.at[s, h.y, 1 - h.x, self.lower], self.last_x.at[s], h.across_x),
        )

    def start(self, s):
        self.swap(s).start()

    def cross(self, s):
        h = self.here
        self.swap(s).wait()

        def rows(r):
            at = pl.ds(r, self.step)
            for y in range(2):
                for x in range(2):
                    self.pairs[s, y, x, at, :] = self.pairs[s, y, x, at, :] + self.part[y, x, h.c, at, :]

        tiles(self.rows, self.step, rows)
        for copy in self.wide(s):
            copy.start()

    def turn(self, s):
        h = self.here
        half = self.rows // 2
        for copy in self.wide(s):
            copy.wait()

        def rows(r):
            at, low = pl.ds(r, self.step), pl.ds(half + r, self.step)
            for k in range(2):
                self.pairs[s, k, h.x, at, :] = self.pairs[s, k, h.x, at, :] + self.wide_x[s, k, at, :]
                self.pairs[s, h.y, k, low, :] = self.pairs[s, h.y, k, low, :] + self.wide_y[s, k, at, :]

        tiles(half, self.step, rows)
        for copy in self.last(s):
            copy.start()

    def done(self, s, out):
        h = self.here
        half = self.rows // 2
        for copy in self.last(s):
            copy.wait()

        def rows(r):
            at, low = pl.ds(r, self.step), pl.ds(half + r, self.step)
            out[at, :] = self.pairs[s, h.y, h.x, at, :] + self.last_y[s, at, :]
            out[low, :] = self.pairs[s, h.y, h.x, low, :] + self.last_x[s, at, :]

        tiles(half, self.step, rows)


def sum_scratch(seqs, hidden, third, rows, cols):
    return [
        pltpu.VMEM((18, hidden, third), BF16),
        pltpu.VMEM((SLOTS, hidden // PIECES, third), BF16),
        pltpu.VMEM((SLOTS, hidden // PIECES, third), BF16),
        pltpu.VMEM((SLOTS, hidden // PIECES, third), BF16),
        pltpu.SemaphoreType.DMA((7, SLOTS)),
        pltpu.SemaphoreType.REGULAR,
        pltpu.SemaphoreType.REGULAR,
        pltpu.SemaphoreType.REGULAR,
        pltpu.VMEM((2, 2, 2, rows, cols), BF16),
        pltpu.VMEM((seqs, 2, 2, rows, cols), BF16),
        pltpu.VMEM((seqs, 2, rows // 2, cols), BF16),
        pltpu.VMEM((seqs, 2, rows // 2, cols), BF16),
        pltpu.VMEM((seqs, rows // 2, cols), BF16),
        pltpu.VMEM((seqs, rows // 2, cols), BF16),
        pltpu.SemaphoreType.DMA((seqs, 5, 2)),
        pltpu.SemaphoreType.DMA((17,)),
    ]


def backward_kernel(second, seqs, hidden, length, width, *refs):
    third = width // THIRDS
    if second:
        d_in, r_in, w_in, pre_in, cell_in, gw_out, d_out, db_out = refs[:8]
        dv, wv, rv, pre, cell, work, edge, grad = refs[8:16]
        rest = refs[16:]
    else:
        d_in, r_in, w_in, h_in, sel_in, dsel_in, db1_in, db2_in = refs[:8]
        gw_out, gx_out, h_out, sel_out, wo_out, db_out = refs[8:14]
        dv, wv, rv, gxv, picked, dsel, wo, heard, hv, dbv, dsem, hsem, psem = refs[14:27]
        rest = refs[27:]
    own, ring_in, ring_mid, total, zsem, *credits = rest[:8]
    rank_refs, lsem = rest[8:15], rest[15]
    here = Here()
    gates = 2 if second else 3
    ar = SeqSum(here, gates, hidden, third, own, ring_in, ring_mid, total, gw_out, zsem, credits)
    rs = RankSum(here, *rank_refs)
    groups, piece = length // LANES, LANES // 8

    def columns_of(s):
        return pl.ds(s * length, length)

    def rhs(t):
        if second:
            src = r_in.at[pl.ds(t * third, third), :]
        else:
            src = r_in.at[:, pl.ds(t * third, third)]
        return pltpu.make_async_copy(src, rv.at[t % 2], lsem.at[t % 2])

    loads = [pltpu.make_async_copy(d_in, dv, lsem.at[2]), pltpu.make_async_copy(w_in, wv, lsem.at[3])]
    if second:
        loads.append(pltpu.make_async_copy(pre_in, pre, lsem.at[4]))
        loads.append(pltpu.make_async_copy(cell_in, cell, lsem.at[5]))
    loads[0].start()
    rhs(0).start()
    for copy in loads[1:]:
        copy.start()
    rhs(1).start()
    if second:
        meet([here.core, here.across_x, here.across_y, here.pair, here.middle])
    else:
        meet(here.peers + here.line)
        load_e = pltpu.make_async_copy(dsel_in, dsel, lsem.at[8])
        load_e.start()

        def halves(start, half):
            size = hidden if half is None else hidden // 2
            return pl.ds(start + (half or 0) * size, size)

        gather = Gather(
            here,
            lambda b, half: sel_out.at[:, halves(b * hidden, half)],
            psem,
            lambda half: sel_in.at[:, halves(0, half)],
        )
        gather.start()
        keep = pltpu.make_async_copy(sel_in, sel_out.at[:, pl.ds(here.b * hidden, hidden)], lsem.at[9])
        keep.start()
        dbv[here.z] = jnp.zeros((8, hidden), F32)
        for layer, db in enumerate((db1_in, db2_in)):
            dbv[here.z, layer : layer + 1, :] = to_row(sum(db[s] for s in range(1, seqs)) + db[0])
        biases = []
        for d, peer in enumerate(here.line, 1):
            biases.append(remote(dbv.at[here.z], dbv.at[here.z], dsem.at[d, 0], dsem.at[d, 1], peer))
        for copy in biases:
            copy.start()
        spread = [pltpu.make_async_copy(h_in.at[here.b], heard.at[here.b], hsem.at[0, 0])]
        for d, peer in enumerate(here.peers, 1):
            spread.append(remote(h_in.at[peer["tm"]], heard.at[here.b], hsem.at[d, 0], hsem.at[d, 1], peer))

    done = [0]

    def units(t, low, high):
        def unit(k, carry):
            block = t * (2 * gates) + k
            rows = pl.ds(pl.multiple_of(ar.product(block) * hidden, 16), hidden)
            own[block] = dot(dv[rows, :], rv[t % 2], NT if second else NN).astype(BF16)
            for i in range(PIECES):
                u = block * PIECES + i

                @pl.when(u < AHEAD)
                def _(u=u):
                    ar.offer(u)

            return carry

        lax.fori_loop(low, high, unit, 0)
        done[0] = (t * 2 * gates + high) * PIECES

    def strips(s, q):
        if second:
            i, start = q // 2, lax.rem(q, 2) * (length // 2)
            lhs = pl.ds(pl.multiple_of(i * (width // 2), LANES), width // 2)

            def strip(c):
                cols = pl.ds(pl.multiple_of(start + c, 256), 256)
                src = pl.ds(pl.multiple_of(s * length + start + c, 256), 256)
                got = dot(wv[:, lhs], dv[:, src], TN).astype(BF16)
                rs.part[i, :, :, :, cols] = got.reshape(2, 2, hidden, 256)

            tiles(length // 2, 256, strip)
        else:

            def strip(c, carry):
                cols = pl.ds(pl.multiple_of(c * 256, 256), 256)
                got = dot(dv[:, columns_of(s)], wv[:, cols], TN).astype(BF16)
                for j in range(groups):
                    block = got[j * LANES : (j + 1) * LANES].reshape(2, 2, 2, piece, 256)
                    rs.part[:, :, :, pl.ds(j * piece, piece), cols] = block
                return carry

            count = width // 256
            lax.fori_loop(count * q // 4, count * (q + 1) // 4, strip, 0)

    spent = [0]

    def tick(count=1):
        for _ in range(count):
            assert spent[0] + AHEAD < min(done[0], ar.units) or done[0] == ar.units
            ar.tick(spent[0])
            spent[0] += 1

    def input_grad(s):
        first = spent[0]
        assert first + 3 + AHEAD < done[0]

        def quarter(q, carry):
            strips(s, q)
            ar.tick(first + q)
            return carry

        lax.fori_loop(0, 4, quarter, 0)
        spent[0] += 4

    def settle(s):
        if second:
            rs.done(s, grad.at[:, columns_of(s)])
        else:
            rs.done(s, gxv.at[s])
            gxv[s] = dot(reorder(piece, groups, True), gxv[s], NN).astype(BF16)

    def outgate_load(t):
        return pltpu.make_async_copy(sel_out.at[:, pl.ds(t * third, third)], picked, lsem.at[10])

    def outgate_store(t, tap):
        return pltpu.make_async_copy(wo.at[tap], wo_out.at[tap, :, pl.ds(t * third, third)], lsem.at[11 + tap])

    def outgate(t):
        outgate_load(t).wait()
        for tap in range(2):
            if t:
                outgate_store(t - 1, tap).wait()
            wo[tap] = dot(dsel[...], picked[tap], NT).astype(BF16)
            outgate_store(t, tap).start()
        if t + 1 < THIRDS:
            outgate_load(t + 1).start()

    count = 2 * gates
    loads[0].wait()
    rhs(0).wait()
    units(0, 0, count)
    rhs(2).start()
    loads[1].wait()
    input_grad(0)
    rs.start(0)
    if second:
        tick()
        rhs(1).wait()
        units(1, 0, 2)
        rs.cross(0)
        tick(2)
        units(1, 2, 4)
        input_grad(1)
        rs.start(1)
        rs.turn(0)
        rhs(2).wait()
        tick(2)
        units(2, 0, 2)
        tick()
        rs.cross(1)
        units(2, 2, 4)
        tick(2)
        settle(0)
        tick(2)
        for copy in loads[2:4]:
            copy.wait()
        stores = [
            pltpu.make_async_copy(dv.at[:, columns_of(s)], d_out.at[:, columns_of(s)], lsem.at[6 + s])
            for s in range(seqs)
        ]

        def pool(s):
            first = s * length
            pool_backward(first, grad, pre, cell, first, dv, db_out.at[s], work, edge, hidden, groups)
            stores[s].start()

        pool(0)
        tick()
        rs.turn(1)
        tick(3)
        settle(1)
        pool(1)
    else:
        gather.relay()
        rhs(1).wait()
        units(1, 0, 2)
        tick()
        units(1, 2, 4)
        tick()
        rs.cross(0)
        tick()
        input_grad(1)
        rs.start(1)
        units(1, 4, 6)
        tick(2)
        gather.share()
        rhs(2).wait()
        units(2, 0, 2)
        tick()
        rs.cross(1)
        tick()
        rs.turn(0)
        tick()
        units(2, 2, 4)
        tick()
        units(2, 4, 6)
        tick(6)
        settle(0)
        rs.turn(1)
        keep.wait()
        load_e.wait()
        outgate_load(0).start()
        tick(2)
        for copy in spread:
            copy.start()
        tick(4)
        settle(1)
        stores = [pltpu.make_async_copy(gxv, gx_out, lsem.at[6])]
        stores[0].start()
        for t in range(THIRDS):
            tick(2)
            outgate(t)
        for copy in spread:
            copy.wait()
        back = reorder(piece, groups, True)
        for s in range(seqs):
            for b in range(8):
                block = heard[b, pl.ds(s * LANES, LANES), :]
                hv[s, :, b * hidden : (b + 1) * hidden] = dot(back, block, NN).astype(BF16)
        stores += [outgate_store(THIRDS - 1, tap) for tap in range(2)]
        stores.append(pltpu.make_async_copy(hv, h_out, lsem.at[13]))
        stores[-1].start()

    def more(n, carry):
        ar.tick(n)
        return carry

    lax.fori_loop(spent[0], ar.units + BEHIND + 2, more, 0)
    ar.drain()
    for copy in stores:
        copy.wait()
    if not second:
        gather.drain()
        for copy in biases:
            copy.wait()
        db_out[...] = dbv[0] + dbv[1] + dbv[2] + dbv[3]


def run_backward(seqs, d, rhs, weight, second, more):
    (wide, width), total = weight.shape, d.shape[1]
    hidden, length = wide // 6, total // seqs
    third, span = width // THIRDS, length // 8
    outs = [shape((6, hidden, width), BF16)]
    scratch = [pltpu.VMEM((wide, total), BF16), pltpu.VMEM((wide, width), BF16)]
    vmem = pl.BlockSpec(memory_space=pltpu.VMEM)
    if second:
        outs += [shape((wide, total), BF16), shape((seqs, hidden, 1), F32)]
        rows, cols = hidden, length
        scratch += [
            pltpu.VMEM((2, third, total), BF16),
            pltpu.VMEM((3 * hidden, total), BF16),
            pltpu.VMEM((hidden, total), F32),
            pltpu.VMEM((2, hidden, length), F32),
            pltpu.VMEM((2, hidden, LANES), F32),
            pltpu.VMEM((hidden, total), BF16),
        ]
    else:
        picked = more[2].shape[1]
        outs += [
            shape((seqs, span, width), BF16),
            shape((seqs, span, width), BF16),
            shape((2, width, picked), BF16),
            shape((2, hidden, width), BF16),
            shape((8, hidden), F32),
        ]
        rows, cols = span, width
        scratch += [
            pltpu.VMEM((2, total, third), BF16),
            pltpu.VMEM((seqs, span, width), BF16),
            pltpu.VMEM((2, third, picked), BF16),
            pltpu.VMEM((hidden, picked), BF16),
            pltpu.VMEM((2, hidden, third), BF16),
            pltpu.VMEM(more[0].shape, BF16),
            pltpu.VMEM((seqs, span, width), BF16),
            pltpu.VMEM((4, 8, hidden), F32),
            pltpu.SemaphoreType.DMA((4, 2)),
            pltpu.SemaphoreType.DMA((8, 2)),
            pltpu.SemaphoreType.DMA((11, 2)),
        ]
    operands = (d, rhs, weight) + more
    return pl.pallas_call(
        functools.partial(backward_kernel, second, seqs, hidden, length, width),
        name="layer_two_backward" if second else "layer_one_backward",
        in_specs=[ANY] * 5 if second else [ANY] * 6 + [vmem] * 2,
        out_specs=[ANY] * (len(outs) - 1) + [vmem],
        out_shape=outs,
        scratch_shapes=scratch + sum_scratch(seqs, hidden, third, rows, cols),
        compiler_params=params(collective_id=1 if second else 2, has_side_effects=True),
    )(*operands)


def reorder(piece, groups, back):
    span = piece * groups
    a = lax.broadcasted_iota(jnp.int32, (span, span), 1 if back else 0)
    b = lax.broadcasted_iota(jnp.int32, (span, span), 0 if back else 1)
    return (b == lax.rem(a, piece) * groups + a // piece).astype(BF16)


def to_row(column):
    n = column.shape[0]
    same = lax.broadcasted_iota(jnp.int32, (n, n), 0) == lax.broadcasted_iota(jnp.int32, (n, n), 1)
    return jnp.sum(jnp.where(same, column, 0.0), axis=0, keepdims=True)


def to_column(row):
    n = row.shape[1]
    same = lax.broadcasted_iota(jnp.int32, (n, n), 0) == lax.broadcasted_iota(jnp.int32, (n, n), 1)
    return jnp.sum(jnp.where(same, row, 0.0), axis=1, keepdims=True)


class Gather:
    def __init__(self, here, region, sems, own=None):
        h, b = here, here.b
        own = own or (lambda half: region(b, half))
        bx, by = h.across_x["tm"], h.across_y["tm"]
        bd = bx + 4 - 8 * h.y
        plan = (
            (b, 1, h.across_x),
            (b, 0, h.across_y),
            (b, 0, h.across_x),
            (b, 1, h.across_y),
            (b, None, h.core),
            (bx, 1, h.across_y),
            (by, 0, h.across_x),
            (bx, None, h.core),
            (by, None, h.core),
            (bd, 0, h.core),
            (bd, 1, h.core),
        )
        self.copies = []
        for k, (block, half, to) in enumerate(plan):
            src = own(half) if k < 5 else region(block, half)
            self.copies.append(remote(src, region(block, half), sems.at[k, 0], sems.at[k, 1], to))

    def start(self):
        for k in range(5):
            self.copies[k].start()

    def relay(self):
        self.copies[0].wait_recv()
        self.copies[5].start()
        self.copies[1].wait_recv()
        self.copies[6].start()

    def share_near(self):
        self.copies[2].wait_recv()
        self.copies[7].start()
        self.copies[4].wait_recv()
        self.copies[7].wait_recv()

    def share_far(self):
        self.copies[3].wait_recv()
        self.copies[8].start()
        self.copies[6].wait_recv()
        self.copies[9].start()
        self.copies[5].wait_recv()
        self.copies[10].start()
        for k in (8, 9, 10):
            self.copies[k].wait_recv()

    def share(self):
        self.share_near()
        self.share_far()

    def drain(self):
        for copy in self.copies:
            copy.wait_send()


def forward_kernel(seqs, hidden, length, width, *refs):
    x_in, w1_in, w2_in, cot_in, b1_in, b2_in, starts = refs[:7]
    x_out, h1_out, pre_out, cell_out, h2_out, d_out, db_out, sel_out, dsel_out = refs[7:16]
    xg, hg, w, p, pre, cell, work, edge, dv, seed, grad, hv, h2t, raw, cot, sent, b1, b2, pick, sel, dsel = refs[16:37]
    xsem, hsem, ssem, zsem, lsem = refs[37:]
    here = Here()
    groups = length // LANES
    piece = LANES // 8

    def columns_of(s):
        return pl.ds(s * length, length)

    def x_region(s):
        def region(b, half):
            js = pl.ds(0, groups) if half is None else pl.ds(half * (groups // 2), groups // 2)
            return xg.at[s, js, b]

        return region

    def h_region(s):
        def region(b, half):
            rows = pl.ds(0, hidden) if half is None else pl.ds(half * (hidden // 2), hidden // 2)
            return hg.at[b, rows, columns_of(s)]

        return region

    def load(src, dst, k):
        return pltpu.make_async_copy(src, dst, lsem.at[k])

    load_w1 = load(w1_in, w, 0)
    load_w2 = load(w2_in, w, 0)
    load_x = [load(x_in.at[s], raw.at[s], 1 + s) for s in range(seqs)]
    load_c = load(cot_in, cot, 14)
    store_x = [load(xg.at[s], x_out.at[s], 3 + s) for s in range(seqs)]
    store_h = [load(hg.at[:, :, columns_of(s)], h1_out.at[:, :, columns_of(s)], 5 + s) for s in range(seqs)]
    store_p = [load(pre.at[:, columns_of(s)], pre_out.at[:, columns_of(s)], 7 + s) for s in range(seqs)]
    store_c = [load(cell.at[:, columns_of(s)], cell_out.at[:, columns_of(s)], 9 + s) for s in range(seqs)]
    store_d = [load(dv.at[s], d_out.at[:, columns_of(s)], 11 + s) for s in range(seqs)]
    store_o = load(h2t, h2_out, 13)

    for copy in load_x:
        copy.start()
    load_w1.start()
    load_c.start()
    meet(here.peers + here.line)
    xs = [Gather(here, x_region(s), xsem.at[s]) for s in range(seqs)]
    hs = [Gather(here, h_region(s), hsem.at[s]) for s in range(seqs)]
    order = reorder(piece, groups, False)

    def place(s):
        load_x[s].wait()
        xg[s, :, here.b] = dot(order, raw[s], NN).astype(BF16).reshape(groups, piece, width)
        xs[s].start()

    def prepare():
        load_c.wait()
        for s in range(seqs):
            turned = dot(order, cot[s], NN).astype(BF16)
            for b in range(8):
                block = turned[:, b * hidden : (b + 1) * hidden]
                sent[b, s] = block.reshape(groups, piece, hidden)
        seed[:, :, pl.ds(0, 4)] = jnp.zeros((seqs, groups, 4, piece, hidden), BF16)
        for s in range(seqs):
            prepare_pick(s)
        b1[...] = to_column(b1_in[...][None, :])
        b2[...] = to_column(b2_in[...][None, :])

    late = [
        (remote(sent.at[peer["tm"]], seed.at[:, :, here.b], ssem.at[d, 0], ssem.at[d, 1], peer), peer)
        for d, peer in enumerate(here.peers, 1)
    ]

    def first_products(s):
        def block(r):
            rows = pl.ds(r, hidden)
            p[rows, :] = dot(w[rows, :], xg[s].reshape(length, width), NT)

        tiles(6 * hidden, hidden, block)

    def second_products(s, near):
        y = here.y if near else 1 - here.y
        depth = pl.ds(pl.multiple_of(y * (width // 2), LANES), width // 2)

        def block(r):
            rows = pl.ds(r, hidden)
            rhs = hg[pl.ds(y * 4, 4), :, columns_of(s)].reshape(width // 2, length)
            got = dot(w[rows, depth], rhs, NN)
            p[rows, :] = got if near else p[rows, :] + got

        tiles(6 * hidden, hidden, block)

    def first_pool(s):
        first = s * length
        pool_forward(first, p, b1, pre, cell, first, hg.at[here.b], work.at[0], edge.at[0], hidden, groups)

    def second_pool(s):
        pool_forward(s * length, p, b2, pre, cell, 0, hv, work.at[0], edge.at[0], hidden, groups)
        rows = lax.broadcasted_iota(jnp.int32, (LANES, LANES), 0)
        cols = lax.broadcasted_iota(jnp.int32, (LANES, LANES), 1)
        eye = (rows == cols).astype(BF16)
        for j in range(groups):
            turned = dot(eye, hv[:, pl.ds(j * LANES, LANES)], NT).astype(BF16)
            at = pl.ds((s * groups + j) * piece, piece)
            h2t[:, at, :] = turned.reshape(8, piece, hidden)

    def incoming(s):
        rows = lax.broadcasted_iota(jnp.int32, (hidden, hidden), 0)
        cols = lax.broadcasted_iota(jnp.int32, (hidden, hidden), 1)
        eye = (rows == cols).astype(BF16)
        lane = lax.broadcasted_iota(jnp.int32, (1, LANES), 1)
        for j in range(groups):
            block = seed[s, j].reshape(LANES, hidden)
            turned = dot(eye, block, NT)
            step = lane * groups + j
            keep = jnp.zeros((1, LANES), jnp.bool_)
            for k in range(starts.shape[1]):
                begin = starts[s, k]
                keep = jnp.logical_or(keep, jnp.logical_and(step >= begin, step < begin + CLUSTER))
            keep = jnp.broadcast_to(keep, (hidden, LANES))
            grad[:, pl.ds(s * length + j * LANES, LANES)] = jnp.where(keep, turned, 0.0).astype(BF16)

    def pool_back(s):
        pool_backward(s * length, grad, pre, cell, 0, dv.at[s], db_out.at[s], work, edge, hidden, groups, True)
        store_d[s].start()

    def cluster_steps(s):
        lane = lax.broadcasted_iota(jnp.int32, (1, LANES), 1)
        step = lax.rem(lane, CLUSTER)
        for k in range(starts.shape[1]):
            step = step + jnp.where(lane // CLUSTER == k, starts[s, k], 0)
        return lane, step

    def prepare_pick(s):
        _, step = cluster_steps(s)
        for j in range(groups):
            code = lax.broadcasted_iota(jnp.int32, (LANES, LANES), 0) * groups + j
            at = pl.ds(j * LANES, LANES)
            pick[s, at, pl.ds(0, LANES)] = (code == step).astype(BF16)
            pick[s, at, pl.ds(LANES, LANES)] = (code == step - 1).astype(BF16)

    def held(s, count):
        start = here.z * (seqs * LANES) + s * LANES
        return pl.ds(pl.multiple_of(start, LANES), count * LANES)

    def pick_hidden(s):
        got = dot(hg[here.b, :, columns_of(s)], pick[s], NN).astype(BF16)
        for tap in range(2):
            sel[tap, :, held(s, 1)] = got[:, tap * LANES : (tap + 1) * LANES]

    def pick_grad(s):
        lane, step = cluster_steps(s)
        again = jnp.zeros((1, LANES), jnp.bool_)
        for k in range(starts.shape[1] - 1):
            begin = starts[s, k]
            inside = jnp.logical_and(step >= begin, step < begin + CLUSTER)
            again = jnp.logical_or(again, jnp.logical_and(inside, lane // CLUSTER > k))
        got = dot(dv[s, pl.ds(2 * hidden, hidden), :], pick[s, :, pl.ds(0, LANES)], NN)
        dsel[:, held(s, 1)] = jnp.where(jnp.broadcast_to(again, (hidden, LANES)), 0.0, got).astype(BF16)

    spread_h = []
    spread_d = []
    for d, peer in enumerate(here.line, 1):
        at = sel.at[:, :, held(0, seqs)]
        spread_h.append(remote(at, at, zsem.at[d, 0], zsem.at[d, 1], peer))
        at = dsel.at[:, held(0, seqs)]
        spread_d.append(remote(at, at, zsem.at[d, 2], zsem.at[d, 3], peer))
    store_s = load(sel, sel_out, 15)
    store_e = load(dsel, dsel_out, 16)

    place(0)
    prepare()
    xs[0].relay()
    place(1)
    xs[0].share()
    store_x[0].start()
    load_w1.wait()
    first_products(0)
    xs[1].relay()
    first_pool(0)
    hs[0].start()
    store_p[0].start()
    store_c[0].start()
    xs[1].share()
    store_x[1].start()
    first_products(1)
    load_w2.start()
    hs[0].relay()
    first_pool(1)
    hs[1].start()
    store_p[1].start()
    store_c[1].start()

    for s in range(seqs):
        pick_hidden(s)
    for copy in spread_h:
        copy.start()
    hs[0].share_near()
    load_w2.wait()
    second_products(0, True)
    hs[0].share_far()
    store_h[0].start()
    second_products(0, False)
    hs[1].relay()

    @pl.when(here.y == 1)
    def _():
        pltpu.make_async_copy(sent.at[here.b], seed.at[:, :, here.b], ssem.at[0, 0]).start()
        for copy, _ in late:
            copy.start()

    store_p[0].wait()
    store_c[0].wait()
    second_pool(0)
    hs[1].share_near()
    second_products(1, True)
    hs[1].share_far()
    store_h[1].start()
    second_products(1, False)
    store_p[1].wait()
    store_c[1].wait()
    second_pool(1)
    store_o.start()

    @pl.when(here.y == 1)
    def _():
        pltpu.make_async_copy(sent.at[here.b], seed.at[:, :, here.b], ssem.at[0, 0]).wait()
        for copy, _ in late:
            copy.wait_send()

    for d, (copy, _) in enumerate(late, 1):
        source = lax.rem(here.b + 8 - d, 8)

        @pl.when(source >= 4)
        def _(copy=copy):
            copy.wait_recv()

    for s in range(seqs):
        incoming(s)
        outgate_backward(s * length, grad, pre, cell, dv.at[s], hidden, groups)
        pick_grad(s)
    for copy in spread_d:
        copy.start()
    for copy in spread_h:
        copy.wait()
    store_s.start()
    for s in range(seqs):
        pool_back(s)
    for gather in xs + hs:
        gather.drain()
    for copy in spread_d:
        copy.wait()
    store_e.start()
    for copy in store_x + store_h + store_d + [store_o, store_s, store_e]:
        copy.wait()


def run_forward(x, w1, b1, w2, b2, cotangent, starts):
    seqs, span, width = x.shape
    hidden, length, piece = w1.shape[0] // 6, span * 8, LANES // 8
    groups = length // LANES
    total, picked = seqs * length, 4 * seqs * LANES
    assert starts.shape[1] * CLUSTER == LANES
    vmem = pl.BlockSpec(memory_space=pltpu.VMEM)
    return pl.pallas_call(
        functools.partial(forward_kernel, seqs, hidden, length, width),
        name="forward",
        in_specs=[ANY, ANY, ANY, ANY, vmem, vmem, pl.BlockSpec(memory_space=pltpu.SMEM)],
        out_specs=[ANY, ANY, ANY, ANY, ANY, ANY, vmem, ANY, ANY],
        out_shape=[
            shape((seqs, groups, 8, piece, width), BF16),
            shape((8, hidden, total), BF16),
            shape((3 * hidden, total), BF16),
            shape((hidden, total), F32),
            shape((8, seqs * groups * piece, hidden), BF16),
            shape((6 * hidden, total), BF16),
            shape((seqs, hidden, 1), F32),
            shape((2, hidden, picked), BF16),
            shape((hidden, picked), BF16),
        ],
        scratch_shapes=[
            pltpu.VMEM((seqs, groups, 8, piece, width), BF16),
            pltpu.VMEM((8, hidden, total), BF16),
            pltpu.VMEM((6 * hidden, width), BF16),
            pltpu.VMEM((6 * hidden, length), F32),
            pltpu.VMEM((3 * hidden, total), BF16),
            pltpu.VMEM((hidden, total), F32),
            pltpu.VMEM((2, hidden, length), F32),
            pltpu.VMEM((2, hidden, LANES), F32),
            pltpu.VMEM((seqs, 6 * hidden, length), BF16),
            pltpu.VMEM((seqs, groups, 8, piece, hidden), BF16),
            pltpu.VMEM((hidden, total), BF16),
            pltpu.VMEM((hidden, length), BF16),
            pltpu.VMEM((8, seqs * groups * piece, hidden), BF16),
            pltpu.VMEM((seqs, span, width), BF16),
            pltpu.VMEM((seqs, span, width), BF16),
            pltpu.VMEM((8, seqs, groups, piece, hidden), BF16),
            pltpu.VMEM((hidden, 1), F32),
            pltpu.VMEM((hidden, 1), F32),
            pltpu.VMEM((seqs, length, 2 * LANES), BF16),
            pltpu.VMEM((2, hidden, picked), BF16),
            pltpu.VMEM((hidden, picked), BF16),
            pltpu.SemaphoreType.DMA((seqs, 11, 2)),
            pltpu.SemaphoreType.DMA((seqs, 11, 2)),
            pltpu.SemaphoreType.DMA((8, 2)),
            pltpu.SemaphoreType.DMA((4, 4)),
            pltpu.SemaphoreType.DMA((17,)),
        ],
        compiler_params=params(collective_id=0, has_side_effects=True),
    )(x, w1, w2, cotangent, b1, b2, starts)


def widen_kernel(one_ref, two_ref, outgate_ref, wide_one_ref, wide_two_ref):
    wide_one_ref[...] = one_ref[...].astype(F32)
    last = lax.rem(pl.program_id(0), 3) == 2

    @pl.when(last)
    def _():
        wide_two_ref[...] = outgate_ref[...].astype(F32)

    @pl.when(jnp.logical_not(last))
    def _():
        wide_two_ref[...] = two_ref[...].astype(F32)


def widen(one, two, outgate):
    _, hidden, width = one.shape
    dims = (1, hidden, width)
    return pl.pallas_call(
        widen_kernel,
        name="weight_gradients",
        grid=(6,),
        in_specs=[
            pl.BlockSpec(dims, lambda k: (k, 0, 0)),
            pl.BlockSpec(dims, lambda k: (k - k % 3 // 2, 0, 0)),
            pl.BlockSpec(dims, lambda k: (k // 3, 0, 0)),
        ],
        out_specs=[pl.BlockSpec(dims, lambda k: (k, 0, 0))] * 2,
        out_shape=[shape(one.shape, F32)] * 2,
        compiler_params=params(),
    )(one, two, outgate)


def per_device(line, inputs, weight_one, fbias_one, weight_two, fbias_two, cotangent, cluster_starts):
    seqs, span, width = inputs.shape
    count = lax.axis_size("tm")
    length = span * count
    groups = length // LANES
    piece = LANES // count
    hidden = weight_one.shape[2]
    total = seqs * length
    w1 = weight_one.reshape(6 * hidden, width)
    w2 = weight_two.reshape(6 * hidden, width)

    if line:
        x, h1, pre1, cell1, h2, d2, db2, *picked = run_forward(
            inputs, w1, fbias_one, w2, fbias_two, cotangent, cluster_starts
        )
        x, h1 = x.reshape(total, width), h1.reshape(width, total)
        gw2, d1, db1 = run_backward(seqs, d2, h1, w2, True, (pre1, cell1))
        gw1, gx1, h2, _, wo, db = run_backward(seqs, d1, x, w1, False, (h2, *picked, db1, db2))
        gw1, gw2 = widen(gw1, gw2, wo)
    else:
        x = inputs.reshape(seqs, piece, groups, width).transpose(0, 2, 1, 3)
        bias1, bias2 = fbias_one[:, None], fbias_two[:, None]
        seed = cotangent.reshape(seqs, piece, groups, count, hidden)
        steps = lax.axis_index("tm") * span + jnp.arange(span, dtype=jnp.int32)
        starts = cluster_starts[:, :, None]
        keep = jnp.any((steps >= starts) & (steps < starts + CLUSTER), axis=1)
        seed = jnp.where(keep.reshape(seqs, piece, groups, 1, 1), seed, jnp.zeros_like(seed))
        seed = lax.all_to_all(seed, "tm", split_axis=3, concat_axis=1, tiled=True)
        seed = seed.reshape(seqs, LANES, groups, hidden).transpose(3, 0, 2, 1).reshape(hidden, total)
        x = lax.all_gather(x, "tm", axis=2, tiled=True).reshape(total, width)
        pre1, cell1, h1 = run_first(seqs, w1, bias1, x)
        h1 = lax.all_gather(h1, "tm", axis=0, tiled=True)
        h2, d2, db2 = run_second(seqs, w2, bias2, h1, seed)
        h2 = h2.reshape(hidden, seqs, groups, count, piece)
        h2 = lax.all_to_all(h2, "tm", split_axis=3, concat_axis=0, tiled=True)
        h2 = h2.reshape(width, seqs, groups, piece).transpose(1, 3, 2, 0)
        gw2 = lax.psum(dot(d2, h1, NT).astype(BF16), "seq").astype(F32)
        gx2 = lax.psum_scatter(dot(w2, d2, TN).astype(BF16), "tm", scatter_dimension=0, tiled=True)
        d1, db1 = run_back(seqs, gx2, pre1, cell1)
        gw1 = lax.psum(dot(d1, x, NN).astype(BF16), "seq").astype(F32)
        gx1 = dot(d1, w1, TN).astype(BF16).reshape(seqs, groups, LANES, width)
        gx1 = lax.psum_scatter(gx1, "tm", scatter_dimension=2, tiled=True)
        gx1 = gx1.transpose(0, 2, 1, 3).reshape(seqs, span, width)
        db = lax.psum(jnp.stack([db1, db2]).sum(axis=(1, 3)), "seq")
    out = h2.reshape(seqs, span, width)
    dims = weight_one.shape
    return (out, gx1, gw1.reshape(dims), db[0], gw2.reshape(dims), db[1])


def solution(mesh):
    placed = (
        P("seq", "tm", None),
        P(None, None, "tm", None),
        P("tm"),
        P(None, None, "tm", None),
        P("tm"),
        P("seq", "tm", None),
        P("seq", None),
    )
    return jax.shard_map(
        functools.partial(per_device, dict(mesh.shape) == {"seq": 4, "tm": 8}),
        mesh=mesh,
        in_specs=placed,
        out_specs=(
            P("seq", "tm", None),
            P("seq", "tm", None),
            P(None, None, "tm", None),
            P("tm"),
            P(None, None, "tm", None),
            P("tm"),
        ),
        check_vma=False,
    )
```

```python
import functools

import jax
import jax.numpy as jnp
from jax import lax
from jax.experimental import pallas as pl
from jax.experimental.pallas import tpu as pltpu
from jax.sharding import PartitionSpec as P

CLUSTER = 32
LANES = 128
ROWS = 48
F32 = jnp.float32
BF16 = jnp.bfloat16
ANY = pl.BlockSpec(memory_space=pl.ANY)
MESH = pl.DeviceIdType.MESH
NN = (((1,), (0,)), ((), ()))
NT = (((1,), (1,)), ((), ()))
TN = (((0,), (0,)), ((), ()))


def dot(a, b, dims):
    return lax.dot_general(a, b, dims, preferred_element_type=F32)


def sigmoid(v):
    return 1.0 / (1.0 + jnp.exp(-v))


def tiles(count, rows, body):
    def step(r, carry):
        body(pl.multiple_of(r * rows, rows))
        return carry

    lax.fori_loop(0, count // rows, step, 0)


def shift_lanes(v, amount, lane, fill):
    moved = pltpu.roll(v, amount % LANES, axis=1)
    gone = lane < amount if amount > 0 else lane >= LANES + amount
    return jnp.where(gone, fill, moved)


def lane_chain(factor, value, lane, sign):
    step = 1
    while step < LANES:
        value = value + factor * shift_lanes(value, sign * step, lane, 0.0)
        factor = factor * shift_lanes(factor, sign * step, lane, 1.0)
        step *= 2
    return value


def pool_forward(first, p_ref, b_ref, pre_ref, cell_ref, target, h_ref, factor_ref, edge_ref, hidden, groups):
    lane = lax.broadcasted_iota(jnp.int32, (ROWS, LANES), 1)

    def at(j, start=0):
        return pl.ds(start + j * LANES, LANES)

    def gates(r):
        rows = pl.ds(r, ROWS)
        value = factor = None
        for j in range(groups):
            got = []
            for g in range(3):
                now = p_ref[pl.ds(g * hidden + r, ROWS), at(j)]
                tap = pl.ds((3 + g) * hidden + r, ROWS)
                if j:
                    past = p_ref[tap, at(j - 1)]
                else:
                    past = shift_lanes(p_ref[tap, at(groups - 1)], 1, lane, 0.0)
                total = now + past
                if g == 1:
                    total = total + b_ref[rows, :]
                total = total.astype(BF16)
                pre_ref[pl.ds(g * hidden + r, ROWS), at(j, first)] = total
                got.append(total.astype(F32))
            forget = sigmoid(got[1])
            fresh = (1.0 - forget) * jnp.tanh(got[0])
            if j:
                value = forget * value + fresh
                factor = forget * factor
            else:
                value, factor = fresh, forget
            cell_ref[rows, at(j, first)] = value
            factor_ref[rows, at(j)] = factor

    tiles(hidden, ROWS, gates)

    def chain(r):
        rows = pl.ds(r, ROWS)
        value = lane_chain(factor_ref[rows, at(groups - 1)], cell_ref[rows, at(groups - 1, first)], lane, 1)
        edge_ref[rows, :] = shift_lanes(value, 1, lane, 0.0)

    tiles(hidden, ROWS, chain)

    def finish(r):
        rows = pl.ds(r, ROWS)
        edge = edge_ref[rows, :]
        for j in range(groups):
            cell = cell_ref[rows, at(j, first)] + factor_ref[rows, at(j)] * edge
            cell_ref[rows, at(j, first)] = cell
            outgate = sigmoid(pre_ref[pl.ds(2 * hidden + r, ROWS), at(j, first)].astype(F32))
            h_ref[rows, at(j, target)] = (outgate * cell).astype(BF16)

    tiles(hidden, ROWS, finish)


def put_gate(d_ref, g, r, j, v, target, lane, hidden, groups):
    d_ref[pl.ds(g * hidden + r, ROWS), pl.ds(target + j * LANES, LANES)] = v
    tap = pl.ds((3 + g) * hidden + r, ROWS)
    if j:
        d_ref[tap, pl.ds(target + (j - 1) * LANES, LANES)] = v
    else:
        moved = shift_lanes(v.astype(F32), -1, lane, 0.0).astype(BF16)
        d_ref[tap, pl.ds(target + (groups - 1) * LANES, LANES)] = moved


def outgate_backward(first, g_ref, pre_ref, cell_ref, d_ref, hidden, groups):
    lane = lax.broadcasted_iota(jnp.int32, (ROWS, LANES), 1)

    def body(r):
        rows = pl.ds(r, ROWS)
        for j in range(groups):
            at = pl.ds(first + j * LANES, LANES)
            outgate = sigmoid(pre_ref[pl.ds(2 * hidden + r, ROWS), at].astype(F32))
            v = g_ref[rows, at].astype(F32) * cell_ref[rows, at] * outgate * (1.0 - outgate)
            put_gate(d_ref, 2, r, j, v.astype(BF16), 0, lane, hidden, groups)

    tiles(hidden, ROWS, body)


def pool_backward(
    first, g_ref, pre_ref, cell_ref, target, d_ref, db_ref, work_ref, edge_ref, hidden, groups, carried_only=False
):
    lane = lax.broadcasted_iota(jnp.int32, (ROWS, LANES), 1)

    def at(j, start=0):
        return pl.ds(start + j * LANES, LANES)

    def gate(g, r, j):
        return pre_ref[pl.ds(g * hidden + r, ROWS), at(j, first)].astype(F32)

    def start(r):
        rows = pl.ds(r, ROWS)
        later = value = factor = None
        for j in reversed(range(groups)):
            own = g_ref[rows, at(j, first)].astype(F32) * sigmoid(gate(2, r, j))
            if later is None:
                value, factor = own, jnp.ones_like(own)
            else:
                value = own + later * value
                factor = later * factor
            work_ref[0, rows, at(j)] = value
            work_ref[1, rows, at(j)] = factor
            later = sigmoid(gate(1, r, j))
        edge_ref[0, rows, :] = later * value
        edge_ref[1, rows, :] = later * factor

    tiles(hidden, ROWS, start)

    def chain(r):
        rows = pl.ds(r, ROWS)
        value = lane_chain(edge_ref[1, rows, :], edge_ref[0, rows, :], lane, -1)
        edge_ref[0, rows, :] = shift_lanes(value, -1, lane, 0.0)

    tiles(hidden, ROWS, chain)

    def finish(r):
        rows = pl.ds(r, ROWS)
        edge = edge_ref[0, rows, :]
        total = jnp.zeros((ROWS, LANES), F32)
        before = shift_lanes(cell_ref[rows, at(groups - 1, first)], 1, lane, 0.0)
        for j in range(groups):
            carried = work_ref[0, rows, at(j)] + work_ref[1, rows, at(j)] * edge
            candidate = jnp.tanh(gate(0, r, j))
            forget = sigmoid(gate(1, r, j))
            cell = cell_ref[rows, at(j, first)]
            keep = carried * (1.0 - forget)
            got = [keep * (1.0 - candidate * candidate), keep * forget * (before - candidate)]
            if not carried_only:
                outgate = sigmoid(gate(2, r, j))
                got.append(g_ref[rows, at(j, first)].astype(F32) * cell * outgate * (1.0 - outgate))
            before = cell
            for g, v in enumerate(got):
                v = v.astype(BF16)
                if g == 1:
                    total = total + v.astype(F32)
                put_gate(d_ref, g, r, j, v, target, lane, hidden, groups)
        db_ref[rows, :] = jnp.sum(total, axis=1, keepdims=True)

    tiles(hidden, ROWS, finish)


def first_kernel(hidden, length, w_ref, b_ref, x_ref, pre_ref, cell_ref, h_ref, p_ref, work_ref, edge_ref):
    def strip(c):
        cols = pl.ds(c, 512)
        p_ref[:, cols] = dot(w_ref[...], x_ref[cols, :], NT)

    tiles(length, 512, strip)
    pool_forward(0, p_ref, b_ref, pre_ref, cell_ref, 0, h_ref, work_ref, edge_ref, hidden, length // LANES)


def second_kernel(
    hidden, length, w_ref, b_ref, x_ref, g_ref, h_ref, d_ref, db_ref, p_ref, pre_ref, cell_ref, work_ref, edge_ref
):
    def strip(c):
        cols = pl.ds(c, 512)
        p_ref[:, cols] = dot(w_ref[...], x_ref[:, cols], NN)

    tiles(length, 512, strip)
    groups = length // LANES
    pool_forward(0, p_ref, b_ref, pre_ref, cell_ref, 0, h_ref, work_ref.at[0], edge_ref.at[0], hidden, groups)
    pool_backward(0, g_ref, pre_ref, cell_ref, 0, d_ref, db_ref.at[0], work_ref, edge_ref, hidden, groups)


def back_kernel(hidden, length, g_ref, pre_ref, cell_ref, d_ref, db_ref, work_ref, edge_ref):
    pool_backward(0, g_ref, pre_ref, cell_ref, 0, d_ref, db_ref.at[0], work_ref, edge_ref, hidden, length // LANES)


def columns(rows, length):
    return pl.BlockSpec((rows, length), lambda s: (0, s))


def fixed(*dims):
    return pl.BlockSpec(dims, lambda s: (0,) * len(dims), pipeline_mode=pl.Buffered(1))


def params(**more):
    return pltpu.CompilerParams(vmem_limit_bytes=63 * 1024 * 1024, **more)


shape = jax.ShapeDtypeStruct


def run_first(seqs, weight, bias, gathered):
    (wide, width), total = weight.shape, gathered.shape[0]
    hidden, length = wide // 6, total // seqs
    return pl.pallas_call(
        functools.partial(first_kernel, hidden, length),
        name="layer_one_forward",
        grid=(seqs,),
        in_specs=[fixed(wide, width), fixed(hidden, 1), pl.BlockSpec((length, width), lambda s: (s, 0))],
        out_specs=[columns(3 * hidden, length), columns(hidden, length), columns(hidden, length)],
        out_shape=[shape((3 * hidden, total), BF16), shape((hidden, total), F32), shape((hidden, total), BF16)],
        scratch_shapes=[
            pltpu.VMEM((wide, length), F32),
            pltpu.VMEM((hidden, length), F32),
            pltpu.VMEM((hidden, LANES), F32),
        ],
        compiler_params=params(),
    )(weight, bias, gathered)


def run_second(seqs, weight, bias, gathered, grad):
    (wide, width), total = weight.shape, gathered.shape[1]
    hidden, length = wide // 6, total // seqs
    return pl.pallas_call(
        functools.partial(second_kernel, hidden, length),
        name="layer_two_forward_and_pool_backward",
        grid=(seqs,),
        in_specs=[fixed(wide, width), fixed(hidden, 1), columns(width, length), columns(hidden, length)],
        out_specs=[columns(hidden, length), columns(wide, length), pl.BlockSpec((1, hidden, 1), lambda s: (s, 0, 0))],
        out_shape=[shape((hidden, total), BF16), shape((wide, total), BF16), shape((seqs, hidden, 1), F32)],
        scratch_shapes=[
            pltpu.VMEM((wide, length), F32),
            pltpu.VMEM((3 * hidden, length), BF16),
            pltpu.VMEM((hidden, length), F32),
            pltpu.VMEM((2, hidden, length), F32),
            pltpu.VMEM((2, hidden, LANES), F32),
        ],
        compiler_params=params(),
    )(weight, bias, gathered, grad)


def run_back(seqs, grad, pre, cell):
    hidden, total = grad.shape
    length = total // seqs
    return pl.pallas_call(
        functools.partial(back_kernel, hidden, length),
        name="layer_one_pool_backward",
        grid=(seqs,),
        in_specs=[columns(hidden, length), columns(3 * hidden, length), columns(hidden, length)],
        out_specs=[columns(6 * hidden, length), pl.BlockSpec((1, hidden, 1), lambda s: (s, 0, 0))],
        out_shape=[shape((6 * hidden, total), BF16), shape((seqs, hidden, 1), F32)],
        scratch_shapes=[pltpu.VMEM((2, hidden, length), F32), pltpu.VMEM((2, hidden, LANES), F32)],
        compiler_params=params(),
    )(grad, pre, cell)


THIRDS = 3
PIECES = 3
SLOTS = 12
AHEAD = 6
BEHIND = 2
LATER = 12
BLOCKS = 30
OWN = 18


class Here:
    def __init__(self):
        self.z = lax.axis_index("seq")
        self.b = lax.axis_index("tm")
        self.c = lax.rem(self.b, 2)
        self.x = lax.rem(self.b // 2, 2)
        self.y = self.b // 4
        self.core = dict(seq=self.z, tm=self.b + 1 - 2 * self.c)
        self.across_x = dict(seq=self.z, tm=self.b + 2 - 4 * self.x)
        self.across_y = dict(seq=self.z, tm=self.b + 4 - 8 * self.y)
        self.pair = dict(seq=self.z + 1 - 2 * lax.rem(self.z, 2), tm=self.b)
        self.middle = dict(seq=3 - self.z, tm=self.b)
        self.line = [dict(seq=lax.rem(self.z + d, 4), tm=self.b) for d in range(1, 4)]
        self.peers = [dict(seq=self.z, tm=lax.rem(self.b + d, 8)) for d in range(1, 8)]
        self.is_end = jnp.logical_or(self.z == 0, self.z == 3)
        self.is_centre = jnp.logical_and(self.z > 0, self.z < 3)


def remote(src, dst, send, recv, target):
    return pltpu.make_async_remote_copy(
        src_ref=src, dst_ref=dst, send_sem=send, recv_sem=recv, device_id=target, device_id_type=MESH
    )


def both(a, b):
    if isinstance(a, bool) and isinstance(b, bool):
        return a and b
    return jnp.logical_and(a, b)


def signal(sem, target):
    pl.semaphore_signal(sem, inc=1, device_id=target, device_id_type=MESH)


def meet(targets):
    barrier = pltpu.get_barrier_semaphore()
    for target in targets:
        signal(barrier, target)
    pl.semaphore_wait(barrier, len(targets))


def pick(condition, a, b):
    if isinstance(condition, bool):
        return a if condition else b
    return jnp.where(condition, a, b)


class SeqSum:
    def __init__(self, here, hidden, third, own, ring_in, ring_mid, total, out, sems, credits):
        self.here, self.third, self.rows = here, third, hidden // PIECES
        self.units = BLOCKS * PIECES
        self.own, self.ring_in, self.ring_mid, self.total, self.out = own, ring_in, ring_mid, total, out
        self.sems = sems
        self.credit_in, self.credit_mid, self.credit_out = credits

    def rows_of(self, u):
        return pl.ds(pl.multiple_of(lax.rem(u, PIECES) * self.rows, 16), self.rows)

    def mine(self, u):
        return self.own.at[lax.rem(u // PIECES, OWN), self.rows_of(u)]

    def inward(self, u):
        i = lax.rem(u, SLOTS)
        return remote(self.mine(u), self.ring_in.at[i], self.sems.at[0, i], self.sems.at[1, i], self.here.pair)

    def across(self, u):
        i = lax.rem(u, SLOTS)
        return remote(self.mine(u), self.ring_mid.at[i], self.sems.at[2, i], self.sems.at[3, i], self.here.middle)

    def outward(self, u):
        i = lax.rem(u, SLOTS)
        return remote(self.total.at[i], self.ring_in.at[i], self.sems.at[4, i], self.sems.at[5, i], self.here.pair)

    def store(self, u, ring):
        i, block = lax.rem(u, SLOTS), u // PIECES
        second = block < LATER
        t = pick(second, block // 4, (block - LATER) // 6)
        cols = pl.ds(pl.multiple_of(t * self.third, LANES), self.third)
        to = self.out.at[self.product(block) + pick(second, 6, 0), self.rows_of(u), cols]
        return pltpu.make_async_copy(ring.at[i], to, self.sems.at[6, i])

    @staticmethod
    def product(block):
        k = lax.rem(block, 4)
        return pick(block < LATER, (k // 2) * 3 + lax.rem(k, 2), lax.rem(block, 6))

    def add(self, dst, a, b):
        def rows(r):
            at = pl.ds(r, ROWS)
            dst[at, :] = a[at, :] + b[at, :]

        tiles(self.rows, ROWS, rows)

    def offer(self, u):
        @pl.when(self.here.is_end)
        def _():
            @pl.when(u >= SLOTS)
            def _():
                pl.semaphore_wait(self.credit_in, 1)
                self.inward(u - SLOTS).wait_send()

            self.inward(u).start()

    def gather(self, u):
        i = lax.rem(u, SLOTS)
        self.inward(u).wait_recv()
        self.add(self.mine(u), self.mine(u), self.ring_in.at[i])

        @pl.when(u + SLOTS < self.units)
        def _():
            signal(self.credit_in, self.here.pair)

        @pl.when(u >= SLOTS)
        def _():
            pl.semaphore_wait(self.credit_mid, 1)
            self.across(u - SLOTS).wait_send()

        self.across(u).start()

    def finish(self, u):
        i = lax.rem(u, SLOTS)
        self.across(u).wait_recv()

        @pl.when(u >= SLOTS)
        def _():
            pl.semaphore_wait(self.credit_out, 1)
            self.outward(u - SLOTS).wait_send()
            self.store(u - SLOTS, self.total).wait()

        self.add(self.total.at[i], self.mine(u), self.ring_mid.at[i])

        @pl.when(u + SLOTS < self.units)
        def _():
            signal(self.credit_mid, self.here.middle)

        self.outward(u).start()
        self.store(u, self.total).start()

    def accept(self, u):
        self.outward(u).wait_recv()
        self.store(u, self.ring_in).start()

        @pl.when(u > 0)
        def _():
            self.store(u - 1, self.ring_in).wait()

            @pl.when(u - 1 + SLOTS < self.units)
            def _():
                signal(self.credit_out, self.here.pair)

    def tick(self, n):
        @pl.when(self.here.is_centre)
        def _():
            @pl.when(n < self.units)
            def _():
                self.gather(n)

            @pl.when(both(n >= BEHIND, n < self.units + BEHIND))
            def _():
                self.finish(n - BEHIND)

        @pl.when(n + AHEAD < self.units)
        def _():
            self.offer(n + AHEAD)

        @pl.when(n >= BEHIND + 2)
        def _():
            @pl.when(self.here.is_end)
            def _():
                self.accept(n - BEHIND - 2)

    def drain(self):
        @pl.when(self.here.is_centre)
        def _():
            for u in range(self.units - SLOTS, self.units):
                self.across(u).wait_send()
                self.outward(u).wait_send()
                self.store(u, self.total).wait()

        @pl.when(self.here.is_end)
        def _():
            for u in range(self.units - SLOTS, self.units):
                self.inward(u).wait_send()
            self.store(self.units - 1, self.ring_in).wait()


class RankSum:
    def __init__(self, here, part, pairs, wide_x, wide_y, last_x, last_y, sems):
        self.here, self.part, self.pairs = here, part, pairs
        self.wide_x, self.wide_y, self.last_x, self.last_y, self.sems = wide_x, wide_y, last_x, last_y, sems
        self.count = part.shape[3]
        self.half = self.count // 2
        self.upper, self.lower = pl.ds(0, self.half), pl.ds(self.half, self.half)

    def copy(self, k, s, src, dst, target):
        return remote(src, dst, self.sems.at[s, k, 0], self.sems.at[s, k, 1], target)

    def swap(self, s):
        return self.copy(0, s, self.part.at[:, :, 1 - self.here.c], self.pairs.at[s], self.here.core)

    def wide(self, s):
        h = self.here
        return (
            self.copy(1, s, self.pairs.at[s, :, 1 - h.x, self.upper], self.wide_x.at[s], h.across_x),
            self.copy(2, s, self.pairs.at[s, 1 - h.y, :, self.lower], self.wide_y.at[s], h.across_y),
        )

    def last(self, s):
        h = self.here
        return (
            self.copy(3, s, self.pairs.at[s, 1 - h.y, h.x, self.upper], self.last_y.at[s], h.across_y),
            self.copy(4, s, self.pairs.at[s, h.y, 1 - h.x, self.lower], self.last_x.at[s], h.across_x),
        )

    def start(self, s):
        self.swap(s).start()

    def cross(self, s):
        h = self.here
        self.swap(s).wait()

        def some(r):
            at = pl.ds(r, 8)
            for y in range(2):
                for x in range(2):
                    self.pairs[s, y, x, at] = self.pairs[s, y, x, at] + self.part[y, x, h.c, at]

        tiles(self.count, 8, some)
        for copy in self.wide(s):
            copy.start()

    def turn(self, s):
        h = self.here
        for copy in self.wide(s):
            copy.wait()

        def some(r):
            at, low = pl.ds(r, 8), pl.ds(self.half + r, 8)
            for k in range(2):
                self.pairs[s, k, h.x, at] = self.pairs[s, k, h.x, at] + self.wide_x[s, k, at]
                self.pairs[s, h.y, k, low] = self.pairs[s, h.y, k, low] + self.wide_y[s, k, at]

        tiles(self.half, 8, some)
        for copy in self.last(s):
            copy.start()

    def done(self, s, down, put):
        h = self.here
        for copy in self.last(s):
            copy.wait()

        def some(r):
            at, low = pl.ds(r, down), pl.ds(self.half + r, down)
            first = pl.multiple_of(r // down * LANES, LANES)
            put(first, (self.pairs[s, h.y, h.x, at] + self.last_y[s, at]).reshape(down * 16, LANES))
            first = pl.multiple_of((self.half + r) // down * LANES, LANES)
            put(first, (self.pairs[s, h.y, h.x, low] + self.last_x[s, at]).reshape(down * 16, LANES))

        tiles(self.half, down, some)


def backward_kernel(seqs, hidden, length, width, *refs):
    third = width // THIRDS
    d_in, h1_in, x_in, w2_in, w1_in, pre_in, cell_in, h_in, sel_in, dsel_in, db2 = refs[:11]
    gw_out, gx_out, h_out, sel_out, wo_out, db_out = refs[11:17]
    dv, wv, rh, rx, pre, cell, work, edge, grad, gxv, dsel, wo, heard, hv, db1, dbv = refs[17:33]
    own, ring_in, ring_mid, total, part, pairs, wide_x, wide_y, last_x, last_y = refs[33:43]
    zsem, rsem, dsem, hsem, psem, lsem, credit_in, credit_mid, credit_out, ready = refs[43:]
    here = Here()
    ar = SeqSum(here, hidden, third, own, ring_in, ring_mid, total, gw_out, zsem, (credit_in, credit_mid, credit_out))
    sums = {
        layer: RankSum(here, part, pairs, wide_x, wide_y, last_x, last_y, rsem.at[layer - 1]) for layer in (1, 2)
    }
    groups, piece = length // LANES, LANES // 8
    half = width // 2

    def columns_of(s):
        return pl.ds(s * length, length)

    def load(src, dst, k):
        return pltpu.make_async_copy(src, dst, lsem.at[k])

    def load_d(k):
        rows = pl.ds(k * hidden, hidden)
        return load(d_in.at[rows], dv.at[rows], k)

    def load_rhs(layer, t):
        at = pl.ds(t * third, third)
        return load(h1_in.at[at], rh, 6) if layer == 2 else load(x_in.at[:, at], rx, 7)

    load_w = {2: load(w2_in, wv, 8), 1: load(w1_in, wv, 8)}
    load_p, load_c, load_e = load(pre_in, pre, 9), load(cell_in, cell, 10), load(dsel_in, dsel, 11)
    keep = load(sel_in, sel_out.at[:, pl.ds(here.b * hidden, hidden)], 12)
    store_g = load(gxv, gx_out, 13)
    store_h = load(hv, h_out, 14)
    load_rhs(2, 0).start()
    for k in range(6):
        load_d(k).start()
    load_w[2].start()
    load_rhs(1, 0).start()
    for copy in (load_p, load_c, load_e, keep):
        copy.start()
    meet(here.peers + here.line)

    def halves(start, i):
        size = hidden if i is None else hidden // 2
        return pl.ds(start + (i or 0) * size, size)

    gather = Gather(
        here,
        lambda b, i: sel_out.at[:, halves(b * hidden, i)],
        psem,
        lambda i: sel_in.at[:, halves(0, i)],
    )
    biases = [
        remote(dbv.at[here.z], dbv.at[here.z], dsem.at[d, 0], dsem.at[d, 1], peer)
        for d, peer in enumerate(here.line, 1)
    ]
    spread = [pltpu.make_async_copy(h_in.at[here.b], heard.at[here.b], hsem.at[0, 0])]
    for d, peer in enumerate(here.peers, 1):
        spread.append(remote(h_in.at[peer["tm"]], heard.at[here.b], hsem.at[d, 0], hsem.at[d, 1], peer))

    done, spent = [0], [0]

    def units(layer, t, low, high):
        start = t * 4 if layer == 2 else LATER + t * 6
        assert start + high <= OWN or spent[0] > (start + high - OWN) * PIECES - 1 + SLOTS

        def unit(k, carry):
            block = start + k
            rows = pl.ds(pl.multiple_of(ar.product(block) * hidden, 16), hidden)
            got = dot(dv[rows, :], rh[...], NT) if layer == 2 else dot(dv[rows, :], rx[...], NN)
            own[lax.rem(block, OWN)] = got.astype(BF16)
            if start == 0:
                for i in range(PIECES):
                    u = block * PIECES + i

                    @pl.when(u < AHEAD)
                    def _(u=u):
                        ar.offer(u)

            return carry

        lax.fori_loop(low, high, unit, 0)
        done[0] = (start + high) * PIECES

    def tick(count=1):
        first = spent[0]
        spent[0] += count
        assert spent[0] - 1 + AHEAD < done[0] or done[0] == ar.units

        def step(n, carry):
            ar.tick(n)
            return carry

        lax.fori_loop(first, spent[0], step, 0)

    def strips(layer, s, q):
        if layer == 2:
            i, start = q // 2, lax.rem(q, 2) * (length // 2)
            down = hidden // 16
            lhs = pl.ds(pl.multiple_of(i * half, LANES), half)

            def strip(c):
                src = pl.ds(pl.multiple_of(s * length + start + c, 256), 256)
                got = dot(wv[:, lhs], dv[:, src], TN).astype(BF16)
                for n in range(2):
                    at = pl.ds(((start + c) // LANES + n) * down, down)
                    part[i, :, :, at] = got[:, n * LANES : (n + 1) * LANES].reshape(2, 2, down, 16, LANES)

            tiles(length // 2, 256, strip)
        else:

            def strip(c, carry):
                cols = pl.ds(pl.multiple_of(c * 256, 256), 256)
                got = dot(dv[:, columns_of(s)], wv[:, cols], TN).astype(BF16)
                for j in range(groups):
                    for n in range(2):
                        block = got[j * LANES : (j + 1) * LANES, n * LANES : (n + 1) * LANES]
                        part[:, :, :, (c * 2 + n) * groups + j] = block.reshape(2, 2, 2, piece, LANES)
                return carry

            count = width // 256
            lax.fori_loop(count * q // 4, count * (q + 1) // 4, strip, 0)

    def input_grad(layer, s):
        first = spent[0]
        spent[0] += 4
        assert spent[0] - 1 + AHEAD < done[0]

        def quarter(q, carry):
            strips(layer, s, q)
            ar.tick(first + q)
            return carry

        lax.fori_loop(0, 4, quarter, 0)

    def settle(layer, s):
        if layer == 2:

            def put(first, v):
                grad[:, pl.ds(s * length + first, LANES)] = v

            sums[2].done(s, hidden // 16, put)
        else:

            def put(first, v):
                gxv[s, :, pl.ds(first, LANES)] = v

            sums[1].done(s, groups, put)
            gxv[s] = dot(reorder(piece, groups, True), gxv[s], NN).astype(BF16)

    def pool(s):
        first = s * length
        pool_backward(first, grad, pre, cell, first, dv, db1.at[s], work, edge, hidden, groups)

    def load_picked(t):
        at = pl.ds(t * third, third)
        size = rh.shape[1] // 2
        return [load(sel_out.at[tap, at], rh.at[:, pl.ds(tap * size, size)], 15 + tap) for tap in range(2)]

    def store_o(t, tap):
        return load(wo.at[tap], wo_out.at[tap, :, pl.ds(t * third, third)], 17 + tap)

    def outgate(t):
        size = rh.shape[1] // 2
        for tap, copy in enumerate(load_picked(t)):
            copy.wait()
            if t:
                store_o(t - 1, tap).wait()
            wo[tap] = dot(dsel[...], rh[:, pl.ds(tap * size, size)], NT).astype(BF16)
            store_o(t, tap).start()
        if t + 1 < THIRDS:
            for copy in load_picked(t + 1):
                copy.start()

    load_rhs(2, 0).wait()
    load_d(0).wait()
    load_d(1).wait()
    units(2, 0, 0, 2)
    for k in range(2, 6):
        load_d(k).wait()
    units(2, 0, 2, 4)
    load_rhs(2, 1).start()
    load_w[2].wait()
    input_grad(2, 0)
    sums[2].start(0)
    tick()
    load_rhs(2, 1).wait()
    units(2, 1, 0, 2)
    sums[2].cross(0)
    tick(2)
    units(2, 1, 2, 4)
    load_rhs(2, 2).start()
    input_grad(2, 1)
    load_w[1].start()
    sums[2].start(1)
    sums[2].turn(0)
    load_rhs(2, 2).wait()
    tick(2)
    units(2, 2, 0, 2)
    tick()
    sums[2].cross(1)
    units(2, 2, 2, 4)
    tick(2)
    settle(2, 0)
    tick(2)
    load_p.wait()
    load_c.wait()
    pool(0)
    tick()
    sums[2].turn(1)
    gather.start()
    tick(3)
    settle(2, 1)
    for target in (here.core, here.across_x, here.across_y):
        signal(ready, target)
    pool(1)
    tick(2)
    load_rhs(1, 0).wait()
    units(1, 0, 0, 3)
    tick()
    gather.relay()
    units(1, 0, 3, 6)
    load_rhs(1, 1).start()
    dbv[here.z] = jnp.zeros((8, hidden), F32)
    for row, db in enumerate((db1, db2)):
        dbv[here.z, row : row + 1, :] = to_row(sum(db[s] for s in range(1, seqs)) + db[0])
    for copy in biases:
        copy.start()
    tick(2)
    load_w[1].wait()
    pl.semaphore_wait(ready, 3)
    input_grad(1, 0)
    sums[1].start(0)
    load_rhs(1, 1).wait()
    units(1, 1, 0, 2)
    tick()
    units(1, 1, 2, 4)
    tick()
    sums[1].cross(0)
    tick()
    input_grad(1, 1)
    sums[1].start(1)
    units(1, 1, 4, 6)
    load_rhs(1, 2).start()
    tick(2)
    gather.share()
    tick()
    sums[1].cross(1)
    tick()
    sums[1].turn(0)
    tick(2)
    load_rhs(1, 2).wait()
    units(1, 2, 0, 2)
    tick(2)
    units(1, 2, 2, 4)
    tick(3)
    units(1, 2, 4, 6)
    tick(4)
    settle(1, 0)
    sums[1].turn(1)
    keep.wait()
    load_e.wait()
    for copy in load_picked(0):
        copy.start()
    tick(2)
    for copy in spread:
        copy.start()
    tick(4)
    settle(1, 1)
    store_g.start()
    for t in range(THIRDS):
        tick(2)
        outgate(t)
    for copy in spread:
        copy.wait()
    back = reorder(piece, groups, True)
    for s in range(seqs):
        for b in range(8):
            block = heard[b, pl.ds(s * LANES, LANES), :]
            hv[s, :, b * hidden : (b + 1) * hidden] = dot(back, block, NN).astype(BF16)
    store_h.start()

    def more(n, carry):
        ar.tick(n)
        return carry

    lax.fori_loop(spent[0], ar.units + BEHIND + 2, more, 0)
    ar.drain()
    gather.drain()
    for copy in [store_g, store_h] + [store_o(THIRDS - 1, tap) for tap in range(2)] + biases:
        copy.wait()
    db_out[...] = dbv[0] + dbv[1] + dbv[2] + dbv[3]


def run_backward(d, h1, x, w2, w1, pre, cell, h, sel, dsel, db):
    (wide, width), total, seqs = w1.shape, d.shape[1], db.shape[0]
    hidden, length = wide // 6, total // seqs
    third, span, picked = width // THIRDS, length // 8, dsel.shape[1]
    rows, count = hidden // PIECES, length // 16 * hidden // LANES
    assert picked == length and length == 8 * LANES
    vmem = pl.BlockSpec(memory_space=pltpu.VMEM)
    scratch = [
        pltpu.VMEM((wide, total), BF16),
        pltpu.VMEM((wide, width), BF16),
        pltpu.VMEM((third, total), BF16),
        pltpu.VMEM((total, third), BF16),
        pltpu.VMEM((3 * hidden, total), BF16),
        pltpu.VMEM((hidden, total), F32),
        pltpu.VMEM((2, hidden, length), F32),
        pltpu.VMEM((2, hidden, LANES), F32),
        pltpu.VMEM((hidden, total), BF16),
        pltpu.VMEM((seqs, span, width), BF16),
        pltpu.VMEM((hidden, picked), BF16),
        pltpu.VMEM((2, hidden, third), BF16),
        pltpu.VMEM(h.shape, BF16),
        pltpu.VMEM((seqs, span, width), BF16),
        pltpu.VMEM((seqs, hidden, 1), F32),
        pltpu.VMEM((4, 8, hidden), F32),
        pltpu.VMEM((OWN, hidden, third), BF16),
        pltpu.VMEM((SLOTS, rows, third), BF16),
        pltpu.VMEM((SLOTS, rows, third), BF16),
        pltpu.VMEM((SLOTS, rows, third), BF16),
        pltpu.VMEM((2, 2, 2, count, 16, LANES), BF16),
        pltpu.VMEM((seqs, 2, 2, count, 16, LANES), BF16),
        pltpu.VMEM((seqs, 2, count // 2, 16, LANES), BF16),
        pltpu.VMEM((seqs, 2, count // 2, 16, LANES), BF16),
        pltpu.VMEM((seqs, count // 2, 16, LANES), BF16),
        pltpu.VMEM((seqs, count // 2, 16, LANES), BF16),
        pltpu.SemaphoreType.DMA((7, SLOTS)),
        pltpu.SemaphoreType.DMA((2, seqs, 5, 2)),
        pltpu.SemaphoreType.DMA((4, 2)),
        pltpu.SemaphoreType.DMA((8, 2)),
        pltpu.SemaphoreType.DMA((11, 2)),
        pltpu.SemaphoreType.DMA((19,)),
    ]
    return pl.pallas_call(
        functools.partial(backward_kernel, seqs, hidden, length, width),
        name="backward",
        in_specs=[ANY] * 10 + [vmem],
        out_specs=[ANY] * 5 + [vmem],
        out_shape=[
            shape((12, hidden, width), BF16),
            shape((seqs, span, width), BF16),
            shape((seqs, span, width), BF16),
            shape((2, width, picked), BF16),
            shape((2, hidden, width), BF16),
            shape((8, hidden), F32),
        ],
        scratch_shapes=scratch + [pltpu.SemaphoreType.REGULAR] * 4,
        compiler_params=params(collective_id=1, has_side_effects=True),
    )(d, h1, x, w2, w1, pre, cell, h, sel, dsel, db)


def reorder(piece, groups, back):
    span = piece * groups
    a = lax.broadcasted_iota(jnp.int32, (span, span), 1 if back else 0)
    b = lax.broadcasted_iota(jnp.int32, (span, span), 0 if back else 1)
    return (b == lax.rem(a, piece) * groups + a // piece).astype(BF16)


def to_row(column):
    n = column.shape[0]
    same = lax.broadcasted_iota(jnp.int32, (n, n), 0) == lax.broadcasted_iota(jnp.int32, (n, n), 1)
    return jnp.sum(jnp.where(same, column, 0.0), axis=0, keepdims=True)


def to_column(row):
    n = row.shape[1]
    same = lax.broadcasted_iota(jnp.int32, (n, n), 0) == lax.broadcasted_iota(jnp.int32, (n, n), 1)
    return jnp.sum(jnp.where(same, row, 0.0), axis=1, keepdims=True)


class Gather:
    def __init__(self, here, region, sems, own=None):
        h, b = here, here.b
        own = own or (lambda half: region(b, half))
        bx, by = h.across_x["tm"], h.across_y["tm"]
        bd = bx + 4 - 8 * h.y
        plan = (
            (b, 1, h.across_x),
            (b, 0, h.across_y),
            (b, 0, h.across_x),
            (b, 1, h.across_y),
            (b, None, h.core),
            (bx, 1, h.across_y),
            (by, 0, h.across_x),
            (bx, None, h.core),
            (by, None, h.core),
            (bd, 0, h.core),
            (bd, 1, h.core),
        )
        self.copies = []
        for k, (block, half, to) in enumerate(plan):
            src = own(half) if k < 5 else region(block, half)
            self.copies.append(remote(src, region(block, half), sems.at[k, 0], sems.at[k, 1], to))

    def start(self):
        for k in range(5):
            self.copies[k].start()

    def relay(self):
        self.copies[0].wait_recv()
        self.copies[5].start()
        self.copies[1].wait_recv()
        self.copies[6].start()

    def share_near(self):
        self.copies[2].wait_recv()
        self.copies[7].start()
        self.copies[4].wait_recv()
        self.copies[7].wait_recv()

    def share_far(self):
        self.copies[3].wait_recv()
        self.copies[8].start()
        self.copies[6].wait_recv()
        self.copies[9].start()
        self.copies[5].wait_recv()
        self.copies[10].start()
        for k in (8, 9, 10):
            self.copies[k].wait_recv()

    def share(self):
        self.share_near()
        self.share_far()

    def drain(self):
        for copy in self.copies:
            copy.wait_send()


def forward_kernel(seqs, hidden, length, width, *refs):
    x_in, w1_in, w2_in, cot_in, b1_in, b2_in, starts = refs[:7]
    x_out, h1_out, pre_out, cell_out, h2_out, d_out, db_out, sel_out, dsel_out = refs[7:16]
    xg, hg, w, p, pre, cell, work, edge, dv, seed, grad, hv, h2t, raw, cot, sent, b1, b2, chosen, sel, dsel = refs[16:37]
    xsem, hsem, ssem, zsem, lsem = refs[37:]
    here = Here()
    groups = length // LANES
    piece = LANES // 8

    def columns_of(s):
        return pl.ds(s * length, length)

    def x_region(s):
        def region(b, half):
            js = pl.ds(0, groups) if half is None else pl.ds(half * (groups // 2), groups // 2)
            return xg.at[s, js, b]

        return region

    def h_region(s):
        def region(b, half):
            rows = pl.ds(0, hidden) if half is None else pl.ds(half * (hidden // 2), hidden // 2)
            return hg.at[b, rows, columns_of(s)]

        return region

    def load(src, dst, k):
        return pltpu.make_async_copy(src, dst, lsem.at[k])

    load_w1 = load(w1_in, w, 0)
    load_w2 = load(w2_in, w, 0)
    load_x = [load(x_in.at[s], raw.at[s], 1 + s) for s in range(seqs)]
    load_c = load(cot_in, cot, 14)
    store_x = [load(xg.at[s], x_out.at[s], 3 + s) for s in range(seqs)]
    store_h = [load(hg.at[:, :, columns_of(s)], h1_out.at[:, :, columns_of(s)], 5 + s) for s in range(seqs)]
    store_p = [load(pre.at[:, columns_of(s)], pre_out.at[:, columns_of(s)], 7 + s) for s in range(seqs)]
    store_c = [load(cell.at[:, columns_of(s)], cell_out.at[:, columns_of(s)], 9 + s) for s in range(seqs)]
    store_d = [load(dv.at[s], d_out.at[:, columns_of(s)], 11 + s) for s in range(seqs)]
    store_o = load(h2t, h2_out, 13)

    for copy in load_x:
        copy.start()
    load_w1.start()
    load_c.start()
    meet(here.peers + here.line)
    xs = [Gather(here, x_region(s), xsem.at[s]) for s in range(seqs)]
    hs = [Gather(here, h_region(s), hsem.at[s]) for s in range(seqs)]
    order = reorder(piece, groups, False)

    def place(s):
        load_x[s].wait()
        xg[s, :, here.b] = dot(order, raw[s], NN).astype(BF16).reshape(groups, piece, width)
        xs[s].start()

    def prepare():
        load_c.wait()
        for s in range(seqs):
            turned = dot(order, cot[s], NN).astype(BF16)
            for b in range(8):
                block = turned[:, b * hidden : (b + 1) * hidden]
                sent[b, s] = block.reshape(groups, piece, hidden)
        seed[:, :, pl.ds(0, 4)] = jnp.zeros((seqs, groups, 4, piece, hidden), BF16)
        for s in range(seqs):
            prepare_pick(s)
        b1[...] = to_column(b1_in[...][None, :])
        b2[...] = to_column(b2_in[...][None, :])

    late = [
        (remote(sent.at[peer["tm"]], seed.at[:, :, here.b], ssem.at[d, 0], ssem.at[d, 1], peer), peer)
        for d, peer in enumerate(here.peers, 1)
    ]

    def first_products(s):
        def block(r):
            rows = pl.ds(r, hidden)
            p[rows, :] = dot(w[rows, :], xg[s].reshape(length, width), NT)

        tiles(6 * hidden, hidden, block)

    def second_products(s, near):
        y = here.y if near else 1 - here.y
        depth = pl.ds(pl.multiple_of(y * (width // 2), LANES), width // 2)

        def block(r):
            rows = pl.ds(r, hidden)
            rhs = hg[pl.ds(y * 4, 4), :, columns_of(s)].reshape(width // 2, length)
            got = dot(w[rows, depth], rhs, NN)
            p[rows, :] = got if near else p[rows, :] + got

        tiles(6 * hidden, hidden, block)

    def first_pool(s):
        first = s * length
        pool_forward(first, p, b1, pre, cell, first, hg.at[here.b], work.at[0], edge.at[0], hidden, groups)

    def second_pool(s):
        pool_forward(s * length, p, b2, pre, cell, 0, hv, work.at[0], edge.at[0], hidden, groups)
        rows = lax.broadcasted_iota(jnp.int32, (LANES, LANES), 0)
        cols = lax.broadcasted_iota(jnp.int32, (LANES, LANES), 1)
        eye = (rows == cols).astype(BF16)
        for j in range(groups):
            turned = dot(eye, hv[:, pl.ds(j * LANES, LANES)], NT).astype(BF16)
            at = pl.ds((s * groups + j) * piece, piece)
            h2t[:, at, :] = turned.reshape(8, piece, hidden)

    def incoming(s):
        rows = lax.broadcasted_iota(jnp.int32, (hidden, hidden), 0)
        cols = lax.broadcasted_iota(jnp.int32, (hidden, hidden), 1)
        eye = (rows == cols).astype(BF16)
        lane = lax.broadcasted_iota(jnp.int32, (1, LANES), 1)
        for j in range(groups):
            block = seed[s, j].reshape(LANES, hidden)
            turned = dot(eye, block, NT)
            step = lane * groups + j
            keep = jnp.zeros((1, LANES), jnp.bool_)
            for k in range(starts.shape[1]):
                begin = starts[s, k]
                keep = jnp.logical_or(keep, jnp.logical_and(step >= begin, step < begin + CLUSTER))
            keep = jnp.broadcast_to(keep, (hidden, LANES))
            grad[:, pl.ds(s * length + j * LANES, LANES)] = jnp.where(keep, turned, 0.0).astype(BF16)

    def pool_back(s):
        pool_backward(s * length, grad, pre, cell, 0, dv.at[s], db_out.at[s], work, edge, hidden, groups, True)
        store_d[s].start()

    def cluster_steps(s):
        lane = lax.broadcasted_iota(jnp.int32, (1, LANES), 1)
        step = lax.rem(lane, CLUSTER)
        for k in range(starts.shape[1]):
            step = step + jnp.where(lane // CLUSTER == k, starts[s, k], 0)
        return lane, step

    def prepare_pick(s):
        _, step = cluster_steps(s)
        for j in range(groups):
            code = lax.broadcasted_iota(jnp.int32, (LANES, LANES), 0) * groups + j
            at = pl.ds(j * LANES, LANES)
            chosen[s, at, pl.ds(0, LANES)] = (code == step).astype(BF16)
            chosen[s, at, pl.ds(LANES, LANES)] = (code == step - 1).astype(BF16)

    def held(s, count):
        start = here.z * (seqs * LANES) + s * LANES
        return pl.ds(pl.multiple_of(start, LANES), count * LANES)

    def pick_hidden(s):
        got = dot(hg[here.b, :, columns_of(s)], chosen[s], NN).astype(BF16)
        for tap in range(2):
            sel[tap, :, held(s, 1)] = got[:, tap * LANES : (tap + 1) * LANES]

    def pick_grad(s):
        lane, step = cluster_steps(s)
        again = jnp.zeros((1, LANES), jnp.bool_)
        for k in range(starts.shape[1] - 1):
            begin = starts[s, k]
            inside = jnp.logical_and(step >= begin, step < begin + CLUSTER)
            again = jnp.logical_or(again, jnp.logical_and(inside, lane // CLUSTER > k))
        got = dot(dv[s, pl.ds(2 * hidden, hidden), :], chosen[s, :, pl.ds(0, LANES)], NN)
        dsel[:, held(s, 1)] = jnp.where(jnp.broadcast_to(again, (hidden, LANES)), 0.0, got).astype(BF16)

    spread_h = []
    spread_d = []
    for d, peer in enumerate(here.line, 1):
        at = sel.at[:, :, held(0, seqs)]
        spread_h.append(remote(at, at, zsem.at[d, 0], zsem.at[d, 1], peer))
        at = dsel.at[:, held(0, seqs)]
        spread_d.append(remote(at, at, zsem.at[d, 2], zsem.at[d, 3], peer))
    store_s = load(sel, sel_out, 15)
    store_e = load(dsel, dsel_out, 16)

    place(0)
    prepare()
    xs[0].relay()
    place(1)
    xs[0].share()
    store_x[0].start()
    load_w1.wait()
    first_products(0)
    xs[1].relay()
    first_pool(0)
    hs[0].start()
    store_p[0].start()
    store_c[0].start()
    xs[1].share()
    store_x[1].start()
    first_products(1)
    load_w2.start()
    hs[0].relay()
    first_pool(1)
    hs[1].start()
    store_p[1].start()
    store_c[1].start()

    for s in range(seqs):
        pick_hidden(s)
    for copy in spread_h:
        copy.start()
    hs[0].share_near()
    load_w2.wait()
    second_products(0, True)
    hs[0].share_far()
    store_h[0].start()
    second_products(0, False)
    hs[1].relay()

    @pl.when(here.y == 1)
    def _():
        pltpu.make_async_copy(sent.at[here.b], seed.at[:, :, here.b], ssem.at[0, 0]).start()
        for copy, _ in late:
            copy.start()

    store_p[0].wait()
    store_c[0].wait()
    second_pool(0)
    hs[1].share_near()
    second_products(1, True)
    hs[1].share_far()
    store_h[1].start()
    second_products(1, False)
    store_p[1].wait()
    store_c[1].wait()
    second_pool(1)
    store_o.start()

    @pl.when(here.y == 1)
    def _():
        pltpu.make_async_copy(sent.at[here.b], seed.at[:, :, here.b], ssem.at[0, 0]).wait()
        for copy, _ in late:
            copy.wait_send()

    for d, (copy, _) in enumerate(late, 1):
        source = lax.rem(here.b + 8 - d, 8)

        @pl.when(source >= 4)
        def _(copy=copy):
            copy.wait_recv()

    for s in range(seqs):
        incoming(s)
        outgate_backward(s * length, grad, pre, cell, dv.at[s], hidden, groups)
        pick_grad(s)
    for copy in spread_d:
        copy.start()
    for copy in spread_h:
        copy.wait()
    store_s.start()
    for s in range(seqs):
        pool_back(s)
    for gather in xs + hs:
        gather.drain()
    for copy in spread_d:
        copy.wait()
    store_e.start()
    for copy in store_x + store_h + store_d + [store_o, store_s, store_e]:
        copy.wait()


def run_forward(x, w1, b1, w2, b2, cotangent, starts):
    seqs, span, width = x.shape
    hidden, length, piece = w1.shape[0] // 6, span * 8, LANES // 8
    groups = length // LANES
    total, picked = seqs * length, 4 * seqs * LANES
    assert starts.shape[1] * CLUSTER == LANES
    vmem = pl.BlockSpec(memory_space=pltpu.VMEM)
    return pl.pallas_call(
        functools.partial(forward_kernel, seqs, hidden, length, width),
        name="forward",
        in_specs=[ANY, ANY, ANY, ANY, vmem, vmem, pl.BlockSpec(memory_space=pltpu.SMEM)],
        out_specs=[ANY, ANY, ANY, ANY, ANY, ANY, vmem, ANY, ANY],
        out_shape=[
            shape((seqs, groups, 8, piece, width), BF16),
            shape((8, hidden, total), BF16),
            shape((3 * hidden, total), BF16),
            shape((hidden, total), F32),
            shape((8, seqs * groups * piece, hidden), BF16),
            shape((6 * hidden, total), BF16),
            shape((seqs, hidden, 1), F32),
            shape((2, hidden, picked), BF16),
            shape((hidden, picked), BF16),
        ],
        scratch_shapes=[
            pltpu.VMEM((seqs, groups, 8, piece, width), BF16),
            pltpu.VMEM((8, hidden, total), BF16),
            pltpu.VMEM((6 * hidden, width), BF16),
            pltpu.VMEM((6 * hidden, length), F32),
            pltpu.VMEM((3 * hidden, total), BF16),
            pltpu.VMEM((hidden, total), F32),
            pltpu.VMEM((2, hidden, length), F32),
            pltpu.VMEM((2, hidden, LANES), F32),
            pltpu.VMEM((seqs, 6 * hidden, length), BF16),
            pltpu.VMEM((seqs, groups, 8, piece, hidden), BF16),
            pltpu.VMEM((hidden, total), BF16),
            pltpu.VMEM((hidden, length), BF16),
            pltpu.VMEM((8, seqs * groups * piece, hidden), BF16),
            pltpu.VMEM((seqs, span, width), BF16),
            pltpu.VMEM((seqs, span, width), BF16),
            pltpu.VMEM((8, seqs, groups, piece, hidden), BF16),
            pltpu.VMEM((hidden, 1), F32),
            pltpu.VMEM((hidden, 1), F32),
            pltpu.VMEM((seqs, length, 2 * LANES), BF16),
            pltpu.VMEM((2, hidden, picked), BF16),
            pltpu.VMEM((hidden, picked), BF16),
            pltpu.SemaphoreType.DMA((seqs, 11, 2)),
            pltpu.SemaphoreType.DMA((seqs, 11, 2)),
            pltpu.SemaphoreType.DMA((8, 2)),
            pltpu.SemaphoreType.DMA((4, 4)),
            pltpu.SemaphoreType.DMA((17,)),
        ],
        compiler_params=params(collective_id=0, has_side_effects=True),
    )(x, w1, w2, cotangent, b1, b2, starts)


def finish_kernel(
    one_ref, two_ref, outgate_ref, h_ref, gx_ref, db_ref, wide_one_ref, wide_two_ref, h_out, gx_out, db1_out, db2_out
):
    i = pl.program_id(0)
    wide_one_ref[...] = one_ref[...].astype(F32)
    last = lax.rem(i, 3) == 2

    @pl.when(last)
    def _():
        wide_two_ref[...] = outgate_ref[...].astype(F32)

    @pl.when(jnp.logical_not(last))
    def _():
        wide_two_ref[...] = two_ref[...].astype(F32)

    h_out[...] = h_ref[...]
    gx_out[...] = gx_ref[...]
    db1_out[...] = db_ref[0]
    db2_out[...] = db_ref[1]


def finish(gw, outgate, h, gx, db):
    _, hidden, width = gw.shape
    total = h.shape[0] * h.shape[1]
    dims = (1, hidden, width)
    small = (total // 4, width)
    weights = pl.BlockSpec(dims, lambda i: (i, 0, 0))
    tokens = pl.BlockSpec(small, lambda i: (jnp.minimum(i, 3), 0))
    bias = pl.BlockSpec((hidden,), lambda i: (0,))
    return pl.pallas_call(
        finish_kernel,
        name="results",
        grid=(6,),
        in_specs=[
            weights,
            pl.BlockSpec(dims, lambda i: (6 + i - i % 3 // 2, 0, 0)),
            pl.BlockSpec(dims, lambda i: (i // 3, 0, 0)),
            tokens,
            tokens,
            pl.BlockSpec(db.shape, lambda i: (0, 0)),
        ],
        out_specs=[weights, weights, tokens, tokens, bias, bias],
        out_shape=[shape((6, hidden, width), F32)] * 2 + [shape((total, width), BF16)] * 2 + [shape((hidden,), F32)] * 2,
        compiler_params=params(),
    )(gw, gw, outgate, h.reshape(total, width), gx.reshape(total, width), db)


def per_device(line, inputs, weight_one, fbias_one, weight_two, fbias_two, cotangent, cluster_starts):
    seqs, span, width = inputs.shape
    count = lax.axis_size("tm")
    length = span * count
    groups = length // LANES
    piece = LANES // count
    hidden = weight_one.shape[2]
    total = seqs * length
    w1 = weight_one.reshape(6 * hidden, width)
    w2 = weight_two.reshape(6 * hidden, width)

    if line:
        x, h1, pre1, cell1, h2, d2, db2, *picked = run_forward(
            inputs, w1, fbias_one, w2, fbias_two, cotangent, cluster_starts
        )
        x, h1 = x.reshape(total, width), h1.reshape(width, total)
        gw, gx1, h2, _, wo, db = run_backward(d2, h1, x, w2, w1, pre1, cell1, h2, *picked, db2)
        gw1, gw2, h2, gx1, *db = finish(gw, wo, h2, gx1, db)
    else:
        x = inputs.reshape(seqs, piece, groups, width).transpose(0, 2, 1, 3)
        bias1, bias2 = fbias_one[:, None], fbias_two[:, None]
        seed = cotangent.reshape(seqs, piece, groups, count, hidden)
        steps = lax.axis_index("tm") * span + jnp.arange(span, dtype=jnp.int32)
        starts = cluster_starts[:, :, None]
        keep = jnp.any((steps >= starts) & (steps < starts + CLUSTER), axis=1)
        seed = jnp.where(keep.reshape(seqs, piece, groups, 1, 1), seed, jnp.zeros_like(seed))
        seed = lax.all_to_all(seed, "tm", split_axis=3, concat_axis=1, tiled=True)
        seed = seed.reshape(seqs, LANES, groups, hidden).transpose(3, 0, 2, 1).reshape(hidden, total)
        x = lax.all_gather(x, "tm", axis=2, tiled=True).reshape(total, width)
        pre1, cell1, h1 = run_first(seqs, w1, bias1, x)
        h1 = lax.all_gather(h1, "tm", axis=0, tiled=True)
        h2, d2, db2 = run_second(seqs, w2, bias2, h1, seed)
        h2 = h2.reshape(hidden, seqs, groups, count, piece)
        h2 = lax.all_to_all(h2, "tm", split_axis=3, concat_axis=0, tiled=True)
        h2 = h2.reshape(width, seqs, groups, piece).transpose(1, 3, 2, 0)
        gw2 = lax.psum(dot(d2, h1, NT).astype(BF16), "seq").astype(F32)
        gx2 = lax.psum_scatter(dot(w2, d2, TN).astype(BF16), "tm", scatter_dimension=0, tiled=True)
        d1, db1 = run_back(seqs, gx2, pre1, cell1)
        gw1 = lax.psum(dot(d1, x, NN).astype(BF16), "seq").astype(F32)
        gx1 = dot(d1, w1, TN).astype(BF16).reshape(seqs, groups, LANES, width)
        gx1 = lax.psum_scatter(gx1, "tm", scatter_dimension=2, tiled=True)
        gx1 = gx1.transpose(0, 2, 1, 3).reshape(seqs, span, width)
        db = lax.psum(jnp.stack([db1, db2]).sum(axis=(1, 3)), "seq")
    out, gx1 = h2.reshape(seqs, span, width), gx1.reshape(seqs, span, width)
    dims = weight_one.shape
    return (out, gx1, gw1.reshape(dims), db[0], gw2.reshape(dims), db[1])


def solution(mesh):
    placed = (
        P("seq", "tm", None),
        P(None, None, "tm", None),
        P("tm"),
        P(None, None, "tm", None),
        P("tm"),
        P("seq", "tm", None),
        P("seq", None),
    )
    return jax.shard_map(
        functools.partial(per_device, dict(mesh.shape) == {"seq": 4, "tm": 8}),
        mesh=mesh,
        in_specs=placed,
        out_specs=(
            P("seq", "tm", None),
            P("seq", "tm", None),
            P(None, None, "tm", None),
            P("tm"),
            P(None, None, "tm", None),
            P("tm"),
        ),
        check_vma=False,
    )
```

```python
import functools

import jax
import jax.numpy as jnp
from jax import lax
from jax.experimental import pallas as pl
from jax.experimental.pallas import tpu as pltpu
from jax.sharding import PartitionSpec as P

CLUSTER = 32
LANES = 128
ROWS = 48
F32 = jnp.float32
BF16 = jnp.bfloat16
ANY = pl.BlockSpec(memory_space=pl.ANY)
MESH = pl.DeviceIdType.MESH
NN = (((1,), (0,)), ((), ()))
NT = (((1,), (1,)), ((), ()))
TN = (((0,), (0,)), ((), ()))


def dot(a, b, dims):
    return lax.dot_general(a, b, dims, preferred_element_type=F32)


def sigmoid(v):
    return 1.0 / (1.0 + jnp.exp(-v))


def tiles(count, rows, body):
    def step(r, carry):
        body(pl.multiple_of(r * rows, rows))
        return carry

    lax.fori_loop(0, count // rows, step, 0)


def shift_lanes(v, amount, lane, fill):
    moved = pltpu.roll(v, amount % LANES, axis=1)
    gone = lane < amount if amount > 0 else lane >= LANES + amount
    return jnp.where(gone, fill, moved)


def lane_chain(factor, value, lane, sign):
    step = 1
    while step < LANES:
        value = value + factor * shift_lanes(value, sign * step, lane, 0.0)
        factor = factor * shift_lanes(factor, sign * step, lane, 1.0)
        step *= 2
    return value


def pool_forward(first, p_ref, b_ref, pre_ref, cell_ref, target, h_ref, factor_ref, edge_ref, hidden, groups):
    lane = lax.broadcasted_iota(jnp.int32, (ROWS, LANES), 1)

    def at(j, start=0):
        return pl.ds(start + j * LANES, LANES)

    def gates(r):
        rows = pl.ds(r, ROWS)
        value = factor = None
        for j in range(groups):
            got = []
            for g in range(3):
                now = p_ref[pl.ds(g * hidden + r, ROWS), at(j)]
                tap = pl.ds((3 + g) * hidden + r, ROWS)
                if j:
                    past = p_ref[tap, at(j - 1)]
                else:
                    past = shift_lanes(p_ref[tap, at(groups - 1)], 1, lane, 0.0)
                total = now + past
                if g == 1:
                    total = total + b_ref[rows, :]
                total = total.astype(BF16)
                pre_ref[pl.ds(g * hidden + r, ROWS), at(j, first)] = total
                got.append(total.astype(F32))
            forget = sigmoid(got[1])
            fresh = (1.0 - forget) * jnp.tanh(got[0])
            if j:
                value = forget * value + fresh
                factor = forget * factor
            else:
                value, factor = fresh, forget
            cell_ref[rows, at(j, first)] = value
            factor_ref[rows, at(j)] = factor

    tiles(hidden, ROWS, gates)

    def chain(r):
        rows = pl.ds(r, ROWS)
        value = lane_chain(factor_ref[rows, at(groups - 1)], cell_ref[rows, at(groups - 1, first)], lane, 1)
        edge_ref[rows, :] = shift_lanes(value, 1, lane, 0.0)

    tiles(hidden, ROWS, chain)

    def finish(r):
        rows = pl.ds(r, ROWS)
        edge = edge_ref[rows, :]
        for j in range(groups):
            cell = cell_ref[rows, at(j, first)] + factor_ref[rows, at(j)] * edge
            cell_ref[rows, at(j, first)] = cell
            outgate = sigmoid(pre_ref[pl.ds(2 * hidden + r, ROWS), at(j, first)].astype(F32))
            h_ref[rows, at(j, target)] = (outgate * cell).astype(BF16)

    tiles(hidden, ROWS, finish)


def put_gate(d_ref, g, r, j, v, target, lane, hidden, groups):
    d_ref[pl.ds(g * hidden + r, ROWS), pl.ds(target + j * LANES, LANES)] = v
    tap = pl.ds((3 + g) * hidden + r, ROWS)
    if j:
        d_ref[tap, pl.ds(target + (j - 1) * LANES, LANES)] = v
    else:
        moved = shift_lanes(v.astype(F32), -1, lane, 0.0).astype(BF16)
        d_ref[tap, pl.ds(target + (groups - 1) * LANES, LANES)] = moved


def outgate_backward(first, g_ref, pre_ref, cell_ref, d_ref, hidden, groups):
    lane = lax.broadcasted_iota(jnp.int32, (ROWS, LANES), 1)

    def body(r):
        rows = pl.ds(r, ROWS)
        for j in range(groups):
            at = pl.ds(first + j * LANES, LANES)
            outgate = sigmoid(pre_ref[pl.ds(2 * hidden + r, ROWS), at].astype(F32))
            v = g_ref[rows, at].astype(F32) * cell_ref[rows, at] * outgate * (1.0 - outgate)
            put_gate(d_ref, 2, r, j, v.astype(BF16), 0, lane, hidden, groups)

    tiles(hidden, ROWS, body)


def pool_backward(
    first, g_ref, pre_ref, cell_ref, target, d_ref, db_ref, work_ref, edge_ref, hidden, groups, carried_only=False
):
    lane = lax.broadcasted_iota(jnp.int32, (ROWS, LANES), 1)

    def at(j, start=0):
        return pl.ds(start + j * LANES, LANES)

    def gate(g, r, j):
        return pre_ref[pl.ds(g * hidden + r, ROWS), at(j, first)].astype(F32)

    def start(r):
        rows = pl.ds(r, ROWS)
        later = value = factor = None
        for j in reversed(range(groups)):
            own = g_ref[rows, at(j, first)].astype(F32) * sigmoid(gate(2, r, j))
            if later is None:
                value, factor = own, jnp.ones_like(own)
            else:
                value = own + later * value
                factor = later * factor
            work_ref[0, rows, at(j)] = value
            work_ref[1, rows, at(j)] = factor
            later = sigmoid(gate(1, r, j))
        edge_ref[0, rows, :] = later * value
        edge_ref[1, rows, :] = later * factor

    tiles(hidden, ROWS, start)

    def chain(r):
        rows = pl.ds(r, ROWS)
        value = lane_chain(edge_ref[1, rows, :], edge_ref[0, rows, :], lane, -1)
        edge_ref[0, rows, :] = shift_lanes(value, -1, lane, 0.0)

    tiles(hidden, ROWS, chain)

    def finish(r):
        rows = pl.ds(r, ROWS)
        edge = edge_ref[0, rows, :]
        total = jnp.zeros((ROWS, LANES), F32)
        before = shift_lanes(cell_ref[rows, at(groups - 1, first)], 1, lane, 0.0)
        for j in range(groups):
            carried = work_ref[0, rows, at(j)] + work_ref[1, rows, at(j)] * edge
            candidate = jnp.tanh(gate(0, r, j))
            forget = sigmoid(gate(1, r, j))
            cell = cell_ref[rows, at(j, first)]
            keep = carried * (1.0 - forget)
            got = [keep * (1.0 - candidate * candidate), keep * forget * (before - candidate)]
            if not carried_only:
                outgate = sigmoid(gate(2, r, j))
                got.append(g_ref[rows, at(j, first)].astype(F32) * cell * outgate * (1.0 - outgate))
            before = cell
            for g, v in enumerate(got):
                v = v.astype(BF16)
                if g == 1:
                    total = total + v.astype(F32)
                put_gate(d_ref, g, r, j, v, target, lane, hidden, groups)
        db_ref[rows, :] = jnp.sum(total, axis=1, keepdims=True)

    tiles(hidden, ROWS, finish)


def first_kernel(hidden, length, w_ref, b_ref, x_ref, pre_ref, cell_ref, h_ref, p_ref, work_ref, edge_ref):
    def strip(c):
        cols = pl.ds(c, 512)
        p_ref[:, cols] = dot(w_ref[...], x_ref[cols, :], NT)

    tiles(length, 512, strip)
    pool_forward(0, p_ref, b_ref, pre_ref, cell_ref, 0, h_ref, work_ref, edge_ref, hidden, length // LANES)


def second_kernel(
    hidden, length, w_ref, b_ref, x_ref, g_ref, h_ref, d_ref, db_ref, p_ref, pre_ref, cell_ref, work_ref, edge_ref
):
    def strip(c):
        cols = pl.ds(c, 512)
        p_ref[:, cols] = dot(w_ref[...], x_ref[:, cols], NN)

    tiles(length, 512, strip)
    groups = length // LANES
    pool_forward(0, p_ref, b_ref, pre_ref, cell_ref, 0, h_ref, work_ref.at[0], edge_ref.at[0], hidden, groups)
    pool_backward(0, g_ref, pre_ref, cell_ref, 0, d_ref, db_ref.at[0], work_ref, edge_ref, hidden, groups)


def back_kernel(hidden, length, g_ref, pre_ref, cell_ref, d_ref, db_ref, work_ref, edge_ref):
    pool_backward(0, g_ref, pre_ref, cell_ref, 0, d_ref, db_ref.at[0], work_ref, edge_ref, hidden, length // LANES)


def columns(rows, length):
    return pl.BlockSpec((rows, length), lambda s: (0, s))


def fixed(*dims):
    return pl.BlockSpec(dims, lambda s: (0,) * len(dims), pipeline_mode=pl.Buffered(1))


def params(**more):
    return pltpu.CompilerParams(vmem_limit_bytes=63 * 1024 * 1024, **more)


shape = jax.ShapeDtypeStruct


def run_first(seqs, weight, bias, gathered):
    (wide, width), total = weight.shape, gathered.shape[0]
    hidden, length = wide // 6, total // seqs
    return pl.pallas_call(
        functools.partial(first_kernel, hidden, length),
        name="layer_one_forward",
        grid=(seqs,),
        in_specs=[fixed(wide, width), fixed(hidden, 1), pl.BlockSpec((length, width), lambda s: (s, 0))],
        out_specs=[columns(3 * hidden, length), columns(hidden, length), columns(hidden, length)],
        out_shape=[shape((3 * hidden, total), BF16), shape((hidden, total), F32), shape((hidden, total), BF16)],
        scratch_shapes=[
            pltpu.VMEM((wide, length), F32),
            pltpu.VMEM((hidden, length), F32),
            pltpu.VMEM((hidden, LANES), F32),
        ],
        compiler_params=params(),
    )(weight, bias, gathered)


def run_second(seqs, weight, bias, gathered, grad):
    (wide, width), total = weight.shape, gathered.shape[1]
    hidden, length = wide // 6, total // seqs
    return pl.pallas_call(
        functools.partial(second_kernel, hidden, length),
        name="layer_two_forward_and_pool_backward",
        grid=(seqs,),
        in_specs=[fixed(wide, width), fixed(hidden, 1), columns(width, length), columns(hidden, length)],
        out_specs=[columns(hidden, length), columns(wide, length), pl.BlockSpec((1, hidden, 1), lambda s: (s, 0, 0))],
        out_shape=[shape((hidden, total), BF16), shape((wide, total), BF16), shape((seqs, hidden, 1), F32)],
        scratch_shapes=[
            pltpu.VMEM((wide, length), F32),
            pltpu.VMEM((3 * hidden, length), BF16),
            pltpu.VMEM((hidden, length), F32),
            pltpu.VMEM((2, hidden, length), F32),
            pltpu.VMEM((2, hidden, LANES), F32),
        ],
        compiler_params=params(),
    )(weight, bias, gathered, grad)


def run_back(seqs, grad, pre, cell):
    hidden, total = grad.shape
    length = total // seqs
    return pl.pallas_call(
        functools.partial(back_kernel, hidden, length),
        name="layer_one_pool_backward",
        grid=(seqs,),
        in_specs=[columns(hidden, length), columns(3 * hidden, length), columns(hidden, length)],
        out_specs=[columns(6 * hidden, length), pl.BlockSpec((1, hidden, 1), lambda s: (s, 0, 0))],
        out_shape=[shape((6 * hidden, total), BF16), shape((seqs, hidden, 1), F32)],
        scratch_shapes=[pltpu.VMEM((2, hidden, length), F32), pltpu.VMEM((2, hidden, LANES), F32)],
        compiler_params=params(),
    )(grad, pre, cell)


THIRDS = 3
PIECES = 3
SLOTS = 12
AHEAD = 6
BEHIND = 2
LATER = 12
BLOCKS = 30
OWN = 18


class Here:
    def __init__(self):
        self.z = lax.axis_index("seq")
        self.b = lax.axis_index("tm")
        self.c = lax.rem(self.b, 2)
        self.x = lax.rem(self.b // 2, 2)
        self.y = self.b // 4
        self.core = dict(seq=self.z, tm=self.b + 1 - 2 * self.c)
        self.across_x = dict(seq=self.z, tm=self.b + 2 - 4 * self.x)
        self.across_y = dict(seq=self.z, tm=self.b + 4 - 8 * self.y)
        self.pair = dict(seq=self.z + 1 - 2 * lax.rem(self.z, 2), tm=self.b)
        self.middle = dict(seq=3 - self.z, tm=self.b)
        self.line = [dict(seq=lax.rem(self.z + d, 4), tm=self.b) for d in range(1, 4)]
        self.peers = [dict(seq=self.z, tm=lax.rem(self.b + d, 8)) for d in range(1, 8)]
        self.is_end = jnp.logical_or(self.z == 0, self.z == 3)
        self.is_centre = jnp.logical_and(self.z > 0, self.z < 3)


def remote(src, dst, send, recv, target):
    return pltpu.make_async_remote_copy(
        src_ref=src, dst_ref=dst, send_sem=send, recv_sem=recv, device_id=target, device_id_type=MESH
    )


def both(a, b):
    if isinstance(a, bool) and isinstance(b, bool):
        return a and b
    return jnp.logical_and(a, b)


def signal(sem, target):
    pl.semaphore_signal(sem, inc=1, device_id=target, device_id_type=MESH)


def meet(targets, between=None):
    barrier = pltpu.get_barrier_semaphore()
    for target in targets:
        signal(barrier, target)
    if between is not None:
        between()
    pl.semaphore_wait(barrier, len(targets))


def pick(condition, a, b):
    if isinstance(condition, bool):
        return a if condition else b
    return jnp.where(condition, a, b)


class SeqSum:
    def __init__(self, here, hidden, third, own, ring_in, ring_mid, total, out, sems, credits):
        self.here, self.third, self.rows = here, third, hidden // PIECES
        self.units = BLOCKS * PIECES
        self.own, self.ring_in, self.ring_mid, self.total, self.out = own, ring_in, ring_mid, total, out
        self.sems = sems
        self.credit_in, self.credit_mid, self.credit_out = credits

    def rows_of(self, u):
        return pl.ds(pl.multiple_of(lax.rem(u, PIECES) * self.rows, 16), self.rows)

    def mine(self, u):
        return self.own.at[lax.rem(u // PIECES, OWN), self.rows_of(u)]

    def inward(self, u):
        i = lax.rem(u, SLOTS)
        return remote(self.mine(u), self.ring_in.at[i], self.sems.at[0, i], self.sems.at[1, i], self.here.pair)

    def across(self, u):
        i = lax.rem(u, SLOTS)
        return remote(self.mine(u), self.ring_mid.at[i], self.sems.at[2, i], self.sems.at[3, i], self.here.middle)

    def outward(self, u):
        i = lax.rem(u, SLOTS)
        return remote(self.total.at[i], self.ring_in.at[i], self.sems.at[4, i], self.sems.at[5, i], self.here.pair)

    def store(self, u, ring):
        i, block = lax.rem(u, SLOTS), u // PIECES
        second = block < LATER
        t = pick(second, block // 4, (block - LATER) // 6)
        cols = pl.ds(pl.multiple_of(t * self.third, LANES), self.third)
        to = self.out.at[self.product(block) + pick(second, 6, 0), self.rows_of(u), cols]
        return pltpu.make_async_copy(ring.at[i], to, self.sems.at[6, i])

    @staticmethod
    def product(block):
        k = lax.rem(block, 4)
        return pick(block < LATER, (k // 2) * 3 + lax.rem(k, 2), lax.rem(block, 6))

    def add(self, dst, a, b):
        def rows(r):
            at = pl.ds(r, ROWS)
            dst[at, :] = a[at, :] + b[at, :]

        tiles(self.rows, ROWS, rows)

    def offer(self, u):
        @pl.when(self.here.is_end)
        def _():
            @pl.when(u >= SLOTS)
            def _():
                pl.semaphore_wait(self.credit_in, 1)
                self.inward(u - SLOTS).wait_send()

            self.inward(u).start()

    def gather(self, u):
        i = lax.rem(u, SLOTS)
        self.inward(u).wait_recv()
        self.add(self.mine(u), self.mine(u), self.ring_in.at[i])

        @pl.when(u + SLOTS < self.units)
        def _():
            signal(self.credit_in, self.here.pair)

        @pl.when(u >= SLOTS)
        def _():
            pl.semaphore_wait(self.credit_mid, 1)
            self.across(u - SLOTS).wait_send()

        self.across(u).start()

    def finish(self, u):
        i = lax.rem(u, SLOTS)
        self.across(u).wait_recv()

        @pl.when(u >= SLOTS)
        def _():
            pl.semaphore_wait(self.credit_out, 1)
            self.outward(u - SLOTS).wait_send()
            self.store(u - SLOTS, self.total).wait()

        self.add(self.total.at[i], self.mine(u), self.ring_mid.at[i])

        @pl.when(u + SLOTS < self.units)
        def _():
            signal(self.credit_mid, self.here.middle)

        self.outward(u).start()
        self.store(u, self.total).start()

    def accept(self, u):
        self.outward(u).wait_recv()
        self.store(u, self.ring_in).start()

        @pl.when(u > 0)
        def _():
            self.store(u - 1, self.ring_in).wait()

            @pl.when(u - 1 + SLOTS < self.units)
            def _():
                signal(self.credit_out, self.here.pair)

    def tick(self, n):
        @pl.when(self.here.is_centre)
        def _():
            @pl.when(n < self.units)
            def _():
                self.gather(n)

            @pl.when(both(n >= BEHIND, n < self.units + BEHIND))
            def _():
                self.finish(n - BEHIND)

        @pl.when(n + AHEAD < self.units)
        def _():
            self.offer(n + AHEAD)

        @pl.when(n >= BEHIND + 2)
        def _():
            @pl.when(self.here.is_end)
            def _():
                self.accept(n - BEHIND - 2)

    def drain(self):
        @pl.when(self.here.is_centre)
        def _():
            for u in range(self.units - SLOTS, self.units):
                self.across(u).wait_send()
                self.outward(u).wait_send()
                self.store(u, self.total).wait()

        @pl.when(self.here.is_end)
        def _():
            for u in range(self.units - SLOTS, self.units):
                self.inward(u).wait_send()
            self.store(self.units - 1, self.ring_in).wait()


class RankSum:
    def __init__(self, here, part, pairs, wide_x, wide_y, last_x, last_y, sems):
        self.here, self.part, self.pairs = here, part, pairs
        self.wide_x, self.wide_y, self.last_x, self.last_y, self.sems = wide_x, wide_y, last_x, last_y, sems
        self.count = part.shape[3]
        self.half = self.count // 2
        self.upper, self.lower = pl.ds(0, self.half), pl.ds(self.half, self.half)

    def copy(self, k, s, src, dst, target):
        return remote(src, dst, self.sems.at[s, k, 0], self.sems.at[s, k, 1], target)

    def swap(self, s):
        return self.copy(0, s, self.part.at[:, :, 1 - self.here.c], self.pairs.at[s], self.here.core)

    def wide(self, s):
        h = self.here
        return (
            self.copy(1, s, self.pairs.at[s, :, 1 - h.x, self.upper], self.wide_x.at[s], h.across_x),
            self.copy(2, s, self.pairs.at[s, 1 - h.y, :, self.lower], self.wide_y.at[s], h.across_y),
        )

    def last(self, s):
        h = self.here
        return (
            self.copy(3, s, self.pairs.at[s, 1 - h.y, h.x, self.upper], self.last_y.at[s], h.across_y),
            self.copy(4, s, self.pairs.at[s, h.y, 1 - h.x, self.lower], self.last_x.at[s], h.across_x),
        )

    def start(self, s):
        self.swap(s).start()

    def cross(self, s):
        h = self.here
        self.swap(s).wait()

        def some(r):
            at = pl.ds(r, 8)
            for y in range(2):
                for x in range(2):
                    self.pairs[s, y, x, at] = self.pairs[s, y, x, at] + self.part[y, x, h.c, at]

        tiles(self.count, 8, some)
        for copy in self.wide(s):
            copy.start()

    def turn(self, s):
        h = self.here
        for copy in self.wide(s):
            copy.wait()

        def some(r):
            at, low = pl.ds(r, 8), pl.ds(self.half + r, 8)
            for k in range(2):
                self.pairs[s, k, h.x, at] = self.pairs[s, k, h.x, at] + self.wide_x[s, k, at]
                self.pairs[s, h.y, k, low] = self.pairs[s, h.y, k, low] + self.wide_y[s, k, at]

        tiles(self.half, 8, some)
        for copy in self.last(s):
            copy.start()

    def done(self, s, down, put):
        h = self.here
        for copy in self.last(s):
            copy.wait()

        def some(r):
            at, low = pl.ds(r, down), pl.ds(self.half + r, down)
            first = pl.multiple_of(r // down * LANES, LANES)
            put(first, (self.pairs[s, h.y, h.x, at] + self.last_y[s, at]).reshape(down * 16, LANES))
            first = pl.multiple_of((self.half + r) // down * LANES, LANES)
            put(first, (self.pairs[s, h.y, h.x, low] + self.last_x[s, at]).reshape(down * 16, LANES))

        tiles(self.half, down, some)


def backward_kernel(seqs, hidden, length, width, *refs):
    third = width // THIRDS
    d_in, h1_in, x_in, w2_in, w1_in, pre_in, cell_in, h_in, sel_in, dsel_in, db2 = refs[:11]
    gw_out, gx_out, h_out, sel_out, wo_out, db_out = refs[11:17]
    dv, wv, rh, rx, pre, cell, work, edge, grad, gxv, dsel, wo, heard, hv, db1, dbv = refs[17:33]
    own, ring_in, ring_mid, total, part, pairs, wide_x, wide_y, last_x, last_y = refs[33:43]
    zsem, rsem, dsem, hsem, psem, lsem, credit_in, credit_mid, credit_out, ready = refs[43:]
    here = Here()
    ar = SeqSum(here, hidden, third, own, ring_in, ring_mid, total, gw_out, zsem, (credit_in, credit_mid, credit_out))
    sums = {
        layer: RankSum(here, part, pairs, wide_x, wide_y, last_x, last_y, rsem.at[layer - 1]) for layer in (1, 2)
    }
    groups, piece = length // LANES, LANES // 8
    half = width // 2

    def columns_of(s):
        return pl.ds(s * length, length)

    def load(src, dst, k):
        return pltpu.make_async_copy(src, dst, lsem.at[k])

    def load_d(k):
        rows = pl.ds(k * hidden, hidden)
        if not isinstance(k, int):
            rows = pl.ds(pl.multiple_of(k * hidden, 16), hidden)
        return load(d_in.at[rows], dv.at[rows], k)

    def load_rhs(layer, t):
        at = pl.ds(t * third, third)
        return load(h1_in.at[at], rh, 6) if layer == 2 else load(x_in.at[:, at], rx, 7)

    load_w = {2: load(w2_in, wv, 8), 1: load(w1_in, wv, 8)}
    load_p, load_c, load_e = load(pre_in, pre, 9), load(cell_in, cell, 10), load(dsel_in, dsel, 11)
    keep = load(sel_in, sel_out.at[:, pl.ds(here.b * hidden, hidden)], 12)
    store_g = load(gxv, gx_out, 13)
    store_h = load(hv, h_out, 14)
    load_rhs(2, 0).start()
    for k in range(6):
        load_d(k).start()
    load_w[2].start()
    load_rhs(1, 0).start()
    for copy in (load_p, load_c, load_e, keep):
        copy.start()
    meet(here.peers + here.line)

    def halves(start, i):
        size = hidden if i is None else hidden // 2
        return pl.ds(start + (i or 0) * size, size)

    gather = Gather(
        here,
        lambda b, i: sel_out.at[:, halves(b * hidden, i)],
        psem,
        lambda i: sel_in.at[:, halves(0, i)],
    )
    biases = [
        remote(dbv.at[here.z], dbv.at[here.z], dsem.at[d, 0], dsem.at[d, 1], peer)
        for d, peer in enumerate(here.line, 1)
    ]
    spread = [pltpu.make_async_copy(h_in.at[here.b], heard.at[here.b], hsem.at[0, 0])]
    for d, peer in enumerate(here.peers, 1):
        spread.append(remote(h_in.at[peer["tm"]], heard.at[here.b], hsem.at[d, 0], hsem.at[d, 1], peer))

    done, spent = [0], [0]

    def units(layer, t):
        count = 4 if layer == 2 else 6
        start = t * count + (LATER if layer == 1 else 0)
        assert start + count <= OWN or spent[0] > (start + count - OWN) * PIECES - 1 + SLOTS
        first = spent[0]

        def unit(k, carry):
            block = start + k
            product = ar.product(block)
            if start == 0:
                load_d(product).wait()
            rows = pl.ds(pl.multiple_of(product * hidden, 16), hidden)
            got = dot(dv[rows, :], rh[...], NT) if layer == 2 else dot(dv[rows, :], rx[...], NN)
            own[lax.rem(block, OWN)] = got.astype(BF16)
            if start == 0:
                for i in range(PIECES):
                    u = block * PIECES + i

                    @pl.when(u < AHEAD)
                    def _(u=u):
                        ar.offer(u)

            else:

                @pl.when(lax.rem(k, 2) == 1)
                def _():
                    ar.tick(first + k // 2)

            return carry

        lax.fori_loop(0, count, unit, 0)
        done[0] = (start + count) * PIECES
        if start:
            spent[0] += count // 2
            assert first + AHEAD < (start + 2) * PIECES and spent[0] - 1 + AHEAD < done[0]

    def tick(count=1):
        first = spent[0]
        spent[0] += count
        assert spent[0] - 1 + AHEAD < done[0] or done[0] == ar.units

        def step(n, carry):
            ar.tick(n)
            return carry

        lax.fori_loop(first, spent[0], step, 0)

    def strips(layer, s, q):
        if layer == 2:
            i, start = q // 2, lax.rem(q, 2) * (length // 2)
            down = hidden // 16
            lhs = pl.ds(pl.multiple_of(i * half, LANES), half)

            def strip(c):
                src = pl.ds(pl.multiple_of(s * length + start + c, 256), 256)
                got = dot(wv[:, lhs], dv[:, src], TN).astype(BF16)
                for n in range(2):
                    at = pl.ds(((start + c) // LANES + n) * down, down)
                    part[i, :, :, at] = got[:, n * LANES : (n + 1) * LANES].reshape(2, 2, down, 16, LANES)

            tiles(length // 2, 256, strip)
        else:

            def strip(c, carry):
                cols = pl.ds(pl.multiple_of(c * 256, 256), 256)
                got = dot(dv[:, columns_of(s)], wv[:, cols], TN).astype(BF16)
                for j in range(groups):
                    for n in range(2):
                        block = got[j * LANES : (j + 1) * LANES, n * LANES : (n + 1) * LANES]
                        part[:, :, :, (c * 2 + n) * groups + j] = block.reshape(2, 2, 2, piece, LANES)
                return carry

            count = width // 256
            lax.fori_loop(count * q // 4, count * (q + 1) // 4, strip, 0)

    def input_grad(layer, s):
        first = spent[0]
        spent[0] += 4
        assert spent[0] - 1 + AHEAD < done[0]

        def quarter(q, carry):
            strips(layer, s, q)
            ar.tick(first + q)
            return carry

        lax.fori_loop(0, 4, quarter, 0)

    def settle(layer, s):
        if layer == 2:

            def put(first, v):
                grad[:, pl.ds(s * length + first, LANES)] = v

            sums[2].done(s, hidden // 16, put)
        else:

            def put(first, v):
                gxv[s, :, pl.ds(first, LANES)] = v

            sums[1].done(s, groups, put)
            gxv[s] = dot(reorder(piece, groups, True), gxv[s], NN).astype(BF16)

    def pool(s):
        first = s * length
        pool_backward(first, grad, pre, cell, first, dv, db1.at[s], work, edge, hidden, groups)

    size = rh.shape[1] // 2

    def third_of(t):
        return pl.ds(pl.multiple_of(t * third, LANES), third)

    def load_picked(t, tap):
        return load(sel_out.at[tap, third_of(t)], rh.at[:, pl.ds(pl.multiple_of(tap * size, LANES), size)], 15 + tap)

    def store_o(t, tap):
        return load(wo.at[tap], wo_out.at[tap, :, third_of(t)], 17 + tap)

    def outgate():
        first = spent[0]
        spent[0] += 6

        def step(i, carry):
            t, tap = i // 2, lax.rem(i, 2)
            load_picked(t, tap).wait()

            @pl.when(t > 0)
            def _():
                store_o(t - 1, tap).wait()

            values = rh[:, pl.ds(pl.multiple_of(tap * size, LANES), size)]
            wo[tap] = dot(dsel[...], values, NT).astype(BF16)
            store_o(t, tap).start()

            @pl.when(t + 1 < THIRDS)
            def _():
                load_picked(t + 1, tap).start()

            ar.tick(first + i)
            return carry

        lax.fori_loop(0, 2 * THIRDS, step, 0)

    load_rhs(2, 0).wait()
    units(2, 0)
    load_rhs(2, 1).start()
    load_d(2).wait()
    load_d(5).wait()
    load_w[2].wait()
    input_grad(2, 0)
    sums[2].start(0)
    tick()
    load_rhs(2, 1).wait()
    units(2, 1)
    load_rhs(2, 2).start()
    sums[2].cross(0)
    tick()
    input_grad(2, 1)
    load_w[1].start()
    sums[2].start(1)
    tick()
    sums[2].turn(0)
    tick()
    load_rhs(2, 2).wait()
    units(2, 2)
    sums[2].cross(1)
    tick()
    settle(2, 0)
    tick(2)
    load_p.wait()
    load_c.wait()
    pool(0)
    tick(2)
    sums[2].turn(1)
    gather.start()
    tick(2)
    settle(2, 1)
    for target in (here.core, here.across_x, here.across_y):
        signal(ready, target)
    pool(1)
    tick(2)
    load_rhs(1, 0).wait()
    units(1, 0)
    gather.relay()
    load_rhs(1, 1).start()
    dbv[here.z] = jnp.zeros((8, hidden), F32)
    for row, db in enumerate((db1, db2)):
        dbv[here.z, row : row + 1, :] = to_row(sum(db[s] for s in range(1, seqs)) + db[0])
    for copy in biases:
        copy.start()
    load_w[1].wait()
    pl.semaphore_wait(ready, 3)
    input_grad(1, 0)
    sums[1].start(0)
    load_rhs(1, 1).wait()
    units(1, 1)
    load_rhs(1, 2).start()
    sums[1].cross(0)
    tick()
    input_grad(1, 1)
    sums[1].start(1)
    tick()
    gather.share()
    tick()
    sums[1].cross(1)
    tick()
    sums[1].turn(0)
    tick(5)
    load_rhs(1, 2).wait()
    units(1, 2)
    tick(2)
    settle(1, 0)
    sums[1].turn(1)
    keep.wait()
    load_e.wait()
    for tap in range(2):
        load_picked(0, tap).start()
    tick(2)
    for copy in spread:
        copy.start()
    tick(4)
    settle(1, 1)
    store_g.start()
    outgate()
    for copy in spread:
        copy.wait()
    back = reorder(piece, groups, True)
    for s in range(seqs):
        for b in range(8):
            block = heard[b, pl.ds(s * LANES, LANES), :]
            hv[s, :, b * hidden : (b + 1) * hidden] = dot(back, block, NN).astype(BF16)
    store_h.start()

    def more(n, carry):
        ar.tick(n)
        return carry

    lax.fori_loop(spent[0], ar.units + BEHIND + 2, more, 0)
    ar.drain()
    gather.drain()
    for copy in [store_g, store_h] + [store_o(THIRDS - 1, tap) for tap in range(2)] + biases:
        copy.wait()
    db_out[...] = dbv[0] + dbv[1] + dbv[2] + dbv[3]


def run_backward(d, h1, x, w2, w1, pre, cell, h, sel, dsel, db):
    (wide, width), total, seqs = w1.shape, d.shape[1], db.shape[0]
    hidden, length = wide // 6, total // seqs
    third, span, picked = width // THIRDS, length // 8, dsel.shape[1]
    rows, count = hidden // PIECES, length // 16 * hidden // LANES
    assert picked == length and length == 8 * LANES
    vmem = pl.BlockSpec(memory_space=pltpu.VMEM)
    scratch = [
        pltpu.VMEM((wide, total), BF16),
        pltpu.VMEM((wide, width), BF16),
        pltpu.VMEM((third, total), BF16),
        pltpu.VMEM((total, third), BF16),
        pltpu.VMEM((3 * hidden, total), BF16),
        pltpu.VMEM((hidden, total), F32),
        pltpu.VMEM((2, hidden, length), F32),
        pltpu.VMEM((2, hidden, LANES), F32),
        pltpu.VMEM((hidden, total), BF16),
        pltpu.VMEM((seqs, span, width), BF16),
        pltpu.VMEM((hidden, picked), BF16),
        pltpu.VMEM((2, hidden, third), BF16),
        pltpu.VMEM(h.shape, BF16),
        pltpu.VMEM((seqs, span, width), BF16),
        pltpu.VMEM((seqs, hidden, 1), F32),
        pltpu.VMEM((4, 8, hidden), F32),
        pltpu.VMEM((OWN, hidden, third), BF16),
        pltpu.VMEM((SLOTS, rows, third), BF16),
        pltpu.VMEM((SLOTS, rows, third), BF16),
        pltpu.VMEM((SLOTS, rows, third), BF16),
        pltpu.VMEM((2, 2, 2, count, 16, LANES), BF16),
        pltpu.VMEM((seqs, 2, 2, count, 16, LANES), BF16),
        pltpu.VMEM((seqs, 2, count // 2, 16, LANES), BF16),
        pltpu.VMEM((seqs, 2, count // 2, 16, LANES), BF16),
        pltpu.VMEM((seqs, count // 2, 16, LANES), BF16),
        pltpu.VMEM((seqs, count // 2, 16, LANES), BF16),
        pltpu.SemaphoreType.DMA((7, SLOTS)),
        pltpu.SemaphoreType.DMA((2, seqs, 5, 2)),
        pltpu.SemaphoreType.DMA((4, 2)),
        pltpu.SemaphoreType.DMA((8, 2)),
        pltpu.SemaphoreType.DMA((11, 2)),
        pltpu.SemaphoreType.DMA((19,)),
    ]
    return pl.pallas_call(
        functools.partial(backward_kernel, seqs, hidden, length, width),
        name="backward",
        in_specs=[ANY] * 10 + [vmem],
        out_specs=[ANY] * 5 + [vmem],
        out_shape=[
            shape((12, hidden, width), BF16),
            shape((seqs, span, width), BF16),
            shape((seqs, span, width), BF16),
            shape((2, width, picked), BF16),
            shape((2, hidden, width), BF16),
            shape((8, hidden), F32),
        ],
        scratch_shapes=scratch + [pltpu.SemaphoreType.REGULAR] * 4,
        compiler_params=params(collective_id=1, has_side_effects=True),
    )(d, h1, x, w2, w1, pre, cell, h, sel, dsel, db)


def reorder(piece, groups, back):
    span = piece * groups
    a = lax.broadcasted_iota(jnp.int32, (span, span), 1 if back else 0)
    b = lax.broadcasted_iota(jnp.int32, (span, span), 0 if back else 1)
    return (b == lax.rem(a, piece) * groups + a // piece).astype(BF16)


def to_row(column):
    n = column.shape[0]
    same = lax.broadcasted_iota(jnp.int32, (n, n), 0) == lax.broadcasted_iota(jnp.int32, (n, n), 1)
    return jnp.sum(jnp.where(same, column, 0.0), axis=0, keepdims=True)


def to_column(row):
    n = row.shape[1]
    same = lax.broadcasted_iota(jnp.int32, (n, n), 0) == lax.broadcasted_iota(jnp.int32, (n, n), 1)
    return jnp.sum(jnp.where(same, row, 0.0), axis=1, keepdims=True)


class Gather:
    def __init__(self, here, region, sems, own=None):
        h, b = here, here.b
        own = own or (lambda half: region(b, half))
        bx, by = h.across_x["tm"], h.across_y["tm"]
        bd = bx + 4 - 8 * h.y
        plan = (
            (b, 1, h.across_x),
            (b, 0, h.across_y),
            (b, 0, h.across_x),
            (b, 1, h.across_y),
            (b, None, h.core),
            (bx, 1, h.across_y),
            (by, 0, h.across_x),
            (bx, None, h.core),
            (by, None, h.core),
            (bd, 0, h.core),
            (bd, 1, h.core),
        )
        self.copies = []
        for k, (block, half, to) in enumerate(plan):
            src = own(half) if k < 5 else region(block, half)
            self.copies.append(remote(src, region(block, half), sems.at[k, 0], sems.at[k, 1], to))

    def start(self):
        for k in range(5):
            self.copies[k].start()

    def relay(self):
        self.copies[0].wait_recv()
        self.copies[5].start()
        self.copies[1].wait_recv()
        self.copies[6].start()

    def share_near(self):
        self.copies[2].wait_recv()
        self.copies[7].start()
        self.copies[4].wait_recv()
        self.copies[7].wait_recv()

    def share_far(self):
        self.copies[3].wait_recv()
        self.copies[8].start()
        self.copies[6].wait_recv()
        self.copies[9].start()
        self.copies[5].wait_recv()
        self.copies[10].start()
        for k in (8, 9, 10):
            self.copies[k].wait_recv()

    def share(self):
        self.share_near()
        self.share_far()

    def drain(self):
        for copy in self.copies:
            copy.wait_send()


def forward_kernel(seqs, hidden, length, width, *refs):
    x_in, w1_in, w2_in, cot_in, b1_in, b2_in, starts = refs[:7]
    x_out, h1_out, pre_out, cell_out, h2_out, d_out, db_out, sel_out, dsel_out = refs[7:16]
    xg, hg, w, p, pre, cell, work, edge, dv, seed, grad, hv, h2t, raw, cot, sent, b1, b2, chosen, sel, dsel = refs[16:37]
    xsem, hsem, ssem, zsem, lsem = refs[37:]
    here = Here()
    groups = length // LANES
    piece = LANES // 8

    def columns_of(s):
        return pl.ds(s * length, length)

    def x_region(s):
        def region(b, half):
            js = pl.ds(0, groups) if half is None else pl.ds(half * (groups // 2), groups // 2)
            return xg.at[s, js, b]

        return region

    def h_region(s):
        def region(b, half):
            rows = pl.ds(0, hidden) if half is None else pl.ds(half * (hidden // 2), hidden // 2)
            return hg.at[b, rows, columns_of(s)]

        return region

    def load(src, dst, k):
        return pltpu.make_async_copy(src, dst, lsem.at[k])

    load_w1 = load(w1_in, w, 0)
    load_w2 = load(w2_in, w, 0)
    load_x = [load(x_in.at[s], raw.at[s], 1 + s) for s in range(seqs)]
    load_c = load(cot_in, cot, 14)
    store_x = [load(xg.at[s], x_out.at[s], 3 + s) for s in range(seqs)]
    store_h = [load(hg.at[:, :, columns_of(s)], h1_out.at[:, :, columns_of(s)], 5 + s) for s in range(seqs)]
    store_p = [load(pre.at[:, columns_of(s)], pre_out.at[:, columns_of(s)], 7 + s) for s in range(seqs)]
    store_c = [load(cell.at[:, columns_of(s)], cell_out.at[:, columns_of(s)], 9 + s) for s in range(seqs)]
    store_d = [load(dv.at[s], d_out.at[:, columns_of(s)], 11 + s) for s in range(seqs)]
    store_o = load(h2t, h2_out, 13)

    for copy in load_x:
        copy.start()
    load_w1.start()
    load_c.start()
    order = reorder(piece, groups, False)

    def place():
        for s in range(seqs):
            load_x[s].wait()
            xg[s, :, here.b] = dot(order, raw[s], NN).astype(BF16).reshape(groups, piece, width)

    meet(here.peers + here.line, place)
    xs = [Gather(here, x_region(s), xsem.at[s]) for s in range(seqs)]
    hs = [Gather(here, h_region(s), hsem.at[s]) for s in range(seqs)]

    def prepare():
        load_c.wait()
        for s in range(seqs):
            turned = dot(order, cot[s], NN).astype(BF16)
            for b in range(8):
                block = turned[:, b * hidden : (b + 1) * hidden]
                sent[b, s] = block.reshape(groups, piece, hidden)
        seed[:, :, pl.ds(0, 4)] = jnp.zeros((seqs, groups, 4, piece, hidden), BF16)
        for s in range(seqs):
            prepare_pick(s)
        b1[...] = to_column(b1_in[...][None, :])
        b2[...] = to_column(b2_in[...][None, :])

    late = [
        (remote(sent.at[peer["tm"]], seed.at[:, :, here.b], ssem.at[d, 0], ssem.at[d, 1], peer), peer)
        for d, peer in enumerate(here.peers, 1)
    ]

    def first_products(s):
        def block(r):
            rows = pl.ds(r, hidden)
            p[rows, :] = dot(w[rows, :], xg[s].reshape(length, width), NT)

        tiles(6 * hidden, hidden, block)

    def second_products(s, near):
        y = here.y if near else 1 - here.y
        depth = pl.ds(pl.multiple_of(y * (width // 2), LANES), width // 2)

        def block(r):
            rows = pl.ds(r, hidden)
            rhs = hg[pl.ds(y * 4, 4), :, columns_of(s)].reshape(width // 2, length)
            got = dot(w[rows, depth], rhs, NN)
            p[rows, :] = got if near else p[rows, :] + got

        tiles(6 * hidden, hidden, block)

    def first_pool(s):
        first = s * length
        pool_forward(first, p, b1, pre, cell, first, hg.at[here.b], work.at[0], edge.at[0], hidden, groups)

    def second_pool(s):
        pool_forward(s * length, p, b2, pre, cell, 0, hv, work.at[0], edge.at[0], hidden, groups)
        rows = lax.broadcasted_iota(jnp.int32, (LANES, LANES), 0)
        cols = lax.broadcasted_iota(jnp.int32, (LANES, LANES), 1)
        eye = (rows == cols).astype(BF16)
        for j in range(groups):
            turned = dot(eye, hv[:, pl.ds(j * LANES, LANES)], NT).astype(BF16)
            at = pl.ds((s * groups + j) * piece, piece)
            h2t[:, at, :] = turned.reshape(8, piece, hidden)

    def incoming(s):
        rows = lax.broadcasted_iota(jnp.int32, (hidden, hidden), 0)
        cols = lax.broadcasted_iota(jnp.int32, (hidden, hidden), 1)
        eye = (rows == cols).astype(BF16)
        lane = lax.broadcasted_iota(jnp.int32, (1, LANES), 1)
        for j in range(groups):
            block = seed[s, j].reshape(LANES, hidden)
            turned = dot(eye, block, NT)
            step = lane * groups + j
            keep = jnp.zeros((1, LANES), jnp.bool_)
            for k in range(starts.shape[1]):
                begin = starts[s, k]
                keep = jnp.logical_or(keep, jnp.logical_and(step >= begin, step < begin + CLUSTER))
            keep = jnp.broadcast_to(keep, (hidden, LANES))
            grad[:, pl.ds(s * length + j * LANES, LANES)] = jnp.where(keep, turned, 0.0).astype(BF16)

    def pool_back(s):
        pool_backward(s * length, grad, pre, cell, 0, dv.at[s], db_out.at[s], work, edge, hidden, groups, True)
        store_d[s].start()

    def cluster_steps(s):
        lane = lax.broadcasted_iota(jnp.int32, (1, LANES), 1)
        step = lax.rem(lane, CLUSTER)
        for k in range(starts.shape[1]):
            step = step + jnp.where(lane // CLUSTER == k, starts[s, k], 0)
        return lane, step

    def prepare_pick(s):
        _, step = cluster_steps(s)
        for j in range(groups):
            code = lax.broadcasted_iota(jnp.int32, (LANES, LANES), 0) * groups + j
            at = pl.ds(j * LANES, LANES)
            chosen[s, at, pl.ds(0, LANES)] = (code == step).astype(BF16)
            chosen[s, at, pl.ds(LANES, LANES)] = (code == step - 1).astype(BF16)

    def held(s, count):
        start = here.z * (seqs * LANES) + s * LANES
        return pl.ds(pl.multiple_of(start, LANES), count * LANES)

    def pick_hidden(s):
        got = dot(hg[here.b, :, columns_of(s)], chosen[s], NN).astype(BF16)
        for tap in range(2):
            sel[tap, :, held(s, 1)] = got[:, tap * LANES : (tap + 1) * LANES]

    def pick_grad(s):
        lane, step = cluster_steps(s)
        again = jnp.zeros((1, LANES), jnp.bool_)
        for k in range(starts.shape[1] - 1):
            begin = starts[s, k]
            inside = jnp.logical_and(step >= begin, step < begin + CLUSTER)
            again = jnp.logical_or(again, jnp.logical_and(inside, lane // CLUSTER > k))
        got = dot(dv[s, pl.ds(2 * hidden, hidden), :], chosen[s, :, pl.ds(0, LANES)], NN)
        dsel[:, held(s, 1)] = jnp.where(jnp.broadcast_to(again, (hidden, LANES)), 0.0, got).astype(BF16)

    spread_h = []
    spread_d = []
    for d, peer in enumerate(here.line, 1):
        at = sel.at[:, :, held(0, seqs)]
        spread_h.append(remote(at, at, zsem.at[d, 0], zsem.at[d, 1], peer))
        at = dsel.at[:, held(0, seqs)]
        spread_d.append(remote(at, at, zsem.at[d, 2], zsem.at[d, 3], peer))
    store_s = load(sel, sel_out, 15)
    store_e = load(dsel, dsel_out, 16)

    xs[0].start()
    prepare()
    xs[0].relay()
    xs[1].start()
    xs[0].share()
    store_x[0].start()
    load_w1.wait()
    first_products(0)
    xs[1].relay()
    first_pool(0)
    hs[0].start()
    store_p[0].start()
    store_c[0].start()
    xs[1].share()
    store_x[1].start()
    first_products(1)
    load_w2.start()
    hs[0].relay()
    first_pool(1)
    hs[1].start()
    store_p[1].start()
    store_c[1].start()

    for s in range(seqs):
        pick_hidden(s)
    for copy in spread_h:
        copy.start()
    hs[0].share_near()
    load_w2.wait()
    second_products(0, True)
    hs[0].share_far()
    store_h[0].start()
    second_products(0, False)
    hs[1].relay()

    @pl.when(here.y == 1)
    def _():
        pltpu.make_async_copy(sent.at[here.b], seed.at[:, :, here.b], ssem.at[0, 0]).start()
        for copy, _ in late:
            copy.start()

    store_p[0].wait()
    store_c[0].wait()
    second_pool(0)
    hs[1].share_near()
    second_products(1, True)
    hs[1].share_far()
    store_h[1].start()
    second_products(1, False)
    store_p[1].wait()
    store_c[1].wait()
    second_pool(1)
    store_o.start()

    @pl.when(here.y == 1)
    def _():
        pltpu.make_async_copy(sent.at[here.b], seed.at[:, :, here.b], ssem.at[0, 0]).wait()
        for copy, _ in late:
            copy.wait_send()

    for d, (copy, _) in enumerate(late, 1):
        source = lax.rem(here.b + 8 - d, 8)

        @pl.when(source >= 4)
        def _(copy=copy):
            copy.wait_recv()

    for s in range(seqs):
        incoming(s)
        outgate_backward(s * length, grad, pre, cell, dv.at[s], hidden, groups)
        pick_grad(s)
    for copy in spread_d:
        copy.start()
    for copy in spread_h:
        copy.wait()
    store_s.start()
    for s in range(seqs):
        pool_back(s)
    for gather in xs + hs:
        gather.drain()
    for copy in spread_d:
        copy.wait()
    store_e.start()
    for copy in store_x + store_h + store_d + [store_o, store_s, store_e]:
        copy.wait()


def run_forward(x, w1, b1, w2, b2, cotangent, starts):
    seqs, span, width = x.shape
    hidden, length, piece = w1.shape[0] // 6, span * 8, LANES // 8
    groups = length // LANES
    total, picked = seqs * length, 4 * seqs * LANES
    assert starts.shape[1] * CLUSTER == LANES
    vmem = pl.BlockSpec(memory_space=pltpu.VMEM)
    return pl.pallas_call(
        functools.partial(forward_kernel, seqs, hidden, length, width),
        name="forward",
        in_specs=[ANY, ANY, ANY, ANY, vmem, vmem, pl.BlockSpec(memory_space=pltpu.SMEM)],
        out_specs=[ANY, ANY, ANY, ANY, ANY, ANY, vmem, ANY, ANY],
        out_shape=[
            shape((seqs, groups, 8, piece, width), BF16),
            shape((8, hidden, total), BF16),
            shape((3 * hidden, total), BF16),
            shape((hidden, total), F32),
            shape((8, seqs * groups * piece, hidden), BF16),
            shape((6 * hidden, total), BF16),
            shape((seqs, hidden, 1), F32),
            shape((2, hidden, picked), BF16),
            shape((hidden, picked), BF16),
        ],
        scratch_shapes=[
            pltpu.VMEM((seqs, groups, 8, piece, width), BF16),
            pltpu.VMEM((8, hidden, total), BF16),
            pltpu.VMEM((6 * hidden, width), BF16),
            pltpu.VMEM((6 * hidden, length), F32),
            pltpu.VMEM((3 * hidden, total), BF16),
            pltpu.VMEM((hidden, total), F32),
            pltpu.VMEM((2, hidden, length), F32),
            pltpu.VMEM((2, hidden, LANES), F32),
            pltpu.VMEM((seqs, 6 * hidden, length), BF16),
            pltpu.VMEM((seqs, groups, 8, piece, hidden), BF16),
            pltpu.VMEM((hidden, total), BF16),
            pltpu.VMEM((hidden, length), BF16),
            pltpu.VMEM((8, seqs * groups * piece, hidden), BF16),
            pltpu.VMEM((seqs, span, width), BF16),
            pltpu.VMEM((seqs, span, width), BF16),
            pltpu.VMEM((8, seqs, groups, piece, hidden), BF16),
            pltpu.VMEM((hidden, 1), F32),
            pltpu.VMEM((hidden, 1), F32),
            pltpu.VMEM((seqs, length, 2 * LANES), BF16),
            pltpu.VMEM((2, hidden, picked), BF16),
            pltpu.VMEM((hidden, picked), BF16),
            pltpu.SemaphoreType.DMA((seqs, 11, 2)),
            pltpu.SemaphoreType.DMA((seqs, 11, 2)),
            pltpu.SemaphoreType.DMA((8, 2)),
            pltpu.SemaphoreType.DMA((4, 4)),
            pltpu.SemaphoreType.DMA((17,)),
        ],
        compiler_params=params(collective_id=0, has_side_effects=True),
    )(x, w1, w2, cotangent, b1, b2, starts)


def finish_kernel(
    one_ref, two_ref, outgate_ref, h_ref, gx_ref, db_ref, wide_one_ref, wide_two_ref, h_out, gx_out, db1_out, db2_out
):
    i = pl.program_id(0)
    wide_one_ref[...] = one_ref[...].astype(F32)
    last = lax.rem(i, 3) == 2

    @pl.when(last)
    def _():
        wide_two_ref[...] = outgate_ref[...].astype(F32)

    @pl.when(jnp.logical_not(last))
    def _():
        wide_two_ref[...] = two_ref[...].astype(F32)

    h_out[...] = h_ref[...]
    gx_out[...] = gx_ref[...]
    db1_out[...] = db_ref[0]
    db2_out[...] = db_ref[1]


def finish(gw, outgate, h, gx, db):
    _, hidden, width = gw.shape
    total = h.shape[0] * h.shape[1]
    dims = (1, hidden, width)
    small = (total // 4, width)
    weights = pl.BlockSpec(dims, lambda i: (i, 0, 0))
    tokens = pl.BlockSpec(small, lambda i: (jnp.minimum(i, 3), 0))
    bias = pl.BlockSpec((hidden,), lambda i: (0,))
    return pl.pallas_call(
        finish_kernel,
        name="results",
        grid=(6,),
        in_specs=[
            weights,
            pl.BlockSpec(dims, lambda i: (6 + i - i % 3 // 2, 0, 0)),
            pl.BlockSpec(dims, lambda i: (i // 3, 0, 0)),
            tokens,
            tokens,
            pl.BlockSpec(db.shape, lambda i: (0, 0)),
        ],
        out_specs=[weights, weights, tokens, tokens, bias, bias],
        out_shape=[shape((6, hidden, width), F32)] * 2 + [shape((total, width), BF16)] * 2 + [shape((hidden,), F32)] * 2,
        compiler_params=params(),
    )(gw, gw, outgate, h.reshape(total, width), gx.reshape(total, width), db)


def per_device(line, inputs, weight_one, fbias_one, weight_two, fbias_two, cotangent, cluster_starts):
    seqs, span, width = inputs.shape
    count = lax.axis_size("tm")
    length = span * count
    groups = length // LANES
    piece = LANES // count
    hidden = weight_one.shape[2]
    total = seqs * length
    w1 = weight_one.reshape(6 * hidden, width)
    w2 = weight_two.reshape(6 * hidden, width)

    if line:
        x, h1, pre1, cell1, h2, d2, db2, *picked = run_forward(
            inputs, w1, fbias_one, w2, fbias_two, cotangent, cluster_starts
        )
        x, h1 = x.reshape(total, width), h1.reshape(width, total)
        gw, gx1, h2, _, wo, db = run_backward(d2, h1, x, w2, w1, pre1, cell1, h2, *picked, db2)
        gw1, gw2, h2, gx1, *db = finish(gw, wo, h2, gx1, db)
    else:
        x = inputs.reshape(seqs, piece, groups, width).transpose(0, 2, 1, 3)
        bias1, bias2 = fbias_one[:, None], fbias_two[:, None]
        seed = cotangent.reshape(seqs, piece, groups, count, hidden)
        steps = lax.axis_index("tm") * span + jnp.arange(span, dtype=jnp.int32)
        starts = cluster_starts[:, :, None]
        keep = jnp.any((steps >= starts) & (steps < starts + CLUSTER), axis=1)
        seed = jnp.where(keep.reshape(seqs, piece, groups, 1, 1), seed, jnp.zeros_like(seed))
        seed = lax.all_to_all(seed, "tm", split_axis=3, concat_axis=1, tiled=True)
        seed = seed.reshape(seqs, LANES, groups, hidden).transpose(3, 0, 2, 1).reshape(hidden, total)
        x = lax.all_gather(x, "tm", axis=2, tiled=True).reshape(total, width)
        pre1, cell1, h1 = run_first(seqs, w1, bias1, x)
        h1 = lax.all_gather(h1, "tm", axis=0, tiled=True)
        h2, d2, db2 = run_second(seqs, w2, bias2, h1, seed)
        h2 = h2.reshape(hidden, seqs, groups, count, piece)
        h2 = lax.all_to_all(h2, "tm", split_axis=3, concat_axis=0, tiled=True)
        h2 = h2.reshape(width, seqs, groups, piece).transpose(1, 3, 2, 0)
        gw2 = lax.psum(dot(d2, h1, NT).astype(BF16), "seq").astype(F32)
        gx2 = lax.psum_scatter(dot(w2, d2, TN).astype(BF16), "tm", scatter_dimension=0, tiled=True)
        d1, db1 = run_back(seqs, gx2, pre1, cell1)
        gw1 = lax.psum(dot(d1, x, NN).astype(BF16), "seq").astype(F32)
        gx1 = dot(d1, w1, TN).astype(BF16).reshape(seqs, groups, LANES, width)
        gx1 = lax.psum_scatter(gx1, "tm", scatter_dimension=2, tiled=True)
        gx1 = gx1.transpose(0, 2, 1, 3).reshape(seqs, span, width)
        db = lax.psum(jnp.stack([db1, db2]).sum(axis=(1, 3)), "seq")
    out, gx1 = h2.reshape(seqs, span, width), gx1.reshape(seqs, span, width)
    dims = weight_one.shape
    return (out, gx1, gw1.reshape(dims), db[0], gw2.reshape(dims), db[1])


def solution(mesh):
    placed = (
        P("seq", "tm", None),
        P(None, None, "tm", None),
        P("tm"),
        P(None, None, "tm", None),
        P("tm"),
        P("seq", "tm", None),
        P("seq", None),
    )
    return jax.shard_map(
        functools.partial(per_device, dict(mesh.shape) == {"seq": 4, "tm": 8}),
        mesh=mesh,
        in_specs=placed,
        out_specs=(
            P("seq", "tm", None),
            P("seq", "tm", None),
            P(None, None, "tm", None),
            P("tm"),
            P(None, None, "tm", None),
            P("tm"),
        ),
        check_vma=False,
    )
```

```python
import functools

import jax
import jax.numpy as jnp
from jax import lax
from jax.experimental import pallas as pl
from jax.experimental.pallas import tpu as pltpu
from jax.sharding import PartitionSpec as P

CLUSTER = 32
LANES = 128
ROWS = 48
F32 = jnp.float32
BF16 = jnp.bfloat16
ANY = pl.BlockSpec(memory_space=pl.ANY)
MESH = pl.DeviceIdType.MESH
NN = (((1,), (0,)), ((), ()))
NT = (((1,), (1,)), ((), ()))
TN = (((0,), (0,)), ((), ()))


def dot(a, b, dims):
    return lax.dot_general(a, b, dims, preferred_element_type=F32)


def sigmoid(v):
    return 1.0 / (1.0 + jnp.exp(-v))


def tiles(count, rows, body):
    def step(r, carry):
        body(pl.multiple_of(r * rows, rows))
        return carry

    lax.fori_loop(0, count // rows, step, 0)


def aligned(start):
    return start if isinstance(start, int) else pl.multiple_of(start, LANES)


def stretch(hidden):
    return 96 if hidden % 96 == 0 else ROWS


def shift_lanes(v, amount, lane, fill):
    moved = pltpu.roll(v, amount % LANES, axis=1)
    gone = lane < amount if amount > 0 else lane >= LANES + amount
    return jnp.where(gone, fill, moved)


def lane_chain(factor, value, lane, sign):
    step = 1
    while step < LANES:
        value = value + factor * shift_lanes(value, sign * step, lane, 0.0)
        factor = factor * shift_lanes(factor, sign * step, lane, 1.0)
        step *= 2
    return value


def pool_forward(first, p_ref, b_ref, pre_ref, cell_ref, target, h_ref, factor_ref, edge_ref, hidden, groups):
    size = stretch(hidden)
    lane = lax.broadcasted_iota(jnp.int32, (size, LANES), 1)

    def at(j, start=0):
        return pl.ds(start + j * LANES, LANES)

    def gates(r):
        rows = pl.ds(r, size)
        value = factor = None
        for j in range(groups):
            got = []
            for g in range(3):
                now = p_ref[pl.ds(g * hidden + r, size), at(j)]
                tap = pl.ds((3 + g) * hidden + r, size)
                if j:
                    past = p_ref[tap, at(j - 1)]
                else:
                    past = shift_lanes(p_ref[tap, at(groups - 1)], 1, lane, 0.0)
                total = now + past
                if g == 1:
                    total = total + b_ref[rows, :]
                total = total.astype(BF16)
                pre_ref[pl.ds(g * hidden + r, size), at(j, first)] = total
                got.append(total.astype(F32))
            forget = sigmoid(got[1])
            fresh = (1.0 - forget) * jnp.tanh(got[0])
            if j:
                value = forget * value + fresh
                factor = forget * factor
            else:
                value, factor = fresh, forget
            cell_ref[rows, at(j, first)] = value
            factor_ref[rows, at(j)] = factor

    tiles(hidden, size, gates)

    everywhere = lax.broadcasted_iota(jnp.int32, (hidden, LANES), 1)
    value = lane_chain(factor_ref[:, at(groups - 1)], cell_ref[:, at(groups - 1, first)], everywhere, 1)
    edge_ref[...] = shift_lanes(value, 1, everywhere, 0.0)

    def finish(r):
        rows = pl.ds(r, size)
        edge = edge_ref[rows, :]
        for j in range(groups):
            cell = cell_ref[rows, at(j, first)] + factor_ref[rows, at(j)] * edge
            cell_ref[rows, at(j, first)] = cell
            outgate = sigmoid(pre_ref[pl.ds(2 * hidden + r, size), at(j, first)].astype(F32))
            h_ref[rows, at(j, target)] = (outgate * cell).astype(BF16)

    tiles(hidden, size, finish)


def put_gate(d_ref, g, r, j, v, target, lane, hidden, groups):
    rows = v.shape[0]
    d_ref[pl.ds(g * hidden + r, rows), pl.ds(target + j * LANES, LANES)] = v
    tap = pl.ds((3 + g) * hidden + r, rows)
    if j:
        d_ref[tap, pl.ds(target + (j - 1) * LANES, LANES)] = v
    else:
        moved = shift_lanes(v.astype(F32), -1, lane, 0.0).astype(BF16)
        d_ref[tap, pl.ds(target + (groups - 1) * LANES, LANES)] = moved


def outgate_backward(first, g_ref, pre_ref, cell_ref, d_ref, hidden, groups):
    size = stretch(hidden)
    lane = lax.broadcasted_iota(jnp.int32, (size, LANES), 1)

    def body(r):
        rows = pl.ds(r, size)
        for j in range(groups):
            at = pl.ds(first + j * LANES, LANES)
            outgate = sigmoid(pre_ref[pl.ds(2 * hidden + r, size), at].astype(F32))
            v = g_ref[rows, at].astype(F32) * cell_ref[rows, at] * outgate * (1.0 - outgate)
            put_gate(d_ref, 2, r, j, v.astype(BF16), 0, lane, hidden, groups)

    tiles(hidden, size, body)


def pool_backward(
    first, g_ref, pre_ref, cell_ref, target, d_ref, db_ref, work_ref, edge_ref, hidden, groups, carried_only=False
):
    size = stretch(hidden)
    lane = lax.broadcasted_iota(jnp.int32, (size, LANES), 1)

    def at(j, start=0):
        return pl.ds(aligned(start + j * LANES), LANES)

    def gate(g, r, j):
        return pre_ref[pl.ds(g * hidden + r, size), at(j, first)].astype(F32)

    def start(r):
        rows = pl.ds(r, size)
        later = value = factor = None
        for j in reversed(range(groups)):
            own = g_ref[rows, at(j, first)].astype(F32) * sigmoid(gate(2, r, j))
            if later is None:
                value, factor = own, jnp.ones_like(own)
            else:
                value = own + later * value
                factor = later * factor
            work_ref[0, rows, at(j)] = value
            work_ref[1, rows, at(j)] = factor
            later = sigmoid(gate(1, r, j))
        edge_ref[0, rows, :] = later * value
        edge_ref[1, rows, :] = later * factor

    tiles(hidden, size, start)

    everywhere = lax.broadcasted_iota(jnp.int32, (hidden, LANES), 1)
    value = lane_chain(edge_ref[1], edge_ref[0], everywhere, -1)
    edge_ref[0] = shift_lanes(value, -1, everywhere, 0.0)

    def finish(r):
        rows = pl.ds(r, size)
        edge = edge_ref[0, rows, :]
        total = jnp.zeros((size, LANES), F32)
        before = shift_lanes(cell_ref[rows, at(groups - 1, first)], 1, lane, 0.0)
        for j in range(groups):
            carried = work_ref[0, rows, at(j)] + work_ref[1, rows, at(j)] * edge
            candidate = jnp.tanh(gate(0, r, j))
            forget = sigmoid(gate(1, r, j))
            cell = cell_ref[rows, at(j, first)]
            keep = carried * (1.0 - forget)
            got = [keep * (1.0 - candidate * candidate), keep * forget * (before - candidate)]
            if not carried_only:
                outgate = sigmoid(gate(2, r, j))
                got.append(g_ref[rows, at(j, first)].astype(F32) * cell * outgate * (1.0 - outgate))
            before = cell
            for g, v in enumerate(got):
                v = v.astype(BF16)
                if g == 1:
                    total = total + v.astype(F32)
                put_gate(d_ref, g, r, j, v, target, lane, hidden, groups)
        db_ref[rows, :] = jnp.sum(total, axis=1, keepdims=True)

    tiles(hidden, size, finish)


def first_kernel(hidden, length, w_ref, b_ref, x_ref, pre_ref, cell_ref, h_ref, p_ref, work_ref, edge_ref):
    def strip(c):
        cols = pl.ds(c, 512)
        p_ref[:, cols] = dot(w_ref[...], x_ref[cols, :], NT)

    tiles(length, 512, strip)
    pool_forward(0, p_ref, b_ref, pre_ref, cell_ref, 0, h_ref, work_ref, edge_ref, hidden, length // LANES)


def second_kernel(
    hidden, length, w_ref, b_ref, x_ref, g_ref, h_ref, d_ref, db_ref, p_ref, pre_ref, cell_ref, work_ref, edge_ref
):
    def strip(c):
        cols = pl.ds(c, 512)
        p_ref[:, cols] = dot(w_ref[...], x_ref[:, cols], NN)

    tiles(length, 512, strip)
    groups = length // LANES
    pool_forward(0, p_ref, b_ref, pre_ref, cell_ref, 0, h_ref, work_ref.at[0], edge_ref.at[0], hidden, groups)
    pool_backward(0, g_ref, pre_ref, cell_ref, 0, d_ref, db_ref.at[0], work_ref, edge_ref, hidden, groups)


def back_kernel(hidden, length, g_ref, pre_ref, cell_ref, d_ref, db_ref, work_ref, edge_ref):
    pool_backward(0, g_ref, pre_ref, cell_ref, 0, d_ref, db_ref.at[0], work_ref, edge_ref, hidden, length // LANES)


def columns(rows, length):
    return pl.BlockSpec((rows, length), lambda s: (0, s))


def fixed(*dims):
    return pl.BlockSpec(dims, lambda s: (0,) * len(dims), pipeline_mode=pl.Buffered(1))


def params(**more):
    return pltpu.CompilerParams(vmem_limit_bytes=63 * 1024 * 1024, **more)


shape = jax.ShapeDtypeStruct


def run_first(seqs, weight, bias, gathered):
    (wide, width), total = weight.shape, gathered.shape[0]
    hidden, length = wide // 6, total // seqs
    return pl.pallas_call(
        functools.partial(first_kernel, hidden, length),
        name="layer_one_forward",
        grid=(seqs,),
        in_specs=[fixed(wide, width), fixed(hidden, 1), pl.BlockSpec((length, width), lambda s: (s, 0))],
        out_specs=[columns(3 * hidden, length), columns(hidden, length), columns(hidden, length)],
        out_shape=[shape((3 * hidden, total), BF16), shape((hidden, total), F32), shape((hidden, total), BF16)],
        scratch_shapes=[
            pltpu.VMEM((wide, length), F32),
            pltpu.VMEM((hidden, length), F32),
            pltpu.VMEM((hidden, LANES), F32),
        ],
        compiler_params=params(),
    )(weight, bias, gathered)


def run_second(seqs, weight, bias, gathered, grad):
    (wide, width), total = weight.shape, gathered.shape[1]
    hidden, length = wide // 6, total // seqs
    return pl.pallas_call(
        functools.partial(second_kernel, hidden, length),
        name="layer_two_forward_and_pool_backward",
        grid=(seqs,),
        in_specs=[fixed(wide, width), fixed(hidden, 1), columns(width, length), columns(hidden, length)],
        out_specs=[columns(hidden, length), columns(wide, length), pl.BlockSpec((1, hidden, 1), lambda s: (s, 0, 0))],
        out_shape=[shape((hidden, total), BF16), shape((wide, total), BF16), shape((seqs, hidden, 1), F32)],
        scratch_shapes=[
            pltpu.VMEM((wide, length), F32),
            pltpu.VMEM((3 * hidden, length), BF16),
            pltpu.VMEM((hidden, length), F32),
            pltpu.VMEM((2, hidden, length), F32),
            pltpu.VMEM((2, hidden, LANES), F32),
        ],
        compiler_params=params(),
    )(weight, bias, gathered, grad)


def run_back(seqs, grad, pre, cell):
    hidden, total = grad.shape
    length = total // seqs
    return pl.pallas_call(
        functools.partial(back_kernel, hidden, length),
        name="layer_one_pool_backward",
        grid=(seqs,),
        in_specs=[columns(hidden, length), columns(3 * hidden, length), columns(hidden, length)],
        out_specs=[columns(6 * hidden, length), pl.BlockSpec((1, hidden, 1), lambda s: (s, 0, 0))],
        out_shape=[shape((6 * hidden, total), BF16), shape((seqs, hidden, 1), F32)],
        scratch_shapes=[pltpu.VMEM((2, hidden, length), F32), pltpu.VMEM((2, hidden, LANES), F32)],
        compiler_params=params(),
    )(grad, pre, cell)


THIRDS = 3
PIECES = 3
SLOTS = 12
AHEAD = 6
BEHIND = 2
LATER = 12
BLOCKS = 30
OWN = 18


class Here:
    def __init__(self):
        self.z = lax.axis_index("seq")
        self.b = lax.axis_index("tm")
        self.c = lax.rem(self.b, 2)
        self.x = lax.rem(self.b // 2, 2)
        self.y = self.b // 4
        self.core = dict(seq=self.z, tm=self.b + 1 - 2 * self.c)
        self.across_x = dict(seq=self.z, tm=self.b + 2 - 4 * self.x)
        self.across_y = dict(seq=self.z, tm=self.b + 4 - 8 * self.y)
        self.pair = dict(seq=self.z + 1 - 2 * lax.rem(self.z, 2), tm=self.b)
        self.middle = dict(seq=3 - self.z, tm=self.b)
        self.line = [dict(seq=lax.rem(self.z + d, 4), tm=self.b) for d in range(1, 4)]
        self.peers = [dict(seq=self.z, tm=lax.rem(self.b + d, 8)) for d in range(1, 8)]
        self.is_end = jnp.logical_or(self.z == 0, self.z == 3)
        self.is_centre = jnp.logical_and(self.z > 0, self.z < 3)


def remote(src, dst, send, recv, target):
    return pltpu.make_async_remote_copy(
        src_ref=src, dst_ref=dst, send_sem=send, recv_sem=recv, device_id=target, device_id_type=MESH
    )


def both(a, b):
    if isinstance(a, bool) and isinstance(b, bool):
        return a and b
    return jnp.logical_and(a, b)


def signal(sem, target):
    pl.semaphore_signal(sem, inc=1, device_id=target, device_id_type=MESH)


def meet(targets, between=None):
    barrier = pltpu.get_barrier_semaphore()
    for target in targets:
        signal(barrier, target)
    if between is not None:
        between()
    pl.semaphore_wait(barrier, len(targets))


def pick(condition, a, b):
    if isinstance(condition, bool):
        return a if condition else b
    return jnp.where(condition, a, b)


class SeqSum:
    def __init__(self, here, hidden, third, own, ring_in, ring_mid, total, out, sems, credits):
        self.here, self.third, self.rows = here, third, hidden // PIECES
        self.units = BLOCKS * PIECES
        self.own, self.ring_in, self.ring_mid, self.total, self.out = own, ring_in, ring_mid, total, out
        self.sems = sems
        self.credit_in, self.credit_mid, self.credit_out = credits

    def rows_of(self, u):
        return pl.ds(pl.multiple_of(lax.rem(u, PIECES) * self.rows, 16), self.rows)

    def mine(self, u):
        return self.own.at[lax.rem(u // PIECES, OWN), self.rows_of(u)]

    def inward(self, u):
        i = lax.rem(u, SLOTS)
        return remote(self.mine(u), self.ring_in.at[i], self.sems.at[0, i], self.sems.at[1, i], self.here.pair)

    def across(self, u):
        i = lax.rem(u, SLOTS)
        return remote(self.mine(u), self.ring_mid.at[i], self.sems.at[2, i], self.sems.at[3, i], self.here.middle)

    def outward(self, u):
        i = lax.rem(u, SLOTS)
        return remote(self.total.at[i], self.ring_in.at[i], self.sems.at[4, i], self.sems.at[5, i], self.here.pair)

    def store(self, u, ring):
        i, block = lax.rem(u, SLOTS), u // PIECES
        second = block < LATER
        t = pick(second, block // 4, (block - LATER) // 6)
        cols = pl.ds(pl.multiple_of(t * self.third, LANES), self.third)
        to = self.out.at[self.product(block) + pick(second, 6, 0), self.rows_of(u), cols]
        return pltpu.make_async_copy(ring.at[i], to, self.sems.at[6, i])

    @staticmethod
    def product(block):
        k = lax.rem(block, 4)
        return pick(block < LATER, (k // 2) * 3 + lax.rem(k, 2), lax.rem(block, 6))

    def add(self, dst, a, b):
        def rows(r):
            at = pl.ds(r, ROWS)
            dst[at, :] = a[at, :] + b[at, :]

        tiles(self.rows, ROWS, rows)

    def offer(self, u):
        @pl.when(self.here.is_end)
        def _():
            @pl.when(u >= SLOTS)
            def _():
                pl.semaphore_wait(self.credit_in, 1)
                self.inward(u - SLOTS).wait_send()

            self.inward(u).start()

    def gather(self, u):
        i = lax.rem(u, SLOTS)
        self.inward(u).wait_recv()
        self.add(self.mine(u), self.mine(u), self.ring_in.at[i])

        @pl.when(u + SLOTS < self.units)
        def _():
            signal(self.credit_in, self.here.pair)

        @pl.when(u >= SLOTS)
        def _():
            pl.semaphore_wait(self.credit_mid, 1)
            self.across(u - SLOTS).wait_send()

        self.across(u).start()

    def finish(self, u):
        i = lax.rem(u, SLOTS)
        self.across(u).wait_recv()

        @pl.when(u >= SLOTS)
        def _():
            pl.semaphore_wait(self.credit_out, 1)
            self.outward(u - SLOTS).wait_send()
            self.store(u - SLOTS, self.total).wait()

        self.add(self.total.at[i], self.mine(u), self.ring_mid.at[i])

        @pl.when(u + SLOTS < self.units)
        def _():
            signal(self.credit_mid, self.here.middle)

        self.outward(u).start()
        self.store(u, self.total).start()

    def accept(self, u):
        self.outward(u).wait_recv()
        self.store(u, self.ring_in).start()

        @pl.when(u > 0)
        def _():
            self.store(u - 1, self.ring_in).wait()

            @pl.when(u - 1 + SLOTS < self.units)
            def _():
                signal(self.credit_out, self.here.pair)

    def tick(self, n):
        @pl.when(self.here.is_centre)
        def _():
            @pl.when(n < self.units)
            def _():
                self.gather(n)

            @pl.when(both(n >= BEHIND, n < self.units + BEHIND))
            def _():
                self.finish(n - BEHIND)

        @pl.when(n + AHEAD < self.units)
        def _():
            self.offer(n + AHEAD)

        @pl.when(n >= BEHIND + 2)
        def _():
            @pl.when(self.here.is_end)
            def _():
                self.accept(n - BEHIND - 2)

    def drain(self):
        @pl.when(self.here.is_centre)
        def _():
            for u in range(self.units - SLOTS, self.units):
                self.across(u).wait_send()
                self.outward(u).wait_send()
                self.store(u, self.total).wait()

        @pl.when(self.here.is_end)
        def _():
            for u in range(self.units - SLOTS, self.units):
                self.inward(u).wait_send()
            self.store(self.units - 1, self.ring_in).wait()


class RankSum:
    def __init__(self, here, part, pairs, wide_x, wide_y, last_x, last_y, sems):
        self.here, self.part, self.pairs = here, part, pairs
        self.wide_x, self.wide_y, self.last_x, self.last_y, self.sems = wide_x, wide_y, last_x, last_y, sems
        self.count = part.shape[3]
        self.half = self.count // 2
        self.upper, self.lower = pl.ds(0, self.half), pl.ds(self.half, self.half)

    def copy(self, k, s, src, dst, target):
        return remote(src, dst, self.sems.at[s, k, 0], self.sems.at[s, k, 1], target)

    def swap(self, s):
        return self.copy(0, s, self.part.at[:, :, 1 - self.here.c], self.pairs.at[s], self.here.core)

    def wide(self, s):
        h = self.here
        return (
            self.copy(1, s, self.pairs.at[s, :, 1 - h.x, self.upper], self.wide_x.at[s], h.across_x),
            self.copy(2, s, self.pairs.at[s, 1 - h.y, :, self.lower], self.wide_y.at[s], h.across_y),
        )

    def last(self, s):
        h = self.here
        return (
            self.copy(3, s, self.pairs.at[s, 1 - h.y, h.x, self.upper], self.last_y.at[s], h.across_y),
            self.copy(4, s, self.pairs.at[s, h.y, 1 - h.x, self.lower], self.last_x.at[s], h.across_x),
        )

    def start(self, s):
        self.swap(s).start()

    def cross(self, s):
        h = self.here
        self.swap(s).wait()

        def some(r):
            at = pl.ds(r, 8)
            for y in range(2):
                for x in range(2):
                    self.pairs[s, y, x, at] = self.pairs[s, y, x, at] + self.part[y, x, h.c, at]

        tiles(self.count, 8, some)
        for copy in self.wide(s):
            copy.start()

    def turn(self, s):
        h = self.here
        for copy in self.wide(s):
            copy.wait()

        def some(r):
            at, low = pl.ds(r, 8), pl.ds(self.half + r, 8)
            for k in range(2):
                self.pairs[s, k, h.x, at] = self.pairs[s, k, h.x, at] + self.wide_x[s, k, at]
                self.pairs[s, h.y, k, low] = self.pairs[s, h.y, k, low] + self.wide_y[s, k, at]

        tiles(self.half, 8, some)
        for copy in self.last(s):
            copy.start()

    def done(self, s, down, put):
        h = self.here
        for copy in self.last(s):
            copy.wait()

        def some(r):
            at, low = pl.ds(r, down), pl.ds(self.half + r, down)
            first = pl.multiple_of(r // down * LANES, LANES)
            put(first, (self.pairs[s, h.y, h.x, at] + self.last_y[s, at]).reshape(down * 16, LANES))
            first = pl.multiple_of((self.half + r) // down * LANES, LANES)
            put(first, (self.pairs[s, h.y, h.x, low] + self.last_x[s, at]).reshape(down * 16, LANES))

        tiles(self.half, down, some)


def backward_kernel(seqs, hidden, length, width, *refs):
    third = width // THIRDS
    d_in, h1_in, x_in, w2_in, w1_in, pre_in, cell_in, h_in, sel_in, dsel_in, db2 = refs[:11]
    gw_out, gx_out, h_out, sel_out, wo_out, db_out = refs[11:17]
    dv, wv, rh, rx, pre, cell, work, edge, grad, gxv, dsel, wo, heard, hv, db1, dbv = refs[17:33]
    own, ring_in, ring_mid, total, part, pairs, wide_x, wide_y, last_x, last_y = refs[33:43]
    zsem, rsem, dsem, hsem, psem, lsem, credit_in, credit_mid, credit_out, ready = refs[43:]
    here = Here()
    ar = SeqSum(here, hidden, third, own, ring_in, ring_mid, total, gw_out, zsem, (credit_in, credit_mid, credit_out))
    sums = {
        layer: RankSum(here, part, pairs, wide_x, wide_y, last_x, last_y, rsem.at[layer - 1]) for layer in (1, 2)
    }
    groups, piece = length // LANES, LANES // 8
    half = width // 2

    def columns_of(s):
        return pl.ds(s * length, length)

    def load(src, dst, k):
        return pltpu.make_async_copy(src, dst, lsem.at[k])

    def load_d(k):
        rows = pl.ds(k * hidden, hidden)
        if not isinstance(k, int):
            rows = pl.ds(pl.multiple_of(k * hidden, 16), hidden)
        return load(d_in.at[rows], dv.at[rows], k)

    def load_rhs(layer, t):
        at = pl.ds(t * third, third)
        return load(h1_in.at[at], rh, 6) if layer == 2 else load(x_in.at[:, at], rx, 7)

    load_w = {2: load(w2_in, wv, 8), 1: load(w1_in, wv, 8)}
    load_p, load_c, load_e = load(pre_in, pre, 9), load(cell_in, cell, 10), load(dsel_in, dsel, 11)
    keep = load(sel_in, sel_out.at[:, pl.ds(here.b * hidden, hidden)], 12)
    store_g = load(gxv, gx_out, 13)
    store_h = load(hv, h_out, 14)
    load_rhs(2, 0).start()
    for k in range(6):
        load_d(k).start()
    load_w[2].start()
    load_rhs(1, 0).start()
    for copy in (load_p, load_c, load_e, keep):
        copy.start()
    meet(here.peers + here.line)

    def halves(start, i):
        size = hidden if i is None else hidden // 2
        return pl.ds(start + (i or 0) * size, size)

    gather = Gather(
        here,
        lambda b, i: sel_out.at[:, halves(b * hidden, i)],
        psem,
        lambda i: sel_in.at[:, halves(0, i)],
    )
    biases = [
        remote(dbv.at[here.z], dbv.at[here.z], dsem.at[d, 0], dsem.at[d, 1], peer)
        for d, peer in enumerate(here.line, 1)
    ]
    spread = [pltpu.make_async_copy(h_in.at[here.b], heard.at[here.b], hsem.at[0, 0])]
    for d, peer in enumerate(here.peers, 1):
        spread.append(remote(h_in.at[peer["tm"]], heard.at[here.b], hsem.at[d, 0], hsem.at[d, 1], peer))

    done, spent = [0], [0]

    def units(layer, t):
        count = 4 if layer == 2 else 6
        start = t * count + (LATER if layer == 1 else 0)
        assert start + count <= OWN or spent[0] > (start + count - OWN) * PIECES - 1 + SLOTS
        first = spent[0]

        def unit(k, carry):
            block = start + k
            product = ar.product(block)
            if start == 0:
                load_d(product).wait()
            rows = pl.ds(pl.multiple_of(product * hidden, 16), hidden)
            got = dot(dv[rows, :], rh[...], NT) if layer == 2 else dot(dv[rows, :], rx[...], NN)
            own[lax.rem(block, OWN)] = got.astype(BF16)
            if start == 0:
                for i in range(PIECES):
                    u = block * PIECES + i

                    @pl.when(u < AHEAD)
                    def _(u=u):
                        ar.offer(u)

            else:

                @pl.when(lax.rem(k, 2) == 1)
                def _():
                    ar.tick(first + k // 2)

            return carry

        lax.fori_loop(0, count, unit, 0)
        done[0] = (start + count) * PIECES
        if start:
            spent[0] += count // 2
            assert first + AHEAD < (start + 2) * PIECES and spent[0] - 1 + AHEAD < done[0]

    def tick(count=1):
        first = spent[0]
        spent[0] += count
        assert spent[0] - 1 + AHEAD < done[0] or done[0] == ar.units

        def step(n, carry):
            ar.tick(n)
            return carry

        lax.fori_loop(first, spent[0], step, 0)

    def strips(layer, s, q):
        if layer == 2:
            i, start = q // 2, lax.rem(q, 2) * (length // 2)
            down = hidden // 16
            lhs = pl.ds(pl.multiple_of(i * half, LANES), half)

            def strip(c):
                src = pl.ds(pl.multiple_of(s * length + start + c, 256), 256)
                got = dot(wv[:, lhs], dv[:, src], TN).astype(BF16)
                for n in range(2):
                    at = pl.ds(((start + c) // LANES + n) * down, down)
                    part[i, :, :, at] = got[:, n * LANES : (n + 1) * LANES].reshape(2, 2, down, 16, LANES)

            tiles(length // 2, 256, strip)
        else:

            def strip(c, carry):
                cols = pl.ds(pl.multiple_of(c * 256, 256), 256)
                got = dot(dv[:, columns_of(s)], wv[:, cols], TN).astype(BF16)
                for j in range(groups):
                    for n in range(2):
                        block = got[j * LANES : (j + 1) * LANES, n * LANES : (n + 1) * LANES]
                        part[:, :, :, (c * 2 + n) * groups + j] = block.reshape(2, 2, 2, piece, LANES)
                return carry

            count = width // 256
            lax.fori_loop(count * q // 4, count * (q + 1) // 4, strip, 0)

    def input_grad(layer, s):
        first = spent[0]
        spent[0] += 4
        assert spent[0] - 1 + AHEAD < done[0]

        def quarter(q, carry):
            strips(layer, s, q)
            ar.tick(first + q)
            return carry

        lax.fori_loop(0, 4, quarter, 0)

    def settle(layer, s):
        if layer == 2:

            def put(first, v):
                grad[:, pl.ds(s * length + first, LANES)] = v

            sums[2].done(s, hidden // 16, put)
        else:

            def put(first, v):
                gxv[s, :, pl.ds(first, LANES)] = v

            sums[1].done(s, groups, put)
            gxv[s] = dot(reorder(piece, groups, True), gxv[s], NN).astype(BF16)

    def pool(s):
        first = s * length
        pool_backward(first, grad, pre, cell, first, dv, db1.at[s], work, edge, hidden, groups)

    size = rh.shape[1] // 2

    def third_of(t):
        return pl.ds(pl.multiple_of(t * third, LANES), third)

    def load_picked(t, tap):
        return load(sel_out.at[tap, third_of(t)], rh.at[:, pl.ds(pl.multiple_of(tap * size, LANES), size)], 15 + tap)

    def store_o(t, tap):
        return load(wo.at[tap], wo_out.at[tap, :, third_of(t)], 17 + tap)

    def outgate():
        first = spent[0]
        spent[0] += 6

        def step(i, carry):
            t, tap = i // 2, lax.rem(i, 2)
            load_picked(t, tap).wait()

            @pl.when(t > 0)
            def _():
                store_o(t - 1, tap).wait()

            values = rh[:, pl.ds(pl.multiple_of(tap * size, LANES), size)]
            wo[tap] = dot(dsel[...], values, NT).astype(BF16)
            store_o(t, tap).start()

            @pl.when(t + 1 < THIRDS)
            def _():
                load_picked(t + 1, tap).start()

            ar.tick(first + i)
            return carry

        lax.fori_loop(0, 2 * THIRDS, step, 0)

    load_rhs(2, 0).wait()
    units(2, 0)
    load_rhs(2, 1).start()
    load_d(2).wait()
    load_d(5).wait()
    load_w[2].wait()
    input_grad(2, 0)
    sums[2].start(0)
    tick()
    load_rhs(2, 1).wait()
    units(2, 1)
    load_rhs(2, 2).start()
    sums[2].cross(0)
    tick()
    input_grad(2, 1)
    load_w[1].start()
    sums[2].start(1)
    tick()
    sums[2].turn(0)
    tick()
    load_rhs(2, 2).wait()
    units(2, 2)
    sums[2].cross(1)
    tick()
    settle(2, 0)
    tick(2)
    load_p.wait()
    load_c.wait()
    pool(0)
    tick(2)
    sums[2].turn(1)
    gather.start()
    tick(2)
    settle(2, 1)
    for target in (here.core, here.across_x, here.across_y):
        signal(ready, target)
    pool(1)
    tick(2)
    load_rhs(1, 0).wait()
    units(1, 0)
    gather.relay()
    load_rhs(1, 1).start()
    dbv[here.z] = jnp.zeros((8, hidden), F32)
    for row, db in enumerate((db1, db2)):
        dbv[here.z, row : row + 1, :] = to_row(sum(db[s] for s in range(1, seqs)) + db[0])
    for copy in biases:
        copy.start()
    load_w[1].wait()
    pl.semaphore_wait(ready, 3)
    input_grad(1, 0)
    sums[1].start(0)
    load_rhs(1, 1).wait()
    units(1, 1)
    load_rhs(1, 2).start()
    sums[1].cross(0)
    tick()
    input_grad(1, 1)
    sums[1].start(1)
    tick()
    gather.share()
    tick()
    sums[1].cross(1)
    tick()
    sums[1].turn(0)
    tick(5)
    load_rhs(1, 2).wait()
    units(1, 2)
    tick(2)
    settle(1, 0)
    sums[1].turn(1)
    keep.wait()
    load_e.wait()
    for tap in range(2):
        load_picked(0, tap).start()
    tick(2)
    for copy in spread:
        copy.start()
    tick(4)
    settle(1, 1)
    store_g.start()
    outgate()
    for copy in spread:
        copy.wait()
    back = reorder(piece, groups, True)
    for s in range(seqs):
        for b in range(8):
            block = heard[b, pl.ds(s * LANES, LANES), :]
            hv[s, :, b * hidden : (b + 1) * hidden] = dot(back, block, NN).astype(BF16)
    store_h.start()

    def more(n, carry):
        ar.tick(n)
        return carry

    lax.fori_loop(spent[0], ar.units + BEHIND + 2, more, 0)
    ar.drain()
    gather.drain()
    for copy in [store_g, store_h] + [store_o(THIRDS - 1, tap) for tap in range(2)] + biases:
        copy.wait()
    db_out[...] = dbv[0] + dbv[1] + dbv[2] + dbv[3]


def run_backward(d, h1, x, w2, w1, pre, cell, h, sel, dsel, db):
    (wide, width), total, seqs = w1.shape, d.shape[1], db.shape[0]
    hidden, length = wide // 6, total // seqs
    third, span, picked = width // THIRDS, length // 8, dsel.shape[1]
    rows, count = hidden // PIECES, length // 16 * hidden // LANES
    assert picked == length and length == 8 * LANES
    vmem = pl.BlockSpec(memory_space=pltpu.VMEM)
    scratch = [
        pltpu.VMEM((wide, total), BF16),
        pltpu.VMEM((wide, width), BF16),
        pltpu.VMEM((third, total), BF16),
        pltpu.VMEM((total, third), BF16),
        pltpu.VMEM((3 * hidden, total), BF16),
        pltpu.VMEM((hidden, total), F32),
        pltpu.VMEM((2, hidden, length), F32),
        pltpu.VMEM((2, hidden, LANES), F32),
        pltpu.VMEM((hidden, total), BF16),
        pltpu.VMEM((seqs, span, width), BF16),
        pltpu.VMEM((hidden, picked), BF16),
        pltpu.VMEM((2, hidden, third), BF16),
        pltpu.VMEM(h.shape, BF16),
        pltpu.VMEM((seqs, span, width), BF16),
        pltpu.VMEM((seqs, hidden, 1), F32),
        pltpu.VMEM((4, 8, hidden), F32),
        pltpu.VMEM((OWN, hidden, third), BF16),
        pltpu.VMEM((SLOTS, rows, third), BF16),
        pltpu.VMEM((SLOTS, rows, third), BF16),
        pltpu.VMEM((SLOTS, rows, third), BF16),
        pltpu.VMEM((2, 2, 2, count, 16, LANES), BF16),
        pltpu.VMEM((seqs, 2, 2, count, 16, LANES), BF16),
        pltpu.VMEM((seqs, 2, count // 2, 16, LANES), BF16),
        pltpu.VMEM((seqs, 2, count // 2, 16, LANES), BF16),
        pltpu.VMEM((seqs, count // 2, 16, LANES), BF16),
        pltpu.VMEM((seqs, count // 2, 16, LANES), BF16),
        pltpu.SemaphoreType.DMA((7, SLOTS)),
        pltpu.SemaphoreType.DMA((2, seqs, 5, 2)),
        pltpu.SemaphoreType.DMA((4, 2)),
        pltpu.SemaphoreType.DMA((8, 2)),
        pltpu.SemaphoreType.DMA((11, 2)),
        pltpu.SemaphoreType.DMA((19,)),
    ]
    return pl.pallas_call(
        functools.partial(backward_kernel, seqs, hidden, length, width),
        name="backward",
        in_specs=[ANY] * 10 + [vmem],
        out_specs=[ANY] * 5 + [vmem],
        out_shape=[
            shape((12, hidden, width), BF16),
            shape((seqs, span, width), BF16),
            shape((seqs, span, width), BF16),
            shape((2, width, picked), BF16),
            shape((2, hidden, width), BF16),
            shape((8, hidden), F32),
        ],
        scratch_shapes=scratch + [pltpu.SemaphoreType.REGULAR] * 4,
        compiler_params=params(collective_id=1, has_side_effects=True),
    )(d, h1, x, w2, w1, pre, cell, h, sel, dsel, db)


def reorder(piece, groups, back):
    span = piece * groups
    a = lax.broadcasted_iota(jnp.int32, (span, span), 1 if back else 0)
    b = lax.broadcasted_iota(jnp.int32, (span, span), 0 if back else 1)
    return (b == lax.rem(a, piece) * groups + a // piece).astype(BF16)


def to_row(column):
    n = column.shape[0]
    same = lax.broadcasted_iota(jnp.int32, (n, n), 0) == lax.broadcasted_iota(jnp.int32, (n, n), 1)
    return jnp.sum(jnp.where(same, column, 0.0), axis=0, keepdims=True)


def to_column(row):
    n = row.shape[1]
    same = lax.broadcasted_iota(jnp.int32, (n, n), 0) == lax.broadcasted_iota(jnp.int32, (n, n), 1)
    return jnp.sum(jnp.where(same, row, 0.0), axis=1, keepdims=True)


class Gather:
    def __init__(self, here, region, sems, own=None):
        h, b = here, here.b
        own = own or (lambda half: region(b, half))
        bx, by = h.across_x["tm"], h.across_y["tm"]
        bd = bx + 4 - 8 * h.y
        plan = (
            (b, 1, h.across_x),
            (b, 0, h.across_y),
            (b, 0, h.across_x),
            (b, 1, h.across_y),
            (b, None, h.core),
            (bx, 1, h.across_y),
            (by, 0, h.across_x),
            (bx, None, h.core),
            (by, None, h.core),
            (bd, 0, h.core),
            (bd, 1, h.core),
        )
        self.copies = []
        for k, (block, half, to) in enumerate(plan):
            src = own(half) if k < 5 else region(block, half)
            self.copies.append(remote(src, region(block, half), sems.at[k, 0], sems.at[k, 1], to))

    def start(self):
        for k in range(5):
            self.copies[k].start()

    def relay(self):
        self.copies[0].wait_recv()
        self.copies[5].start()
        self.copies[1].wait_recv()
        self.copies[6].start()

    def share_near(self):
        self.copies[2].wait_recv()
        self.copies[7].start()
        self.copies[4].wait_recv()
        self.copies[7].wait_recv()

    def share_far(self):
        self.copies[3].wait_recv()
        self.copies[8].start()
        self.copies[6].wait_recv()
        self.copies[9].start()
        self.copies[5].wait_recv()
        self.copies[10].start()
        for k in (8, 9, 10):
            self.copies[k].wait_recv()

    def share(self):
        self.share_near()
        self.share_far()

    def drain(self):
        for copy in self.copies:
            copy.wait_send()


def forward_kernel(seqs, hidden, length, width, *refs):
    x_in, w1_in, w2_in, cot_in, b1_in, b2_in, starts = refs[:7]
    x_out, h1_out, pre_out, cell_out, h2_out, d_out, db_out, sel_out, dsel_out = refs[7:16]
    xg, hg, w, p, pre, cell, work, edge, dv, seed, grad, hv, h2t, raw, cot, sent, b1, b2, chosen, sel, dsel = refs[16:37]
    xsem, hsem, ssem, zsem, lsem = refs[37:]
    here = Here()
    groups = length // LANES
    piece = LANES // 8

    def columns_of(s):
        return pl.ds(aligned(s * length), length)

    def x_region(s):
        def region(b, half):
            js = pl.ds(0, groups) if half is None else pl.ds(half * (groups // 2), groups // 2)
            return xg.at[s, js, b]

        return region

    def h_region(s):
        def region(b, half):
            rows = pl.ds(0, hidden) if half is None else pl.ds(half * (hidden // 2), hidden // 2)
            return hg.at[b, rows, columns_of(s)]

        return region

    def load(src, dst, k):
        return pltpu.make_async_copy(src, dst, lsem.at[k])

    load_w1 = load(w1_in, w, 0)
    load_w2 = load(w2_in, w, 0)
    load_x = [load(x_in.at[s], raw.at[s], 1 + s) for s in range(seqs)]
    load_c = load(cot_in, cot, 14)
    store_x = [load(xg.at[s], x_out.at[s], 3 + s) for s in range(seqs)]
    store_h = [load(hg.at[:, :, columns_of(s)], h1_out.at[:, :, columns_of(s)], 5 + s) for s in range(seqs)]
    store_p = [load(pre.at[:, columns_of(s)], pre_out.at[:, columns_of(s)], 7 + s) for s in range(seqs)]
    store_c = [load(cell.at[:, columns_of(s)], cell_out.at[:, columns_of(s)], 9 + s) for s in range(seqs)]

    def store_d(s):
        return load(dv.at[s], d_out.at[:, columns_of(s)], 11 + s)

    store_o = load(h2t, h2_out, 13)

    for copy in load_x:
        copy.start()
    load_w1.start()
    load_c.start()
    order = reorder(piece, groups, False)

    def place():
        for s in range(seqs):
            load_x[s].wait()
            xg[s, :, here.b] = dot(order, raw[s], NN).astype(BF16).reshape(groups, piece, width)

    meet(here.peers + here.line, place)
    xs = [Gather(here, x_region(s), xsem.at[s]) for s in range(seqs)]
    hs = [Gather(here, h_region(s), hsem.at[s]) for s in range(seqs)]

    def prepare():
        load_c.wait()
        for s in range(seqs):
            turned = dot(order, cot[s], NN).astype(BF16)
            for b in range(8):
                block = turned[:, b * hidden : (b + 1) * hidden]
                sent[b, s] = block.reshape(groups, piece, hidden)
        seed[:, :, pl.ds(0, 4)] = jnp.zeros((seqs, groups, 4, piece, hidden), BF16)
        for s in range(seqs):
            prepare_pick(s)
        b1[...] = to_column(b1_in[...][None, :])
        b2[...] = to_column(b2_in[...][None, :])

    late = [
        (remote(sent.at[peer["tm"]], seed.at[:, :, here.b], ssem.at[d, 0], ssem.at[d, 1], peer), peer)
        for d, peer in enumerate(here.peers, 1)
    ]

    def first_products(s):
        def block(r):
            rows = pl.ds(r, hidden)
            p[rows, :] = dot(w[rows, :], xg[s].reshape(length, width), NT)

        tiles(6 * hidden, hidden, block)

    def second_products(s, near):
        y = here.y if near else 1 - here.y
        depth = pl.ds(pl.multiple_of(y * (width // 2), LANES), width // 2)

        def block(r):
            rows = pl.ds(r, hidden)
            rhs = hg[pl.ds(y * 4, 4), :, columns_of(s)].reshape(width // 2, length)
            got = dot(w[rows, depth], rhs, NN)
            p[rows, :] = got if near else p[rows, :] + got

        tiles(6 * hidden, hidden, block)

    def first_pool(s):
        first = s * length
        pool_forward(first, p, b1, pre, cell, first, hg.at[here.b], work.at[0], edge.at[0], hidden, groups)

    def second_pool(s):
        pool_forward(s * length, p, b2, pre, cell, 0, hv, work.at[0], edge.at[0], hidden, groups)
        rows = lax.broadcasted_iota(jnp.int32, (LANES, LANES), 0)
        cols = lax.broadcasted_iota(jnp.int32, (LANES, LANES), 1)
        eye = (rows == cols).astype(BF16)
        for j in range(groups):
            turned = dot(eye, hv[:, pl.ds(j * LANES, LANES)], NT).astype(BF16)
            at = pl.ds((s * groups + j) * piece, piece)
            h2t[:, at, :] = turned.reshape(8, piece, hidden)

    def incoming(s):
        rows = lax.broadcasted_iota(jnp.int32, (hidden, hidden), 0)
        cols = lax.broadcasted_iota(jnp.int32, (hidden, hidden), 1)
        eye = (rows == cols).astype(BF16)
        lane = lax.broadcasted_iota(jnp.int32, (1, LANES), 1)
        for j in range(groups):
            block = seed[s, j].reshape(LANES, hidden)
            turned = dot(eye, block, NT)
            step = lane * groups + j
            keep = jnp.zeros((1, LANES), jnp.bool_)
            for k in range(starts.shape[1]):
                begin = starts[s, k]
                keep = jnp.logical_or(keep, jnp.logical_and(step >= begin, step < begin + CLUSTER))
            keep = jnp.broadcast_to(keep, (hidden, LANES))
            grad[:, pl.ds(s * length + j * LANES, LANES)] = jnp.where(keep, turned, 0.0).astype(BF16)

    def pool_back(s):
        pool_backward(s * length, grad, pre, cell, 0, dv.at[s], db_out.at[s], work, edge, hidden, groups, True)
        store_d(s).start()

    def cluster_steps(s):
        lane = lax.broadcasted_iota(jnp.int32, (1, LANES), 1)
        step = lax.rem(lane, CLUSTER)
        for k in range(starts.shape[1]):
            step = step + jnp.where(lane // CLUSTER == k, starts[s, k], 0)
        return lane, step

    def prepare_pick(s):
        _, step = cluster_steps(s)
        for j in range(groups):
            code = lax.broadcasted_iota(jnp.int32, (LANES, LANES), 0) * groups + j
            at = pl.ds(j * LANES, LANES)
            chosen[s, at, pl.ds(0, LANES)] = (code == step).astype(BF16)
            chosen[s, at, pl.ds(LANES, LANES)] = (code == step - 1).astype(BF16)

    def held(s, count):
        start = here.z * (seqs * LANES) + s * LANES
        return pl.ds(pl.multiple_of(start, LANES), count * LANES)

    def pick_hidden(s):
        got = dot(hg[here.b, :, columns_of(s)], chosen[s], NN).astype(BF16)
        for tap in range(2):
            sel[tap, :, held(s, 1)] = got[:, tap * LANES : (tap + 1) * LANES]

    def pick_grad(s):
        lane, step = cluster_steps(s)
        again = jnp.zeros((1, LANES), jnp.bool_)
        for k in range(starts.shape[1] - 1):
            begin = starts[s, k]
            inside = jnp.logical_and(step >= begin, step < begin + CLUSTER)
            again = jnp.logical_or(again, jnp.logical_and(inside, lane // CLUSTER > k))
        got = dot(dv[s, pl.ds(2 * hidden, hidden), :], chosen[s, :, pl.ds(0, LANES)], NN)
        dsel[:, held(s, 1)] = jnp.where(jnp.broadcast_to(again, (hidden, LANES)), 0.0, got).astype(BF16)

    spread_h = []
    spread_d = []
    for d, peer in enumerate(here.line, 1):
        at = sel.at[:, :, held(0, seqs)]
        spread_h.append(remote(at, at, zsem.at[d, 0], zsem.at[d, 1], peer))
        at = dsel.at[:, held(0, seqs)]
        spread_d.append(remote(at, at, zsem.at[d, 2], zsem.at[d, 3], peer))
    store_s = load(sel, sel_out, 15)
    store_e = load(dsel, dsel_out, 16)

    xs[0].start()
    prepare()
    xs[0].relay()
    xs[1].start()
    xs[0].share()
    store_x[0].start()
    load_w1.wait()
    first_products(0)
    xs[1].relay()
    first_pool(0)
    hs[0].start()
    store_p[0].start()
    store_c[0].start()
    xs[1].share()
    store_x[1].start()
    first_products(1)
    load_w2.start()
    hs[0].relay()
    first_pool(1)
    hs[1].start()
    store_p[1].start()
    store_c[1].start()

    for s in range(seqs):
        pick_hidden(s)
    for copy in spread_h:
        copy.start()
    hs[0].share_near()
    load_w2.wait()
    second_products(0, True)
    hs[0].share_far()
    store_h[0].start()
    second_products(0, False)
    hs[1].relay()

    @pl.when(here.y == 1)
    def _():
        pltpu.make_async_copy(sent.at[here.b], seed.at[:, :, here.b], ssem.at[0, 0]).start()
        for copy, _ in late:
            copy.start()

    store_p[0].wait()
    store_c[0].wait()
    second_pool(0)
    hs[1].share_near()
    second_products(1, True)
    hs[1].share_far()
    store_h[1].start()
    second_products(1, False)
    store_p[1].wait()
    store_c[1].wait()
    second_pool(1)
    store_o.start()

    @pl.when(here.y == 1)
    def _():
        pltpu.make_async_copy(sent.at[here.b], seed.at[:, :, here.b], ssem.at[0, 0]).wait()
        for copy, _ in late:
            copy.wait_send()

    for d, (copy, _) in enumerate(late, 1):
        source = lax.rem(here.b + 8 - d, 8)

        @pl.when(source >= 4)
        def _(copy=copy):
            copy.wait_recv()

    for s in range(seqs):
        incoming(s)
        outgate_backward(s * length, grad, pre, cell, dv.at[s], hidden, groups)
        pick_grad(s)
    for copy in spread_d:
        copy.start()
    for copy in spread_h:
        copy.wait()
    store_s.start()

    def back(s, carry):
        pool_back(s)
        return carry

    lax.fori_loop(0, seqs, back, 0)
    for gather in xs + hs:
        gather.drain()
    for copy in spread_d:
        copy.wait()
    store_e.start()
    for copy in store_x + store_h + [store_d(s) for s in range(seqs)] + [store_o, store_s, store_e]:
        copy.wait()


def run_forward(x, w1, b1, w2, b2, cotangent, starts):
    seqs, span, width = x.shape
    hidden, length, piece = w1.shape[0] // 6, span * 8, LANES // 8
    groups = length // LANES
    total, picked = seqs * length, 4 * seqs * LANES
    assert starts.shape[1] * CLUSTER == LANES
    vmem = pl.BlockSpec(memory_space=pltpu.VMEM)
    return pl.pallas_call(
        functools.partial(forward_kernel, seqs, hidden, length, width),
        name="forward",
        in_specs=[ANY, ANY, ANY, ANY, vmem, vmem, pl.BlockSpec(memory_space=pltpu.SMEM)],
        out_specs=[ANY, ANY, ANY, ANY, ANY, ANY, vmem, ANY, ANY],
        out_shape=[
            shape((seqs, groups, 8, piece, width), BF16),
            shape((8, hidden, total), BF16),
            shape((3 * hidden, total), BF16),
            shape((hidden, total), F32),
            shape((8, seqs * groups * piece, hidden), BF16),
            shape((6 * hidden, total), BF16),
            shape((seqs, hidden, 1), F32),
            shape((2, hidden, picked), BF16),
            shape((hidden, picked), BF16),
        ],
        scratch_shapes=[
            pltpu.VMEM((seqs, groups, 8, piece, width), BF16),
            pltpu.VMEM((8, hidden, total), BF16),
            pltpu.VMEM((6 * hidden, width), BF16),
            pltpu.VMEM((6 * hidden, length), F32),
            pltpu.VMEM((3 * hidden, total), BF16),
            pltpu.VMEM((hidden, total), F32),
            pltpu.VMEM((2, hidden, length), F32),
            pltpu.VMEM((2, hidden, LANES), F32),
            pltpu.VMEM((seqs, 6 * hidden, length), BF16),
            pltpu.VMEM((seqs, groups, 8, piece, hidden), BF16),
            pltpu.VMEM((hidden, total), BF16),
            pltpu.VMEM((hidden, length), BF16),
            pltpu.VMEM((8, seqs * groups * piece, hidden), BF16),
            pltpu.VMEM((seqs, span, width), BF16),
            pltpu.VMEM((seqs, span, width), BF16),
            pltpu.VMEM((8, seqs, groups, piece, hidden), BF16),
            pltpu.VMEM((hidden, 1), F32),
            pltpu.VMEM((hidden, 1), F32),
            pltpu.VMEM((seqs, length, 2 * LANES), BF16),
            pltpu.VMEM((2, hidden, picked), BF16),
            pltpu.VMEM((hidden, picked), BF16),
            pltpu.SemaphoreType.DMA((seqs, 11, 2)),
            pltpu.SemaphoreType.DMA((seqs, 11, 2)),
            pltpu.SemaphoreType.DMA((8, 2)),
            pltpu.SemaphoreType.DMA((4, 4)),
            pltpu.SemaphoreType.DMA((17,)),
        ],
        compiler_params=params(collective_id=0, has_side_effects=True),
    )(x, w1, w2, cotangent, b1, b2, starts)


def finish_kernel(
    one_ref, two_ref, outgate_ref, h_ref, gx_ref, db_ref, wide_one_ref, wide_two_ref, h_out, gx_out, db1_out, db2_out
):
    i = pl.program_id(0)
    wide_one_ref[...] = one_ref[...].astype(F32)
    last = lax.rem(i, 3) == 2

    @pl.when(last)
    def _():
        wide_two_ref[...] = outgate_ref[...].astype(F32)

    @pl.when(jnp.logical_not(last))
    def _():
        wide_two_ref[...] = two_ref[...].astype(F32)

    h_out[...] = h_ref[...]
    gx_out[...] = gx_ref[...]
    db1_out[...] = db_ref[0]
    db2_out[...] = db_ref[1]


def finish(gw, outgate, h, gx, db):
    _, hidden, width = gw.shape
    total = h.shape[0] * h.shape[1]
    dims = (1, hidden, width)
    small = (total // 4, width)
    weights = pl.BlockSpec(dims, lambda i: (i, 0, 0))
    tokens = pl.BlockSpec(small, lambda i: (jnp.minimum(i, 3), 0))
    bias = pl.BlockSpec((hidden,), lambda i: (0,))
    return pl.pallas_call(
        finish_kernel,
        name="results",
        grid=(6,),
        in_specs=[
            weights,
            pl.BlockSpec(dims, lambda i: (6 + i - i % 3 // 2, 0, 0)),
            pl.BlockSpec(dims, lambda i: (i // 3, 0, 0)),
            tokens,
            tokens,
            pl.BlockSpec(db.shape, lambda i: (0, 0)),
        ],
        out_specs=[weights, weights, tokens, tokens, bias, bias],
        out_shape=[shape((6, hidden, width), F32)] * 2 + [shape((total, width), BF16)] * 2 + [shape((hidden,), F32)] * 2,
        compiler_params=params(),
    )(gw, gw, outgate, h.reshape(total, width), gx.reshape(total, width), db)


def per_device(line, inputs, weight_one, fbias_one, weight_two, fbias_two, cotangent, cluster_starts):
    seqs, span, width = inputs.shape
    count = lax.axis_size("tm")
    length = span * count
    groups = length // LANES
    piece = LANES // count
    hidden = weight_one.shape[2]
    total = seqs * length
    w1 = weight_one.reshape(6 * hidden, width)
    w2 = weight_two.reshape(6 * hidden, width)

    if line:
        x, h1, pre1, cell1, h2, d2, db2, *picked = run_forward(
            inputs, w1, fbias_one, w2, fbias_two, cotangent, cluster_starts
        )
        x, h1 = x.reshape(total, width), h1.reshape(width, total)
        gw, gx1, h2, _, wo, db = run_backward(d2, h1, x, w2, w1, pre1, cell1, h2, *picked, db2)
        gw1, gw2, h2, gx1, *db = finish(gw, wo, h2, gx1, db)
    else:
        x = inputs.reshape(seqs, piece, groups, width).transpose(0, 2, 1, 3)
        bias1, bias2 = fbias_one[:, None], fbias_two[:, None]
        seed = cotangent.reshape(seqs, piece, groups, count, hidden)
        steps = lax.axis_index("tm") * span + jnp.arange(span, dtype=jnp.int32)
        starts = cluster_starts[:, :, None]
        keep = jnp.any((steps >= starts) & (steps < starts + CLUSTER), axis=1)
        seed = jnp.where(keep.reshape(seqs, piece, groups, 1, 1), seed, jnp.zeros_like(seed))
        seed = lax.all_to_all(seed, "tm", split_axis=3, concat_axis=1, tiled=True)
        seed = seed.reshape(seqs, LANES, groups, hidden).transpose(3, 0, 2, 1).reshape(hidden, total)
        x = lax.all_gather(x, "tm", axis=2, tiled=True).reshape(total, width)
        pre1, cell1, h1 = run_first(seqs, w1, bias1, x)
        h1 = lax.all_gather(h1, "tm", axis=0, tiled=True)
        h2, d2, db2 = run_second(seqs, w2, bias2, h1, seed)
        h2 = h2.reshape(hidden, seqs, groups, count, piece)
        h2 = lax.all_to_all(h2, "tm", split_axis=3, concat_axis=0, tiled=True)
        h2 = h2.reshape(width, seqs, groups, piece).transpose(1, 3, 2, 0)
        gw2 = lax.psum(dot(d2, h1, NT).astype(BF16), "seq").astype(F32)
        gx2 = lax.psum_scatter(dot(w2, d2, TN).astype(BF16), "tm", scatter_dimension=0, tiled=True)
        d1, db1 = run_back(seqs, gx2, pre1, cell1)
        gw1 = lax.psum(dot(d1, x, NN).astype(BF16), "seq").astype(F32)
        gx1 = dot(d1, w1, TN).astype(BF16).reshape(seqs, groups, LANES, width)
        gx1 = lax.psum_scatter(gx1, "tm", scatter_dimension=2, tiled=True)
        gx1 = gx1.transpose(0, 2, 1, 3).reshape(seqs, span, width)
        db = lax.psum(jnp.stack([db1, db2]).sum(axis=(1, 3)), "seq")
    out, gx1 = h2.reshape(seqs, span, width), gx1.reshape(seqs, span, width)
    dims = weight_one.shape
    return (out, gx1, gw1.reshape(dims), db[0], gw2.reshape(dims), db[1])


def solution(mesh):
    placed = (
        P("seq", "tm", None),
        P(None, None, "tm", None),
        P("tm"),
        P(None, None, "tm", None),
        P("tm"),
        P("seq", "tm", None),
        P("seq", None),
    )
    return jax.shard_map(
        functools.partial(per_device, dict(mesh.shape) == {"seq": 4, "tm": 8}),
        mesh=mesh,
        in_specs=placed,
        out_specs=(
            P("seq", "tm", None),
            P("seq", "tm", None),
            P(None, None, "tm", None),
            P("tm"),
            P(None, None, "tm", None),
            P("tm"),
        ),
        check_vma=False,
    )
```

```python
import functools

import jax
import jax.numpy as jnp
from jax import lax
from jax.experimental import pallas as pl
from jax.experimental.pallas import tpu as pltpu
from jax.sharding import PartitionSpec as P

CLUSTER = 32
LANES = 128
ROWS = 48
F32 = jnp.float32
BF16 = jnp.bfloat16
ANY = pl.BlockSpec(memory_space=pl.ANY)
MESH = pl.DeviceIdType.MESH
NN = (((1,), (0,)), ((), ()))
NT = (((1,), (1,)), ((), ()))
TN = (((0,), (0,)), ((), ()))


def dot(a, b, dims):
    return lax.dot_general(a, b, dims, preferred_element_type=F32)


def sigmoid(v):
    return 1.0 / (1.0 + jnp.exp(-v))


def tiles(count, rows, body):
    def step(r, carry):
        body(pl.multiple_of(r * rows, rows))
        return carry

    lax.fori_loop(0, count // rows, step, 0)


def aligned(start):
    return start if isinstance(start, int) else pl.multiple_of(start, LANES)


def stretch(hidden):
    return 96 if hidden % 96 == 0 else ROWS


def shift_lanes(v, amount, lane, fill):
    moved = pltpu.roll(v, amount % LANES, axis=1)
    gone = lane < amount if amount > 0 else lane >= LANES + amount
    return jnp.where(gone, fill, moved)


def lane_chain(factor, value, lane, sign):
    step = 1
    while step < LANES:
        value = value + factor * shift_lanes(value, sign * step, lane, 0.0)
        factor = factor * shift_lanes(factor, sign * step, lane, 1.0)
        step *= 2
    return value


def pool_forward(first, p_ref, b_ref, pre_ref, cell_ref, target, h_ref, factor_ref, edge_ref, hidden, groups):
    size = stretch(hidden)
    lane = lax.broadcasted_iota(jnp.int32, (size, LANES), 1)

    def at(j, start=0):
        return pl.ds(start + j * LANES, LANES)

    def gates(r):
        rows = pl.ds(r, size)
        value = factor = None
        for j in range(groups):
            got = []
            for g in range(3):
                now = p_ref[pl.ds(g * hidden + r, size), at(j)]
                tap = pl.ds((3 + g) * hidden + r, size)
                if j:
                    past = p_ref[tap, at(j - 1)]
                else:
                    past = shift_lanes(p_ref[tap, at(groups - 1)], 1, lane, 0.0)
                total = now + past
                if g == 1:
                    total = total + b_ref[rows, :]
                total = total.astype(BF16)
                pre_ref[pl.ds(g * hidden + r, size), at(j, first)] = total
                got.append(total.astype(F32))
            forget = sigmoid(got[1])
            fresh = (1.0 - forget) * jnp.tanh(got[0])
            if j:
                value = forget * value + fresh
                factor = forget * factor
            else:
                value, factor = fresh, forget
            cell_ref[rows, at(j, first)] = value
            factor_ref[rows, at(j)] = factor

    tiles(hidden, size, gates)

    everywhere = lax.broadcasted_iota(jnp.int32, (hidden, LANES), 1)
    value = lane_chain(factor_ref[:, at(groups - 1)], cell_ref[:, at(groups - 1, first)], everywhere, 1)
    edge_ref[...] = shift_lanes(value, 1, everywhere, 0.0)

    def finish(r):
        rows = pl.ds(r, size)
        edge = edge_ref[rows, :]
        for j in range(groups):
            cell = cell_ref[rows, at(j, first)] + factor_ref[rows, at(j)] * edge
            cell_ref[rows, at(j, first)] = cell
            outgate = sigmoid(pre_ref[pl.ds(2 * hidden + r, size), at(j, first)].astype(F32))
            h_ref[rows, at(j, target)] = (outgate * cell).astype(BF16)

    tiles(hidden, size, finish)


def put_gate(d_ref, g, r, j, v, target, lane, hidden, groups):
    rows = v.shape[0]
    d_ref[pl.ds(g * hidden + r, rows), pl.ds(target + j * LANES, LANES)] = v
    tap = pl.ds((3 + g) * hidden + r, rows)
    if j:
        d_ref[tap, pl.ds(target + (j - 1) * LANES, LANES)] = v
    else:
        moved = shift_lanes(v.astype(F32), -1, lane, 0.0).astype(BF16)
        d_ref[tap, pl.ds(target + (groups - 1) * LANES, LANES)] = moved


def outgate_backward(first, g_ref, pre_ref, cell_ref, d_ref, hidden, groups):
    size = stretch(hidden)
    lane = lax.broadcasted_iota(jnp.int32, (size, LANES), 1)

    def body(r):
        rows = pl.ds(r, size)
        for j in range(groups):
            at = pl.ds(first + j * LANES, LANES)
            outgate = sigmoid(pre_ref[pl.ds(2 * hidden + r, size), at].astype(F32))
            v = g_ref[rows, at].astype(F32) * cell_ref[rows, at] * outgate * (1.0 - outgate)
            put_gate(d_ref, 2, r, j, v.astype(BF16), 0, lane, hidden, groups)

    tiles(hidden, size, body)


def pool_backward(
    first, g_ref, pre_ref, cell_ref, target, d_ref, db_ref, work_ref, edge_ref, hidden, groups, carried_only=False
):
    size = stretch(hidden)
    lane = lax.broadcasted_iota(jnp.int32, (size, LANES), 1)

    def at(j, start=0):
        return pl.ds(aligned(start + j * LANES), LANES)

    def gate(g, r, j):
        return pre_ref[pl.ds(g * hidden + r, size), at(j, first)].astype(F32)

    def start(r):
        rows = pl.ds(r, size)
        later = value = factor = None
        for j in reversed(range(groups)):
            own = g_ref[rows, at(j, first)].astype(F32) * sigmoid(gate(2, r, j))
            if later is None:
                value, factor = own, jnp.ones_like(own)
            else:
                value = own + later * value
                factor = later * factor
            work_ref[0, rows, at(j)] = value
            work_ref[1, rows, at(j)] = factor
            later = sigmoid(gate(1, r, j))
        edge_ref[0, rows, :] = later * value
        edge_ref[1, rows, :] = later * factor

    tiles(hidden, size, start)

    everywhere = lax.broadcasted_iota(jnp.int32, (hidden, LANES), 1)
    value = lane_chain(edge_ref[1], edge_ref[0], everywhere, -1)
    edge_ref[0] = shift_lanes(value, -1, everywhere, 0.0)

    def finish(r):
        rows = pl.ds(r, size)
        edge = edge_ref[0, rows, :]
        total = jnp.zeros((size, LANES), F32)
        before = shift_lanes(cell_ref[rows, at(groups - 1, first)], 1, lane, 0.0)
        for j in range(groups):
            carried = work_ref[0, rows, at(j)] + work_ref[1, rows, at(j)] * edge
            candidate = jnp.tanh(gate(0, r, j))
            forget = sigmoid(gate(1, r, j))
            cell = cell_ref[rows, at(j, first)]
            keep = carried * (1.0 - forget)
            got = [keep * (1.0 - candidate * candidate), keep * forget * (before - candidate)]
            if not carried_only:
                outgate = sigmoid(gate(2, r, j))
                got.append(g_ref[rows, at(j, first)].astype(F32) * cell * outgate * (1.0 - outgate))
            before = cell
            for g, v in enumerate(got):
                v = v.astype(BF16)
                if g == 1:
                    total = total + v.astype(F32)
                put_gate(d_ref, g, r, j, v, target, lane, hidden, groups)
        db_ref[rows, :] = jnp.sum(total, axis=1, keepdims=True)

    tiles(hidden, size, finish)


def first_kernel(hidden, length, w_ref, b_ref, x_ref, pre_ref, cell_ref, h_ref, p_ref, work_ref, edge_ref):
    def strip(c):
        cols = pl.ds(c, 512)
        p_ref[:, cols] = dot(w_ref[...], x_ref[cols, :], NT)

    tiles(length, 512, strip)
    pool_forward(0, p_ref, b_ref, pre_ref, cell_ref, 0, h_ref, work_ref, edge_ref, hidden, length // LANES)


def second_kernel(
    hidden, length, w_ref, b_ref, x_ref, g_ref, h_ref, d_ref, db_ref, p_ref, pre_ref, cell_ref, work_ref, edge_ref
):
    def strip(c):
        cols = pl.ds(c, 512)
        p_ref[:, cols] = dot(w_ref[...], x_ref[:, cols], NN)

    tiles(length, 512, strip)
    groups = length // LANES
    pool_forward(0, p_ref, b_ref, pre_ref, cell_ref, 0, h_ref, work_ref.at[0], edge_ref.at[0], hidden, groups)
    pool_backward(0, g_ref, pre_ref, cell_ref, 0, d_ref, db_ref.at[0], work_ref, edge_ref, hidden, groups)


def back_kernel(hidden, length, g_ref, pre_ref, cell_ref, d_ref, db_ref, work_ref, edge_ref):
    pool_backward(0, g_ref, pre_ref, cell_ref, 0, d_ref, db_ref.at[0], work_ref, edge_ref, hidden, length // LANES)


def columns(rows, length):
    return pl.BlockSpec((rows, length), lambda s: (0, s))


def fixed(*dims):
    return pl.BlockSpec(dims, lambda s: (0,) * len(dims), pipeline_mode=pl.Buffered(1))


def params(**more):
    return pltpu.CompilerParams(vmem_limit_bytes=63 * 1024 * 1024, **more)


shape = jax.ShapeDtypeStruct


def run_first(seqs, weight, bias, gathered):
    (wide, width), total = weight.shape, gathered.shape[0]
    hidden, length = wide // 6, total // seqs
    return pl.pallas_call(
        functools.partial(first_kernel, hidden, length),
        name="layer_one_forward",
        grid=(seqs,),
        in_specs=[fixed(wide, width), fixed(hidden, 1), pl.BlockSpec((length, width), lambda s: (s, 0))],
        out_specs=[columns(3 * hidden, length), columns(hidden, length), columns(hidden, length)],
        out_shape=[shape((3 * hidden, total), BF16), shape((hidden, total), F32), shape((hidden, total), BF16)],
        scratch_shapes=[
            pltpu.VMEM((wide, length), F32),
            pltpu.VMEM((hidden, length), F32),
            pltpu.VMEM((hidden, LANES), F32),
        ],
        compiler_params=params(),
    )(weight, bias, gathered)


def run_second(seqs, weight, bias, gathered, grad):
    (wide, width), total = weight.shape, gathered.shape[1]
    hidden, length = wide // 6, total // seqs
    return pl.pallas_call(
        functools.partial(second_kernel, hidden, length),
        name="layer_two_forward_and_pool_backward",
        grid=(seqs,),
        in_specs=[fixed(wide, width), fixed(hidden, 1), columns(width, length), columns(hidden, length)],
        out_specs=[columns(hidden, length), columns(wide, length), pl.BlockSpec((1, hidden, 1), lambda s: (s, 0, 0))],
        out_shape=[shape((hidden, total), BF16), shape((wide, total), BF16), shape((seqs, hidden, 1), F32)],
        scratch_shapes=[
            pltpu.VMEM((wide, length), F32),
            pltpu.VMEM((3 * hidden, length), BF16),
            pltpu.VMEM((hidden, length), F32),
            pltpu.VMEM((2, hidden, length), F32),
            pltpu.VMEM((2, hidden, LANES), F32),
        ],
        compiler_params=params(),
    )(weight, bias, gathered, grad)


def run_back(seqs, grad, pre, cell):
    hidden, total = grad.shape
    length = total // seqs
    return pl.pallas_call(
        functools.partial(back_kernel, hidden, length),
        name="layer_one_pool_backward",
        grid=(seqs,),
        in_specs=[columns(hidden, length), columns(3 * hidden, length), columns(hidden, length)],
        out_specs=[columns(6 * hidden, length), pl.BlockSpec((1, hidden, 1), lambda s: (s, 0, 0))],
        out_shape=[shape((6 * hidden, total), BF16), shape((seqs, hidden, 1), F32)],
        scratch_shapes=[pltpu.VMEM((2, hidden, length), F32), pltpu.VMEM((2, hidden, LANES), F32)],
        compiler_params=params(),
    )(grad, pre, cell)


THIRDS = 3
PIECES = 3
SLOTS = 11
AHEAD = 6
BEHIND = 2
LATER = 12
BLOCKS = 30
OWN = 18


class Here:
    def __init__(self):
        self.z = lax.axis_index("seq")
        self.b = lax.axis_index("tm")
        self.c = lax.rem(self.b, 2)
        self.x = lax.rem(self.b // 2, 2)
        self.y = self.b // 4
        self.core = dict(seq=self.z, tm=self.b + 1 - 2 * self.c)
        self.across_x = dict(seq=self.z, tm=self.b + 2 - 4 * self.x)
        self.across_y = dict(seq=self.z, tm=self.b + 4 - 8 * self.y)
        self.pair = dict(seq=self.z + 1 - 2 * lax.rem(self.z, 2), tm=self.b)
        self.middle = dict(seq=3 - self.z, tm=self.b)
        self.line = [dict(seq=lax.rem(self.z + d, 4), tm=self.b) for d in range(1, 4)]
        self.peers = [dict(seq=self.z, tm=lax.rem(self.b + d, 8)) for d in range(1, 8)]
        self.is_end = jnp.logical_or(self.z == 0, self.z == 3)
        self.is_centre = jnp.logical_and(self.z > 0, self.z < 3)


def remote(src, dst, send, recv, target):
    return pltpu.make_async_remote_copy(
        src_ref=src, dst_ref=dst, send_sem=send, recv_sem=recv, device_id=target, device_id_type=MESH
    )


def both(a, b):
    if isinstance(a, bool) and isinstance(b, bool):
        return a and b
    return jnp.logical_and(a, b)


def signal(sem, target):
    pl.semaphore_signal(sem, inc=1, device_id=target, device_id_type=MESH)


def meet(targets, between=None):
    barrier = pltpu.get_barrier_semaphore()
    for target in targets:
        signal(barrier, target)
    if between is not None:
        between()
    pl.semaphore_wait(barrier, len(targets))


def pick(condition, a, b):
    if isinstance(condition, bool):
        return a if condition else b
    return jnp.where(condition, a, b)


class SeqSum:
    def __init__(self, here, hidden, third, own, ring_in, ring_mid, total, out, sems, credits):
        self.here, self.third, self.rows = here, third, hidden // PIECES
        self.units = BLOCKS * PIECES
        self.own, self.ring_in, self.ring_mid, self.total, self.out = own, ring_in, ring_mid, total, out
        self.sems = sems
        self.credit_in, self.credit_mid, self.credit_out = credits

    def rows_of(self, u):
        return pl.ds(pl.multiple_of(lax.rem(u, PIECES) * self.rows, 16), self.rows)

    def mine(self, u):
        return self.own.at[lax.rem(u // PIECES, OWN), self.rows_of(u)]

    def inward(self, u):
        i = lax.rem(u, SLOTS)
        return remote(self.mine(u), self.ring_in.at[i], self.sems.at[0, i], self.sems.at[1, i], self.here.pair)

    def across(self, u):
        i = lax.rem(u, SLOTS)
        return remote(self.mine(u), self.ring_mid.at[i], self.sems.at[2, i], self.sems.at[3, i], self.here.middle)

    def outward(self, u):
        i = lax.rem(u, SLOTS)
        return remote(self.total.at[i], self.ring_in.at[i], self.sems.at[4, i], self.sems.at[5, i], self.here.pair)

    def store(self, u, ring):
        i, block = lax.rem(u, SLOTS), u // PIECES
        second = block < LATER
        t = pick(second, block // 4, (block - LATER) // 6)
        cols = pl.ds(pl.multiple_of(t * self.third, LANES), self.third)
        to = self.out.at[self.product(block) + pick(second, 6, 0), self.rows_of(u), cols]
        return pltpu.make_async_copy(ring.at[i], to, self.sems.at[6, i])

    @staticmethod
    def product(block):
        k = lax.rem(block, 4)
        return pick(block < LATER, (k // 2) * 3 + lax.rem(k, 2), lax.rem(block, 6))

    def add(self, dst, a, b):
        def rows(r):
            at = pl.ds(r, ROWS)
            dst[at, :] = a[at, :] + b[at, :]

        tiles(self.rows, ROWS, rows)

    def offer(self, u):
        @pl.when(self.here.is_end)
        def _():
            @pl.when(u >= SLOTS)
            def _():
                pl.semaphore_wait(self.credit_in, 1)
                self.inward(u - SLOTS).wait_send()

            self.inward(u).start()

    def gather(self, u):
        i = lax.rem(u, SLOTS)
        self.inward(u).wait_recv()
        self.add(self.mine(u), self.mine(u), self.ring_in.at[i])

        @pl.when(u + SLOTS < self.units)
        def _():
            signal(self.credit_in, self.here.pair)

        @pl.when(u >= SLOTS)
        def _():
            pl.semaphore_wait(self.credit_mid, 1)
            self.across(u - SLOTS).wait_send()

        self.across(u).start()

    def finish(self, u):
        i = lax.rem(u, SLOTS)
        self.across(u).wait_recv()

        @pl.when(u >= SLOTS)
        def _():
            pl.semaphore_wait(self.credit_out, 1)
            self.outward(u - SLOTS).wait_send()
            self.store(u - SLOTS, self.total).wait()

        self.add(self.total.at[i], self.mine(u), self.ring_mid.at[i])

        @pl.when(u + SLOTS < self.units)
        def _():
            signal(self.credit_mid, self.here.middle)

        self.outward(u).start()
        self.store(u, self.total).start()

    def accept(self, u):
        self.outward(u).wait_recv()
        self.store(u, self.ring_in).start()

        @pl.when(u > 0)
        def _():
            self.store(u - 1, self.ring_in).wait()

            @pl.when(u - 1 + SLOTS < self.units)
            def _():
                signal(self.credit_out, self.here.pair)

    def tick(self, n):
        @pl.when(self.here.is_centre)
        def _():
            @pl.when(n < self.units)
            def _():
                self.gather(n)

            @pl.when(both(n >= BEHIND, n < self.units + BEHIND))
            def _():
                self.finish(n - BEHIND)

        @pl.when(n + AHEAD < self.units)
        def _():
            self.offer(n + AHEAD)

        @pl.when(n >= BEHIND + 2)
        def _():
            @pl.when(self.here.is_end)
            def _():
                self.accept(n - BEHIND - 2)

    def drain(self):
        @pl.when(self.here.is_centre)
        def _():
            for u in range(self.units - SLOTS, self.units):
                self.across(u).wait_send()
                self.outward(u).wait_send()
                self.store(u, self.total).wait()

        @pl.when(self.here.is_end)
        def _():
            for u in range(self.units - SLOTS, self.units):
                self.inward(u).wait_send()
            self.store(self.units - 1, self.ring_in).wait()


class RankSum:
    def __init__(self, here, part, pairs, wide_x, wide_y, last_x, last_y, sems):
        self.here, self.part, self.pairs = here, part, pairs
        self.wide_x, self.wide_y, self.last_x, self.last_y, self.sems = wide_x, wide_y, last_x, last_y, sems
        self.count = part.shape[3]
        self.half = self.count // 2
        self.upper, self.lower = pl.ds(0, self.half), pl.ds(self.half, self.half)

    def copy(self, k, s, src, dst, target):
        return remote(src, dst, self.sems.at[s, k, 0], self.sems.at[s, k, 1], target)

    def swap(self, s):
        return self.copy(0, s, self.part.at[:, :, 1 - self.here.c], self.pairs.at[s], self.here.core)

    def wide(self, s):
        h = self.here
        return (
            self.copy(1, s, self.pairs.at[s, :, 1 - h.x, self.upper], self.wide_x.at[s], h.across_x),
            self.copy(2, s, self.pairs.at[s, 1 - h.y, :, self.lower], self.wide_y.at[s], h.across_y),
        )

    def last(self, s):
        h = self.here
        return (
            self.copy(3, s, self.pairs.at[s, 1 - h.y, h.x, self.upper], self.last_y.at[s], h.across_y),
            self.copy(4, s, self.pairs.at[s, h.y, 1 - h.x, self.lower], self.last_x.at[s], h.across_x),
        )

    def start(self, s):
        self.swap(s).start()

    def cross(self, s):
        h = self.here
        self.swap(s).wait()

        def some(r):
            at = pl.ds(r, 8)
            for y in range(2):
                for x in range(2):
                    self.pairs[s, y, x, at] = self.pairs[s, y, x, at] + self.part[y, x, h.c, at]

        tiles(self.count, 8, some)
        for copy in self.wide(s):
            copy.start()

    def turn(self, s):
        h = self.here
        for copy in self.wide(s):
            copy.wait()

        def some(r):
            at, low = pl.ds(r, 8), pl.ds(self.half + r, 8)
            for k in range(2):
                self.pairs[s, k, h.x, at] = self.pairs[s, k, h.x, at] + self.wide_x[s, k, at]
                self.pairs[s, h.y, k, low] = self.pairs[s, h.y, k, low] + self.wide_y[s, k, at]

        tiles(self.half, 8, some)
        for copy in self.last(s):
            copy.start()

    def done(self, s, down, put):
        h = self.here
        for copy in self.last(s):
            copy.wait()

        def some(r):
            at, low = pl.ds(r, down), pl.ds(self.half + r, down)
            first = pl.multiple_of(r // down * LANES, LANES)
            put(first, (self.pairs[s, h.y, h.x, at] + self.last_y[s, at]).reshape(down * 16, LANES))
            first = pl.multiple_of((self.half + r) // down * LANES, LANES)
            put(first, (self.pairs[s, h.y, h.x, low] + self.last_x[s, at]).reshape(down * 16, LANES))

        tiles(self.half, down, some)


def backward_kernel(seqs, hidden, length, width, *refs):
    third = width // THIRDS
    d_in, h1_in, x_in, w2_in, w1_in, pre_in, cell_in, h_in, sel_in, dsel_in, db2 = refs[:11]
    gw_out, gx_out, h_out, sel_out, wo_out, db_out = refs[11:17]
    dv, wv, rh, rx, pre, cell, work, edge, grad, gxv, dsel, wo, heard, hv, db1, dbv, told = refs[17:34]
    own, ring_in, ring_mid, total, part, pairs, wide_x, wide_y, last_x, last_y = refs[34:44]
    zsem, rsem, dsem, hsem, psem, lsem, credit_in, credit_mid, credit_out, ready = refs[44:]
    here = Here()
    ar = SeqSum(here, hidden, third, own, ring_in, ring_mid, total, gw_out, zsem, (credit_in, credit_mid, credit_out))
    sums = {
        layer: RankSum(here, part, pairs, wide_x, wide_y, last_x, last_y, rsem.at[layer - 1]) for layer in (1, 2)
    }
    groups, piece = length // LANES, LANES // 8
    half = width // 2

    def columns_of(s):
        return pl.ds(s * length, length)

    def load(src, dst, k):
        return pltpu.make_async_copy(src, dst, lsem.at[k])

    def load_d(k):
        rows = pl.ds(k * hidden, hidden)
        if not isinstance(k, int):
            rows = pl.ds(pl.multiple_of(k * hidden, 16), hidden)
        return load(d_in.at[rows], dv.at[rows], k)

    def load_rhs(layer, t):
        at = pl.ds(t * third, third)
        return load(h1_in.at[at], rh, 6) if layer == 2 else load(x_in.at[:, at], rx, 7)

    load_w = {2: load(w2_in, wv, 8), 1: load(w1_in, wv, 8)}
    load_p, load_c, load_e = load(pre_in, pre, 9), load(cell_in, cell, 10), load(dsel_in, dsel, 11)
    keep = load(sel_in, sel_out.at[:, pl.ds(here.b * hidden, hidden)], 12)
    store_g = load(gxv, gx_out, 13)
    store_h = load(hv, h_out, 14)
    load_rhs(2, 0).start()
    for k in range(6):
        load_d(k).start()
    load_w[2].start()
    load_rhs(1, 0).start()
    for copy in (load_p, load_c, load_e, keep):
        copy.start()
    meet(here.peers + here.line)

    def halves(start, i):
        size = hidden if i is None else hidden // 2
        return pl.ds(start + (i or 0) * size, size)

    gather = Gather(
        here,
        lambda b, i: sel_out.at[:, halves(b * hidden, i)],
        psem,
        lambda i: sel_in.at[:, halves(0, i)],
    )
    biases = [
        remote(dbv.at[here.z], dbv.at[here.z], dsem.at[d, 0], dsem.at[d, 1], peer)
        for d, peer in enumerate(here.line, 1)
    ]
    load_h = load(h_in, grad, 19)
    spread = [pltpu.make_async_copy(told.at[here.b], heard.at[here.b], hsem.at[0, 0])]
    for d, peer in enumerate(here.peers, 1):
        spread.append(remote(told.at[peer["tm"]], heard.at[here.b], hsem.at[d, 0], hsem.at[d, 1], peer))

    done, spent = [0], [0]

    def units(layer, t):
        count = 4 if layer == 2 else 6
        start = t * count + (LATER if layer == 1 else 0)
        assert start + count <= OWN or spent[0] > (start + count - OWN) * PIECES - 1 + SLOTS
        first = spent[0]

        def unit(k, carry):
            block = start + k
            product = ar.product(block)
            if start == 0:
                load_d(product).wait()
            rows = pl.ds(pl.multiple_of(product * hidden, 16), hidden)
            got = dot(dv[rows, :], rh[...], NT) if layer == 2 else dot(dv[rows, :], rx[...], NN)
            own[lax.rem(block, OWN)] = got.astype(BF16)
            if start == 0:
                for i in range(PIECES):
                    u = block * PIECES + i

                    @pl.when(u < AHEAD)
                    def _(u=u):
                        ar.offer(u)

            else:

                @pl.when(lax.rem(k, 2) == 1)
                def _():
                    ar.tick(first + k // 2)

            return carry

        lax.fori_loop(0, count, unit, 0)
        done[0] = (start + count) * PIECES
        if start:
            spent[0] += count // 2
            assert first + AHEAD < (start + 2) * PIECES and spent[0] - 1 + AHEAD < done[0]

    def tick(count=1):
        first = spent[0]
        spent[0] += count
        assert spent[0] - 1 + AHEAD < done[0] or done[0] == ar.units

        def step(n, carry):
            ar.tick(n)
            return carry

        lax.fori_loop(first, spent[0], step, 0)

    def strips(layer, s, q):
        if layer == 2:
            i, start = q // 2, lax.rem(q, 2) * (length // 2)
            down = hidden // 16
            lhs = pl.ds(pl.multiple_of(i * half, LANES), half)

            def strip(c):
                src = pl.ds(pl.multiple_of(s * length + start + c, 256), 256)
                got = dot(wv[:, lhs], dv[:, src], TN).astype(BF16)
                for n in range(2):
                    at = pl.ds(((start + c) // LANES + n) * down, down)
                    part[i, :, :, at] = got[:, n * LANES : (n + 1) * LANES].reshape(2, 2, down, 16, LANES)

            tiles(length // 2, 256, strip)
        else:

            def strip(c, carry):
                cols = pl.ds(pl.multiple_of(c * 256, 256), 256)
                got = dot(dv[:, columns_of(s)], wv[:, cols], TN).astype(BF16)
                for j in range(groups):
                    for n in range(2):
                        block = got[j * LANES : (j + 1) * LANES, n * LANES : (n + 1) * LANES]
                        part[:, :, :, (c * 2 + n) * groups + j] = block.reshape(2, 2, 2, piece, LANES)
                return carry

            count = width // 256
            lax.fori_loop(count * q // 4, count * (q + 1) // 4, strip, 0)

    def input_grad(layer, s):
        first = spent[0]
        spent[0] += 4
        assert spent[0] - 1 + AHEAD < done[0]

        def quarter(q, carry):
            strips(layer, s, q)
            ar.tick(first + q)
            return carry

        lax.fori_loop(0, 4, quarter, 0)

    def settle(layer, s):
        if layer == 2:

            def put(first, v):
                grad[:, pl.ds(s * length + first, LANES)] = v

            sums[2].done(s, hidden // 16, put)
        else:

            def put(first, v):
                gxv[s, :, pl.ds(first, LANES)] = v

            sums[1].done(s, groups, put)
            gxv[s] = dot(reorder(piece, groups, True), gxv[s], NN).astype(BF16)

    def pool(s):
        first = s * length
        pool_backward(first, grad, pre, cell, first, dv, db1.at[s], work, edge, hidden, groups)

    size = rh.shape[1] // 2

    def third_of(t):
        return pl.ds(pl.multiple_of(t * third, LANES), third)

    def load_picked(t, tap):
        return load(sel_out.at[tap, third_of(t)], rh.at[:, pl.ds(pl.multiple_of(tap * size, LANES), size)], 15 + tap)

    def store_o(t, tap):
        return load(wo.at[tap], wo_out.at[tap, :, third_of(t)], 17 + tap)

    def outgate():
        first = spent[0]
        spent[0] += 6

        def step(i, carry):
            t, tap = i // 2, lax.rem(i, 2)
            load_picked(t, tap).wait()

            @pl.when(t > 0)
            def _():
                store_o(t - 1, tap).wait()

            values = rh[:, pl.ds(pl.multiple_of(tap * size, LANES), size)]
            wo[tap] = dot(dsel[...], values, NT).astype(BF16)
            store_o(t, tap).start()

            @pl.when(t + 1 < THIRDS)
            def _():
                load_picked(t + 1, tap).start()

            ar.tick(first + i)
            return carry

        lax.fori_loop(0, 2 * THIRDS, step, 0)

    load_rhs(2, 0).wait()
    units(2, 0)
    load_rhs(2, 1).start()
    load_d(2).wait()
    load_d(5).wait()
    load_w[2].wait()
    input_grad(2, 0)
    sums[2].start(0)
    tick()
    load_rhs(2, 1).wait()
    units(2, 1)
    load_rhs(2, 2).start()
    sums[2].cross(0)
    tick()
    input_grad(2, 1)
    load_w[1].start()
    sums[2].start(1)
    tick()
    sums[2].turn(0)
    tick()
    load_rhs(2, 2).wait()
    units(2, 2)
    sums[2].cross(1)
    tick()
    settle(2, 0)
    tick(2)
    load_p.wait()
    load_c.wait()
    pool(0)
    tick(2)
    sums[2].turn(1)
    gather.start()
    tick(2)
    settle(2, 1)
    for target in (here.core, here.across_x, here.across_y):
        signal(ready, target)
    pool(1)
    load_h.start()
    tick(2)
    load_rhs(1, 0).wait()
    units(1, 0)
    gather.relay()
    load_rhs(1, 1).start()
    dbv[here.z] = jnp.zeros((8, hidden), F32)
    for row, db in enumerate((db1, db2)):
        dbv[here.z, row : row + 1, :] = to_row(sum(db[s] for s in range(1, seqs)) + db[0])
    for copy in biases:
        copy.start()
    load_w[1].wait()
    pl.semaphore_wait(ready, 3)
    input_grad(1, 0)
    sums[1].start(0)
    load_rhs(1, 1).wait()
    units(1, 1)
    load_rhs(1, 2).start()
    sums[1].cross(0)
    tick()
    input_grad(1, 1)
    sums[1].start(1)
    tick()
    gather.share()
    tick()
    sums[1].cross(1)
    tick()
    sums[1].turn(0)
    tick(5)
    load_rhs(1, 2).wait()
    units(1, 2)
    tick(2)
    settle(1, 0)
    sums[1].turn(1)
    keep.wait()
    load_e.wait()
    for tap in range(2):
        load_picked(0, tap).start()
    tick(2)
    load_h.wait()
    eye = identity(LANES)
    for n in range(seqs * groups):
        turned = dot(eye, grad[:, pl.ds(n * LANES, LANES)], NT).astype(BF16)
        told[:, pl.ds(n * piece, piece), :] = turned.reshape(8, piece, hidden)
    for copy in spread:
        copy.start()
    tick(4)
    settle(1, 1)
    store_g.start()
    outgate()
    for copy in spread:
        copy.wait()
    back = reorder(piece, groups, True)
    for s in range(seqs):
        for b in range(8):
            block = heard[b, pl.ds(s * LANES, LANES), :]
            hv[s, :, b * hidden : (b + 1) * hidden] = dot(back, block, NN).astype(BF16)
    store_h.start()

    def more(n, carry):
        ar.tick(n)
        return carry

    lax.fori_loop(spent[0], ar.units + BEHIND + 2, more, 0)
    ar.drain()
    gather.drain()
    for copy in [store_g, store_h] + [store_o(THIRDS - 1, tap) for tap in range(2)] + biases:
        copy.wait()
    db_out[...] = dbv[0] + dbv[1] + dbv[2] + dbv[3]


def run_backward(d, h1, x, w2, w1, pre, cell, h, sel, dsel, db):
    (wide, width), total, seqs = w1.shape, d.shape[1], db.shape[0]
    hidden, length = wide // 6, total // seqs
    third, span, picked = width // THIRDS, length // 8, dsel.shape[1]
    rows, count = hidden // PIECES, length // 16 * hidden // LANES
    assert picked == length and length == 8 * LANES
    vmem = pl.BlockSpec(memory_space=pltpu.VMEM)
    scratch = [
        pltpu.VMEM((wide, total), BF16),
        pltpu.VMEM((wide, width), BF16),
        pltpu.VMEM((third, total), BF16),
        pltpu.VMEM((total, third), BF16),
        pltpu.VMEM((3 * hidden, total), BF16),
        pltpu.VMEM((hidden, total), F32),
        pltpu.VMEM((2, hidden, length), F32),
        pltpu.VMEM((2, hidden, LANES), F32),
        pltpu.VMEM((hidden, total), BF16),
        pltpu.VMEM((seqs, span, width), BF16),
        pltpu.VMEM((hidden, picked), BF16),
        pltpu.VMEM((2, hidden, third), BF16),
        pltpu.VMEM((8, total // 8, hidden), BF16),
        pltpu.VMEM((seqs, span, width), BF16),
        pltpu.VMEM((seqs, hidden, 1), F32),
        pltpu.VMEM((4, 8, hidden), F32),
        pltpu.VMEM((8, total // 8, hidden), BF16),
        pltpu.VMEM((OWN, hidden, third), BF16),
        pltpu.VMEM((SLOTS, rows, third), BF16),
        pltpu.VMEM((SLOTS, rows, third), BF16),
        pltpu.VMEM((SLOTS, rows, third), BF16),
        pltpu.VMEM((2, 2, 2, count, 16, LANES), BF16),
        pltpu.VMEM((seqs, 2, 2, count, 16, LANES), BF16),
        pltpu.VMEM((seqs, 2, count // 2, 16, LANES), BF16),
        pltpu.VMEM((seqs, 2, count // 2, 16, LANES), BF16),
        pltpu.VMEM((seqs, count // 2, 16, LANES), BF16),
        pltpu.VMEM((seqs, count // 2, 16, LANES), BF16),
        pltpu.SemaphoreType.DMA((7, SLOTS)),
        pltpu.SemaphoreType.DMA((2, seqs, 5, 2)),
        pltpu.SemaphoreType.DMA((4, 2)),
        pltpu.SemaphoreType.DMA((8, 2)),
        pltpu.SemaphoreType.DMA((11, 2)),
        pltpu.SemaphoreType.DMA((20,)),
    ]
    return pl.pallas_call(
        functools.partial(backward_kernel, seqs, hidden, length, width),
        name="backward",
        in_specs=[ANY] * 10 + [vmem],
        out_specs=[ANY] * 5 + [vmem],
        out_shape=[
            shape((12, hidden, width), BF16),
            shape((seqs, span, width), BF16),
            shape((seqs, span, width), BF16),
            shape((2, width, picked), BF16),
            shape((2, hidden, width), BF16),
            shape((8, hidden), F32),
        ],
        scratch_shapes=scratch + [pltpu.SemaphoreType.REGULAR] * 4,
        compiler_params=params(collective_id=1, has_side_effects=True),
    )(d, h1, x, w2, w1, pre, cell, h, sel, dsel, db)


def reorder(piece, groups, back):
    span = piece * groups
    a = lax.broadcasted_iota(jnp.int32, (span, span), 1 if back else 0)
    b = lax.broadcasted_iota(jnp.int32, (span, span), 0 if back else 1)
    return (b == lax.rem(a, piece) * groups + a // piece).astype(BF16)


def identity(n):
    rows, cols = (lax.broadcasted_iota(jnp.int32, (n, n), axis) for axis in range(2))
    return (rows == cols).astype(BF16)


def to_row(column):
    n = column.shape[0]
    same = lax.broadcasted_iota(jnp.int32, (n, n), 0) == lax.broadcasted_iota(jnp.int32, (n, n), 1)
    return jnp.sum(jnp.where(same, column, 0.0), axis=0, keepdims=True)


def to_column(row):
    n = row.shape[1]
    same = lax.broadcasted_iota(jnp.int32, (n, n), 0) == lax.broadcasted_iota(jnp.int32, (n, n), 1)
    return jnp.sum(jnp.where(same, row, 0.0), axis=1, keepdims=True)


class Gather:
    def __init__(self, here, region, sems, own=None):
        h, b = here, here.b
        own = own or (lambda half: region(b, half))
        bx, by = h.across_x["tm"], h.across_y["tm"]
        bd = bx + 4 - 8 * h.y
        plan = (
            (b, 1, h.across_x),
            (b, 0, h.across_y),
            (b, 0, h.across_x),
            (b, 1, h.across_y),
            (b, None, h.core),
            (bx, 1, h.across_y),
            (by, 0, h.across_x),
            (bx, None, h.core),
            (by, None, h.core),
            (bd, 0, h.core),
            (bd, 1, h.core),
        )
        self.copies = []
        for k, (block, half, to) in enumerate(plan):
            src = own(half) if k < 5 else region(block, half)
            self.copies.append(remote(src, region(block, half), sems.at[k, 0], sems.at[k, 1], to))

    def start(self):
        for k in range(5):
            self.copies[k].start()

    def relay(self):
        self.copies[0].wait_recv()
        self.copies[5].start()
        self.copies[1].wait_recv()
        self.copies[6].start()

    def share_near(self):
        self.copies[2].wait_recv()
        self.copies[7].start()
        self.copies[4].wait_recv()
        self.copies[7].wait_recv()

    def share_far(self):
        self.copies[3].wait_recv()
        self.copies[8].start()
        self.copies[6].wait_recv()
        self.copies[9].start()
        self.copies[5].wait_recv()
        self.copies[10].start()
        for k in (8, 9, 10):
            self.copies[k].wait_recv()

    def share(self):
        self.share_near()
        self.share_far()

    def drain(self):
        for copy in self.copies:
            copy.wait_send()


def forward_kernel(seqs, hidden, length, width, *refs):
    x_in, w1_in, w2_in, cot_in, b1_in, b2_in, starts = refs[:7]
    x_out, h1_out, pre_out, cell_out, h2_out, d_out, db_out, sel_out, dsel_out = refs[7:16]
    xg, hg, w, p, pre, cell, work, edge, dv, seed, grad, hv, raw, cot, sent, b1, b2, chosen, sel, dsel = refs[16:36]
    xsem, hsem, ssem, zsem, lsem = refs[36:]
    here = Here()
    groups = length // LANES
    piece = LANES // 8

    def columns_of(s):
        return pl.ds(aligned(s * length), length)

    def x_region(s):
        def region(b, half):
            js = pl.ds(0, groups) if half is None else pl.ds(half * (groups // 2), groups // 2)
            return xg.at[s, js, b]

        return region

    def h_region(s):
        def region(b, half):
            rows = pl.ds(0, hidden) if half is None else pl.ds(half * (hidden // 2), hidden // 2)
            return hg.at[b, rows, columns_of(s)]

        return region

    def load(src, dst, k):
        return pltpu.make_async_copy(src, dst, lsem.at[k])

    load_w1 = load(w1_in, w, 0)
    load_w2 = load(w2_in, w, 0)
    load_x = [load(x_in.at[s], raw.at[s], 1 + s) for s in range(seqs)]
    load_c = load(cot_in, cot, 14)
    store_x = [load(xg.at[s], x_out.at[s], 3 + s) for s in range(seqs)]
    store_h = [load(hg.at[:, :, columns_of(s)], h1_out.at[:, :, columns_of(s)], 5 + s) for s in range(seqs)]
    store_p = [load(pre.at[:, columns_of(s)], pre_out.at[:, columns_of(s)], 7 + s) for s in range(seqs)]
    store_c = [load(cell.at[:, columns_of(s)], cell_out.at[:, columns_of(s)], 9 + s) for s in range(seqs)]

    def store_d(s):
        return load(dv.at[s], d_out.at[:, columns_of(s)], 11 + s)

    store_o = load(hv, h2_out, 13)

    for copy in load_x:
        copy.start()
    load_w1.start()
    load_c.start()
    order = reorder(piece, groups, False)

    def place():
        for s in range(seqs):
            load_x[s].wait()
            xg[s, :, here.b] = dot(order, raw[s], NN).astype(BF16).reshape(groups, piece, width)

    meet(here.peers + here.line, place)
    xs = [Gather(here, x_region(s), xsem.at[s]) for s in range(seqs)]
    hs = [Gather(here, h_region(s), hsem.at[s]) for s in range(seqs)]

    def prepare():
        load_c.wait()
        for s in range(seqs):
            turned = dot(order, cot[s], NN).astype(BF16)
            for b in range(8):
                block = turned[:, b * hidden : (b + 1) * hidden]
                sent[b, s] = block.reshape(groups, piece, hidden)
        seed[:, :, pl.ds(0, 4)] = jnp.zeros((seqs, groups, 4, piece, hidden), BF16)
        for s in range(seqs):
            prepare_pick(s)
        b1[...] = to_column(b1_in[...][None, :])
        b2[...] = to_column(b2_in[...][None, :])

    late = [
        [
            remote(sent.at[peer["tm"], s], seed.at[s, :, here.b], ssem.at[d, s, 0], ssem.at[d, s, 1], peer)
            for d, peer in enumerate(here.peers, 1)
        ]
        for s in range(seqs)
    ]
    early = pltpu.make_async_copy(sent.at[here.b], seed.at[:, :, here.b], ssem.at[0, 0, 0])

    def first_products(s):
        def block(r):
            rows = pl.ds(r, hidden)
            p[rows, :] = dot(w[rows, :], xg[s].reshape(length, width), NT)

        tiles(6 * hidden, hidden, block)

    def second_products(s, near):
        y = here.y if near else 1 - here.y
        depth = pl.ds(pl.multiple_of(y * (width // 2), LANES), width // 2)

        def block(r):
            rows = pl.ds(r, hidden)
            rhs = hg[pl.ds(y * 4, 4), :, columns_of(s)].reshape(width // 2, length)
            got = dot(w[rows, depth], rhs, NN)
            p[rows, :] = got if near else p[rows, :] + got

        tiles(6 * hidden, hidden, block)

    def first_pool(s):
        first = s * length
        pool_forward(first, p, b1, pre, cell, first, hg.at[here.b], work.at[0], edge.at[0], hidden, groups)

    def second_pool(s):
        pool_forward(s * length, p, b2, pre, cell, s * length, hv, work.at[0], edge.at[0], hidden, groups)

    def incoming(s):
        eye = identity(LANES)
        lane = lax.broadcasted_iota(jnp.int32, (1, LANES), 1)
        for j in range(groups):
            block = seed[s, j].reshape(LANES, hidden)
            turned = dot(block, eye, TN)
            step = lane * groups + j
            keep = jnp.zeros((1, LANES), jnp.bool_)
            for k in range(starts.shape[1]):
                begin = starts[s, k]
                keep = jnp.logical_or(keep, jnp.logical_and(step >= begin, step < begin + CLUSTER))
            keep = jnp.broadcast_to(keep, (hidden, LANES))
            grad[:, pl.ds(s * length + j * LANES, LANES)] = jnp.where(keep, turned, 0.0).astype(BF16)

    def pool_back(s):
        pool_backward(s * length, grad, pre, cell, 0, dv.at[s], db_out.at[s], work, edge, hidden, groups, True)
        store_d(s).start()

    def cluster_steps(s):
        lane = lax.broadcasted_iota(jnp.int32, (1, LANES), 1)
        step = lax.rem(lane, CLUSTER)
        for k in range(starts.shape[1]):
            step = step + jnp.where(lane // CLUSTER == k, starts[s, k], 0)
        return lane, step

    def prepare_pick(s):
        _, step = cluster_steps(s)
        for j in range(groups):
            code = lax.broadcasted_iota(jnp.int32, (LANES, LANES), 0) * groups + j
            at = pl.ds(j * LANES, LANES)
            chosen[s, at, pl.ds(0, LANES)] = (code == step).astype(BF16)
            chosen[s, at, pl.ds(LANES, LANES)] = (code == step - 1).astype(BF16)

    def held(s, count):
        start = here.z * (seqs * LANES) + s * LANES
        return pl.ds(pl.multiple_of(start, LANES), count * LANES)

    def pick_hidden(s):
        got = dot(hg[here.b, :, columns_of(s)], chosen[s], NN).astype(BF16)
        for tap in range(2):
            sel[tap, :, held(s, 1)] = got[:, tap * LANES : (tap + 1) * LANES]

    def pick_grad(s):
        lane, step = cluster_steps(s)
        again = jnp.zeros((1, LANES), jnp.bool_)
        for k in range(starts.shape[1] - 1):
            begin = starts[s, k]
            inside = jnp.logical_and(step >= begin, step < begin + CLUSTER)
            again = jnp.logical_or(again, jnp.logical_and(inside, lane // CLUSTER > k))
        got = dot(dv[s, pl.ds(2 * hidden, hidden), :], chosen[s, :, pl.ds(0, LANES)], NN)
        dsel[:, held(s, 1)] = jnp.where(jnp.broadcast_to(again, (hidden, LANES)), 0.0, got).astype(BF16)

    spread_h = []
    spread_d = [[] for _ in range(seqs)]
    for d, peer in enumerate(here.line, 1):
        at = sel.at[:, :, held(0, seqs)]
        spread_h.append(remote(at, at, zsem.at[d, 0], zsem.at[d, 1], peer))
        for s in range(seqs):
            at = dsel.at[:, held(s, 1)]
            spread_d[s].append(remote(at, at, zsem.at[d, 2 + 2 * s], zsem.at[d, 3 + 2 * s], peer))
    store_s = load(sel, sel_out, 15)
    store_e = load(dsel, dsel_out, 16)

    xs[0].start()
    prepare()
    xs[0].relay()
    xs[1].start()
    xs[0].share()
    store_x[0].start()
    load_w1.wait()
    first_products(0)
    xs[1].relay()
    first_pool(0)
    hs[0].start()
    store_p[0].start()
    store_c[0].start()
    xs[1].share()
    store_x[1].start()
    first_products(1)
    load_w2.start()
    hs[0].relay()
    first_pool(1)
    hs[1].start()
    store_p[1].start()
    store_c[1].start()

    for s in range(seqs):
        pick_hidden(s)
    for copy in spread_h:
        copy.start()
    hs[0].share_near()
    load_w2.wait()
    second_products(0, True)
    hs[0].share_far()
    store_h[0].start()
    second_products(0, False)
    hs[1].relay()

    @pl.when(here.y == 1)
    def _():
        early.start()
        for copy in late[0] + late[1]:
            copy.start()

    store_p[0].wait()
    store_c[0].wait()
    second_pool(0)
    hs[1].share_near()
    second_products(1, True)
    hs[1].share_far()
    store_h[1].start()
    second_products(1, False)
    store_p[1].wait()
    store_c[1].wait()
    second_pool(1)
    store_o.start()

    @pl.when(here.y == 1)
    def _():
        early.wait()

    for s in range(seqs):
        for d, copy in enumerate(late[s], 1):

            @pl.when(lax.rem(here.b + 8 - d, 8) >= 4)
            def _(copy=copy):
                copy.wait_recv()

        incoming(s)
        outgate_backward(s * length, grad, pre, cell, dv.at[s], hidden, groups)
        pick_grad(s)
        for copy in spread_d[s]:
            copy.start()
    for copy in spread_h:
        copy.wait()
    store_s.start()

    def back(s, carry):
        pool_back(s)
        return carry

    lax.fori_loop(0, seqs, back, 0)
    @pl.when(here.y == 1)
    def _():
        for copy in late[0] + late[1]:
            copy.wait_send()

    for gather in xs + hs:
        gather.drain()
    for copy in spread_d[0] + spread_d[1]:
        copy.wait()
    store_e.start()
    for copy in store_x + store_h + [store_d(s) for s in range(seqs)] + [store_o, store_s, store_e]:
        copy.wait()


def run_forward(x, w1, b1, w2, b2, cotangent, starts):
    seqs, span, width = x.shape
    hidden, length, piece = w1.shape[0] // 6, span * 8, LANES // 8
    groups = length // LANES
    total, picked = seqs * length, 4 * seqs * LANES
    assert starts.shape[1] * CLUSTER == LANES
    vmem = pl.BlockSpec(memory_space=pltpu.VMEM)
    return pl.pallas_call(
        functools.partial(forward_kernel, seqs, hidden, length, width),
        name="forward",
        in_specs=[ANY, ANY, ANY, ANY, vmem, vmem, pl.BlockSpec(memory_space=pltpu.SMEM)],
        out_specs=[ANY, ANY, ANY, ANY, ANY, ANY, vmem, ANY, ANY],
        out_shape=[
            shape((seqs, groups, 8, piece, width), BF16),
            shape((8, hidden, total), BF16),
            shape((3 * hidden, total), BF16),
            shape((hidden, total), F32),
            shape((hidden, total), BF16),
            shape((6 * hidden, total), BF16),
            shape((seqs, hidden, 1), F32),
            shape((2, hidden, picked), BF16),
            shape((hidden, picked), BF16),
        ],
        scratch_shapes=[
            pltpu.VMEM((seqs, groups, 8, piece, width), BF16),
            pltpu.VMEM((8, hidden, total), BF16),
            pltpu.VMEM((6 * hidden, width), BF16),
            pltpu.VMEM((6 * hidden, length), F32),
            pltpu.VMEM((3 * hidden, total), BF16),
            pltpu.VMEM((hidden, total), F32),
            pltpu.VMEM((2, hidden, length), F32),
            pltpu.VMEM((2, hidden, LANES), F32),
            pltpu.VMEM((seqs, 6 * hidden, length), BF16),
            pltpu.VMEM((seqs, groups, 8, piece, hidden), BF16),
            pltpu.VMEM((hidden, total), BF16),
            pltpu.VMEM((hidden, total), BF16),
            pltpu.VMEM((seqs, span, width), BF16),
            pltpu.VMEM((seqs, span, width), BF16),
            pltpu.VMEM((8, seqs, groups, piece, hidden), BF16),
            pltpu.VMEM((hidden, 1), F32),
            pltpu.VMEM((hidden, 1), F32),
            pltpu.VMEM((seqs, length, 2 * LANES), BF16),
            pltpu.VMEM((2, hidden, picked), BF16),
            pltpu.VMEM((hidden, picked), BF16),
            pltpu.SemaphoreType.DMA((seqs, 11, 2)),
            pltpu.SemaphoreType.DMA((seqs, 11, 2)),
            pltpu.SemaphoreType.DMA((8, seqs, 2)),
            pltpu.SemaphoreType.DMA((4, 2 + 2 * seqs)),
            pltpu.SemaphoreType.DMA((17,)),
        ],
        compiler_params=params(collective_id=0, has_side_effects=True),
    )(x, w1, w2, cotangent, b1, b2, starts)


def finish_kernel(
    one_ref, two_ref, outgate_ref, h_ref, gx_ref, db_ref, wide_one_ref, wide_two_ref, h_out, gx_out, db1_out, db2_out
):
    i = pl.program_id(0)
    wide_one_ref[...] = one_ref[...].astype(F32)
    last = lax.rem(i, 3) == 2

    @pl.when(last)
    def _():
        wide_two_ref[...] = outgate_ref[...].astype(F32)

    @pl.when(jnp.logical_not(last))
    def _():
        wide_two_ref[...] = two_ref[...].astype(F32)

    h_out[...] = h_ref[...]
    gx_out[...] = gx_ref[...]
    db1_out[...] = db_ref[0]
    db2_out[...] = db_ref[1]


def finish(gw, outgate, h, gx, db):
    _, hidden, width = gw.shape
    total = h.shape[0] * h.shape[1]
    dims = (1, hidden, width)
    small = (total // 4, width)
    weights = pl.BlockSpec(dims, lambda i: (i, 0, 0))
    tokens = pl.BlockSpec(small, lambda i: (jnp.minimum(i, 3), 0))
    bias = pl.BlockSpec((hidden,), lambda i: (0,))
    return pl.pallas_call(
        finish_kernel,
        name="results",
        grid=(6,),
        in_specs=[
            weights,
            pl.BlockSpec(dims, lambda i: (6 + i - i % 3 // 2, 0, 0)),
            pl.BlockSpec(dims, lambda i: (i // 3, 0, 0)),
            tokens,
            tokens,
            pl.BlockSpec(db.shape, lambda i: (0, 0)),
        ],
        out_specs=[weights, weights, tokens, tokens, bias, bias],
        out_shape=[shape((6, hidden, width), F32)] * 2 + [shape((total, width), BF16)] * 2 + [shape((hidden,), F32)] * 2,
        compiler_params=params(),
    )(gw, gw, outgate, h.reshape(total, width), gx.reshape(total, width), db)


def per_device(line, inputs, weight_one, fbias_one, weight_two, fbias_two, cotangent, cluster_starts):
    seqs, span, width = inputs.shape
    count = lax.axis_size("tm")
    length = span * count
    groups = length // LANES
    piece = LANES // count
    hidden = weight_one.shape[2]
    total = seqs * length
    w1 = weight_one.reshape(6 * hidden, width)
    w2 = weight_two.reshape(6 * hidden, width)

    if line:
        x, h1, pre1, cell1, h2, d2, db2, *picked = run_forward(
            inputs, w1, fbias_one, w2, fbias_two, cotangent, cluster_starts
        )
        x, h1 = x.reshape(total, width), h1.reshape(width, total)
        gw, gx1, h2, _, wo, db = run_backward(d2, h1, x, w2, w1, pre1, cell1, h2, *picked, db2)
        gw1, gw2, h2, gx1, *db = finish(gw, wo, h2, gx1, db)
    else:
        x = inputs.reshape(seqs, piece, groups, width).transpose(0, 2, 1, 3)
        bias1, bias2 = fbias_one[:, None], fbias_two[:, None]
        seed = cotangent.reshape(seqs, piece, groups, count, hidden)
        steps = lax.axis_index("tm") * span + jnp.arange(span, dtype=jnp.int32)
        starts = cluster_starts[:, :, None]
        keep = jnp.any((steps >= starts) & (steps < starts + CLUSTER), axis=1)
        seed = jnp.where(keep.reshape(seqs, piece, groups, 1, 1), seed, jnp.zeros_like(seed))
        seed = lax.all_to_all(seed, "tm", split_axis=3, concat_axis=1, tiled=True)
        seed = seed.reshape(seqs, LANES, groups, hidden).transpose(3, 0, 2, 1).reshape(hidden, total)
        x = lax.all_gather(x, "tm", axis=2, tiled=True).reshape(total, width)
        pre1, cell1, h1 = run_first(seqs, w1, bias1, x)
        h1 = lax.all_gather(h1, "tm", axis=0, tiled=True)
        h2, d2, db2 = run_second(seqs, w2, bias2, h1, seed)
        h2 = h2.reshape(hidden, seqs, groups, count, piece)
        h2 = lax.all_to_all(h2, "tm", split_axis=3, concat_axis=0, tiled=True)
        h2 = h2.reshape(width, seqs, groups, piece).transpose(1, 3, 2, 0)
        gw2 = lax.psum(dot(d2, h1, NT).astype(BF16), "seq").astype(F32)
        gx2 = lax.psum_scatter(dot(w2, d2, TN).astype(BF16), "tm", scatter_dimension=0, tiled=True)
        d1, db1 = run_back(seqs, gx2, pre1, cell1)
        gw1 = lax.psum(dot(d1, x, NN).astype(BF16), "seq").astype(F32)
        gx1 = dot(d1, w1, TN).astype(BF16).reshape(seqs, groups, LANES, width)
        gx1 = lax.psum_scatter(gx1, "tm", scatter_dimension=2, tiled=True)
        gx1 = gx1.transpose(0, 2, 1, 3).reshape(seqs, span, width)
        db = lax.psum(jnp.stack([db1, db2]).sum(axis=(1, 3)), "seq")
    out, gx1 = h2.reshape(seqs, span, width), gx1.reshape(seqs, span, width)
    dims = weight_one.shape
    return (out, gx1, gw1.reshape(dims), db[0], gw2.reshape(dims), db[1])


def solution(mesh):
    placed = (
        P("seq", "tm", None),
        P(None, None, "tm", None),
        P("tm"),
        P(None, None, "tm", None),
        P("tm"),
        P("seq", "tm", None),
        P("seq", None),
    )
    return jax.shard_map(
        functools.partial(per_device, dict(mesh.shape) == {"seq": 4, "tm": 8}),
        mesh=mesh,
        in_specs=placed,
        out_specs=(
            P("seq", "tm", None),
            P("seq", "tm", None),
            P(None, None, "tm", None),
            P("tm"),
            P(None, None, "tm", None),
            P("tm"),
        ),
        check_vma=False,
    )
```

```python
import functools

import jax
import jax.numpy as jnp
from jax import lax
from jax.experimental import pallas as pl
from jax.experimental.pallas import tpu as pltpu
from jax.sharding import PartitionSpec as P

CLUSTER = 32
LANES = 128
ROWS = 48
F32 = jnp.float32
BF16 = jnp.bfloat16
ANY = pl.BlockSpec(memory_space=pl.ANY)
MESH = pl.DeviceIdType.MESH
NN = (((1,), (0,)), ((), ()))
NT = (((1,), (1,)), ((), ()))
TN = (((0,), (0,)), ((), ()))


def dot(a, b, dims):
    return lax.dot_general(a, b, dims, preferred_element_type=F32)


def sigmoid(v):
    return 1.0 / (1.0 + jnp.exp(-v))


def tiles(count, rows, body):
    def step(r, carry):
        body(pl.multiple_of(r * rows, rows))
        return carry

    lax.fori_loop(0, count // rows, step, 0)


def aligned(start):
    return start if isinstance(start, int) else pl.multiple_of(start, LANES)


def stretch(hidden):
    return 96 if hidden % 96 == 0 else ROWS


def shift_lanes(v, amount, lane, fill):
    moved = pltpu.roll(v, amount % LANES, axis=1)
    gone = lane < amount if amount > 0 else lane >= LANES + amount
    return jnp.where(gone, fill, moved)


def lane_chain(factor, value, lane, sign):
    step = 1
    while step < LANES:
        value = value + factor * shift_lanes(value, sign * step, lane, 0.0)
        factor = factor * shift_lanes(factor, sign * step, lane, 1.0)
        step *= 2
    return value


def pool_forward(first, p_ref, b_ref, pre_ref, cell_ref, target, h_ref, factor_ref, edge_ref, hidden, groups):
    size = stretch(hidden)
    lane = lax.broadcasted_iota(jnp.int32, (size, LANES), 1)

    def at(j, start=0):
        return pl.ds(start + j * LANES, LANES)

    def gates(r):
        rows = pl.ds(r, size)
        value = factor = None
        for j in range(groups):
            got = []
            for g in range(3):
                now = p_ref[pl.ds(g * hidden + r, size), at(j)]
                tap = pl.ds((3 + g) * hidden + r, size)
                if j:
                    past = p_ref[tap, at(j - 1)]
                else:
                    past = shift_lanes(p_ref[tap, at(groups - 1)], 1, lane, 0.0)
                total = now + past
                if g == 1:
                    total = total + b_ref[rows, :]
                total = total.astype(BF16)
                pre_ref[pl.ds(g * hidden + r, size), at(j, first)] = total
                got.append(total.astype(F32))
            forget = sigmoid(got[1])
            fresh = (1.0 - forget) * jnp.tanh(got[0])
            if j:
                value = forget * value + fresh
                factor = forget * factor
            else:
                value, factor = fresh, forget
            cell_ref[rows, at(j, first)] = value
            factor_ref[rows, at(j)] = factor

    tiles(hidden, size, gates)

    everywhere = lax.broadcasted_iota(jnp.int32, (hidden, LANES), 1)
    value = lane_chain(factor_ref[:, at(groups - 1)], cell_ref[:, at(groups - 1, first)], everywhere, 1)
    edge_ref[...] = shift_lanes(value, 1, everywhere, 0.0)

    def finish(r):
        rows = pl.ds(r, size)
        edge = edge_ref[rows, :]
        for j in range(groups):
            cell = cell_ref[rows, at(j, first)] + factor_ref[rows, at(j)] * edge
            cell_ref[rows, at(j, first)] = cell
            outgate = sigmoid(pre_ref[pl.ds(2 * hidden + r, size), at(j, first)].astype(F32))
            h_ref[rows, at(j, target)] = (outgate * cell).astype(BF16)

    tiles(hidden, size, finish)


def put_gate(d_ref, g, r, j, v, target, lane, hidden, groups):
    rows = v.shape[0]
    d_ref[pl.ds(g * hidden + r, rows), pl.ds(target + j * LANES, LANES)] = v
    tap = pl.ds((3 + g) * hidden + r, rows)
    if j:
        d_ref[tap, pl.ds(target + (j - 1) * LANES, LANES)] = v
    else:
        moved = shift_lanes(v.astype(F32), -1, lane, 0.0).astype(BF16)
        d_ref[tap, pl.ds(target + (groups - 1) * LANES, LANES)] = moved


def outgate_backward(first, g_ref, pre_ref, cell_ref, d_ref, hidden, groups):
    size = stretch(hidden)
    lane = lax.broadcasted_iota(jnp.int32, (size, LANES), 1)

    def body(r):
        rows = pl.ds(r, size)
        for j in range(groups):
            at = pl.ds(first + j * LANES, LANES)
            outgate = sigmoid(pre_ref[pl.ds(2 * hidden + r, size), at].astype(F32))
            v = g_ref[rows, at].astype(F32) * cell_ref[rows, at] * outgate * (1.0 - outgate)
            put_gate(d_ref, 2, r, j, v.astype(BF16), 0, lane, hidden, groups)

    tiles(hidden, size, body)


def pool_backward(
    first, g_ref, pre_ref, cell_ref, target, d_ref, db_ref, work_ref, edge_ref, hidden, groups, carried_only=False
):
    size = stretch(hidden)
    lane = lax.broadcasted_iota(jnp.int32, (size, LANES), 1)

    def at(j, start=0):
        return pl.ds(aligned(start + j * LANES), LANES)

    def gate(g, r, j):
        return pre_ref[pl.ds(g * hidden + r, size), at(j, first)].astype(F32)

    def start(r):
        rows = pl.ds(r, size)
        later = value = factor = None
        for j in reversed(range(groups)):
            own = g_ref[rows, at(j, first)].astype(F32) * sigmoid(gate(2, r, j))
            if later is None:
                value, factor = own, jnp.ones_like(own)
            else:
                value = own + later * value
                factor = later * factor
            work_ref[0, rows, at(j)] = value
            work_ref[1, rows, at(j)] = factor
            later = sigmoid(gate(1, r, j))
        edge_ref[0, rows, :] = later * value
        edge_ref[1, rows, :] = later * factor

    tiles(hidden, size, start)

    everywhere = lax.broadcasted_iota(jnp.int32, (hidden, LANES), 1)
    value = lane_chain(edge_ref[1], edge_ref[0], everywhere, -1)
    edge_ref[0] = shift_lanes(value, -1, everywhere, 0.0)

    def finish(r):
        rows = pl.ds(r, size)
        edge = edge_ref[0, rows, :]
        total = jnp.zeros((size, LANES), F32)
        before = shift_lanes(cell_ref[rows, at(groups - 1, first)], 1, lane, 0.0)
        for j in range(groups):
            carried = work_ref[0, rows, at(j)] + work_ref[1, rows, at(j)] * edge
            candidate = jnp.tanh(gate(0, r, j))
            forget = sigmoid(gate(1, r, j))
            cell = cell_ref[rows, at(j, first)]
            keep = carried * (1.0 - forget)
            got = [keep * (1.0 - candidate * candidate), keep * forget * (before - candidate)]
            if not carried_only:
                outgate = sigmoid(gate(2, r, j))
                got.append(g_ref[rows, at(j, first)].astype(F32) * cell * outgate * (1.0 - outgate))
            before = cell
            for g, v in enumerate(got):
                v = v.astype(BF16)
                if g == 1:
                    total = total + v.astype(F32)
                put_gate(d_ref, g, r, j, v, target, lane, hidden, groups)
        db_ref[rows, :] = jnp.sum(total, axis=1, keepdims=True)

    tiles(hidden, size, finish)


def first_kernel(hidden, length, w_ref, b_ref, x_ref, pre_ref, cell_ref, h_ref, p_ref, work_ref, edge_ref):
    def strip(c):
        cols = pl.ds(c, 512)
        p_ref[:, cols] = dot(w_ref[...], x_ref[cols, :], NT)

    tiles(length, 512, strip)
    pool_forward(0, p_ref, b_ref, pre_ref, cell_ref, 0, h_ref, work_ref, edge_ref, hidden, length // LANES)


def second_kernel(
    hidden, length, w_ref, b_ref, x_ref, g_ref, h_ref, d_ref, db_ref, p_ref, pre_ref, cell_ref, work_ref, edge_ref
):
    def strip(c):
        cols = pl.ds(c, 512)
        p_ref[:, cols] = dot(w_ref[...], x_ref[:, cols], NN)

    tiles(length, 512, strip)
    groups = length // LANES
    pool_forward(0, p_ref, b_ref, pre_ref, cell_ref, 0, h_ref, work_ref.at[0], edge_ref.at[0], hidden, groups)
    pool_backward(0, g_ref, pre_ref, cell_ref, 0, d_ref, db_ref.at[0], work_ref, edge_ref, hidden, groups)


def back_kernel(hidden, length, g_ref, pre_ref, cell_ref, d_ref, db_ref, work_ref, edge_ref):
    pool_backward(0, g_ref, pre_ref, cell_ref, 0, d_ref, db_ref.at[0], work_ref, edge_ref, hidden, length // LANES)


def columns(rows, length):
    return pl.BlockSpec((rows, length), lambda s: (0, s))


def fixed(*dims):
    return pl.BlockSpec(dims, lambda s: (0,) * len(dims), pipeline_mode=pl.Buffered(1))


def params(**more):
    return pltpu.CompilerParams(vmem_limit_bytes=63 * 1024 * 1024, **more)


shape = jax.ShapeDtypeStruct


def run_first(seqs, weight, bias, gathered):
    (wide, width), total = weight.shape, gathered.shape[0]
    hidden, length = wide // 6, total // seqs
    return pl.pallas_call(
        functools.partial(first_kernel, hidden, length),
        name="layer_one_forward",
        grid=(seqs,),
        in_specs=[fixed(wide, width), fixed(hidden, 1), pl.BlockSpec((length, width), lambda s: (s, 0))],
        out_specs=[columns(3 * hidden, length), columns(hidden, length), columns(hidden, length)],
        out_shape=[shape((3 * hidden, total), BF16), shape((hidden, total), F32), shape((hidden, total), BF16)],
        scratch_shapes=[
            pltpu.VMEM((wide, length), F32),
            pltpu.VMEM((hidden, length), F32),
            pltpu.VMEM((hidden, LANES), F32),
        ],
        compiler_params=params(),
    )(weight, bias, gathered)


def run_second(seqs, weight, bias, gathered, grad):
    (wide, width), total = weight.shape, gathered.shape[1]
    hidden, length = wide // 6, total // seqs
    return pl.pallas_call(
        functools.partial(second_kernel, hidden, length),
        name="layer_two_forward_and_pool_backward",
        grid=(seqs,),
        in_specs=[fixed(wide, width), fixed(hidden, 1), columns(width, length), columns(hidden, length)],
        out_specs=[columns(hidden, length), columns(wide, length), pl.BlockSpec((1, hidden, 1), lambda s: (s, 0, 0))],
        out_shape=[shape((hidden, total), BF16), shape((wide, total), BF16), shape((seqs, hidden, 1), F32)],
        scratch_shapes=[
            pltpu.VMEM((wide, length), F32),
            pltpu.VMEM((3 * hidden, length), BF16),
            pltpu.VMEM((hidden, length), F32),
            pltpu.VMEM((2, hidden, length), F32),
            pltpu.VMEM((2, hidden, LANES), F32),
        ],
        compiler_params=params(),
    )(weight, bias, gathered, grad)


def run_back(seqs, grad, pre, cell):
    hidden, total = grad.shape
    length = total // seqs
    return pl.pallas_call(
        functools.partial(back_kernel, hidden, length),
        name="layer_one_pool_backward",
        grid=(seqs,),
        in_specs=[columns(hidden, length), columns(3 * hidden, length), columns(hidden, length)],
        out_specs=[columns(6 * hidden, length), pl.BlockSpec((1, hidden, 1), lambda s: (s, 0, 0))],
        out_shape=[shape((6 * hidden, total), BF16), shape((seqs, hidden, 1), F32)],
        scratch_shapes=[pltpu.VMEM((2, hidden, length), F32), pltpu.VMEM((2, hidden, LANES), F32)],
        compiler_params=params(),
    )(grad, pre, cell)


THIRDS = 3
PIECES = 3
SLOTS = 11
AHEAD = 6
BEHIND = 3
LATER = 12
BLOCKS = 30
OWN = 18


class Here:
    def __init__(self):
        self.z = lax.axis_index("seq")
        self.b = lax.axis_index("tm")
        self.c = lax.rem(self.b, 2)
        self.x = lax.rem(self.b // 2, 2)
        self.y = self.b // 4
        self.core = dict(seq=self.z, tm=self.b + 1 - 2 * self.c)
        self.across_x = dict(seq=self.z, tm=self.b + 2 - 4 * self.x)
        self.across_y = dict(seq=self.z, tm=self.b + 4 - 8 * self.y)
        self.pair = dict(seq=self.z + 1 - 2 * lax.rem(self.z, 2), tm=self.b)
        self.middle = dict(seq=3 - self.z, tm=self.b)
        self.line = [dict(seq=lax.rem(self.z + d, 4), tm=self.b) for d in range(1, 4)]
        self.peers = [dict(seq=self.z, tm=lax.rem(self.b + d, 8)) for d in range(1, 8)]
        self.is_end = jnp.logical_or(self.z == 0, self.z == 3)
        self.is_centre = jnp.logical_and(self.z > 0, self.z < 3)


def remote(src, dst, send, recv, target):
    return pltpu.make_async_remote_copy(
        src_ref=src, dst_ref=dst, send_sem=send, recv_sem=recv, device_id=target, device_id_type=MESH
    )


def both(a, b):
    if isinstance(a, bool) and isinstance(b, bool):
        return a and b
    return jnp.logical_and(a, b)


def signal(sem, target):
    pl.semaphore_signal(sem, inc=1, device_id=target, device_id_type=MESH)


def meet(targets, between=None):
    barrier = pltpu.get_barrier_semaphore()
    for target in targets:
        signal(barrier, target)
    if between is not None:
        between()
    pl.semaphore_wait(barrier, len(targets))


def pick(condition, a, b):
    if isinstance(condition, bool):
        return a if condition else b
    return jnp.where(condition, a, b)


class SeqSum:
    def __init__(self, here, hidden, third, own, ring_in, ring_mid, total, out, sems, credits):
        self.here, self.third, self.rows = here, third, hidden // PIECES
        self.units = BLOCKS * PIECES
        self.own, self.ring_in, self.ring_mid, self.total, self.out = own, ring_in, ring_mid, total, out
        self.sems = sems
        self.credit_in, self.credit_mid, self.credit_out = credits

    def rows_of(self, u):
        return pl.ds(pl.multiple_of(lax.rem(u, PIECES) * self.rows, 16), self.rows)

    def mine(self, u):
        return self.own.at[lax.rem(u // PIECES, OWN), self.rows_of(u)]

    def inward(self, u):
        i = lax.rem(u, SLOTS)
        return remote(self.mine(u), self.ring_in.at[i], self.sems.at[0, i], self.sems.at[1, i], self.here.pair)

    def across(self, u):
        i = lax.rem(u, SLOTS)
        return remote(self.mine(u), self.ring_mid.at[i], self.sems.at[2, i], self.sems.at[3, i], self.here.middle)

    def outward(self, u):
        i = lax.rem(u, SLOTS)
        return remote(self.total.at[i], self.ring_in.at[i], self.sems.at[4, i], self.sems.at[5, i], self.here.pair)

    def store(self, u, ring):
        i, block = lax.rem(u, SLOTS), u // PIECES
        second = block < LATER
        t = pick(second, block // 4, (block - LATER) // 6)
        cols = pl.ds(pl.multiple_of(t * self.third, LANES), self.third)
        to = self.out.at[self.product(block) + pick(second, 6, 0), self.rows_of(u), cols]
        return pltpu.make_async_copy(ring.at[i], to, self.sems.at[6, i])

    @staticmethod
    def product(block):
        k = lax.rem(block, 4)
        return pick(block < LATER, (k // 2) * 3 + lax.rem(k, 2), lax.rem(block, 6))

    def add(self, dst, a, b):
        def rows(r):
            at = pl.ds(r, ROWS)
            dst[at, :] = a[at, :] + b[at, :]

        tiles(self.rows, ROWS, rows)

    def offer(self, u):
        @pl.when(self.here.is_end)
        def _():
            @pl.when(u >= SLOTS)
            def _():
                pl.semaphore_wait(self.credit_in, 1)
                self.inward(u - SLOTS).wait_send()

            self.inward(u).start()

    def gather(self, u):
        i = lax.rem(u, SLOTS)
        self.inward(u).wait_recv()
        self.add(self.mine(u), self.mine(u), self.ring_in.at[i])

        @pl.when(u + SLOTS < self.units)
        def _():
            signal(self.credit_in, self.here.pair)

        @pl.when(u >= SLOTS)
        def _():
            pl.semaphore_wait(self.credit_mid, 1)
            self.across(u - SLOTS).wait_send()

        self.across(u).start()

    def finish(self, u):
        i = lax.rem(u, SLOTS)
        self.across(u).wait_recv()

        @pl.when(u >= SLOTS)
        def _():
            pl.semaphore_wait(self.credit_out, 1)
            self.outward(u - SLOTS).wait_send()
            self.store(u - SLOTS, self.total).wait()

        self.add(self.total.at[i], self.mine(u), self.ring_mid.at[i])

        @pl.when(u + SLOTS < self.units)
        def _():
            signal(self.credit_mid, self.here.middle)

        self.outward(u).start()
        self.store(u, self.total).start()

    def accept(self, u):
        self.outward(u).wait_recv()
        self.store(u, self.ring_in).start()

        @pl.when(u > 0)
        def _():
            self.store(u - 1, self.ring_in).wait()

            @pl.when(u - 1 + SLOTS < self.units)
            def _():
                signal(self.credit_out, self.here.pair)

    def tick(self, n):
        @pl.when(self.here.is_centre)
        def _():
            @pl.when(n < self.units)
            def _():
                self.gather(n)

            @pl.when(both(n >= BEHIND, n < self.units + BEHIND))
            def _():
                self.finish(n - BEHIND)

        @pl.when(n + AHEAD < self.units)
        def _():
            self.offer(n + AHEAD)

        @pl.when(n >= BEHIND + 2)
        def _():
            @pl.when(self.here.is_end)
            def _():
                self.accept(n - BEHIND - 2)

    def drain(self):
        @pl.when(self.here.is_centre)
        def _():
            for u in range(self.units - SLOTS, self.units):
                self.across(u).wait_send()
                self.outward(u).wait_send()
                self.store(u, self.total).wait()

        @pl.when(self.here.is_end)
        def _():
            for u in range(self.units - SLOTS, self.units):
                self.inward(u).wait_send()
            self.store(self.units - 1, self.ring_in).wait()


class RankSum:
    def __init__(self, here, part, pairs, wide_x, wide_y, last_x, last_y, sems):
        self.here, self.part, self.pairs = here, part, pairs
        self.wide_x, self.wide_y, self.last_x, self.last_y, self.sems = wide_x, wide_y, last_x, last_y, sems
        self.count = part.shape[3]
        self.half = self.count // 2
        self.upper, self.lower = pl.ds(0, self.half), pl.ds(self.half, self.half)

    def copy(self, k, s, src, dst, target):
        return remote(src, dst, self.sems.at[s, k, 0], self.sems.at[s, k, 1], target)

    def swap(self, s):
        return self.copy(0, s, self.part.at[:, :, 1 - self.here.c], self.pairs.at[s], self.here.core)

    def wide(self, s):
        h = self.here
        return (
            self.copy(1, s, self.pairs.at[s, :, 1 - h.x, self.upper], self.wide_x.at[s], h.across_x),
            self.copy(2, s, self.pairs.at[s, 1 - h.y, :, self.lower], self.wide_y.at[s], h.across_y),
        )

    def last(self, s):
        h = self.here
        return (
            self.copy(3, s, self.pairs.at[s, 1 - h.y, h.x, self.upper], self.last_y.at[s], h.across_y),
            self.copy(4, s, self.pairs.at[s, h.y, 1 - h.x, self.lower], self.last_x.at[s], h.across_x),
        )

    def start(self, s):
        self.swap(s).start()

    def cross(self, s):
        h = self.here
        self.swap(s).wait()

        def some(r):
            at = pl.ds(r, 8)
            for y in range(2):
                for x in range(2):
                    self.pairs[s, y, x, at] = self.pairs[s, y, x, at] + self.part[y, x, h.c, at]

        tiles(self.count, 8, some)
        for copy in self.wide(s):
            copy.start()

    def turn(self, s):
        h = self.here
        for copy in self.wide(s):
            copy.wait()

        def some(r):
            at, low = pl.ds(r, 8), pl.ds(self.half + r, 8)
            for k in range(2):
                self.pairs[s, k, h.x, at] = self.pairs[s, k, h.x, at] + self.wide_x[s, k, at]
                self.pairs[s, h.y, k, low] = self.pairs[s, h.y, k, low] + self.wide_y[s, k, at]

        tiles(self.half, 8, some)
        for copy in self.last(s):
            copy.start()

    def done(self, s, down, put):
        h = self.here
        for copy in self.last(s):
            copy.wait()

        def some(r):
            at, low = pl.ds(r, down), pl.ds(self.half + r, down)
            first = pl.multiple_of(r // down * LANES, LANES)
            put(first, (self.pairs[s, h.y, h.x, at] + self.last_y[s, at]).reshape(down * 16, LANES))
            first = pl.multiple_of((self.half + r) // down * LANES, LANES)
            put(first, (self.pairs[s, h.y, h.x, low] + self.last_x[s, at]).reshape(down * 16, LANES))

        tiles(self.half, down, some)


def backward_kernel(seqs, hidden, length, width, *refs):
    third = width // THIRDS
    d_in, h1_in, x_in, w2_in, w1_in, pre_in, cell_in, h_in, sel_in, dsel_in, db2 = refs[:11]
    gw_out, gx_out, h_out, sel_out, wo_out, db_out = refs[11:17]
    dv, wv, rh, rx, pre, cell, work, edge, grad, gxv, dsel, wo, heard, hv, db1, dbv, told = refs[17:34]
    own, ring_in, ring_mid, total, part, pairs, wide_x, wide_y, last_x, last_y = refs[34:44]
    zsem, rsem, dsem, hsem, psem, lsem, credit_in, credit_mid, credit_out, ready = refs[44:]
    here = Here()
    ar = SeqSum(here, hidden, third, own, ring_in, ring_mid, total, gw_out, zsem, (credit_in, credit_mid, credit_out))
    sums = {
        layer: RankSum(here, part, pairs, wide_x, wide_y, last_x, last_y, rsem.at[layer - 1]) for layer in (1, 2)
    }
    groups, piece = length // LANES, LANES // 8
    half = width // 2

    def columns_of(s):
        return pl.ds(s * length, length)

    def load(src, dst, k):
        return pltpu.make_async_copy(src, dst, lsem.at[k])

    def load_d(k):
        rows = pl.ds(k * hidden, hidden)
        if not isinstance(k, int):
            rows = pl.ds(pl.multiple_of(k * hidden, 16), hidden)
        return load(d_in.at[rows], dv.at[rows], k)

    def load_rhs(layer, t):
        at = pl.ds(t * third, third)
        return load(h1_in.at[at], rh, 6) if layer == 2 else load(x_in.at[:, at], rx, 7)

    load_w = {2: load(w2_in, wv, 8), 1: load(w1_in, wv, 8)}
    load_p, load_c, load_e = load(pre_in, pre, 9), load(cell_in, cell, 10), load(dsel_in, dsel, 11)
    keep = load(sel_in, sel_out.at[:, pl.ds(here.b * hidden, hidden)], 12)
    store_g = load(gxv, gx_out, 13)
    store_h = load(hv, h_out, 14)
    load_rhs(2, 0).start()
    for k in range(6):
        load_d(k).start()
    load_w[2].start()
    load_rhs(1, 0).start()
    for copy in (load_p, load_c, load_e, keep):
        copy.start()
    meet(here.peers + here.line)

    def halves(start, i):
        size = hidden if i is None else hidden // 2
        return pl.ds(start + (i or 0) * size, size)

    gather = Gather(
        here,
        lambda b, i: sel_out.at[:, halves(b * hidden, i)],
        psem,
        lambda i: sel_in.at[:, halves(0, i)],
    )
    biases = [
        remote(dbv.at[here.z], dbv.at[here.z], dsem.at[d, 0], dsem.at[d, 1], peer)
        for d, peer in enumerate(here.line, 1)
    ]
    load_h = load(h_in, grad, 19)
    spread = [pltpu.make_async_copy(told.at[here.b], heard.at[here.b], hsem.at[0, 0])]
    for d, peer in enumerate(here.peers, 1):
        spread.append(remote(told.at[peer["tm"]], heard.at[here.b], hsem.at[d, 0], hsem.at[d, 1], peer))

    done, spent = [0], [0]

    def units(layer, t):
        count = 4 if layer == 2 else 6
        start = t * count + (LATER if layer == 1 else 0)
        assert start + count <= OWN or spent[0] > (start + count - OWN) * PIECES - 1 + SLOTS
        first = spent[0]

        def unit(k, carry):
            block = start + k
            product = ar.product(block)
            if start == 0:
                load_d(product).wait()
            rows = pl.ds(pl.multiple_of(product * hidden, 16), hidden)
            got = dot(dv[rows, :], rh[...], NT) if layer == 2 else dot(dv[rows, :], rx[...], NN)
            own[lax.rem(block, OWN)] = got.astype(BF16)
            if start == 0:
                for i in range(PIECES):
                    u = block * PIECES + i

                    @pl.when(u < AHEAD)
                    def _(u=u):
                        ar.offer(u)

            else:

                @pl.when(lax.rem(k, 2) == 1)
                def _():
                    ar.tick(first + k // 2)

            return carry

        lax.fori_loop(0, count, unit, 0)
        done[0] = (start + count) * PIECES
        if start:
            spent[0] += count // 2
            assert first + AHEAD < (start + 2) * PIECES and spent[0] - 1 + AHEAD < done[0]

    def tick(count=1):
        first = spent[0]
        spent[0] += count
        assert spent[0] - 1 + AHEAD < done[0] or done[0] == ar.units

        def step(n, carry):
            ar.tick(n)
            return carry

        lax.fori_loop(first, spent[0], step, 0)

    def strips(layer, s, q):
        if layer == 2:
            i, start = q // 2, lax.rem(q, 2) * (length // 2)
            down = hidden // 16
            lhs = pl.ds(pl.multiple_of(i * half, LANES), half)

            def strip(c):
                src = pl.ds(pl.multiple_of(s * length + start + c, 256), 256)
                got = dot(wv[:, lhs], dv[:, src], TN).astype(BF16)
                for n in range(2):
                    at = pl.ds(((start + c) // LANES + n) * down, down)
                    part[i, :, :, at] = got[:, n * LANES : (n + 1) * LANES].reshape(2, 2, down, 16, LANES)

            tiles(length // 2, 256, strip)
        else:

            def strip(c, carry):
                cols = pl.ds(pl.multiple_of(c * 256, 256), 256)
                got = dot(dv[:, columns_of(s)], wv[:, cols], TN).astype(BF16)
                for j in range(groups):
                    for n in range(2):
                        block = got[j * LANES : (j + 1) * LANES, n * LANES : (n + 1) * LANES]
                        part[:, :, :, (c * 2 + n) * groups + j] = block.reshape(2, 2, 2, piece, LANES)
                return carry

            count = width // 256
            lax.fori_loop(count * q // 4, count * (q + 1) // 4, strip, 0)

    def input_grad(layer, s):
        first = spent[0]
        spent[0] += 4
        assert spent[0] - 1 + AHEAD < done[0]

        def quarter(q, carry):
            strips(layer, s, q)
            ar.tick(first + q)
            return carry

        lax.fori_loop(0, 4, quarter, 0)

    def settle(layer, s):
        if layer == 2:

            def put(first, v):
                grad[:, pl.ds(s * length + first, LANES)] = v

            sums[2].done(s, hidden // 16, put)
        else:

            def put(first, v):
                gxv[s, :, pl.ds(first, LANES)] = v

            sums[1].done(s, groups, put)
            gxv[s] = dot(reorder(piece, groups, True), gxv[s], NN).astype(BF16)

    def pool(s):
        first = s * length
        pool_backward(first, grad, pre, cell, first, dv, db1.at[s], work, edge, hidden, groups)

    size = rh.shape[1] // 2

    def third_of(t):
        return pl.ds(pl.multiple_of(t * third, LANES), third)

    def load_picked(t, tap):
        return load(sel_out.at[tap, third_of(t)], rh.at[:, pl.ds(pl.multiple_of(tap * size, LANES), size)], 15 + tap)

    def store_o(t, tap):
        return load(wo.at[tap], wo_out.at[tap, :, third_of(t)], 17 + tap)

    def outgate():
        first = spent[0]
        spent[0] += 6

        def step(i, carry):
            t, tap = i // 2, lax.rem(i, 2)
            load_picked(t, tap).wait()

            @pl.when(t > 0)
            def _():
                store_o(t - 1, tap).wait()

            values = rh[:, pl.ds(pl.multiple_of(tap * size, LANES), size)]
            wo[tap] = dot(dsel[...], values, NT).astype(BF16)
            store_o(t, tap).start()

            @pl.when(t + 1 < THIRDS)
            def _():
                load_picked(t + 1, tap).start()

            ar.tick(first + i)
            return carry

        lax.fori_loop(0, 2 * THIRDS, step, 0)

    load_rhs(2, 0).wait()
    units(2, 0)
    load_rhs(2, 1).start()
    load_d(2).wait()
    load_d(5).wait()
    load_w[2].wait()
    input_grad(2, 0)
    sums[2].start(0)
    tick()
    load_rhs(2, 1).wait()
    units(2, 1)
    load_rhs(2, 2).start()
    sums[2].cross(0)
    tick()
    input_grad(2, 1)
    load_w[1].start()
    sums[2].start(1)
    tick()
    sums[2].turn(0)
    tick()
    load_rhs(2, 2).wait()
    units(2, 2)
    sums[2].cross(1)
    tick()
    settle(2, 0)
    tick(2)
    load_p.wait()
    load_c.wait()
    pool(0)
    tick(2)
    sums[2].turn(1)
    gather.start()
    tick(2)
    settle(2, 1)
    for target in (here.core, here.across_x, here.across_y):
        signal(ready, target)
    pool(1)
    load_h.start()
    tick(2)
    load_rhs(1, 0).wait()
    units(1, 0)
    gather.relay()
    load_rhs(1, 1).start()
    dbv[here.z] = jnp.zeros((8, hidden), F32)
    for row, db in enumerate((db1, db2)):
        dbv[here.z, row : row + 1, :] = to_row(sum(db[s] for s in range(1, seqs)) + db[0])
    for copy in biases:
        copy.start()
    load_w[1].wait()
    pl.semaphore_wait(ready, 3)
    input_grad(1, 0)
    sums[1].start(0)
    load_rhs(1, 1).wait()
    units(1, 1)
    load_rhs(1, 2).start()
    sums[1].cross(0)
    tick()
    input_grad(1, 1)
    sums[1].start(1)
    tick()
    gather.share()
    tick()
    sums[1].cross(1)
    tick()
    sums[1].turn(0)
    tick(5)
    load_rhs(1, 2).wait()
    units(1, 2)
    tick(2)
    settle(1, 0)
    sums[1].turn(1)
    keep.wait()
    load_e.wait()
    for tap in range(2):
        load_picked(0, tap).start()
    tick(2)
    load_h.wait()
    eye = identity(LANES)
    for n in range(seqs * groups):
        turned = dot(eye, grad[:, pl.ds(n * LANES, LANES)], NT).astype(BF16)
        told[:, pl.ds(n * piece, piece), :] = turned.reshape(8, piece, hidden)
    for copy in spread:
        copy.start()
    tick(4)
    settle(1, 1)
    store_g.start()
    outgate()
    for copy in spread:
        copy.wait()
    back = reorder(piece, groups, True)
    for s in range(seqs):
        for b in range(8):
            block = heard[b, pl.ds(s * LANES, LANES), :]
            hv[s, :, b * hidden : (b + 1) * hidden] = dot(back, block, NN).astype(BF16)
    store_h.start()

    def more(n, carry):
        ar.tick(n)
        return carry

    lax.fori_loop(spent[0], ar.units + BEHIND + 2, more, 0)
    ar.drain()
    gather.drain()
    for copy in [store_g, store_h] + [store_o(THIRDS - 1, tap) for tap in range(2)] + biases:
        copy.wait()
    db_out[...] = dbv[0] + dbv[1] + dbv[2] + dbv[3]


def run_backward(d, h1, x, w2, w1, pre, cell, h, sel, dsel, db):
    (wide, width), total, seqs = w1.shape, d.shape[1], db.shape[0]
    hidden, length = wide // 6, total // seqs
    third, span, picked = width // THIRDS, length // 8, dsel.shape[1]
    rows, count = hidden // PIECES, length // 16 * hidden // LANES
    assert picked == length and length == 8 * LANES
    vmem = pl.BlockSpec(memory_space=pltpu.VMEM)
    scratch = [
        pltpu.VMEM((wide, total), BF16),
        pltpu.VMEM((wide, width), BF16),
        pltpu.VMEM((third, total), BF16),
        pltpu.VMEM((total, third), BF16),
        pltpu.VMEM((3 * hidden, total), BF16),
        pltpu.VMEM((hidden, total), F32),
        pltpu.VMEM((2, hidden, length), F32),
        pltpu.VMEM((2, hidden, LANES), F32),
        pltpu.VMEM((hidden, total), BF16),
        pltpu.VMEM((seqs, span, width), BF16),
        pltpu.VMEM((hidden, picked), BF16),
        pltpu.VMEM((2, hidden, third), BF16),
        pltpu.VMEM((8, total // 8, hidden), BF16),
        pltpu.VMEM((seqs, span, width), BF16),
        pltpu.VMEM((seqs, hidden, 1), F32),
        pltpu.VMEM((4, 8, hidden), F32),
        pltpu.VMEM((8, total // 8, hidden), BF16),
        pltpu.VMEM((OWN, hidden, third), BF16),
        pltpu.VMEM((SLOTS, rows, third), BF16),
        pltpu.VMEM((SLOTS, rows, third), BF16),
        pltpu.VMEM((SLOTS, rows, third), BF16),
        pltpu.VMEM((2, 2, 2, count, 16, LANES), BF16),
        pltpu.VMEM((seqs, 2, 2, count, 16, LANES), BF16),
        pltpu.VMEM((seqs, 2, count // 2, 16, LANES), BF16),
        pltpu.VMEM((seqs, 2, count // 2, 16, LANES), BF16),
        pltpu.VMEM((seqs, count // 2, 16, LANES), BF16),
        pltpu.VMEM((seqs, count // 2, 16, LANES), BF16),
        pltpu.SemaphoreType.DMA((7, SLOTS)),
        pltpu.SemaphoreType.DMA((2, seqs, 5, 2)),
        pltpu.SemaphoreType.DMA((4, 2)),
        pltpu.SemaphoreType.DMA((8, 2)),
        pltpu.SemaphoreType.DMA((11, 2)),
        pltpu.SemaphoreType.DMA((20,)),
    ]
    return pl.pallas_call(
        functools.partial(backward_kernel, seqs, hidden, length, width),
        name="backward",
        in_specs=[ANY] * 10 + [vmem],
        out_specs=[ANY] * 5 + [vmem],
        out_shape=[
            shape((12, hidden, width), BF16),
            shape((seqs, span, width), BF16),
            shape((seqs, span, width), BF16),
            shape((2, width, picked), BF16),
            shape((2, hidden, width), BF16),
            shape((8, hidden), F32),
        ],
        scratch_shapes=scratch + [pltpu.SemaphoreType.REGULAR] * 4,
        compiler_params=params(collective_id=1, has_side_effects=True),
    )(d, h1, x, w2, w1, pre, cell, h, sel, dsel, db)


def reorder(piece, groups, back):
    span = piece * groups
    a = lax.broadcasted_iota(jnp.int32, (span, span), 1 if back else 0)
    b = lax.broadcasted_iota(jnp.int32, (span, span), 0 if back else 1)
    return (b == lax.rem(a, piece) * groups + a // piece).astype(BF16)


def identity(n):
    rows, cols = (lax.broadcasted_iota(jnp.int32, (n, n), axis) for axis in range(2))
    return (rows == cols).astype(BF16)


def to_row(column):
    n = column.shape[0]
    same = lax.broadcasted_iota(jnp.int32, (n, n), 0) == lax.broadcasted_iota(jnp.int32, (n, n), 1)
    return jnp.sum(jnp.where(same, column, 0.0), axis=0, keepdims=True)


def to_column(row):
    n = row.shape[1]
    same = lax.broadcasted_iota(jnp.int32, (n, n), 0) == lax.broadcasted_iota(jnp.int32, (n, n), 1)
    return jnp.sum(jnp.where(same, row, 0.0), axis=1, keepdims=True)


class Gather:
    def __init__(self, here, region, sems, own=None):
        h, b = here, here.b
        own = own or (lambda half: region(b, half))
        bx, by = h.across_x["tm"], h.across_y["tm"]
        bd = bx + 4 - 8 * h.y
        plan = (
            (b, 1, h.across_x),
            (b, 0, h.across_y),
            (b, 0, h.across_x),
            (b, 1, h.across_y),
            (b, None, h.core),
            (bx, 1, h.across_y),
            (by, 0, h.across_x),
            (bx, None, h.core),
            (by, None, h.core),
            (bd, 0, h.core),
            (bd, 1, h.core),
        )
        self.copies = []
        for k, (block, half, to) in enumerate(plan):
            src = own(half) if k < 5 else region(block, half)
            self.copies.append(remote(src, region(block, half), sems.at[k, 0], sems.at[k, 1], to))

    def start(self):
        for k in range(5):
            self.copies[k].start()

    def relay(self):
        self.copies[0].wait_recv()
        self.copies[5].start()
        self.copies[1].wait_recv()
        self.copies[6].start()

    def share_near(self):
        self.copies[2].wait_recv()
        self.copies[7].start()
        self.copies[4].wait_recv()
        self.copies[7].wait_recv()

    def share_far(self):
        self.copies[3].wait_recv()
        self.copies[8].start()
        self.copies[6].wait_recv()
        self.copies[9].start()
        self.copies[5].wait_recv()
        self.copies[10].start()
        for k in (8, 9, 10):
            self.copies[k].wait_recv()

    def share(self):
        self.share_near()
        self.share_far()

    def drain(self):
        for copy in self.copies:
            copy.wait_send()


def forward_kernel(seqs, hidden, length, width, *refs):
    x_in, w1_in, w2_in, cot_in, b1_in, b2_in, starts = refs[:7]
    x_out, h1_out, pre_out, cell_out, h2_out, d_out, db_out, sel_out, dsel_out = refs[7:16]
    xg, hg, w, p, pre, cell, work, edge, dv, seed, grad, hv, raw, cot, sent, b1, b2, chosen, sel, dsel = refs[16:36]
    xsem, hsem, ssem, zsem, lsem = refs[36:]
    here = Here()
    groups = length // LANES
    piece = LANES // 8

    def columns_of(s):
        return pl.ds(aligned(s * length), length)

    def x_region(s):
        def region(b, half):
            js = pl.ds(0, groups) if half is None else pl.ds(half * (groups // 2), groups // 2)
            return xg.at[s, js, b]

        return region

    def h_region(s):
        def region(b, half):
            rows = pl.ds(0, hidden) if half is None else pl.ds(half * (hidden // 2), hidden // 2)
            return hg.at[b, rows, columns_of(s)]

        return region

    def load(src, dst, k):
        return pltpu.make_async_copy(src, dst, lsem.at[k])

    load_w1 = load(w1_in, w, 0)
    load_w2 = load(w2_in, w, 0)
    load_x = [load(x_in.at[s], raw.at[s], 1 + s) for s in range(seqs)]
    load_c = load(cot_in, cot, 14)
    store_x = [load(xg.at[s], x_out.at[s], 3 + s) for s in range(seqs)]
    store_h = [load(hg.at[:, :, columns_of(s)], h1_out.at[:, :, columns_of(s)], 5 + s) for s in range(seqs)]
    store_p = [load(pre.at[:, columns_of(s)], pre_out.at[:, columns_of(s)], 7 + s) for s in range(seqs)]
    store_c = [load(cell.at[:, columns_of(s)], cell_out.at[:, columns_of(s)], 9 + s) for s in range(seqs)]

    def store_d(s):
        return load(dv.at[s], d_out.at[:, columns_of(s)], 11 + s)

    store_o = load(hv, h2_out, 13)

    for copy in load_x:
        copy.start()
    load_w1.start()
    load_c.start()
    order = reorder(piece, groups, False)

    def place():
        for s in range(seqs):
            load_x[s].wait()
            xg[s, :, here.b] = dot(order, raw[s], NN).astype(BF16).reshape(groups, piece, width)

    meet(here.peers + here.line, place)
    xs = [Gather(here, x_region(s), xsem.at[s]) for s in range(seqs)]
    hs = [Gather(here, h_region(s), hsem.at[s]) for s in range(seqs)]

    def prepare():
        load_c.wait()
        for s in range(seqs):
            turned = dot(order, cot[s], NN).astype(BF16)
            for b in range(8):
                block = turned[:, b * hidden : (b + 1) * hidden]
                sent[b, s] = block.reshape(groups, piece, hidden)
        seed[:, :, pl.ds(0, 4)] = jnp.zeros((seqs, groups, 4, piece, hidden), BF16)
        for s in range(seqs):
            prepare_pick(s)
        b1[...] = to_column(b1_in[...][None, :])
        b2[...] = to_column(b2_in[...][None, :])

    late = [
        [
            remote(sent.at[peer["tm"], s], seed.at[s, :, here.b], ssem.at[d, s, 0], ssem.at[d, s, 1], peer)
            for d, peer in enumerate(here.peers, 1)
        ]
        for s in range(seqs)
    ]
    early = pltpu.make_async_copy(sent.at[here.b], seed.at[:, :, here.b], ssem.at[0, 0, 0])

    def first_products(s):
        def block(r):
            rows = pl.ds(r, hidden)
            p[rows, :] = dot(w[rows, :], xg[s].reshape(length, width), NT)

        tiles(6 * hidden, hidden, block)

    def second_products(s, near):
        y = here.y if near else 1 - here.y
        depth = pl.ds(pl.multiple_of(y * (width // 2), LANES), width // 2)

        def block(r):
            rows = pl.ds(r, hidden)
            rhs = hg[pl.ds(y * 4, 4), :, columns_of(s)].reshape(width // 2, length)
            got = dot(w[rows, depth], rhs, NN)
            p[rows, :] = got if near else p[rows, :] + got

        tiles(6 * hidden, hidden, block)

    def first_pool(s):
        first = s * length
        pool_forward(first, p, b1, pre, cell, first, hg.at[here.b], work.at[0], edge.at[0], hidden, groups)

    def second_pool(s):
        pool_forward(s * length, p, b2, pre, cell, s * length, hv, work.at[0], edge.at[0], hidden, groups)

    def incoming(s):
        eye = identity(LANES)
        lane = lax.broadcasted_iota(jnp.int32, (1, LANES), 1)
        for j in range(groups):
            block = seed[s, j].reshape(LANES, hidden)
            turned = dot(block, eye, TN)
            step = lane * groups + j
            keep = jnp.zeros((1, LANES), jnp.bool_)
            for k in range(starts.shape[1]):
                begin = starts[s, k]
                keep = jnp.logical_or(keep, jnp.logical_and(step >= begin, step < begin + CLUSTER))
            keep = jnp.broadcast_to(keep, (hidden, LANES))
            grad[:, pl.ds(s * length + j * LANES, LANES)] = jnp.where(keep, turned, 0.0).astype(BF16)

    def pool_back(s):
        pool_backward(s * length, grad, pre, cell, 0, dv.at[s], db_out.at[s], work, edge, hidden, groups, True)
        store_d(s).start()

    def cluster_steps(s):
        lane = lax.broadcasted_iota(jnp.int32, (1, LANES), 1)
        step = lax.rem(lane, CLUSTER)
        for k in range(starts.shape[1]):
            step = step + jnp.where(lane // CLUSTER == k, starts[s, k], 0)
        return lane, step

    def prepare_pick(s):
        _, step = cluster_steps(s)
        for j in range(groups):
            code = lax.broadcasted_iota(jnp.int32, (LANES, LANES), 0) * groups + j
            at = pl.ds(j * LANES, LANES)
            chosen[s, at, pl.ds(0, LANES)] = (code == step).astype(BF16)
            chosen[s, at, pl.ds(LANES, LANES)] = (code == step - 1).astype(BF16)

    def held(s, count):
        start = here.z * (seqs * LANES) + s * LANES
        return pl.ds(pl.multiple_of(start, LANES), count * LANES)

    def pick_hidden(s):
        got = dot(hg[here.b, :, columns_of(s)], chosen[s], NN).astype(BF16)
        for tap in range(2):
            sel[tap, :, held(s, 1)] = got[:, tap * LANES : (tap + 1) * LANES]

    def pick_grad(s):
        lane, step = cluster_steps(s)
        again = jnp.zeros((1, LANES), jnp.bool_)
        for k in range(starts.shape[1] - 1):
            begin = starts[s, k]
            inside = jnp.logical_and(step >= begin, step < begin + CLUSTER)
            again = jnp.logical_or(again, jnp.logical_and(inside, lane // CLUSTER > k))
        got = dot(dv[s, pl.ds(2 * hidden, hidden), :], chosen[s, :, pl.ds(0, LANES)], NN)
        dsel[:, held(s, 1)] = jnp.where(jnp.broadcast_to(again, (hidden, LANES)), 0.0, got).astype(BF16)

    spread_h = []
    spread_d = [[] for _ in range(seqs)]
    for d, peer in enumerate(here.line, 1):
        at = sel.at[:, :, held(0, seqs)]
        spread_h.append(remote(at, at, zsem.at[d, 0], zsem.at[d, 1], peer))
        for s in range(seqs):
            at = dsel.at[:, held(s, 1)]
            spread_d[s].append(remote(at, at, zsem.at[d, 2 + 2 * s], zsem.at[d, 3 + 2 * s], peer))
    store_s = load(sel, sel_out, 15)
    store_e = load(dsel, dsel_out, 16)

    xs[0].start()
    prepare()
    xs[0].relay()
    xs[1].start()
    xs[0].share()
    store_x[0].start()
    load_w1.wait()
    first_products(0)
    xs[1].relay()
    first_pool(0)
    hs[0].start()
    store_p[0].start()
    store_c[0].start()
    xs[1].share()
    store_x[1].start()
    first_products(1)
    load_w2.start()
    hs[0].relay()
    first_pool(1)
    hs[1].start()
    store_p[1].start()
    store_c[1].start()

    for s in range(seqs):
        pick_hidden(s)
    for copy in spread_h:
        copy.start()
    hs[0].share_near()
    load_w2.wait()
    second_products(0, True)
    hs[0].share_far()
    store_h[0].start()
    second_products(0, False)
    hs[1].relay()

    @pl.when(here.y == 1)
    def _():
        early.start()
        for copy in late[0] + late[1]:
            copy.start()

    store_p[0].wait()
    store_c[0].wait()
    second_pool(0)
    hs[1].share_near()
    second_products(1, True)
    hs[1].share_far()
    store_h[1].start()
    second_products(1, False)
    store_p[1].wait()
    store_c[1].wait()
    second_pool(1)
    store_o.start()

    @pl.when(here.y == 1)
    def _():
        early.wait()

    for s in range(seqs):
        for d, copy in enumerate(late[s], 1):

            @pl.when(lax.rem(here.b + 8 - d, 8) >= 4)
            def _(copy=copy):
                copy.wait_recv()

        incoming(s)
        outgate_backward(s * length, grad, pre, cell, dv.at[s], hidden, groups)
        pick_grad(s)
        for copy in spread_d[s]:
            copy.start()
    for copy in spread_h:
        copy.wait()
    store_s.start()

    def back(s, carry):
        pool_back(s)
        return carry

    lax.fori_loop(0, seqs, back, 0)
    @pl.when(here.y == 1)
    def _():
        for copy in late[0] + late[1]:
            copy.wait_send()

    for gather in xs + hs:
        gather.drain()
    for copy in spread_d[0] + spread_d[1]:
        copy.wait()
    store_e.start()
    for copy in store_x + store_h + [store_d(s) for s in range(seqs)] + [store_o, store_s, store_e]:
        copy.wait()


def run_forward(x, w1, b1, w2, b2, cotangent, starts):
    seqs, span, width = x.shape
    hidden, length, piece = w1.shape[0] // 6, span * 8, LANES // 8
    groups = length // LANES
    total, picked = seqs * length, 4 * seqs * LANES
    assert starts.shape[1] * CLUSTER == LANES
    vmem = pl.BlockSpec(memory_space=pltpu.VMEM)
    return pl.pallas_call(
        functools.partial(forward_kernel, seqs, hidden, length, width),
        name="forward",
        in_specs=[ANY, ANY, ANY, ANY, vmem, vmem, pl.BlockSpec(memory_space=pltpu.SMEM)],
        out_specs=[ANY, ANY, ANY, ANY, ANY, ANY, vmem, ANY, ANY],
        out_shape=[
            shape((seqs, groups, 8, piece, width), BF16),
            shape((8, hidden, total), BF16),
            shape((3 * hidden, total), BF16),
            shape((hidden, total), F32),
            shape((hidden, total), BF16),
            shape((6 * hidden, total), BF16),
            shape((seqs, hidden, 1), F32),
            shape((2, hidden, picked), BF16),
            shape((hidden, picked), BF16),
        ],
        scratch_shapes=[
            pltpu.VMEM((seqs, groups, 8, piece, width), BF16),
            pltpu.VMEM((8, hidden, total), BF16),
            pltpu.VMEM((6 * hidden, width), BF16),
            pltpu.VMEM((6 * hidden, length), F32),
            pltpu.VMEM((3 * hidden, total), BF16),
            pltpu.VMEM((hidden, total), F32),
            pltpu.VMEM((2, hidden, length), F32),
            pltpu.VMEM((2, hidden, LANES), F32),
            pltpu.VMEM((seqs, 6 * hidden, length), BF16),
            pltpu.VMEM((seqs, groups, 8, piece, hidden), BF16),
            pltpu.VMEM((hidden, total), BF16),
            pltpu.VMEM((hidden, total), BF16),
            pltpu.VMEM((seqs, span, width), BF16),
            pltpu.VMEM((seqs, span, width), BF16),
            pltpu.VMEM((8, seqs, groups, piece, hidden), BF16),
            pltpu.VMEM((hidden, 1), F32),
            pltpu.VMEM((hidden, 1), F32),
            pltpu.VMEM((seqs, length, 2 * LANES), BF16),
            pltpu.VMEM((2, hidden, picked), BF16),
            pltpu.VMEM((hidden, picked), BF16),
            pltpu.SemaphoreType.DMA((seqs, 11, 2)),
            pltpu.SemaphoreType.DMA((seqs, 11, 2)),
            pltpu.SemaphoreType.DMA((8, seqs, 2)),
            pltpu.SemaphoreType.DMA((4, 2 + 2 * seqs)),
            pltpu.SemaphoreType.DMA((17,)),
        ],
        compiler_params=params(collective_id=0, has_side_effects=True),
    )(x, w1, w2, cotangent, b1, b2, starts)


def finish_kernel(
    one_ref, two_ref, outgate_ref, h_ref, gx_ref, db_ref, wide_one_ref, wide_two_ref, h_out, gx_out, db1_out, db2_out
):
    i = pl.program_id(0)
    wide_one_ref[...] = one_ref[...].astype(F32)
    last = lax.rem(i, 3) == 2

    @pl.when(last)
    def _():
        wide_two_ref[...] = outgate_ref[...].astype(F32)

    @pl.when(jnp.logical_not(last))
    def _():
        wide_two_ref[...] = two_ref[...].astype(F32)

    h_out[...] = h_ref[...]
    gx_out[...] = gx_ref[...]
    db1_out[...] = db_ref[0]
    db2_out[...] = db_ref[1]


def finish(gw, outgate, h, gx, db):
    _, hidden, width = gw.shape
    total = h.shape[0] * h.shape[1]
    dims = (1, hidden, width)
    small = (total // 4, width)
    weights = pl.BlockSpec(dims, lambda i: (i, 0, 0))
    tokens = pl.BlockSpec(small, lambda i: (jnp.minimum(i, 3), 0))
    bias = pl.BlockSpec((hidden,), lambda i: (0,))
    return pl.pallas_call(
        finish_kernel,
        name="results",
        grid=(6,),
        in_specs=[
            weights,
            pl.BlockSpec(dims, lambda i: (6 + i - i % 3 // 2, 0, 0)),
            pl.BlockSpec(dims, lambda i: (i // 3, 0, 0)),
            tokens,
            tokens,
            pl.BlockSpec(db.shape, lambda i: (0, 0)),
        ],
        out_specs=[weights, weights, tokens, tokens, bias, bias],
        out_shape=[shape((6, hidden, width), F32)] * 2 + [shape((total, width), BF16)] * 2 + [shape((hidden,), F32)] * 2,
        compiler_params=params(),
    )(gw, gw, outgate, h.reshape(total, width), gx.reshape(total, width), db)


def per_device(line, inputs, weight_one, fbias_one, weight_two, fbias_two, cotangent, cluster_starts):
    seqs, span, width = inputs.shape
    count = lax.axis_size("tm")
    length = span * count
    groups = length // LANES
    piece = LANES // count
    hidden = weight_one.shape[2]
    total = seqs * length
    w1 = weight_one.reshape(6 * hidden, width)
    w2 = weight_two.reshape(6 * hidden, width)

    if line:
        x, h1, pre1, cell1, h2, d2, db2, *picked = run_forward(
            inputs, w1, fbias_one, w2, fbias_two, cotangent, cluster_starts
        )
        x, h1 = x.reshape(total, width), h1.reshape(width, total)
        gw, gx1, h2, _, wo, db = run_backward(d2, h1, x, w2, w1, pre1, cell1, h2, *picked, db2)
        gw1, gw2, h2, gx1, *db = finish(gw, wo, h2, gx1, db)
    else:
        x = inputs.reshape(seqs, piece, groups, width).transpose(0, 2, 1, 3)
        bias1, bias2 = fbias_one[:, None], fbias_two[:, None]
        seed = cotangent.reshape(seqs, piece, groups, count, hidden)
        steps = lax.axis_index("tm") * span + jnp.arange(span, dtype=jnp.int32)
        starts = cluster_starts[:, :, None]
        keep = jnp.any((steps >= starts) & (steps < starts + CLUSTER), axis=1)
        seed = jnp.where(keep.reshape(seqs, piece, groups, 1, 1), seed, jnp.zeros_like(seed))
        seed = lax.all_to_all(seed, "tm", split_axis=3, concat_axis=1, tiled=True)
        seed = seed.reshape(seqs, LANES, groups, hidden).transpose(3, 0, 2, 1).reshape(hidden, total)
        x = lax.all_gather(x, "tm", axis=2, tiled=True).reshape(total, width)
        pre1, cell1, h1 = run_first(seqs, w1, bias1, x)
        h1 = lax.all_gather(h1, "tm", axis=0, tiled=True)
        h2, d2, db2 = run_second(seqs, w2, bias2, h1, seed)
        h2 = h2.reshape(hidden, seqs, groups, count, piece)
        h2 = lax.all_to_all(h2, "tm", split_axis=3, concat_axis=0, tiled=True)
        h2 = h2.reshape(width, seqs, groups, piece).transpose(1, 3, 2, 0)
        gw2 = lax.psum(dot(d2, h1, NT).astype(BF16), "seq").astype(F32)
        gx2 = lax.psum_scatter(dot(w2, d2, TN).astype(BF16), "tm", scatter_dimension=0, tiled=True)
        d1, db1 = run_back(seqs, gx2, pre1, cell1)
        gw1 = lax.psum(dot(d1, x, NN).astype(BF16), "seq").astype(F32)
        gx1 = dot(d1, w1, TN).astype(BF16).reshape(seqs, groups, LANES, width)
        gx1 = lax.psum_scatter(gx1, "tm", scatter_dimension=2, tiled=True)
        gx1 = gx1.transpose(0, 2, 1, 3).reshape(seqs, span, width)
        db = lax.psum(jnp.stack([db1, db2]).sum(axis=(1, 3)), "seq")
    out, gx1 = h2.reshape(seqs, span, width), gx1.reshape(seqs, span, width)
    dims = weight_one.shape
    return (out, gx1, gw1.reshape(dims), db[0], gw2.reshape(dims), db[1])


def solution(mesh):
    placed = (
        P("seq", "tm", None),
        P(None, None, "tm", None),
        P("tm"),
        P(None, None, "tm", None),
        P("tm"),
        P("seq", "tm", None),
        P("seq", None),
    )
    return jax.shard_map(
        functools.partial(per_device, dict(mesh.shape) == {"seq": 4, "tm": 8}),
        mesh=mesh,
        in_specs=placed,
        out_specs=(
            P("seq", "tm", None),
            P("seq", "tm", None),
            P(None, None, "tm", None),
            P("tm"),
            P(None, None, "tm", None),
            P("tm"),
        ),
        check_vma=False,
    )
```
